256 devices in a mesh: seq: 16 (over y, x), chan: 16 (over z, core).
Axes of the slice: x: 4, y: 4, z: 8, core: 2. Of those that a mesh axis runs over, the one named last changes fastest.
Arguments:
- tokens: bfloat16 [57344, 2048], P('seq', 'chan'), may hold values from -6 to 6
- w_query: bfloat16 [2048, 256], replicated, may hold values from -0.125 to 0.125
- w_key: bfloat16 [2048, 256], replicated, may hold values from -0.125 to 0.125
- w_value: bfloat16 [2048, 2048], P(None, 'chan'), may hold values from -0.125 to 0.125
- w_out: bfloat16 [2048, 2048], replicated, may hold values from -0.125 to 0.125
- gain: float32 [2048], replicated, may hold values from 0.1 to 1.9
Outputs:
- mixed: bfloat16 [57344, 2048], P('seq', 'chan')
The draws below stay inside these ranges and needn't reach their ends.
All inputs are finite; a program needn't handle non-finite values.
Results may differ from the reference program's by a relative error of at most 0.019.
Values may be sent and summed in bfloat16 or wider, within the bound.
A program may use at most 128 MiB of HBM per device.

```python
import jax
import jax.numpy as jnp
from jax import lax

D = 2048
HEADS = 16
FEAT = 16
HEAD_DIM = 128
BLOCK = 896
LENGTH = 57344
HEAD_GROUPS = 16


def steps_of(own_key, extent, cuts, smallest, high):
    def one(position, shards_of):
        draws = jax.random.uniform(jax.random.fold_in(jax.random.fold_in(own_key, 6), position), (shards_of,), jnp.float32, smallest / len(cuts), high / len(cuts))
        return jnp.repeat(jnp.exp(draws), extent[position] // shards_of).reshape((-1,) + (1,) * (len(extent) - position - 1))

    level = one(*cuts[0])
    for cut in cuts[1:]:
        level = level * one(*cut)
    return level


def normal_values(key, extent, width, most, pieces=(), kind=jnp.bfloat16):
    result = jax.random.normal(key, extent, jnp.float32) * width
    if len(pieces) > 0:
        result = steps_of(key, extent, pieces, -0.22, 0.18) * result
    return jnp.clip(result, min=-most, max=most).astype(kind)


def setup_inputs(seed: int = 0) -> dict:
    key_list = jax.random.split(jax.random.key(seed), 7)
    return {
        "tokens": normal_values(key_list[0], (LENGTH, D), 1.0, 6.0, ((0, 16), (1, 16))),
        "w_query": normal_values(key_list[1], (D, HEADS * FEAT), D ** -0.5, 0.125),
        "w_key": normal_values(key_list[2], (D, HEADS * FEAT), D ** -0.5, 0.125),
        "w_value": normal_values(key_list[3], (D, HEADS * HEAD_DIM), D ** -0.5, 0.125, ((1, 16),)),
        "w_out": normal_values(key_list[4], (HEADS * HEAD_DIM, D), (HEADS * HEAD_DIM) ** -0.5, 0.125),
        "gain": jnp.clip(1.0 + 0.18 * jax.random.normal(key_list[5], (HEADS * HEAD_DIM,), jnp.float32), 0.1, 1.9),
    }


def feature_map(rows):
    first = jnp.ones(rows.shape[:-1] + (1,), jnp.float32)
    linear = rows * FEAT ** (-0.25)
    square = (rows[..., :, None] * rows[..., None, :]).reshape(rows.shape[:-1] + (FEAT * FEAT,)) * (2.0 * FEAT) ** (-0.5)
    return jnp.concatenate([first, linear, square], axis=-1)

def reference(tokens, w_query, w_key, w_value, w_out, gain):
    highest = lax.Precision.HIGHEST
    query = jnp.dot(tokens, w_query, preferred_element_type=jnp.float32).astype(jnp.bfloat16)
    key = jnp.dot(tokens, w_key, preferred_element_type=jnp.float32).astype(jnp.bfloat16)
    value = jnp.dot(tokens, w_value, preferred_element_type=jnp.float32).astype(jnp.bfloat16)
    count = LENGTH // BLOCK
    query_blocks = query.reshape(count, BLOCK, HEADS, FEAT)
    key_blocks = key.reshape(count, BLOCK, HEADS, FEAT)
    value_blocks = value.reshape(count, BLOCK, HEADS, HEAD_DIM)
    causal = jnp.arange(BLOCK)[:, None] >= jnp.arange(BLOCK)[None, :]

    def advance(state, block):
        query_now, key_now, value_now = block
        query_f = query_now.astype(jnp.float32)
        key_f = key_now.astype(jnp.float32)
        value_f = value_now.astype(jnp.float32)
        scores = jnp.einsum('thf,shf->hts', query_f, key_f) / jnp.sqrt(jnp.float32(FEAT))
        kernel = 1.0 + scores + 0.5 * scores * scores
        weights = lax.optimization_barrier(jnp.where(causal[None], kernel, 0.0).astype(jnp.bfloat16))
        intra = jnp.einsum('hts,she->the', weights.astype(jnp.float32), value_f)
        inter = jnp.einsum('thp,hpe->the', feature_map(query_f), state, precision=highest)
        grown = state + jnp.einsum('thp,the->hpe', feature_map(key_f), value_f, precision=highest)
        return (grown, intra + inter)
    start = jnp.zeros((HEADS, 1 + FEAT + FEAT * FEAT, HEAD_DIM), jnp.float32)
    final_state, numerator = lax.scan(advance, start, (query_blocks, key_blocks, value_blocks))
    numerator = numerator.reshape(LENGTH, HEADS, HEAD_DIM)
    mean_square = lax.optimization_barrier(jnp.mean(numerator * numerator, axis=-1, keepdims=True))
    hidden = (numerator * lax.rsqrt(mean_square + 1e-05) * gain.reshape(HEADS, HEAD_DIM)).astype(jnp.bfloat16)
    hidden = hidden.reshape(LENGTH, HEADS * HEAD_DIM)
    columns = HEADS * HEAD_DIM // HEAD_GROUPS
    total = jnp.zeros((LENGTH, D), jnp.float32)
    for group in range(HEAD_GROUPS):
        part = jnp.dot(hidden[:, group * columns:(group + 1) * columns], w_out[group * columns:(group + 1) * columns], preferred_element_type=jnp.float32)
        total = total + lax.optimization_barrier(part.astype(jnp.bfloat16)).astype(jnp.float32)
    return total.astype(jnp.bfloat16)
```

```python
import jax
import jax.numpy as jnp
from jax import lax
from jax.sharding import PartitionSpec as P

HEADS = 16
FEAT = 16
HEAD_DIM = 128
BLOCK = 896


def feature_parts(rows):
    linear = rows * FEAT ** (-0.25)
    square = (rows[..., :, None] * rows[..., None, :]).reshape(rows.shape[:-1] + (FEAT * FEAT,)) * (
        2.0 * FEAT
    ) ** (-0.5)
    return (linear, square)


def attend(query_rows, key_rows, value_rows, gain_mine, my_slab):
    highest = lax.Precision.HIGHEST
    tok_rows, per_group, _ = value_rows.shape
    blocks = tok_rows // BLOCK
    query_blocks = query_rows.reshape(blocks, BLOCK, per_group, FEAT)
    key_blocks = key_rows.reshape(blocks, BLOCK, per_group, FEAT)
    value_blocks = value_rows.reshape(blocks, BLOCK, per_group, HEAD_DIM)
    value_f32 = value_blocks.astype(jnp.float32)
    key_linear, key_square = feature_parts(key_blocks.astype(jnp.float32))
    own_zero = jnp.sum(value_f32, axis=1)[:, :, None, :]
    own_one = jnp.einsum("bthf,bthe->bhfe", key_linear, value_f32, precision=highest)
    own_two = jnp.einsum("bthf,bthe->bhfe", key_square, value_f32, precision=highest)
    own = jnp.concatenate([own_zero, own_one, own_two], axis=2)
    slab_total = jnp.sum(own, axis=0)
    pieces = lax.all_gather(
        slab_total[None].astype(jnp.bfloat16), "seq", axis=0, tiled=True
    ).astype(jnp.float32)
    count = pieces.shape[0]
    earlier_mask = jnp.arange(count, dtype=jnp.int32) < my_slab
    prefix = jnp.sum(jnp.where(earlier_mask[:, None, None, None], pieces, 0.0), axis=0)
    earlier = jnp.concatenate([jnp.zeros_like(own[:1]), jnp.cumsum(own, axis=0)[:-1]], axis=0) + prefix[None]
    query_linear, query_square = feature_parts(query_blocks.astype(jnp.float32))
    inter = earlier[:, :, 0][:, None] + jnp.einsum(
        "bthf,bhfe->bthe", query_linear, earlier[:, :, 1 : 1 + FEAT], precision=highest
    )
    inter = inter + jnp.einsum(
        "bthf,bhfe->bthe", query_square, earlier[:, :, 1 + FEAT :], precision=highest
    )
    scores = jnp.einsum(
        "bthf,bshf->bhts", query_blocks, key_blocks, preferred_element_type=jnp.float32
    ) * FEAT ** (-0.5)
    kernel = 1.0 + scores + 0.5 * scores * scores
    causal = jnp.arange(BLOCK)[:, None] >= jnp.arange(BLOCK)[None, :]
    weights = jnp.where(causal, kernel, 0.0).astype(jnp.bfloat16)
    intra = jnp.einsum("bhts,bshe->bthe", weights, value_blocks, preferred_element_type=jnp.float32)
    numerator = (intra + inter).reshape(tok_rows, per_group, HEAD_DIM)
    mean_square = jnp.mean(numerator * numerator, axis=-1, keepdims=True)
    hidden = (numerator * lax.rsqrt(mean_square + 1e-05) * gain_mine).astype(jnp.bfloat16)
    return hidden.reshape(tok_rows, per_group * HEAD_DIM)


def per_device(tokens, w_query, w_key, w_value, w_out, gain):
    groups = lax.axis_size("chan")
    per_group = HEADS // groups
    my_group = lax.axis_index("chan")
    my_slab = lax.axis_index("seq")
    value_full = lax.all_gather(w_value, "chan", axis=1, tiled=True)
    rows = lax.all_to_all(tokens, "chan", 0, 1, tiled=True)
    chunk = rows.shape[0]
    weight = jnp.concatenate([w_query, w_key, value_full], axis=1)
    proj = jnp.dot(rows, weight, preferred_element_type=jnp.float32).astype(jnp.bfloat16)
    qk_cols = HEADS * FEAT
    query = proj[:, :qk_cols].reshape(chunk, groups, per_group * FEAT)
    key = proj[:, qk_cols : 2 * qk_cols].reshape(chunk, groups, per_group * FEAT)
    value = proj[:, 2 * qk_cols :].reshape(chunk, groups, per_group * HEAD_DIM)
    packed = jnp.concatenate([query, key, value], axis=2)
    mine = lax.all_to_all(packed, "chan", 1, 0, tiled=True)
    tok_rows = mine.shape[0]
    qf = per_group * FEAT
    query_rows = mine[:, 0, :qf].reshape(tok_rows, per_group, FEAT)
    key_rows = mine[:, 0, qf : 2 * qf].reshape(tok_rows, per_group, FEAT)
    value_rows = mine[:, 0, 2 * qf :].reshape(tok_rows, per_group, HEAD_DIM)
    value_cols = per_group * HEAD_DIM
    gain_mine = lax.dynamic_slice_in_dim(gain, my_group * value_cols, value_cols, 0).reshape(
        per_group, HEAD_DIM
    )
    hidden = attend(query_rows, key_rows, value_rows, gain_mine, my_slab)
    hidden_rows = lax.all_to_all(hidden, "chan", 0, 1, tiled=True)
    mixed_rows = jnp.dot(hidden_rows, w_out, preferred_element_type=jnp.float32).astype(jnp.bfloat16)
    return lax.all_to_all(mixed_rows, "chan", 1, 0, tiled=True)


def solution(mesh):
    return jax.shard_map(
        per_device,
        mesh=mesh,
        in_specs=(P("seq", "chan"), P(), P(), P(None, "chan"), P(), P()),
        out_specs=P("seq", "chan"),
        check_vma=False,
    )
```

```python
import jax
import jax.numpy as jnp
from jax import lax
from jax.experimental import pallas as pl
from jax.experimental.pallas import tpu as pltpu
from jax.sharding import PartitionSpec as P

MESH = pl.DeviceIdType.MESH

HEADS = 16
FEAT = 16
HEAD_DIM = 128
BLOCK = 896


def feature_parts(rows):
    linear = rows * FEAT ** (-0.25)
    square = (rows[..., :, None] * rows[..., None, :]).reshape(rows.shape[:-1] + (FEAT * FEAT,)) * (
        2.0 * FEAT
    ) ** (-0.5)
    return (linear, square)


def exchange_kernel(x_ref, y_ref, buf, send_sem, recv_sem, own_sem):
    n = x_ref.shape[0]
    me = lax.axis_index("chan")
    slab = lax.axis_index("seq")
    barrier = pltpu.get_barrier_semaphore()
    for step in range(1, n):
        peer = lax.rem(me + step, n)
        pl.semaphore_signal(barrier, inc=1, device_id=(slab, peer), device_id_type=MESH)
    pl.semaphore_wait(barrier, n - 1)
    own = pltpu.make_async_copy(x_ref.at[me], buf.at[me], own_sem)
    own.start()
    sends = []
    for step in range(1, n):
        peer = lax.rem(me + step, n)
        copy = pltpu.make_async_remote_copy(
            src_ref=x_ref.at[peer],
            dst_ref=buf.at[me],
            send_sem=send_sem.at[peer],
            recv_sem=recv_sem.at[me],
            device_id=(slab, peer),
            device_id_type=MESH,
        )
        copy.start()
        sends.append(copy)
    for step in range(1, n):
        source = lax.rem(me + n - step, n)
        pltpu.make_async_remote_copy(
            src_ref=x_ref.at[source],
            dst_ref=buf.at[source],
            send_sem=send_sem.at[source],
            recv_sem=recv_sem.at[source],
            device_id=(slab, source),
            device_id_type=MESH,
        ).wait_recv()
    for copy in sends:
        copy.wait_send()
    own.wait()
    y_ref[...] = buf[...]


def exchange(x, collective_id):
    n = x.shape[0]
    return pl.pallas_call(
        exchange_kernel,
        out_shape=jax.ShapeDtypeStruct(x.shape, x.dtype),
        in_specs=[pl.BlockSpec(memory_space=pltpu.VMEM)],
        out_specs=pl.BlockSpec(memory_space=pltpu.VMEM),
        scratch_shapes=[
            pltpu.VMEM(x.shape, x.dtype),
            pltpu.SemaphoreType.DMA((n,)),
            pltpu.SemaphoreType.DMA((n,)),
            pltpu.SemaphoreType.DMA(()),
        ],
        compiler_params=pltpu.CompilerParams(collective_id=collective_id, has_side_effects=True),
    )(x)


def split_rows(x, groups, collective_id):
    rows, cols = x.shape
    got = exchange(x.reshape(groups, rows // groups, cols), collective_id)
    return got.transpose(1, 0, 2).reshape(rows // groups, groups * cols)


def split_cols(x, groups, collective_id):
    rows, _, cols = x.shape
    got = exchange(x.transpose(1, 0, 2), collective_id)
    return got.reshape(groups * rows, cols)


def attend(query_rows, key_rows, value_rows, gain_mine, my_slab):
    highest = lax.Precision.HIGHEST
    tok_rows, per_group, _ = value_rows.shape
    blocks = tok_rows // BLOCK
    query_blocks = query_rows.reshape(blocks, BLOCK, per_group, FEAT)
    key_blocks = key_rows.reshape(blocks, BLOCK, per_group, FEAT)
    value_blocks = value_rows.reshape(blocks, BLOCK, per_group, HEAD_DIM)
    value_f32 = value_blocks.astype(jnp.float32)
    key_linear, key_square = feature_parts(key_blocks.astype(jnp.float32))
    own_zero = jnp.sum(value_f32, axis=1)[:, :, None, :]
    own_one = jnp.einsum("bthf,bthe->bhfe", key_linear, value_f32, precision=highest)
    own_two = jnp.einsum("bthf,bthe->bhfe", key_square, value_f32, precision=highest)
    own = jnp.concatenate([own_zero, own_one, own_two], axis=2)
    slab_total = jnp.sum(own, axis=0)
    pieces = lax.all_gather(
        slab_total[None].astype(jnp.bfloat16), "seq", axis=0, tiled=True
    ).astype(jnp.float32)
    count = pieces.shape[0]
    earlier_mask = jnp.arange(count, dtype=jnp.int32) < my_slab
    prefix = jnp.sum(jnp.where(earlier_mask[:, None, None, None], pieces, 0.0), axis=0)
    earlier = jnp.concatenate([jnp.zeros_like(own[:1]), jnp.cumsum(own, axis=0)[:-1]], axis=0) + prefix[None]
    query_linear, query_square = feature_parts(query_blocks.astype(jnp.float32))
    inter = earlier[:, :, 0][:, None] + jnp.einsum(
        "bthf,bhfe->bthe", query_linear, earlier[:, :, 1 : 1 + FEAT], precision=highest
    )
    inter = inter + jnp.einsum(
        "bthf,bhfe->bthe", query_square, earlier[:, :, 1 + FEAT :], precision=highest
    )
    scores = jnp.einsum(
        "bthf,bshf->bhts", query_blocks, key_blocks, preferred_element_type=jnp.float32
    ) * FEAT ** (-0.5)
    kernel = 1.0 + scores + 0.5 * scores * scores
    causal = jnp.arange(BLOCK)[:, None] >= jnp.arange(BLOCK)[None, :]
    weights = jnp.where(causal, kernel, 0.0).astype(jnp.bfloat16)
    intra = jnp.einsum("bhts,bshe->bthe", weights, value_blocks, preferred_element_type=jnp.float32)
    numerator = (intra + inter).reshape(tok_rows, per_group, HEAD_DIM)
    mean_square = jnp.mean(numerator * numerator, axis=-1, keepdims=True)
    hidden = (numerator * lax.rsqrt(mean_square + 1e-05) * gain_mine).astype(jnp.bfloat16)
    return hidden.reshape(tok_rows, per_group * HEAD_DIM)


def per_device(tokens, w_query, w_key, w_value, w_out, gain):
    groups = lax.axis_size("chan")
    per_group = HEADS // groups
    my_group = lax.axis_index("chan")
    my_slab = lax.axis_index("seq")
    value_full = lax.all_gather(w_value, "chan", axis=1, tiled=True)
    rows = split_rows(tokens, groups, 1)
    chunk = rows.shape[0]
    weight = jnp.concatenate([w_query, w_key, value_full], axis=1)
    proj = jnp.dot(rows, weight, preferred_element_type=jnp.float32).astype(jnp.bfloat16)
    qk_cols = HEADS * FEAT
    query = proj[:, :qk_cols].reshape(chunk, groups, per_group * FEAT)
    key = proj[:, qk_cols : 2 * qk_cols].reshape(chunk, groups, per_group * FEAT)
    value = proj[:, 2 * qk_cols :].reshape(chunk, groups, per_group * HEAD_DIM)
    packed = jnp.concatenate([query, key, value], axis=2)
    mine = split_cols(packed, groups, 2)[:, None]
    tok_rows = mine.shape[0]
    qf = per_group * FEAT
    query_rows = mine[:, 0, :qf].reshape(tok_rows, per_group, FEAT)
    key_rows = mine[:, 0, qf : 2 * qf].reshape(tok_rows, per_group, FEAT)
    value_rows = mine[:, 0, 2 * qf :].reshape(tok_rows, per_group, HEAD_DIM)
    value_cols = per_group * HEAD_DIM
    gain_mine = lax.dynamic_slice_in_dim(gain, my_group * value_cols, value_cols, 0).reshape(
        per_group, HEAD_DIM
    )
    hidden = attend(query_rows, key_rows, value_rows, gain_mine, my_slab)
    hidden_rows = split_rows(hidden, groups, 3)
    mixed_rows = jnp.dot(hidden_rows, w_out, preferred_element_type=jnp.float32).astype(jnp.bfloat16)
    return split_cols(mixed_rows.reshape(chunk, groups, -1), groups, 4)


def solution(mesh):
    return jax.shard_map(
        per_device,
        mesh=mesh,
        in_specs=(P("seq", "chan"), P(), P(), P(None, "chan"), P(), P()),
        out_specs=P("seq", "chan"),
        check_vma=False,
    )
```

```python
import jax
import jax.numpy as jnp
from jax import lax
from jax.experimental import pallas as pl
from jax.experimental.pallas import tpu as pltpu
from jax.sharding import PartitionSpec as P

MESH = pl.DeviceIdType.MESH
CHAN = ("z", "core")


def chan_index():
    return lax.axis_index("z") * lax.axis_size("core") + lax.axis_index("core")


def chan_device(slab, peer):
    cores = lax.axis_size("core")
    return (slab, peer // cores, peer % cores)

HEADS = 16
FEAT = 16
HEAD_DIM = 128
BLOCK = 896


def feature_parts(rows):
    linear = rows * FEAT ** (-0.25)
    square = (rows[..., :, None] * rows[..., None, :]).reshape(rows.shape[:-1] + (FEAT * FEAT,)) * (
        2.0 * FEAT
    ) ** (-0.5)
    return (linear, square)


def exchange_kernel(x_ref, y_ref, buf, send_sem, recv_sem, own_sem):
    n = x_ref.shape[0]
    me = chan_index()
    slab = lax.axis_index("seq")
    barrier = pltpu.get_barrier_semaphore()
    for step in range(1, n):
        peer = lax.rem(me + step, n)
        pl.semaphore_signal(barrier, inc=1, device_id=chan_device(slab, peer), device_id_type=MESH)
    pl.semaphore_wait(barrier, n - 1)
    own = pltpu.make_async_copy(x_ref.at[me], buf.at[me], own_sem)
    own.start()
    sends = []
    for step in range(1, n):
        peer = lax.rem(me + step, n)
        copy = pltpu.make_async_remote_copy(
            src_ref=x_ref.at[peer],
            dst_ref=buf.at[me],
            send_sem=send_sem.at[peer],
            recv_sem=recv_sem.at[me],
            device_id=chan_device(slab, peer),
            device_id_type=MESH,
        )
        copy.start()
        sends.append(copy)
    for step in range(1, n):
        source = lax.rem(me + n - step, n)
        pltpu.make_async_remote_copy(
            src_ref=x_ref.at[source],
            dst_ref=buf.at[source],
            send_sem=send_sem.at[source],
            recv_sem=recv_sem.at[source],
            device_id=chan_device(slab, source),
            device_id_type=MESH,
        ).wait_recv()
    for copy in sends:
        copy.wait_send()
    own.wait()
    y_ref[...] = buf[...]


def exchange(x, collective_id):
    n = x.shape[0]
    return pl.pallas_call(
        exchange_kernel,
        out_shape=jax.ShapeDtypeStruct(x.shape, x.dtype),
        in_specs=[pl.BlockSpec(memory_space=pltpu.VMEM)],
        out_specs=pl.BlockSpec(memory_space=pltpu.VMEM),
        scratch_shapes=[
            pltpu.VMEM(x.shape, x.dtype),
            pltpu.SemaphoreType.DMA((n,)),
            pltpu.SemaphoreType.DMA((n,)),
            pltpu.SemaphoreType.DMA(()),
        ],
        compiler_params=pltpu.CompilerParams(collective_id=collective_id, has_side_effects=True),
    )(x)


def gather_kernel(x_ref, y_ref, buf, send_sem, recv_sem, own_sem):
    n = buf.shape[0]
    me = lax.axis_index("seq")
    here = (lax.axis_index("z"), lax.axis_index("core"))
    barrier = pltpu.get_barrier_semaphore()
    for step in range(1, n):
        peer = lax.rem(me + step, n)
        pl.semaphore_signal(barrier, inc=1, device_id=(peer,) + here, device_id_type=MESH)
    pl.semaphore_wait(barrier, n - 1)
    own = pltpu.make_async_copy(x_ref, buf.at[me], own_sem)
    own.start()
    sends = []
    for step in range(1, n):
        peer = lax.rem(me + step, n)
        copy = pltpu.make_async_remote_copy(
            src_ref=x_ref,
            dst_ref=buf.at[me],
            send_sem=send_sem.at[peer],
            recv_sem=recv_sem.at[me],
            device_id=(peer,) + here,
            device_id_type=MESH,
        )
        copy.start()
        sends.append(copy)
    for step in range(1, n):
        source = lax.rem(me + n - step, n)
        pltpu.make_async_remote_copy(
            src_ref=x_ref,
            dst_ref=buf.at[source],
            send_sem=send_sem.at[source],
            recv_sem=recv_sem.at[source],
            device_id=(source,) + here,
            device_id_type=MESH,
        ).wait_recv()
    for copy in sends:
        copy.wait_send()
    own.wait()
    y_ref[...] = buf[...]


def gather_seq(x, slabs, collective_id):
    shape = (slabs,) + x.shape
    return pl.pallas_call(
        gather_kernel,
        out_shape=jax.ShapeDtypeStruct(shape, x.dtype),
        in_specs=[pl.BlockSpec(memory_space=pltpu.VMEM)],
        out_specs=pl.BlockSpec(memory_space=pltpu.VMEM),
        scratch_shapes=[
            pltpu.VMEM(shape, x.dtype),
            pltpu.SemaphoreType.DMA((slabs,)),
            pltpu.SemaphoreType.DMA((slabs,)),
            pltpu.SemaphoreType.DMA(()),
        ],
        compiler_params=pltpu.CompilerParams(collective_id=collective_id, has_side_effects=True),
    )(x)


def split_rows(x, groups, collective_id):
    rows, cols = x.shape
    got = exchange(x.reshape(groups, rows // groups, cols), collective_id)
    return got.transpose(1, 0, 2).reshape(rows // groups, groups * cols)


def split_cols(x, groups, collective_id):
    rows, _, cols = x.shape
    got = exchange(x.transpose(1, 0, 2), collective_id)
    return got.reshape(groups * rows, cols)


def attend(query_rows, key_rows, value_rows, gain_mine, my_slab):
    highest = lax.Precision.HIGHEST
    tok_rows, per_group, _ = value_rows.shape
    blocks = tok_rows // BLOCK
    query_blocks = query_rows.reshape(blocks, BLOCK, per_group, FEAT)
    key_blocks = key_rows.reshape(blocks, BLOCK, per_group, FEAT)
    value_blocks = value_rows.reshape(blocks, BLOCK, per_group, HEAD_DIM)
    value_f32 = value_blocks.astype(jnp.float32)
    key_linear, key_square = feature_parts(key_blocks.astype(jnp.float32))
    own_zero = jnp.sum(value_f32, axis=1)[:, :, None, :]
    own_one = jnp.einsum("bthf,bthe->bhfe", key_linear, value_f32, precision=highest)
    own_two = jnp.einsum("bthf,bthe->bhfe", key_square, value_f32, precision=highest)
    own = jnp.concatenate([own_zero, own_one, own_two], axis=2)
    slab_total = jnp.sum(own, axis=0)
    state_rows = slab_total.shape[0] * slab_total.shape[1]
    pieces = gather_seq(
        slab_total.astype(jnp.bfloat16).reshape(state_rows, HEAD_DIM), lax.axis_size("seq"), 5
    ).astype(jnp.float32).reshape((-1,) + slab_total.shape)
    count = pieces.shape[0]
    earlier_mask = jnp.arange(count, dtype=jnp.int32) < my_slab
    prefix = jnp.sum(jnp.where(earlier_mask[:, None, None, None], pieces, 0.0), axis=0)
    earlier = jnp.concatenate([jnp.zeros_like(own[:1]), jnp.cumsum(own, axis=0)[:-1]], axis=0) + prefix[None]
    query_linear, query_square = feature_parts(query_blocks.astype(jnp.float32))
    inter = earlier[:, :, 0][:, None] + jnp.einsum(
        "bthf,bhfe->bthe", query_linear, earlier[:, :, 1 : 1 + FEAT], precision=highest
    )
    inter = inter + jnp.einsum(
        "bthf,bhfe->bthe", query_square, earlier[:, :, 1 + FEAT :], precision=highest
    )
    scores = jnp.einsum(
        "bthf,bshf->bhts", query_blocks, key_blocks, preferred_element_type=jnp.float32
    ) * FEAT ** (-0.5)
    kernel = 1.0 + scores + 0.5 * scores * scores
    causal = jnp.arange(BLOCK)[:, None] >= jnp.arange(BLOCK)[None, :]
    weights = jnp.where(causal, kernel, 0.0).astype(jnp.bfloat16)
    intra = jnp.einsum("bhts,bshe->bthe", weights, value_blocks, preferred_element_type=jnp.float32)
    numerator = (intra + inter).reshape(tok_rows, per_group, HEAD_DIM)
    mean_square = jnp.mean(numerator * numerator, axis=-1, keepdims=True)
    hidden = (numerator * lax.rsqrt(mean_square + 1e-05) * gain_mine).astype(jnp.bfloat16)
    return hidden.reshape(tok_rows, per_group * HEAD_DIM)


def per_device(tokens, w_query, w_key, w_value, w_out, gain):
    groups = lax.axis_size(CHAN)
    per_group = HEADS // groups
    my_group = chan_index()
    my_slab = lax.axis_index("seq")
    value_z = lax.all_gather(w_value, "z", axis=0)
    value_all = lax.all_gather(value_z, "core", axis=0)
    rows = split_rows(tokens, groups, 1)
    chunk = rows.shape[0]
    query = jnp.dot(rows, w_query, preferred_element_type=jnp.float32).astype(jnp.bfloat16)
    key = jnp.dot(rows, w_key, preferred_element_type=jnp.float32).astype(jnp.bfloat16)
    value = jnp.einsum("tf,czfe->tzce", rows, value_all, preferred_element_type=jnp.float32)
    value = value.astype(jnp.bfloat16).reshape(chunk, groups, per_group * HEAD_DIM)
    query = query.reshape(chunk, groups, per_group * FEAT)
    key = key.reshape(chunk, groups, per_group * FEAT)
    packed = jnp.concatenate([query, key, value], axis=2)
    width = packed.shape[2]
    lanes = chunk * width // HEAD_DIM
    sent = exchange(packed.transpose(1, 0, 2).reshape(groups, lanes, HEAD_DIM), 2)
    mine = sent.reshape(groups * chunk, 1, width)
    tok_rows = mine.shape[0]
    qf = per_group * FEAT
    query_rows = mine[:, 0, :qf].reshape(tok_rows, per_group, FEAT)
    key_rows = mine[:, 0, qf : 2 * qf].reshape(tok_rows, per_group, FEAT)
    value_rows = mine[:, 0, 2 * qf :].reshape(tok_rows, per_group, HEAD_DIM)
    value_cols = per_group * HEAD_DIM
    gain_mine = lax.dynamic_slice_in_dim(gain, my_group * value_cols, value_cols, 0).reshape(
        per_group, HEAD_DIM
    )
    hidden = attend(query_rows, key_rows, value_rows, gain_mine, my_slab)
    hidden_rows = split_rows(hidden, groups, 3)
    mixed_rows = jnp.dot(hidden_rows, w_out, preferred_element_type=jnp.float32).astype(jnp.bfloat16)
    return split_cols(mixed_rows.reshape(chunk, groups, -1), groups, 4)


def solution(mesh):
    seq, chan = mesh.devices.shape
    cores = 2 if chan % 2 == 0 else 1
    split = jax.sharding.Mesh(mesh.devices.reshape(seq, chan // cores, cores), ("seq", "z", "core"))
    return jax.shard_map(
        per_device,
        mesh=split,
        in_specs=(P("seq", CHAN), P(), P(), P(None, CHAN), P(), P()),
        out_specs=P("seq", CHAN),
        check_vma=False,
    )
```

```python
import jax
import jax.numpy as jnp
from jax import lax
from jax.experimental import pallas as pl
from jax.experimental.pallas import tpu as pltpu
from jax.sharding import PartitionSpec as P

MESH = pl.DeviceIdType.MESH
CHAN = ("z", "core")


def chan_index():
    return lax.axis_index("z") * lax.axis_size("core") + lax.axis_index("core")


def chan_device(slab, peer):
    cores = lax.axis_size("core")
    return (slab, peer // cores, peer % cores)

HEADS = 16
FEAT = 16
HEAD_DIM = 128
BLOCK = 896


def feature_parts(rows):
    linear = rows * FEAT ** (-0.25)
    square = (rows[..., :, None] * rows[..., None, :]).reshape(rows.shape[:-1] + (FEAT * FEAT,)) * (
        2.0 * FEAT
    ) ** (-0.5)
    return (linear, square)


def exchange_kernel(x_ref, y_ref, buf, send_sem, recv_sem, own_sem):
    n = x_ref.shape[0]
    me = chan_index()
    slab = lax.axis_index("seq")
    barrier = pltpu.get_barrier_semaphore()
    for step in range(1, n):
        peer = lax.rem(me + step, n)
        pl.semaphore_signal(barrier, inc=1, device_id=chan_device(slab, peer), device_id_type=MESH)
    pl.semaphore_wait(barrier, n - 1)
    own = pltpu.make_async_copy(x_ref.at[me], buf.at[me], own_sem)
    own.start()
    sends = []
    for step in range(1, n):
        peer = lax.rem(me + step, n)
        copy = pltpu.make_async_remote_copy(
            src_ref=x_ref.at[peer],
            dst_ref=buf.at[me],
            send_sem=send_sem.at[peer],
            recv_sem=recv_sem.at[me],
            device_id=chan_device(slab, peer),
            device_id_type=MESH,
        )
        copy.start()
        sends.append(copy)
    for step in range(1, n):
        source = lax.rem(me + n - step, n)
        pltpu.make_async_remote_copy(
            src_ref=x_ref.at[source],
            dst_ref=buf.at[source],
            send_sem=send_sem.at[source],
            recv_sem=recv_sem.at[source],
            device_id=chan_device(slab, source),
            device_id_type=MESH,
        ).wait_recv()
    for copy in sends:
        copy.wait_send()
    own.wait()
    y_ref[...] = buf[...]


def exchange(x, collective_id):
    n = x.shape[0]
    return pl.pallas_call(
        exchange_kernel,
        out_shape=jax.ShapeDtypeStruct(x.shape, x.dtype),
        in_specs=[pl.BlockSpec(memory_space=pltpu.VMEM)],
        out_specs=pl.BlockSpec(memory_space=pltpu.VMEM),
        scratch_shapes=[
            pltpu.VMEM(x.shape, x.dtype),
            pltpu.SemaphoreType.DMA((n,)),
            pltpu.SemaphoreType.DMA((n,)),
            pltpu.SemaphoreType.DMA(()),
        ],
        compiler_params=pltpu.CompilerParams(collective_id=collective_id, has_side_effects=True),
    )(x)


def gather_kernel(x_ref, y_ref, buf, send_sem, recv_sem, own_sem):
    n = buf.shape[0]
    me = lax.axis_index("seq")
    here = (lax.axis_index("z"), lax.axis_index("core"))
    barrier = pltpu.get_barrier_semaphore()
    for step in range(1, n):
        peer = lax.rem(me + step, n)
        pl.semaphore_signal(barrier, inc=1, device_id=(peer,) + here, device_id_type=MESH)
    pl.semaphore_wait(barrier, n - 1)
    own = pltpu.make_async_copy(x_ref, buf.at[me], own_sem)
    own.start()
    sends = []
    for step in range(1, n):
        peer = lax.rem(me + step, n)
        copy = pltpu.make_async_remote_copy(
            src_ref=x_ref,
            dst_ref=buf.at[me],
            send_sem=send_sem.at[peer],
            recv_sem=recv_sem.at[me],
            device_id=(peer,) + here,
            device_id_type=MESH,
        )
        copy.start()
        sends.append(copy)
    for step in range(1, n):
        source = lax.rem(me + n - step, n)
        pltpu.make_async_remote_copy(
            src_ref=x_ref,
            dst_ref=buf.at[source],
            send_sem=send_sem.at[source],
            recv_sem=recv_sem.at[source],
            device_id=(source,) + here,
            device_id_type=MESH,
        ).wait_recv()
    for copy in sends:
        copy.wait_send()
    own.wait()
    y_ref[...] = buf[...]


def gather_seq(x, slabs, collective_id):
    shape = (slabs,) + x.shape
    return pl.pallas_call(
        gather_kernel,
        out_shape=jax.ShapeDtypeStruct(shape, x.dtype),
        in_specs=[pl.BlockSpec(memory_space=pltpu.VMEM)],
        out_specs=pl.BlockSpec(memory_space=pltpu.VMEM),
        scratch_shapes=[
            pltpu.VMEM(shape, x.dtype),
            pltpu.SemaphoreType.DMA((slabs,)),
            pltpu.SemaphoreType.DMA((slabs,)),
            pltpu.SemaphoreType.DMA(()),
        ],
        compiler_params=pltpu.CompilerParams(collective_id=collective_id, has_side_effects=True),
    )(x)


def swap_kernel(x_ref, y_ref, send_sem, recv_sem):
    here = (lax.axis_index("seq"), lax.axis_index("z"))
    other = lax.axis_size("core") - 1 - lax.axis_index("core")
    barrier = pltpu.get_barrier_semaphore()
    pl.semaphore_signal(barrier, inc=1, device_id=here + (other,), device_id_type=MESH)
    pl.semaphore_wait(barrier, 1)
    copy = pltpu.make_async_remote_copy(
        src_ref=x_ref,
        dst_ref=y_ref,
        send_sem=send_sem,
        recv_sem=recv_sem,
        device_id=here + (other,),
        device_id_type=MESH,
    )
    copy.start()
    copy.wait()


def swap_cores(x, collective_id):
    return pl.pallas_call(
        swap_kernel,
        out_shape=jax.ShapeDtypeStruct(x.shape, x.dtype),
        in_specs=[pl.BlockSpec(memory_space=pl.ANY)],
        out_specs=pl.BlockSpec(memory_space=pl.ANY),
        scratch_shapes=[pltpu.SemaphoreType.DMA(()), pltpu.SemaphoreType.DMA(())],
        compiler_params=pltpu.CompilerParams(collective_id=collective_id, has_side_effects=True),
    )(x)


def split_rows(x, groups, collective_id):
    rows, cols = x.shape
    got = exchange(x.reshape(groups, rows // groups, cols), collective_id)
    return got.transpose(1, 0, 2).reshape(rows // groups, groups * cols)


def split_cols(x, groups, collective_id):
    rows, _, cols = x.shape
    got = exchange(x.transpose(1, 0, 2), collective_id)
    return got.reshape(groups * rows, cols)


def attend(query_rows, key_rows, value_rows, gain_mine, my_slab):
    highest = lax.Precision.HIGHEST
    tok_rows, per_group, _ = value_rows.shape
    blocks = tok_rows // BLOCK
    query_blocks = query_rows.reshape(blocks, BLOCK, per_group, FEAT)
    key_blocks = key_rows.reshape(blocks, BLOCK, per_group, FEAT)
    value_blocks = value_rows.reshape(blocks, BLOCK, per_group, HEAD_DIM)
    value_f32 = value_blocks.astype(jnp.float32)
    key_linear, key_square = feature_parts(key_blocks.astype(jnp.float32))
    own_zero = jnp.sum(value_f32, axis=1)[:, :, None, :]
    own_one = jnp.einsum("bthf,bthe->bhfe", key_linear, value_f32, precision=highest)
    own_two = jnp.einsum("bthf,bthe->bhfe", key_square, value_f32, precision=highest)
    own = jnp.concatenate([own_zero, own_one, own_two], axis=2)
    slab_total = jnp.sum(own, axis=0)
    state_rows = slab_total.shape[0] * slab_total.shape[1]
    pieces = gather_seq(
        slab_total.astype(jnp.bfloat16).reshape(state_rows, HEAD_DIM), lax.axis_size("seq"), 5
    ).astype(jnp.float32).reshape((-1,) + slab_total.shape)
    count = pieces.shape[0]
    earlier_mask = jnp.arange(count, dtype=jnp.int32) < my_slab
    prefix = jnp.sum(jnp.where(earlier_mask[:, None, None, None], pieces, 0.0), axis=0)
    earlier = jnp.concatenate([jnp.zeros_like(own[:1]), jnp.cumsum(own, axis=0)[:-1]], axis=0) + prefix[None]
    query_linear, query_square = feature_parts(query_blocks.astype(jnp.float32))
    inter = earlier[:, :, 0][:, None] + jnp.einsum(
        "bthf,bhfe->bthe", query_linear, earlier[:, :, 1 : 1 + FEAT], precision=highest
    )
    inter = inter + jnp.einsum(
        "bthf,bhfe->bthe", query_square, earlier[:, :, 1 + FEAT :], precision=highest
    )
    scores = jnp.einsum(
        "bthf,bshf->bhts", query_blocks, key_blocks, preferred_element_type=jnp.float32
    ) * FEAT ** (-0.5)
    kernel = 1.0 + scores + 0.5 * scores * scores
    causal = jnp.arange(BLOCK)[:, None] >= jnp.arange(BLOCK)[None, :]
    weights = jnp.where(causal, kernel, 0.0).astype(jnp.bfloat16)
    intra = jnp.einsum("bhts,bshe->bthe", weights, value_blocks, preferred_element_type=jnp.float32)
    numerator = (intra + inter).reshape(tok_rows, per_group, HEAD_DIM)
    mean_square = jnp.mean(numerator * numerator, axis=-1, keepdims=True)
    hidden = (numerator * lax.rsqrt(mean_square + 1e-05) * gain_mine).astype(jnp.bfloat16)
    return hidden.reshape(tok_rows, per_group * HEAD_DIM)


def per_device(tokens, w_query, w_key, w_value, w_out, gain):
    groups = lax.axis_size(CHAN)
    per_group = HEADS // groups
    my_group = chan_index()
    my_slab = lax.axis_index("seq")
    value_z = lax.all_gather(w_value, "z", axis=0)
    rows = split_rows(tokens, groups, 1)
    value_z, rows = lax.optimization_barrier((value_z, rows))
    value_other = swap_cores(value_z, 6)
    chunk = rows.shape[0]
    query = jnp.dot(rows, w_query, preferred_element_type=jnp.float32).astype(jnp.bfloat16)
    key = jnp.dot(rows, w_key, preferred_element_type=jnp.float32).astype(jnp.bfloat16)
    value_mine = jnp.einsum("tf,zfe->tze", rows, value_z, preferred_element_type=jnp.float32)
    value_pair = jnp.einsum("tf,zfe->tze", rows, value_other, preferred_element_type=jnp.float32)
    first = lax.axis_index("core") == 0
    value = jnp.where(
        first,
        jnp.stack([value_mine, value_pair], axis=2),
        jnp.stack([value_pair, value_mine], axis=2),
    )
    value = value.astype(jnp.bfloat16).reshape(chunk, groups, per_group * HEAD_DIM)
    query = query.reshape(chunk, groups, per_group * FEAT)
    key = key.reshape(chunk, groups, per_group * FEAT)
    packed = jnp.concatenate([query, key, value], axis=2)
    width = packed.shape[2]
    lanes = chunk * width // HEAD_DIM
    sent = exchange(packed.transpose(1, 0, 2).reshape(groups, lanes, HEAD_DIM), 2)
    mine = sent.reshape(groups * chunk, 1, width)
    tok_rows = mine.shape[0]
    qf = per_group * FEAT
    query_rows = mine[:, 0, :qf].reshape(tok_rows, per_group, FEAT)
    key_rows = mine[:, 0, qf : 2 * qf].reshape(tok_rows, per_group, FEAT)
    value_rows = mine[:, 0, 2 * qf :].reshape(tok_rows, per_group, HEAD_DIM)
    value_cols = per_group * HEAD_DIM
    gain_mine = lax.dynamic_slice_in_dim(gain, my_group * value_cols, value_cols, 0).reshape(
        per_group, HEAD_DIM
    )
    hidden = attend(query_rows, key_rows, value_rows, gain_mine, my_slab)
    hidden_rows = split_rows(hidden, groups, 3)
    mixed_rows = jnp.dot(hidden_rows, w_out, preferred_element_type=jnp.float32).astype(jnp.bfloat16)
    return split_cols(mixed_rows.reshape(chunk, groups, -1), groups, 4)


def solution(mesh):
    seq, chan = mesh.devices.shape
    cores = 2 if chan % 2 == 0 else 1
    split = jax.sharding.Mesh(mesh.devices.reshape(seq, chan // cores, cores), ("seq", "z", "core"))
    return jax.shard_map(
        per_device,
        mesh=split,
        in_specs=(P("seq", CHAN), P(), P(), P(None, CHAN), P(), P()),
        out_specs=P("seq", CHAN),
        check_vma=False,
    )
```

```python
import jax
import jax.numpy as jnp
from jax import lax
from jax.experimental import pallas as pl
from jax.experimental.pallas import tpu as pltpu
from jax.sharding import PartitionSpec as P

MESH = pl.DeviceIdType.MESH
CHAN = ("z", "core")


def chan_index():
    return lax.axis_index("z") * lax.axis_size("core") + lax.axis_index("core")


def chan_device(slab, peer):
    cores = lax.axis_size("core")
    return (slab, peer // cores, peer % cores)

HEADS = 16
FEAT = 16
HEAD_DIM = 128
BLOCK = 896


def feature_parts(rows):
    linear = rows * FEAT ** (-0.25)
    square = (rows[..., :, None] * rows[..., None, :]).reshape(rows.shape[:-1] + (FEAT * FEAT,)) * (
        2.0 * FEAT
    ) ** (-0.5)
    return (linear, square)


def exchange_kernel(x_ref, y_ref, buf, send_sem, recv_sem, own_sem):
    n = x_ref.shape[0]
    me = chan_index()
    slab = lax.axis_index("seq")
    barrier = pltpu.get_barrier_semaphore()
    for step in range(1, n):
        peer = lax.rem(me + step, n)
        pl.semaphore_signal(barrier, inc=1, device_id=chan_device(slab, peer), device_id_type=MESH)
    pl.semaphore_wait(barrier, n - 1)
    own = pltpu.make_async_copy(x_ref.at[me], buf.at[me], own_sem)
    own.start()
    sends = []
    for step in range(1, n):
        peer = lax.rem(me + step, n)
        copy = pltpu.make_async_remote_copy(
            src_ref=x_ref.at[peer],
            dst_ref=buf.at[me],
            send_sem=send_sem.at[peer],
            recv_sem=recv_sem.at[me],
            device_id=chan_device(slab, peer),
            device_id_type=MESH,
        )
        copy.start()
        sends.append(copy)
    for step in range(1, n):
        source = lax.rem(me + n - step, n)
        pltpu.make_async_remote_copy(
            src_ref=x_ref.at[source],
            dst_ref=buf.at[source],
            send_sem=send_sem.at[source],
            recv_sem=recv_sem.at[source],
            device_id=chan_device(slab, source),
            device_id_type=MESH,
        ).wait_recv()
    for copy in sends:
        copy.wait_send()
    own.wait()
    y_ref[...] = buf[...]


def exchange(x, collective_id):
    n = x.shape[0]
    return pl.pallas_call(
        exchange_kernel,
        out_shape=jax.ShapeDtypeStruct(x.shape, x.dtype),
        in_specs=[pl.BlockSpec(memory_space=pltpu.VMEM)],
        out_specs=pl.BlockSpec(memory_space=pltpu.VMEM),
        scratch_shapes=[
            pltpu.VMEM(x.shape, x.dtype),
            pltpu.SemaphoreType.DMA((n,)),
            pltpu.SemaphoreType.DMA((n,)),
            pltpu.SemaphoreType.DMA(()),
        ],
        compiler_params=pltpu.CompilerParams(collective_id=collective_id, has_side_effects=True),
    )(x)


def gather_kernel(x_ref, y_ref, buf, send_sem, recv_sem, own_sem):
    n = buf.shape[0]
    me = lax.axis_index("seq")
    here = (lax.axis_index("z"), lax.axis_index("core"))
    barrier = pltpu.get_barrier_semaphore()
    for step in range(1, n):
        peer = lax.rem(me + step, n)
        pl.semaphore_signal(barrier, inc=1, device_id=(peer,) + here, device_id_type=MESH)
    pl.semaphore_wait(barrier, n - 1)
    own = pltpu.make_async_copy(x_ref, buf.at[me], own_sem)
    own.start()
    sends = []
    for step in range(1, n):
        peer = lax.rem(me + step, n)
        copy = pltpu.make_async_remote_copy(
            src_ref=x_ref,
            dst_ref=buf.at[me],
            send_sem=send_sem.at[peer],
            recv_sem=recv_sem.at[me],
            device_id=(peer,) + here,
            device_id_type=MESH,
        )
        copy.start()
        sends.append(copy)
    for step in range(1, n):
        source = lax.rem(me + n - step, n)
        pltpu.make_async_remote_copy(
            src_ref=x_ref,
            dst_ref=buf.at[source],
            send_sem=send_sem.at[source],
            recv_sem=recv_sem.at[source],
            device_id=(source,) + here,
            device_id_type=MESH,
        ).wait_recv()
    for copy in sends:
        copy.wait_send()
    own.wait()
    y_ref[...] = buf[...]


def gather_seq(x, slabs, collective_id):
    shape = (slabs,) + x.shape
    return pl.pallas_call(
        gather_kernel,
        out_shape=jax.ShapeDtypeStruct(shape, x.dtype),
        in_specs=[pl.BlockSpec(memory_space=pltpu.VMEM)],
        out_specs=pl.BlockSpec(memory_space=pltpu.VMEM),
        scratch_shapes=[
            pltpu.VMEM(shape, x.dtype),
            pltpu.SemaphoreType.DMA((slabs,)),
            pltpu.SemaphoreType.DMA((slabs,)),
            pltpu.SemaphoreType.DMA(()),
        ],
        compiler_params=pltpu.CompilerParams(collective_id=collective_id, has_side_effects=True),
    )(x)


def swap_kernel(x_ref, y_ref, send_sem, recv_sem):
    here = (lax.axis_index("seq"), lax.axis_index("z"))
    other = lax.axis_size("core") - 1 - lax.axis_index("core")
    barrier = pltpu.get_barrier_semaphore()
    pl.semaphore_signal(barrier, inc=1, device_id=here + (other,), device_id_type=MESH)
    pl.semaphore_wait(barrier, 1)
    copy = pltpu.make_async_remote_copy(
        src_ref=x_ref,
        dst_ref=y_ref,
        send_sem=send_sem,
        recv_sem=recv_sem,
        device_id=here + (other,),
        device_id_type=MESH,
    )
    copy.start()
    copy.wait()


def swap_cores(x, collective_id):
    return pl.pallas_call(
        swap_kernel,
        out_shape=jax.ShapeDtypeStruct(x.shape, x.dtype),
        in_specs=[pl.BlockSpec(memory_space=pl.ANY)],
        out_specs=pl.BlockSpec(memory_space=pl.ANY),
        scratch_shapes=[pltpu.SemaphoreType.DMA(()), pltpu.SemaphoreType.DMA(())],
        compiler_params=pltpu.CompilerParams(collective_id=collective_id, has_side_effects=True),
    )(x)


def opening_kernel(x_ref, w_ref, y_ref, w_all, buf, send_sem, recv_sem, own_sem, w_send, w_recv, w_own):
    n = x_ref.shape[0]
    cores = lax.axis_size("core")
    ring = n // cores
    me = chan_index()
    slab = lax.axis_index("seq")
    z = lax.axis_index("z")
    core = lax.axis_index("core")
    barrier = pltpu.get_barrier_semaphore()
    for step in range(1, n):
        peer = lax.rem(me + step, n)
        pl.semaphore_signal(barrier, inc=1, device_id=chan_device(slab, peer), device_id_type=MESH)
    pl.semaphore_wait(barrier, n - 1)
    own = pltpu.make_async_copy(x_ref.at[me], buf.at[me], own_sem)
    own.start()
    sends = []
    for step in range(1, n):
        peer = lax.rem(me + step, n)
        copy = pltpu.make_async_remote_copy(
            src_ref=x_ref.at[peer],
            dst_ref=buf.at[me],
            send_sem=send_sem.at[peer],
            recv_sem=recv_sem.at[me],
            device_id=chan_device(slab, peer),
            device_id_type=MESH,
        )
        copy.start()
        sends.append(copy)
    w_local = pltpu.make_async_copy(w_ref, w_all.at[me], w_own)
    w_local.start()
    right = (slab, lax.rem(z + 1, ring), core)
    left = (slab, lax.rem(z + ring - 1, ring), core)
    partner = (slab, z, cores - 1 - core)

    def slot(origin):
        return lax.rem(origin + ring, ring) * cores + core

    def send(source, h, kind, target):
        copy = pltpu.make_async_remote_copy(
            src_ref=source,
            dst_ref=w_all.at[h],
            send_sem=w_send.at[h, kind],
            recv_sem=w_recv.at[h],
            device_id=target,
            device_id_type=MESH,
        )
        copy.start()
        sends.append(copy)

    def arrive(h, source):
        pltpu.make_async_remote_copy(
            src_ref=w_ref,
            dst_ref=w_all.at[h],
            send_sem=w_send.at[h, 0],
            recv_sem=w_recv.at[h],
            device_id=source,
            device_id_type=MESH,
        ).wait_recv()

    rightward = ring // 2
    leftward = ring - 1 - rightward
    send(w_ref, me, 0, right)
    if leftward > 0:
        send(w_ref, me, 1, left)
    send(w_ref, me, 2, partner)
    for step in range(1, rightward + 1):
        h = slot(z - step)
        arrive(h, left)
        if step < rightward:
            send(w_all.at[h], h, 0, right)
        send(w_all.at[h], h, 2, partner)
        if step <= leftward:
            h = slot(z + step)
            arrive(h, right)
            if step < leftward:
                send(w_all.at[h], h, 1, left)
            send(w_all.at[h], h, 2, partner)
    for origin in range(ring):
        arrive(origin * cores + (cores - 1 - core), partner)
    for step in range(1, n):
        source = lax.rem(me + n - step, n)
        pltpu.make_async_remote_copy(
            src_ref=x_ref.at[source],
            dst_ref=buf.at[source],
            send_sem=send_sem.at[source],
            recv_sem=recv_sem.at[source],
            device_id=chan_device(slab, source),
            device_id_type=MESH,
        ).wait_recv()
    for copy in sends:
        copy.wait_send()
    own.wait()
    w_local.wait()
    y_ref[...] = buf[...]


def opening(x, w, collective_id):
    n = x.shape[0]
    return pl.pallas_call(
        opening_kernel,
        out_shape=(
            jax.ShapeDtypeStruct(x.shape, x.dtype),
            jax.ShapeDtypeStruct((n,) + w.shape, w.dtype),
        ),
        in_specs=[pl.BlockSpec(memory_space=pltpu.VMEM), pl.BlockSpec(memory_space=pl.ANY)],
        out_specs=(pl.BlockSpec(memory_space=pltpu.VMEM), pl.BlockSpec(memory_space=pl.ANY)),
        scratch_shapes=[
            pltpu.VMEM(x.shape, x.dtype),
            pltpu.SemaphoreType.DMA((n,)),
            pltpu.SemaphoreType.DMA((n,)),
            pltpu.SemaphoreType.DMA(()),
            pltpu.SemaphoreType.DMA((n, 3)),
            pltpu.SemaphoreType.DMA((n,)),
            pltpu.SemaphoreType.DMA(()),
        ],
        compiler_params=pltpu.CompilerParams(collective_id=collective_id, has_side_effects=True),
    )(x, w)


def split_rows(x, groups, collective_id):
    rows, cols = x.shape
    got = exchange(x.reshape(groups, rows // groups, cols), collective_id)
    return got.transpose(1, 0, 2).reshape(rows // groups, groups * cols)


def split_cols(x, groups, collective_id):
    rows, _, cols = x.shape
    got = exchange(x.transpose(1, 0, 2), collective_id)
    return got.reshape(groups * rows, cols)


def attend(query_rows, key_rows, value_rows, gain_mine, my_slab):
    highest = lax.Precision.HIGHEST
    tok_rows, per_group, _ = value_rows.shape
    blocks = tok_rows // BLOCK
    query_blocks = query_rows.reshape(blocks, BLOCK, per_group, FEAT)
    key_blocks = key_rows.reshape(blocks, BLOCK, per_group, FEAT)
    value_blocks = value_rows.reshape(blocks, BLOCK, per_group, HEAD_DIM)
    value_f32 = value_blocks.astype(jnp.float32)
    key_linear, key_square = feature_parts(key_blocks.astype(jnp.float32))
    own_zero = jnp.sum(value_f32, axis=1)[:, :, None, :]
    own_one = jnp.einsum("bthf,bthe->bhfe", key_linear, value_f32, precision=highest)
    own_two = jnp.einsum("bthf,bthe->bhfe", key_square, value_f32, precision=highest)
    own = jnp.concatenate([own_zero, own_one, own_two], axis=2)
    slab_total = jnp.sum(own, axis=0)
    state_rows = slab_total.shape[0] * slab_total.shape[1]
    pieces = gather_seq(
        slab_total.astype(jnp.bfloat16).reshape(state_rows, HEAD_DIM), lax.axis_size("seq"), 5
    ).astype(jnp.float32).reshape((-1,) + slab_total.shape)
    count = pieces.shape[0]
    earlier_mask = jnp.arange(count, dtype=jnp.int32) < my_slab
    prefix = jnp.sum(jnp.where(earlier_mask[:, None, None, None], pieces, 0.0), axis=0)
    earlier = jnp.concatenate([jnp.zeros_like(own[:1]), jnp.cumsum(own, axis=0)[:-1]], axis=0) + prefix[None]
    query_linear, query_square = feature_parts(query_blocks.astype(jnp.float32))
    inter = earlier[:, :, 0][:, None] + jnp.einsum(
        "bthf,bhfe->bthe", query_linear, earlier[:, :, 1 : 1 + FEAT], precision=highest
    )
    inter = inter + jnp.einsum(
        "bthf,bhfe->bthe", query_square, earlier[:, :, 1 + FEAT :], precision=highest
    )
    scores = jnp.einsum(
        "bthf,bshf->bhts", query_blocks, key_blocks, preferred_element_type=jnp.float32
    ) * FEAT ** (-0.5)
    kernel = 1.0 + scores + 0.5 * scores * scores
    causal = jnp.arange(BLOCK)[:, None] >= jnp.arange(BLOCK)[None, :]
    weights = jnp.where(causal, kernel, 0.0).astype(jnp.bfloat16)
    intra = jnp.einsum("bhts,bshe->bthe", weights, value_blocks, preferred_element_type=jnp.float32)
    numerator = (intra + inter).reshape(tok_rows, per_group, HEAD_DIM)
    mean_square = jnp.mean(numerator * numerator, axis=-1, keepdims=True)
    hidden = (numerator * lax.rsqrt(mean_square + 1e-05) * gain_mine).astype(jnp.bfloat16)
    return hidden.reshape(tok_rows, per_group * HEAD_DIM)


def per_device(tokens, w_query, w_key, w_value, w_out, gain):
    groups = lax.axis_size(CHAN)
    per_group = HEADS // groups
    my_group = chan_index()
    my_slab = lax.axis_index("seq")
    tok_rows_total, tok_cols = tokens.shape
    got, value_all = opening(tokens.reshape(groups, tok_rows_total // groups, tok_cols), w_value, 1)
    rows = got.transpose(1, 0, 2).reshape(tok_rows_total // groups, groups * tok_cols)
    chunk = rows.shape[0]
    query = jnp.dot(rows, w_query, preferred_element_type=jnp.float32).astype(jnp.bfloat16)
    key = jnp.dot(rows, w_key, preferred_element_type=jnp.float32).astype(jnp.bfloat16)
    value = jnp.einsum("tf,hfe->the", rows, value_all, preferred_element_type=jnp.float32)
    value = value.astype(jnp.bfloat16).reshape(chunk, groups, per_group * HEAD_DIM)
    query = query.reshape(chunk, groups, per_group * FEAT)
    key = key.reshape(chunk, groups, per_group * FEAT)
    packed = jnp.concatenate([query, key, value], axis=2)
    width = packed.shape[2]
    lanes = chunk * width // HEAD_DIM
    sent = exchange(packed.transpose(1, 0, 2).reshape(groups, lanes, HEAD_DIM), 2)
    mine = sent.reshape(groups * chunk, 1, width)
    tok_rows = mine.shape[0]
    qf = per_group * FEAT
    query_rows = mine[:, 0, :qf].reshape(tok_rows, per_group, FEAT)
    key_rows = mine[:, 0, qf : 2 * qf].reshape(tok_rows, per_group, FEAT)
    value_rows = mine[:, 0, 2 * qf :].reshape(tok_rows, per_group, HEAD_DIM)
    value_cols = per_group * HEAD_DIM
    gain_mine = lax.dynamic_slice_in_dim(gain, my_group * value_cols, value_cols, 0).reshape(
        per_group, HEAD_DIM
    )
    hidden = attend(query_rows, key_rows, value_rows, gain_mine, my_slab)
    hidden_rows = split_rows(hidden, groups, 3)
    mixed_rows = jnp.dot(hidden_rows, w_out, preferred_element_type=jnp.float32).astype(jnp.bfloat16)
    return split_cols(mixed_rows.reshape(chunk, groups, -1), groups, 4)


def solution(mesh):
    seq, chan = mesh.devices.shape
    cores = 2 if chan % 2 == 0 else 1
    split = jax.sharding.Mesh(mesh.devices.reshape(seq, chan // cores, cores), ("seq", "z", "core"))
    return jax.shard_map(
        per_device,
        mesh=split,
        in_specs=(P("seq", CHAN), P(), P(), P(None, CHAN), P(), P()),
        out_specs=P("seq", CHAN),
        check_vma=False,
    )
```

```python
import jax
import jax.numpy as jnp
from jax import lax
from jax.experimental import pallas as pl
from jax.experimental.pallas import tpu as pltpu
from jax.sharding import PartitionSpec as P

MESH = pl.DeviceIdType.MESH
CHAN = ("z", "core")
W_PIECES = 4


def chan_index():
    return lax.axis_index("z") * lax.axis_size("core") + lax.axis_index("core")


def chan_device(slab, peer):
    cores = lax.axis_size("core")
    return (slab, peer // cores, peer % cores)

HEADS = 16
FEAT = 16
HEAD_DIM = 128
BLOCK = 896


def feature_parts(rows):
    linear = rows * FEAT ** (-0.25)
    square = (rows[..., :, None] * rows[..., None, :]).reshape(rows.shape[:-1] + (FEAT * FEAT,)) * (
        2.0 * FEAT
    ) ** (-0.5)
    return (linear, square)


def exchange_kernel(x_ref, y_ref, buf, send_sem, recv_sem, own_sem):
    n = x_ref.shape[0]
    me = chan_index()
    slab = lax.axis_index("seq")
    barrier = pltpu.get_barrier_semaphore()
    for step in range(1, n):
        peer = lax.rem(me + step, n)
        pl.semaphore_signal(barrier, inc=1, device_id=chan_device(slab, peer), device_id_type=MESH)
    pl.semaphore_wait(barrier, n - 1)
    own = pltpu.make_async_copy(x_ref.at[me], buf.at[me], own_sem)
    own.start()
    sends = []
    for step in range(1, n):
        peer = lax.rem(me + step, n)
        copy = pltpu.make_async_remote_copy(
            src_ref=x_ref.at[peer],
            dst_ref=buf.at[me],
            send_sem=send_sem.at[peer],
            recv_sem=recv_sem.at[me],
            device_id=chan_device(slab, peer),
            device_id_type=MESH,
        )
        copy.start()
        sends.append(copy)
    for step in range(1, n):
        source = lax.rem(me + n - step, n)
        pltpu.make_async_remote_copy(
            src_ref=x_ref.at[source],
            dst_ref=buf.at[source],
            send_sem=send_sem.at[source],
            recv_sem=recv_sem.at[source],
            device_id=chan_device(slab, source),
            device_id_type=MESH,
        ).wait_recv()
    for copy in sends:
        copy.wait_send()
    own.wait()
    y_ref[...] = buf[...]


def exchange(x, collective_id):
    n = x.shape[0]
    return pl.pallas_call(
        exchange_kernel,
        out_shape=jax.ShapeDtypeStruct(x.shape, x.dtype),
        in_specs=[pl.BlockSpec(memory_space=pltpu.VMEM)],
        out_specs=pl.BlockSpec(memory_space=pltpu.VMEM),
        scratch_shapes=[
            pltpu.VMEM(x.shape, x.dtype),
            pltpu.SemaphoreType.DMA((n,)),
            pltpu.SemaphoreType.DMA((n,)),
            pltpu.SemaphoreType.DMA(()),
        ],
        compiler_params=pltpu.CompilerParams(collective_id=collective_id, has_side_effects=True),
    )(x)


def gather_kernel(x_ref, y_ref, buf, send_sem, recv_sem, own_sem):
    n = buf.shape[0]
    me = lax.axis_index("seq")
    here = (lax.axis_index("z"), lax.axis_index("core"))
    barrier = pltpu.get_barrier_semaphore()
    for step in range(1, n):
        peer = lax.rem(me + step, n)
        pl.semaphore_signal(barrier, inc=1, device_id=(peer,) + here, device_id_type=MESH)
    pl.semaphore_wait(barrier, n - 1)
    own = pltpu.make_async_copy(x_ref, buf.at[me], own_sem)
    own.start()
    sends = []
    for step in range(1, n):
        peer = lax.rem(me + step, n)
        copy = pltpu.make_async_remote_copy(
            src_ref=x_ref,
            dst_ref=buf.at[me],
            send_sem=send_sem.at[peer],
            recv_sem=recv_sem.at[me],
            device_id=(peer,) + here,
            device_id_type=MESH,
        )
        copy.start()
        sends.append(copy)
    for step in range(1, n):
        source = lax.rem(me + n - step, n)
        pltpu.make_async_remote_copy(
            src_ref=x_ref,
            dst_ref=buf.at[source],
            send_sem=send_sem.at[source],
            recv_sem=recv_sem.at[source],
            device_id=(source,) + here,
            device_id_type=MESH,
        ).wait_recv()
    for copy in sends:
        copy.wait_send()
    own.wait()
    y_ref[...] = buf[...]


def gather_seq(x, slabs, collective_id):
    shape = (slabs,) + x.shape
    return pl.pallas_call(
        gather_kernel,
        out_shape=jax.ShapeDtypeStruct(shape, x.dtype),
        in_specs=[pl.BlockSpec(memory_space=pltpu.VMEM)],
        out_specs=pl.BlockSpec(memory_space=pltpu.VMEM),
        scratch_shapes=[
            pltpu.VMEM(shape, x.dtype),
            pltpu.SemaphoreType.DMA((slabs,)),
            pltpu.SemaphoreType.DMA((slabs,)),
            pltpu.SemaphoreType.DMA(()),
        ],
        compiler_params=pltpu.CompilerParams(collective_id=collective_id, has_side_effects=True),
    )(x)


def swap_kernel(x_ref, y_ref, send_sem, recv_sem):
    here = (lax.axis_index("seq"), lax.axis_index("z"))
    other = lax.axis_size("core") - 1 - lax.axis_index("core")
    barrier = pltpu.get_barrier_semaphore()
    pl.semaphore_signal(barrier, inc=1, device_id=here + (other,), device_id_type=MESH)
    pl.semaphore_wait(barrier, 1)
    copy = pltpu.make_async_remote_copy(
        src_ref=x_ref,
        dst_ref=y_ref,
        send_sem=send_sem,
        recv_sem=recv_sem,
        device_id=here + (other,),
        device_id_type=MESH,
    )
    copy.start()
    copy.wait()


def swap_cores(x, collective_id):
    return pl.pallas_call(
        swap_kernel,
        out_shape=jax.ShapeDtypeStruct(x.shape, x.dtype),
        in_specs=[pl.BlockSpec(memory_space=pl.ANY)],
        out_specs=pl.BlockSpec(memory_space=pl.ANY),
        scratch_shapes=[pltpu.SemaphoreType.DMA(()), pltpu.SemaphoreType.DMA(())],
        compiler_params=pltpu.CompilerParams(collective_id=collective_id, has_side_effects=True),
    )(x)


def opening_kernel(x_ref, w_ref, y_ref, w_all, buf, send_sem, recv_sem, own_sem, w_send, w_recv, w_own):
    n = x_ref.shape[0]
    cores = lax.axis_size("core")
    ring = n // cores
    me = chan_index()
    slab = lax.axis_index("seq")
    z = lax.axis_index("z")
    core = lax.axis_index("core")
    barrier = pltpu.get_barrier_semaphore()
    for step in range(1, n):
        peer = lax.rem(me + step, n)
        pl.semaphore_signal(barrier, inc=1, device_id=chan_device(slab, peer), device_id_type=MESH)
    pl.semaphore_wait(barrier, n - 1)
    own = pltpu.make_async_copy(x_ref.at[me], buf.at[me], own_sem)
    own.start()
    sends = []
    for step in range(1, n):
        peer = lax.rem(me + step, n)
        copy = pltpu.make_async_remote_copy(
            src_ref=x_ref.at[peer],
            dst_ref=buf.at[me],
            send_sem=send_sem.at[peer],
            recv_sem=recv_sem.at[me],
            device_id=chan_device(slab, peer),
            device_id_type=MESH,
        )
        copy.start()
        sends.append(copy)
    w_local = pltpu.make_async_copy(w_ref, w_all.at[me], w_own)
    w_local.start()
    right = (slab, lax.rem(z + 1, ring), core)
    left = (slab, lax.rem(z + ring - 1, ring), core)
    partner = (slab, z, cores - 1 - core)

    pieces = W_PIECES
    depth = w_ref.shape[0] // pieces

    def slot(origin):
        return lax.rem(origin + ring, ring) * cores + core

    def held(h, j):
        return w_all.at[h, pl.ds(j * depth, depth)]

    def send(source, h, j, kind, target):
        copy = pltpu.make_async_remote_copy(
            src_ref=source,
            dst_ref=held(h, j),
            send_sem=w_send.at[h, kind, j],
            recv_sem=w_recv.at[h, j],
            device_id=target,
            device_id_type=MESH,
        )
        copy.start()
        sends.append(copy)

    def arrive(h, j, source):
        pltpu.make_async_remote_copy(
            src_ref=w_ref.at[pl.ds(j * depth, depth)],
            dst_ref=held(h, j),
            send_sem=w_send.at[h, 0, j],
            recv_sem=w_recv.at[h, j],
            device_id=source,
            device_id_type=MESH,
        ).wait_recv()

    rightward = ring // 2
    leftward = ring - 1 - rightward
    for j in range(pieces):
        mine = w_ref.at[pl.ds(j * depth, depth)]
        send(mine, me, j, 0, right)
        if leftward > 0:
            send(mine, me, j, 1, left)
        send(mine, me, j, 2, partner)
    for step in range(1, rightward + 1):
        for j in range(pieces):
            h = slot(z - step)
            arrive(h, j, left)
            if step < rightward:
                send(held(h, j), h, j, 0, right)
            send(held(h, j), h, j, 2, partner)
            if step <= leftward:
                h = slot(z + step)
                arrive(h, j, right)
                if step < leftward:
                    send(held(h, j), h, j, 1, left)
                send(held(h, j), h, j, 2, partner)
    for origin in range(ring):
        for j in range(pieces):
            arrive(origin * cores + (cores - 1 - core), j, partner)
    for step in range(1, n):
        source = lax.rem(me + n - step, n)
        pltpu.make_async_remote_copy(
            src_ref=x_ref.at[source],
            dst_ref=buf.at[source],
            send_sem=send_sem.at[source],
            recv_sem=recv_sem.at[source],
            device_id=chan_device(slab, source),
            device_id_type=MESH,
        ).wait_recv()
    for copy in sends:
        copy.wait_send()
    own.wait()
    w_local.wait()
    y_ref[...] = buf[...]


def opening(x, w, collective_id):
    n = x.shape[0]
    return pl.pallas_call(
        opening_kernel,
        out_shape=(
            jax.ShapeDtypeStruct(x.shape, x.dtype),
            jax.ShapeDtypeStruct((n,) + w.shape, w.dtype),
        ),
        in_specs=[pl.BlockSpec(memory_space=pltpu.VMEM), pl.BlockSpec(memory_space=pl.ANY)],
        out_specs=(pl.BlockSpec(memory_space=pltpu.VMEM), pl.BlockSpec(memory_space=pl.ANY)),
        scratch_shapes=[
            pltpu.VMEM(x.shape, x.dtype),
            pltpu.SemaphoreType.DMA((n,)),
            pltpu.SemaphoreType.DMA((n,)),
            pltpu.SemaphoreType.DMA(()),
            pltpu.SemaphoreType.DMA((n, 3, W_PIECES)),
            pltpu.SemaphoreType.DMA((n, W_PIECES)),
            pltpu.SemaphoreType.DMA(()),
        ],
        compiler_params=pltpu.CompilerParams(collective_id=collective_id, has_side_effects=True),
    )(x, w)


def split_rows(x, groups, collective_id):
    rows, cols = x.shape
    got = exchange(x.reshape(groups, rows // groups, cols), collective_id)
    return got.transpose(1, 0, 2).reshape(rows // groups, groups * cols)


def split_cols(x, groups, collective_id):
    rows, _, cols = x.shape
    got = exchange(x.transpose(1, 0, 2), collective_id)
    return got.reshape(groups * rows, cols)


def attend(query_rows, key_rows, value_rows, gain_mine, my_slab):
    highest = lax.Precision.HIGHEST
    tok_rows, per_group, _ = value_rows.shape
    blocks = tok_rows // BLOCK
    query_blocks = query_rows.reshape(blocks, BLOCK, per_group, FEAT)
    key_blocks = key_rows.reshape(blocks, BLOCK, per_group, FEAT)
    value_blocks = value_rows.reshape(blocks, BLOCK, per_group, HEAD_DIM)
    value_f32 = value_blocks.astype(jnp.float32)
    key_linear, key_square = feature_parts(key_blocks.astype(jnp.float32))
    own_zero = jnp.sum(value_f32, axis=1)[:, :, None, :]
    own_one = jnp.einsum("bthf,bthe->bhfe", key_linear, value_f32, precision=highest)
    own_two = jnp.einsum("bthf,bthe->bhfe", key_square, value_f32, precision=highest)
    own = jnp.concatenate([own_zero, own_one, own_two], axis=2)
    slab_total = jnp.sum(own, axis=0)
    state_rows = slab_total.shape[0] * slab_total.shape[1]
    pieces = gather_seq(
        slab_total.astype(jnp.bfloat16).reshape(state_rows, HEAD_DIM), lax.axis_size("seq"), 5
    ).astype(jnp.float32).reshape((-1,) + slab_total.shape)
    count = pieces.shape[0]
    earlier_mask = jnp.arange(count, dtype=jnp.int32) < my_slab
    prefix = jnp.sum(jnp.where(earlier_mask[:, None, None, None], pieces, 0.0), axis=0)
    earlier = jnp.concatenate([jnp.zeros_like(own[:1]), jnp.cumsum(own, axis=0)[:-1]], axis=0) + prefix[None]
    query_linear, query_square = feature_parts(query_blocks.astype(jnp.float32))
    inter = earlier[:, :, 0][:, None] + jnp.einsum(
        "bthf,bhfe->bthe", query_linear, earlier[:, :, 1 : 1 + FEAT], precision=highest
    )
    inter = inter + jnp.einsum(
        "bthf,bhfe->bthe", query_square, earlier[:, :, 1 + FEAT :], precision=highest
    )
    scores = jnp.einsum(
        "bthf,bshf->bhts", query_blocks, key_blocks, preferred_element_type=jnp.float32
    ) * FEAT ** (-0.5)
    kernel = 1.0 + scores + 0.5 * scores * scores
    causal = jnp.arange(BLOCK)[:, None] >= jnp.arange(BLOCK)[None, :]
    weights = jnp.where(causal, kernel, 0.0).astype(jnp.bfloat16)
    intra = jnp.einsum("bhts,bshe->bthe", weights, value_blocks, preferred_element_type=jnp.float32)
    numerator = (intra + inter).reshape(tok_rows, per_group, HEAD_DIM)
    mean_square = jnp.mean(numerator * numerator, axis=-1, keepdims=True)
    hidden = (numerator * lax.rsqrt(mean_square + 1e-05) * gain_mine).astype(jnp.bfloat16)
    return hidden.reshape(tok_rows, per_group * HEAD_DIM)


def per_device(tokens, w_query, w_key, w_value, w_out, gain):
    groups = lax.axis_size(CHAN)
    per_group = HEADS // groups
    my_group = chan_index()
    my_slab = lax.axis_index("seq")
    tok_rows_total, tok_cols = tokens.shape
    got, value_all = opening(tokens.reshape(groups, tok_rows_total // groups, tok_cols), w_value, 1)
    rows = got.transpose(1, 0, 2).reshape(tok_rows_total // groups, groups * tok_cols)
    chunk = rows.shape[0]
    query = jnp.dot(rows, w_query, preferred_element_type=jnp.float32).astype(jnp.bfloat16)
    key = jnp.dot(rows, w_key, preferred_element_type=jnp.float32).astype(jnp.bfloat16)
    value = jnp.einsum("tf,hfe->the", rows, value_all, preferred_element_type=jnp.float32)
    value = value.astype(jnp.bfloat16).reshape(chunk, groups, per_group * HEAD_DIM)
    query = query.reshape(chunk, groups, per_group * FEAT)
    key = key.reshape(chunk, groups, per_group * FEAT)
    packed = jnp.concatenate([query, key, value], axis=2)
    width = packed.shape[2]
    lanes = chunk * width // HEAD_DIM
    sent = exchange(packed.transpose(1, 0, 2).reshape(groups, lanes, HEAD_DIM), 2)
    mine = sent.reshape(groups * chunk, 1, width)
    tok_rows = mine.shape[0]
    qf = per_group * FEAT
    query_rows = mine[:, 0, :qf].reshape(tok_rows, per_group, FEAT)
    key_rows = mine[:, 0, qf : 2 * qf].reshape(tok_rows, per_group, FEAT)
    value_rows = mine[:, 0, 2 * qf :].reshape(tok_rows, per_group, HEAD_DIM)
    value_cols = per_group * HEAD_DIM
    gain_mine = lax.dynamic_slice_in_dim(gain, my_group * value_cols, value_cols, 0).reshape(
        per_group, HEAD_DIM
    )
    hidden = attend(query_rows, key_rows, value_rows, gain_mine, my_slab)
    hidden_rows = split_rows(hidden, groups, 3)
    mixed_rows = jnp.dot(hidden_rows, w_out, preferred_element_type=jnp.float32).astype(jnp.bfloat16)
    return split_cols(mixed_rows.reshape(chunk, groups, -1), groups, 4)


def solution(mesh):
    seq, chan = mesh.devices.shape
    cores = 2 if chan % 2 == 0 else 1
    split = jax.sharding.Mesh(mesh.devices.reshape(seq, chan // cores, cores), ("seq", "z", "core"))
    return jax.shard_map(
        per_device,
        mesh=split,
        in_specs=(P("seq", CHAN), P(), P(), P(None, CHAN), P(), P()),
        out_specs=P("seq", CHAN),
        check_vma=False,
    )
```

```python
import jax
import jax.numpy as jnp
from jax import lax
from jax.experimental import pallas as pl
from jax.experimental.pallas import tpu as pltpu
from jax.sharding import PartitionSpec as P

MESH = pl.DeviceIdType.MESH
CHAN = ("z", "core")
W_PIECES = 4


def chan_index():
    return lax.axis_index("z") * lax.axis_size("core") + lax.axis_index("core")


def chan_device(slab, peer):
    cores = lax.axis_size("core")
    return (slab, peer // cores, peer % cores)

HEADS = 16
FEAT = 16
HEAD_DIM = 128
BLOCK = 896


def feature_parts(rows):
    linear = rows * FEAT ** (-0.25)
    square = (rows[..., :, None] * rows[..., None, :]).reshape(rows.shape[:-1] + (FEAT * FEAT,)) * (
        2.0 * FEAT
    ) ** (-0.5)
    return (linear, square)


def exchange_kernel(x_ref, y_ref, buf, send_sem, recv_sem, own_sem):
    n = x_ref.shape[0]
    me = chan_index()
    slab = lax.axis_index("seq")
    barrier = pltpu.get_barrier_semaphore()
    for step in range(1, n):
        peer = lax.rem(me + step, n)
        pl.semaphore_signal(barrier, inc=1, device_id=chan_device(slab, peer), device_id_type=MESH)
    pl.semaphore_wait(barrier, n - 1)
    own = pltpu.make_async_copy(x_ref.at[me], buf.at[me], own_sem)
    own.start()
    sends = []
    for step in range(1, n):
        peer = lax.rem(me + step, n)
        copy = pltpu.make_async_remote_copy(
            src_ref=x_ref.at[peer],
            dst_ref=buf.at[me],
            send_sem=send_sem.at[peer],
            recv_sem=recv_sem.at[me],
            device_id=chan_device(slab, peer),
            device_id_type=MESH,
        )
        copy.start()
        sends.append(copy)
    for step in range(1, n):
        source = lax.rem(me + n - step, n)
        pltpu.make_async_remote_copy(
            src_ref=x_ref.at[source],
            dst_ref=buf.at[source],
            send_sem=send_sem.at[source],
            recv_sem=recv_sem.at[source],
            device_id=chan_device(slab, source),
            device_id_type=MESH,
        ).wait_recv()
    for copy in sends:
        copy.wait_send()
    own.wait()
    y_ref[...] = buf[...]


def exchange(x, collective_id):
    n = x.shape[0]
    return pl.pallas_call(
        exchange_kernel,
        out_shape=jax.ShapeDtypeStruct(x.shape, x.dtype),
        in_specs=[pl.BlockSpec(memory_space=pltpu.VMEM)],
        out_specs=pl.BlockSpec(memory_space=pltpu.VMEM),
        scratch_shapes=[
            pltpu.VMEM(x.shape, x.dtype),
            pltpu.SemaphoreType.DMA((n,)),
            pltpu.SemaphoreType.DMA((n,)),
            pltpu.SemaphoreType.DMA(()),
        ],
        compiler_params=pltpu.CompilerParams(collective_id=collective_id, has_side_effects=True),
    )(x)


def gather_kernel(x_ref, y_ref, buf, send_sem, recv_sem, own_sem):
    n = buf.shape[0]
    me = lax.axis_index("seq")
    here = (lax.axis_index("z"), lax.axis_index("core"))
    barrier = pltpu.get_barrier_semaphore()
    for step in range(1, n):
        peer = lax.rem(me + step, n)
        pl.semaphore_signal(barrier, inc=1, device_id=(peer,) + here, device_id_type=MESH)
    pl.semaphore_wait(barrier, n - 1)
    own = pltpu.make_async_copy(x_ref, buf.at[me], own_sem)
    own.start()
    sends = []
    for step in range(1, n):
        peer = lax.rem(me + step, n)
        copy = pltpu.make_async_remote_copy(
            src_ref=x_ref,
            dst_ref=buf.at[me],
            send_sem=send_sem.at[peer],
            recv_sem=recv_sem.at[me],
            device_id=(peer,) + here,
            device_id_type=MESH,
        )
        copy.start()
        sends.append(copy)
    for step in range(1, n):
        source = lax.rem(me + n - step, n)
        pltpu.make_async_remote_copy(
            src_ref=x_ref,
            dst_ref=buf.at[source],
            send_sem=send_sem.at[source],
            recv_sem=recv_sem.at[source],
            device_id=(source,) + here,
            device_id_type=MESH,
        ).wait_recv()
    for copy in sends:
        copy.wait_send()
    own.wait()
    y_ref[...] = buf[...]


def gather_seq(x, slabs, collective_id):
    shape = (slabs,) + x.shape
    return pl.pallas_call(
        gather_kernel,
        out_shape=jax.ShapeDtypeStruct(shape, x.dtype),
        in_specs=[pl.BlockSpec(memory_space=pltpu.VMEM)],
        out_specs=pl.BlockSpec(memory_space=pltpu.VMEM),
        scratch_shapes=[
            pltpu.VMEM(shape, x.dtype),
            pltpu.SemaphoreType.DMA((slabs,)),
            pltpu.SemaphoreType.DMA((slabs,)),
            pltpu.SemaphoreType.DMA(()),
        ],
        compiler_params=pltpu.CompilerParams(collective_id=collective_id, has_side_effects=True),
    )(x)


def swap_kernel(x_ref, y_ref, send_sem, recv_sem):
    here = (lax.axis_index("seq"), lax.axis_index("z"))
    other = lax.axis_size("core") - 1 - lax.axis_index("core")
    barrier = pltpu.get_barrier_semaphore()
    pl.semaphore_signal(barrier, inc=1, device_id=here + (other,), device_id_type=MESH)
    pl.semaphore_wait(barrier, 1)
    copy = pltpu.make_async_remote_copy(
        src_ref=x_ref,
        dst_ref=y_ref,
        send_sem=send_sem,
        recv_sem=recv_sem,
        device_id=here + (other,),
        device_id_type=MESH,
    )
    copy.start()
    copy.wait()


def swap_cores(x, collective_id):
    return pl.pallas_call(
        swap_kernel,
        out_shape=jax.ShapeDtypeStruct(x.shape, x.dtype),
        in_specs=[pl.BlockSpec(memory_space=pl.ANY)],
        out_specs=pl.BlockSpec(memory_space=pl.ANY),
        scratch_shapes=[pltpu.SemaphoreType.DMA(()), pltpu.SemaphoreType.DMA(())],
        compiler_params=pltpu.CompilerParams(collective_id=collective_id, has_side_effects=True),
    )(x)


def opening_kernel(x_ref, w_ref, y_ref, w_all, buf, send_sem, recv_sem, own_sem, w_send, w_recv, w_own):
    n = x_ref.shape[0]
    cores = lax.axis_size("core")
    ring = n // cores
    me = chan_index()
    slab = lax.axis_index("seq")
    z = lax.axis_index("z")
    core = lax.axis_index("core")
    barrier = pltpu.get_barrier_semaphore()
    for step in range(1, n):
        peer = lax.rem(me + step, n)
        pl.semaphore_signal(barrier, inc=1, device_id=chan_device(slab, peer), device_id_type=MESH)
    pl.semaphore_wait(barrier, n - 1)
    own = pltpu.make_async_copy(x_ref.at[me], buf.at[me], own_sem)
    own.start()
    sends = []
    for step in range(1, n):
        peer = lax.rem(me + step, n)
        copy = pltpu.make_async_remote_copy(
            src_ref=x_ref.at[peer],
            dst_ref=buf.at[me],
            send_sem=send_sem.at[peer],
            recv_sem=recv_sem.at[me],
            device_id=chan_device(slab, peer),
            device_id_type=MESH,
        )
        copy.start()
        sends.append(copy)
    w_local = pltpu.make_async_copy(w_ref, w_all.at[me], w_own)
    w_local.start()
    right = (slab, lax.rem(z + 1, ring), core)
    left = (slab, lax.rem(z + ring - 1, ring), core)
    partner = (slab, z, cores - 1 - core)

    pieces = W_PIECES
    depth = w_ref.shape[0] // pieces

    def slot(origin):
        return lax.rem(origin + ring, ring) * cores + core

    def held(h, j):
        return w_all.at[h, pl.ds(j * depth, depth)]

    def send(source, h, j, kind, target):
        copy = pltpu.make_async_remote_copy(
            src_ref=source,
            dst_ref=held(h, j),
            send_sem=w_send.at[h, kind, j],
            recv_sem=w_recv.at[h, j],
            device_id=target,
            device_id_type=MESH,
        )
        copy.start()
        sends.append(copy)

    def arrive(h, j, source):
        pltpu.make_async_remote_copy(
            src_ref=w_ref.at[pl.ds(j * depth, depth)],
            dst_ref=held(h, j),
            send_sem=w_send.at[h, 0, j],
            recv_sem=w_recv.at[h, j],
            device_id=source,
            device_id_type=MESH,
        ).wait_recv()

    half = ring // 2
    full = half - 1 if ring % 2 == 0 else half

    def goes_right(step):
        return range(pieces) if step <= full else range(pieces // 2) if step == half else range(0)

    def goes_left(step):
        return range(pieces) if step <= full else range(pieces // 2, pieces) if step == half else range(0)

    for j in range(pieces):
        mine = w_ref.at[pl.ds(j * depth, depth)]
        if j in goes_right(1):
            send(mine, me, j, 0, right)
        if j in goes_left(1):
            send(mine, me, j, 1, left)
        send(mine, me, j, 2, partner)
    for step in range(1, half + 1):
        for j in range(pieces):
            if j in goes_right(step):
                h = slot(z - step)
                arrive(h, j, left)
                if j in goes_right(step + 1):
                    send(held(h, j), h, j, 0, right)
                send(held(h, j), h, j, 2, partner)
            if j in goes_left(step):
                h = slot(z + step)
                arrive(h, j, right)
                if j in goes_left(step + 1):
                    send(held(h, j), h, j, 1, left)
                send(held(h, j), h, j, 2, partner)
    for origin in range(ring):
        for j in range(pieces):
            arrive(origin * cores + (cores - 1 - core), j, partner)
    for step in range(1, n):
        source = lax.rem(me + n - step, n)
        pltpu.make_async_remote_copy(
            src_ref=x_ref.at[source],
            dst_ref=buf.at[source],
            send_sem=send_sem.at[source],
            recv_sem=recv_sem.at[source],
            device_id=chan_device(slab, source),
            device_id_type=MESH,
        ).wait_recv()
    for copy in sends:
        copy.wait_send()
    own.wait()
    w_local.wait()
    y_ref[...] = buf[...]


def opening(x, w, collective_id):
    n = x.shape[0]
    return pl.pallas_call(
        opening_kernel,
        out_shape=(
            jax.ShapeDtypeStruct(x.shape, x.dtype),
            jax.ShapeDtypeStruct((n,) + w.shape, w.dtype),
        ),
        in_specs=[pl.BlockSpec(memory_space=pltpu.VMEM), pl.BlockSpec(memory_space=pl.ANY)],
        out_specs=(pl.BlockSpec(memory_space=pltpu.VMEM), pl.BlockSpec(memory_space=pl.ANY)),
        scratch_shapes=[
            pltpu.VMEM(x.shape, x.dtype),
            pltpu.SemaphoreType.DMA((n,)),
            pltpu.SemaphoreType.DMA((n,)),
            pltpu.SemaphoreType.DMA(()),
            pltpu.SemaphoreType.DMA((n, 3, W_PIECES)),
            pltpu.SemaphoreType.DMA((n, W_PIECES)),
            pltpu.SemaphoreType.DMA(()),
        ],
        compiler_params=pltpu.CompilerParams(collective_id=collective_id, has_side_effects=True),
    )(x, w)


def split_rows(x, groups, collective_id):
    rows, cols = x.shape
    got = exchange(x.reshape(groups, rows // groups, cols), collective_id)
    return got.transpose(1, 0, 2).reshape(rows // groups, groups * cols)


def split_cols(x, groups, collective_id):
    rows, _, cols = x.shape
    got = exchange(x.transpose(1, 0, 2), collective_id)
    return got.reshape(groups * rows, cols)


def attend(query_rows, key_rows, value_rows, gain_mine, my_slab):
    highest = lax.Precision.HIGHEST
    tok_rows, per_group, _ = value_rows.shape
    blocks = tok_rows // BLOCK
    query_blocks = query_rows.reshape(blocks, BLOCK, per_group, FEAT)
    key_blocks = key_rows.reshape(blocks, BLOCK, per_group, FEAT)
    value_blocks = value_rows.reshape(blocks, BLOCK, per_group, HEAD_DIM)
    value_f32 = value_blocks.astype(jnp.float32)
    key_linear, key_square = feature_parts(key_blocks.astype(jnp.float32))
    own_zero = jnp.sum(value_f32, axis=1)[:, :, None, :]
    own_one = jnp.einsum("bthf,bthe->bhfe", key_linear, value_f32, precision=highest)
    own_two = jnp.einsum("bthf,bthe->bhfe", key_square, value_f32, precision=highest)
    own = jnp.concatenate([own_zero, own_one, own_two], axis=2)
    slab_total = jnp.sum(own, axis=0)
    state_rows = slab_total.shape[0] * slab_total.shape[1]
    pieces = gather_seq(
        slab_total.astype(jnp.bfloat16).reshape(state_rows, HEAD_DIM), lax.axis_size("seq"), 5
    ).astype(jnp.float32).reshape((-1,) + slab_total.shape)
    count = pieces.shape[0]
    earlier_mask = jnp.arange(count, dtype=jnp.int32) < my_slab
    prefix = jnp.sum(jnp.where(earlier_mask[:, None, None, None], pieces, 0.0), axis=0)
    earlier = jnp.concatenate([jnp.zeros_like(own[:1]), jnp.cumsum(own, axis=0)[:-1]], axis=0) + prefix[None]
    query_linear, query_square = feature_parts(query_blocks.astype(jnp.float32))
    inter = earlier[:, :, 0][:, None] + jnp.einsum(
        "bthf,bhfe->bthe", query_linear, earlier[:, :, 1 : 1 + FEAT], precision=highest
    )
    inter = inter + jnp.einsum(
        "bthf,bhfe->bthe", query_square, earlier[:, :, 1 + FEAT :], precision=highest
    )
    scores = jnp.einsum(
        "bthf,bshf->bhts", query_blocks, key_blocks, preferred_element_type=jnp.float32
    ) * FEAT ** (-0.5)
    kernel = 1.0 + scores + 0.5 * scores * scores
    causal = jnp.arange(BLOCK)[:, None] >= jnp.arange(BLOCK)[None, :]
    weights = jnp.where(causal, kernel, 0.0).astype(jnp.bfloat16)
    intra = jnp.einsum("bhts,bshe->bthe", weights, value_blocks, preferred_element_type=jnp.float32)
    numerator = (intra + inter).reshape(tok_rows, per_group, HEAD_DIM)
    mean_square = jnp.mean(numerator * numerator, axis=-1, keepdims=True)
    hidden = (numerator * lax.rsqrt(mean_square + 1e-05) * gain_mine).astype(jnp.bfloat16)
    return hidden.reshape(tok_rows, per_group * HEAD_DIM)


def per_device(tokens, w_query, w_key, w_value, w_out, gain):
    groups = lax.axis_size(CHAN)
    per_group = HEADS // groups
    my_group = chan_index()
    my_slab = lax.axis_index("seq")
    tok_rows_total, tok_cols = tokens.shape
    got, value_all = opening(tokens.reshape(groups, tok_rows_total // groups, tok_cols), w_value, 1)
    rows = got.transpose(1, 0, 2).reshape(tok_rows_total // groups, groups * tok_cols)
    chunk = rows.shape[0]
    query = jnp.dot(rows, w_query, preferred_element_type=jnp.float32).astype(jnp.bfloat16)
    key = jnp.dot(rows, w_key, preferred_element_type=jnp.float32).astype(jnp.bfloat16)
    value = jnp.einsum("tf,hfe->the", rows, value_all, preferred_element_type=jnp.float32)
    value = value.astype(jnp.bfloat16).reshape(chunk, groups, per_group * HEAD_DIM)
    query = query.reshape(chunk, groups, per_group * FEAT)
    key = key.reshape(chunk, groups, per_group * FEAT)
    packed = jnp.concatenate([query, key, value], axis=2)
    width = packed.shape[2]
    lanes = chunk * width // HEAD_DIM
    sent = exchange(packed.transpose(1, 0, 2).reshape(groups, lanes, HEAD_DIM), 2)
    mine = sent.reshape(groups * chunk, 1, width)
    tok_rows = mine.shape[0]
    qf = per_group * FEAT
    query_rows = mine[:, 0, :qf].reshape(tok_rows, per_group, FEAT)
    key_rows = mine[:, 0, qf : 2 * qf].reshape(tok_rows, per_group, FEAT)
    value_rows = mine[:, 0, 2 * qf :].reshape(tok_rows, per_group, HEAD_DIM)
    value_cols = per_group * HEAD_DIM
    gain_mine = lax.dynamic_slice_in_dim(gain, my_group * value_cols, value_cols, 0).reshape(
        per_group, HEAD_DIM
    )
    hidden = attend(query_rows, key_rows, value_rows, gain_mine, my_slab)
    hidden_rows = split_rows(hidden, groups, 3)
    mixed_rows = jnp.dot(hidden_rows, w_out, preferred_element_type=jnp.float32).astype(jnp.bfloat16)
    return split_cols(mixed_rows.reshape(chunk, groups, -1), groups, 4)


def solution(mesh):
    seq, chan = mesh.devices.shape
    cores = 2 if chan % 2 == 0 else 1
    split = jax.sharding.Mesh(mesh.devices.reshape(seq, chan // cores, cores), ("seq", "z", "core"))
    return jax.shard_map(
        per_device,
        mesh=split,
        in_specs=(P("seq", CHAN), P(), P(), P(None, CHAN), P(), P()),
        out_specs=P("seq", CHAN),
        check_vma=False,
    )
```

```python
import functools

import jax
import jax.numpy as jnp
from jax import lax
from jax.experimental import pallas as pl
from jax.experimental.pallas import tpu as pltpu
from jax.sharding import PartitionSpec as P

MESH = pl.DeviceIdType.MESH
CHAN = ("z", "core")
W_PIECES = 4


def chan_index():
    return lax.axis_index("z") * lax.axis_size("core") + lax.axis_index("core")


def chan_device(slab, peer):
    cores = lax.axis_size("core")
    return (slab, peer // cores, peer % cores)

HEADS = 16
FEAT = 16
HEAD_DIM = 128
BLOCK = 896


def feature_parts(rows):
    linear = rows * FEAT ** (-0.25)
    square = (rows[..., :, None] * rows[..., None, :]).reshape(rows.shape[:-1] + (FEAT * FEAT,)) * (
        2.0 * FEAT
    ) ** (-0.5)
    return (linear, square)


def exchange_kernel(count, *refs):
    xs, ys, bufs = refs[:count], refs[count : 2 * count], refs[2 * count : 3 * count]
    send_sem, recv_sem, own_sem = refs[3 * count :]
    n = xs[0].shape[0]
    me = chan_index()
    slab = lax.axis_index("seq")
    barrier = pltpu.get_barrier_semaphore()
    for step in range(1, n):
        peer = lax.rem(me + step, n)
        pl.semaphore_signal(barrier, inc=1, device_id=chan_device(slab, peer), device_id_type=MESH)
    pl.semaphore_wait(barrier, n - 1)
    owns = []
    sends = []
    for a in range(count):
        own = pltpu.make_async_copy(xs[a].at[me], bufs[a].at[me], own_sem.at[a])
        own.start()
        owns.append(own)
    for step in range(1, n):
        peer = lax.rem(me + step, n)
        for a in range(count):
            copy = pltpu.make_async_remote_copy(
                src_ref=xs[a].at[peer],
                dst_ref=bufs[a].at[me],
                send_sem=send_sem.at[a, peer],
                recv_sem=recv_sem.at[a, me],
                device_id=chan_device(slab, peer),
                device_id_type=MESH,
            )
            copy.start()
            sends.append(copy)
    for step in range(1, n):
        source = lax.rem(me + n - step, n)
        for a in range(count):
            pltpu.make_async_remote_copy(
                src_ref=xs[a].at[source],
                dst_ref=bufs[a].at[source],
                send_sem=send_sem.at[a, source],
                recv_sem=recv_sem.at[a, source],
                device_id=chan_device(slab, source),
                device_id_type=MESH,
            ).wait_recv()
    for copy in sends:
        copy.wait_send()
    for a in range(count):
        owns[a].wait()
        ys[a][...] = bufs[a][...]


def exchange_many(xs, collective_id):
    count = len(xs)
    n = xs[0].shape[0]
    return pl.pallas_call(
        functools.partial(exchange_kernel, count),
        out_shape=tuple(jax.ShapeDtypeStruct(x.shape, x.dtype) for x in xs),
        in_specs=[pl.BlockSpec(memory_space=pltpu.VMEM)] * count,
        out_specs=tuple(pl.BlockSpec(memory_space=pltpu.VMEM) for _ in xs),
        scratch_shapes=[pltpu.VMEM(x.shape, x.dtype) for x in xs]
        + [
            pltpu.SemaphoreType.DMA((count, n)),
            pltpu.SemaphoreType.DMA((count, n)),
            pltpu.SemaphoreType.DMA((count,)),
        ],
        compiler_params=pltpu.CompilerParams(collective_id=collective_id, has_side_effects=True),
    )(*xs)


def exchange(x, collective_id):
    return exchange_many((x,), collective_id)[0]


def gather_kernel(x_ref, y_ref, buf, send_sem, recv_sem, own_sem):
    n = buf.shape[0]
    me = lax.axis_index("seq")
    here = (lax.axis_index("z"), lax.axis_index("core"))
    barrier = pltpu.get_barrier_semaphore()
    for step in range(1, n):
        peer = lax.rem(me + step, n)
        pl.semaphore_signal(barrier, inc=1, device_id=(peer,) + here, device_id_type=MESH)
    pl.semaphore_wait(barrier, n - 1)
    own = pltpu.make_async_copy(x_ref, buf.at[me], own_sem)
    own.start()
    sends = []
    for step in range(1, n):
        peer = lax.rem(me + step, n)
        copy = pltpu.make_async_remote_copy(
            src_ref=x_ref,
            dst_ref=buf.at[me],
            send_sem=send_sem.at[peer],
            recv_sem=recv_sem.at[me],
            device_id=(peer,) + here,
            device_id_type=MESH,
        )
        copy.start()
        sends.append(copy)
    for step in range(1, n):
        source = lax.rem(me + n - step, n)
        pltpu.make_async_remote_copy(
            src_ref=x_ref,
            dst_ref=buf.at[source],
            send_sem=send_sem.at[source],
            recv_sem=recv_sem.at[source],
            device_id=(source,) + here,
            device_id_type=MESH,
        ).wait_recv()
    for copy in sends:
        copy.wait_send()
    own.wait()
    y_ref[...] = buf[...]


def gather_seq(x, slabs, collective_id):
    shape = (slabs,) + x.shape
    return pl.pallas_call(
        gather_kernel,
        out_shape=jax.ShapeDtypeStruct(shape, x.dtype),
        in_specs=[pl.BlockSpec(memory_space=pltpu.VMEM)],
        out_specs=pl.BlockSpec(memory_space=pltpu.VMEM),
        scratch_shapes=[
            pltpu.VMEM(shape, x.dtype),
            pltpu.SemaphoreType.DMA((slabs,)),
            pltpu.SemaphoreType.DMA((slabs,)),
            pltpu.SemaphoreType.DMA(()),
        ],
        compiler_params=pltpu.CompilerParams(collective_id=collective_id, has_side_effects=True),
    )(x)


def swap_kernel(x_ref, y_ref, send_sem, recv_sem):
    here = (lax.axis_index("seq"), lax.axis_index("z"))
    other = lax.axis_size("core") - 1 - lax.axis_index("core")
    barrier = pltpu.get_barrier_semaphore()
    pl.semaphore_signal(barrier, inc=1, device_id=here + (other,), device_id_type=MESH)
    pl.semaphore_wait(barrier, 1)
    copy = pltpu.make_async_remote_copy(
        src_ref=x_ref,
        dst_ref=y_ref,
        send_sem=send_sem,
        recv_sem=recv_sem,
        device_id=here + (other,),
        device_id_type=MESH,
    )
    copy.start()
    copy.wait()


def swap_cores(x, collective_id):
    return pl.pallas_call(
        swap_kernel,
        out_shape=jax.ShapeDtypeStruct(x.shape, x.dtype),
        in_specs=[pl.BlockSpec(memory_space=pl.ANY)],
        out_specs=pl.BlockSpec(memory_space=pl.ANY),
        scratch_shapes=[pltpu.SemaphoreType.DMA(()), pltpu.SemaphoreType.DMA(())],
        compiler_params=pltpu.CompilerParams(collective_id=collective_id, has_side_effects=True),
    )(x)


def opening_kernel(x_ref, w_ref, y_ref, w_all, buf, send_sem, recv_sem, own_sem, w_send, w_recv, w_own):
    n = x_ref.shape[0]
    cores = lax.axis_size("core")
    ring = n // cores
    me = chan_index()
    slab = lax.axis_index("seq")
    z = lax.axis_index("z")
    core = lax.axis_index("core")
    barrier = pltpu.get_barrier_semaphore()
    for step in range(1, n):
        peer = lax.rem(me + step, n)
        pl.semaphore_signal(barrier, inc=1, device_id=chan_device(slab, peer), device_id_type=MESH)
    pl.semaphore_wait(barrier, n - 1)
    own = pltpu.make_async_copy(x_ref.at[me], buf.at[me], own_sem)
    own.start()
    sends = []
    for step in range(1, n):
        peer = lax.rem(me + step, n)
        copy = pltpu.make_async_remote_copy(
            src_ref=x_ref.at[peer],
            dst_ref=buf.at[me],
            send_sem=send_sem.at[peer],
            recv_sem=recv_sem.at[me],
            device_id=chan_device(slab, peer),
            device_id_type=MESH,
        )
        copy.start()
        sends.append(copy)
    w_local = pltpu.make_async_copy(w_ref, w_all.at[me], w_own)
    w_local.start()
    right = (slab, lax.rem(z + 1, ring), core)
    left = (slab, lax.rem(z + ring - 1, ring), core)
    partner = (slab, z, cores - 1 - core)

    pieces = W_PIECES
    depth = w_ref.shape[0] // pieces

    def slot(origin):
        return lax.rem(origin + ring, ring) * cores + core

    def held(h, j):
        return w_all.at[h, pl.ds(j * depth, depth)]

    def send(source, h, j, kind, target):
        copy = pltpu.make_async_remote_copy(
            src_ref=source,
            dst_ref=held(h, j),
            send_sem=w_send.at[h, kind, j],
            recv_sem=w_recv.at[h, j],
            device_id=target,
            device_id_type=MESH,
        )
        copy.start()
        sends.append(copy)

    def arrive(h, j, source):
        pltpu.make_async_remote_copy(
            src_ref=w_ref.at[pl.ds(j * depth, depth)],
            dst_ref=held(h, j),
            send_sem=w_send.at[h, 0, j],
            recv_sem=w_recv.at[h, j],
            device_id=source,
            device_id_type=MESH,
        ).wait_recv()

    half = ring // 2
    full = half - 1 if ring % 2 == 0 else half

    def goes_right(step):
        return range(pieces) if step <= full else range(pieces // 2) if step == half else range(0)

    def goes_left(step):
        return range(pieces) if step <= full else range(pieces // 2, pieces) if step == half else range(0)

    for j in range(pieces):
        mine = w_ref.at[pl.ds(j * depth, depth)]
        if j in goes_right(1):
            send(mine, me, j, 0, right)
        if j in goes_left(1):
            send(mine, me, j, 1, left)
        send(mine, me, j, 2, partner)
    for step in range(1, half + 1):
        for j in range(pieces):
            if j in goes_right(step):
                h = slot(z - step)
                arrive(h, j, left)
                if j in goes_right(step + 1):
                    send(held(h, j), h, j, 0, right)
                send(held(h, j), h, j, 2, partner)
            if j in goes_left(step):
                h = slot(z + step)
                arrive(h, j, right)
                if j in goes_left(step + 1):
                    send(held(h, j), h, j, 1, left)
                send(held(h, j), h, j, 2, partner)
    for origin in range(ring):
        for j in range(pieces):
            arrive(origin * cores + (cores - 1 - core), j, partner)
    for step in range(1, n):
        source = lax.rem(me + n - step, n)
        pltpu.make_async_remote_copy(
            src_ref=x_ref.at[source],
            dst_ref=buf.at[source],
            send_sem=send_sem.at[source],
            recv_sem=recv_sem.at[source],
            device_id=chan_device(slab, source),
            device_id_type=MESH,
        ).wait_recv()
    for copy in sends:
        copy.wait_send()
    own.wait()
    w_local.wait()
    y_ref[...] = buf[...]


def opening(x, w, collective_id):
    n = x.shape[0]
    return pl.pallas_call(
        opening_kernel,
        out_shape=(
            jax.ShapeDtypeStruct(x.shape, x.dtype),
            jax.ShapeDtypeStruct((n,) + w.shape, w.dtype),
        ),
        in_specs=[pl.BlockSpec(memory_space=pltpu.VMEM), pl.BlockSpec(memory_space=pl.ANY)],
        out_specs=(pl.BlockSpec(memory_space=pltpu.VMEM), pl.BlockSpec(memory_space=pl.ANY)),
        scratch_shapes=[
            pltpu.VMEM(x.shape, x.dtype),
            pltpu.SemaphoreType.DMA((n,)),
            pltpu.SemaphoreType.DMA((n,)),
            pltpu.SemaphoreType.DMA(()),
            pltpu.SemaphoreType.DMA((n, 3, W_PIECES)),
            pltpu.SemaphoreType.DMA((n, W_PIECES)),
            pltpu.SemaphoreType.DMA(()),
        ],
        compiler_params=pltpu.CompilerParams(collective_id=collective_id, has_side_effects=True),
    )(x, w)


def split_rows(x, groups, collective_id):
    rows, cols = x.shape
    got = exchange(x.reshape(groups, rows // groups, cols), collective_id)
    return got.transpose(1, 0, 2).reshape(rows // groups, groups * cols)


def split_cols(x, groups, collective_id):
    rows, _, cols = x.shape
    got = exchange(x.transpose(1, 0, 2), collective_id)
    return got.reshape(groups * rows, cols)


def attend(query_rows, key_rows, value_rows, gain_mine, my_slab):
    highest = lax.Precision.HIGHEST
    tok_rows, per_group, _ = value_rows.shape
    blocks = tok_rows // BLOCK
    query_blocks = query_rows.reshape(blocks, BLOCK, per_group, FEAT)
    key_blocks = key_rows.reshape(blocks, BLOCK, per_group, FEAT)
    value_blocks = value_rows.reshape(blocks, BLOCK, per_group, HEAD_DIM)
    value_f32 = value_blocks.astype(jnp.float32)
    key_linear, key_square = feature_parts(key_blocks.astype(jnp.float32))
    own_zero = jnp.sum(value_f32, axis=1)[:, :, None, :]
    own_one = jnp.einsum("bthf,bthe->bhfe", key_linear, value_f32, precision=highest)
    own_two = jnp.einsum("bthf,bthe->bhfe", key_square, value_f32, precision=highest)
    own = jnp.concatenate([own_zero, own_one, own_two], axis=2)
    slab_total = jnp.sum(own, axis=0)
    state_rows = slab_total.shape[0] * slab_total.shape[1]
    pieces = gather_seq(
        slab_total.astype(jnp.bfloat16).reshape(state_rows, HEAD_DIM), lax.axis_size("seq"), 5
    ).astype(jnp.float32).reshape((-1,) + slab_total.shape)
    count = pieces.shape[0]
    earlier_mask = jnp.arange(count, dtype=jnp.int32) < my_slab
    prefix = jnp.sum(jnp.where(earlier_mask[:, None, None, None], pieces, 0.0), axis=0)
    earlier = jnp.concatenate([jnp.zeros_like(own[:1]), jnp.cumsum(own, axis=0)[:-1]], axis=0) + prefix[None]
    query_linear, query_square = feature_parts(query_blocks.astype(jnp.float32))
    inter = earlier[:, :, 0][:, None] + jnp.einsum(
        "bthf,bhfe->bthe", query_linear, earlier[:, :, 1 : 1 + FEAT], precision=highest
    )
    inter = inter + jnp.einsum(
        "bthf,bhfe->bthe", query_square, earlier[:, :, 1 + FEAT :], precision=highest
    )
    scores = jnp.einsum(
        "bthf,bshf->bhts", query_blocks, key_blocks, preferred_element_type=jnp.float32
    ) * FEAT ** (-0.5)
    kernel = 1.0 + scores + 0.5 * scores * scores
    causal = jnp.arange(BLOCK)[:, None] >= jnp.arange(BLOCK)[None, :]
    weights = jnp.where(causal, kernel, 0.0).astype(jnp.bfloat16)
    intra = jnp.einsum("bhts,bshe->bthe", weights, value_blocks, preferred_element_type=jnp.float32)
    numerator = (intra + inter).reshape(tok_rows, per_group, HEAD_DIM)
    mean_square = jnp.mean(numerator * numerator, axis=-1, keepdims=True)
    hidden = (numerator * lax.rsqrt(mean_square + 1e-05) * gain_mine).astype(jnp.bfloat16)
    return hidden.reshape(tok_rows, per_group * HEAD_DIM)


def per_device(tokens, w_query, w_key, w_value, w_out, gain):
    groups = lax.axis_size(CHAN)
    per_group = HEADS // groups
    my_group = chan_index()
    my_slab = lax.axis_index("seq")
    tok_rows_total, tok_cols = tokens.shape
    got, value_all = opening(tokens.reshape(groups, tok_rows_total // groups, tok_cols), w_value, 1)
    rows = got.transpose(1, 0, 2).reshape(tok_rows_total // groups, groups * tok_cols)
    chunk = rows.shape[0]
    pf = per_group * FEAT
    d_model = w_query.shape[0]
    w_qk = jnp.concatenate(
        [w_query.reshape(d_model, groups, pf), w_key.reshape(d_model, groups, pf)], axis=2
    )
    qk_t = jnp.einsum("tf,fgd->gdt", rows, w_qk, preferred_element_type=jnp.float32).astype(jnp.bfloat16)
    value = jnp.einsum("tf,gfe->gte", rows, value_all, preferred_element_type=jnp.float32).astype(jnp.bfloat16)
    qk_got, value_got = exchange_many((qk_t, value), 2)
    tok_rows = groups * chunk
    qk_rows = qk_got.transpose(0, 2, 1).reshape(tok_rows, 2 * pf)
    query_rows = qk_rows[:, :pf].reshape(tok_rows, per_group, FEAT)
    key_rows = qk_rows[:, pf:].reshape(tok_rows, per_group, FEAT)
    value_rows = value_got.reshape(tok_rows, per_group, HEAD_DIM)
    value_cols = per_group * HEAD_DIM
    gain_mine = lax.dynamic_slice_in_dim(gain, my_group * value_cols, value_cols, 0).reshape(
        per_group, HEAD_DIM
    )
    hidden = attend(query_rows, key_rows, value_rows, gain_mine, my_slab)
    hidden_got = exchange(hidden.reshape(groups, chunk, per_group * HEAD_DIM), 3)
    out_cols = w_out.shape[1] // groups
    mixed_blocks = jnp.einsum(
        "gte,gecj->ctj",
        hidden_got,
        w_out.reshape(groups, per_group * HEAD_DIM, groups, out_cols),
        preferred_element_type=jnp.float32,
    ).astype(jnp.bfloat16)
    return exchange(mixed_blocks, 4).reshape(tok_rows, out_cols)


def solution(mesh):
    seq, chan = mesh.devices.shape
    cores = 2 if chan % 2 == 0 else 1
    split = jax.sharding.Mesh(mesh.devices.reshape(seq, chan // cores, cores), ("seq", "z", "core"))
    return jax.shard_map(
        per_device,
        mesh=split,
        in_specs=(P("seq", CHAN), P(), P(), P(None, CHAN), P(), P()),
        out_specs=P("seq", CHAN),
        check_vma=False,
    )
```

```python
import functools

import jax
import jax.numpy as jnp
from jax import lax
from jax.experimental import pallas as pl
from jax.experimental.pallas import tpu as pltpu
from jax.sharding import PartitionSpec as P

MESH = pl.DeviceIdType.MESH
CHAN = ("z", "core")
W_PIECES = 4


def chan_index():
    return lax.axis_index("z") * lax.axis_size("core") + lax.axis_index("core")


def chan_device(slab, peer):
    cores = lax.axis_size("core")
    return (slab, peer // cores, peer % cores)

HEADS = 16
FEAT = 16
HEAD_DIM = 128
BLOCK = 896


def feature_parts(rows):
    linear = rows * FEAT ** (-0.25)
    square = (rows[..., :, None] * rows[..., None, :]).reshape(rows.shape[:-1] + (FEAT * FEAT,)) * (
        2.0 * FEAT
    ) ** (-0.5)
    return (linear, square)


def exchange_kernel(count, *refs):
    xs, ys, bufs = refs[:count], refs[count : 2 * count], refs[2 * count : 3 * count]
    send_sem, recv_sem, own_sem = refs[3 * count :]
    n = xs[0].shape[0]
    me = chan_index()
    slab = lax.axis_index("seq")
    barrier = pltpu.get_barrier_semaphore()
    for step in range(1, n):
        peer = lax.rem(me + step, n)
        pl.semaphore_signal(barrier, inc=1, device_id=chan_device(slab, peer), device_id_type=MESH)
    pl.semaphore_wait(barrier, n - 1)
    owns = []
    sends = []
    for a in range(count):
        own = pltpu.make_async_copy(xs[a].at[me], bufs[a].at[me], own_sem.at[a])
        own.start()
        owns.append(own)
    for step in range(1, n):
        peer = lax.rem(me + step, n)
        for a in range(count):
            copy = pltpu.make_async_remote_copy(
                src_ref=xs[a].at[peer],
                dst_ref=bufs[a].at[me],
                send_sem=send_sem.at[a, peer],
                recv_sem=recv_sem.at[a, me],
                device_id=chan_device(slab, peer),
                device_id_type=MESH,
            )
            copy.start()
            sends.append(copy)
    for step in range(1, n):
        source = lax.rem(me + n - step, n)
        for a in range(count):
            pltpu.make_async_remote_copy(
                src_ref=xs[a].at[source],
                dst_ref=bufs[a].at[source],
                send_sem=send_sem.at[a, source],
                recv_sem=recv_sem.at[a, source],
                device_id=chan_device(slab, source),
                device_id_type=MESH,
            ).wait_recv()
    for copy in sends:
        copy.wait_send()
    for a in range(count):
        owns[a].wait()
        ys[a][...] = bufs[a][...]


def exchange_many(xs, collective_id):
    count = len(xs)
    n = xs[0].shape[0]
    return pl.pallas_call(
        functools.partial(exchange_kernel, count),
        out_shape=tuple(jax.ShapeDtypeStruct(x.shape, x.dtype) for x in xs),
        in_specs=[pl.BlockSpec(memory_space=pltpu.VMEM)] * count,
        out_specs=tuple(pl.BlockSpec(memory_space=pltpu.VMEM) for _ in xs),
        scratch_shapes=[pltpu.VMEM(x.shape, x.dtype) for x in xs]
        + [
            pltpu.SemaphoreType.DMA((count, n)),
            pltpu.SemaphoreType.DMA((count, n)),
            pltpu.SemaphoreType.DMA((count,)),
        ],
        compiler_params=pltpu.CompilerParams(collective_id=collective_id, has_side_effects=True),
    )(*xs)


def exchange(x, collective_id):
    return exchange_many((x,), collective_id)[0]


def gather_kernel(x_ref, y_ref, buf, send_sem, recv_sem, own_sem):
    n = buf.shape[0]
    me = lax.axis_index("seq")
    here = (lax.axis_index("z"), lax.axis_index("core"))
    barrier = pltpu.get_barrier_semaphore()
    for step in range(1, n):
        peer = lax.rem(me + step, n)
        pl.semaphore_signal(barrier, inc=1, device_id=(peer,) + here, device_id_type=MESH)
    pl.semaphore_wait(barrier, n - 1)
    own = pltpu.make_async_copy(x_ref, buf.at[me], own_sem)
    own.start()
    sends = []
    for step in range(1, n):
        peer = lax.rem(me + step, n)
        copy = pltpu.make_async_remote_copy(
            src_ref=x_ref,
            dst_ref=buf.at[me],
            send_sem=send_sem.at[peer],
            recv_sem=recv_sem.at[me],
            device_id=(peer,) + here,
            device_id_type=MESH,
        )
        copy.start()
        sends.append(copy)
    for step in range(1, n):
        source = lax.rem(me + n - step, n)
        pltpu.make_async_remote_copy(
            src_ref=x_ref,
            dst_ref=buf.at[source],
            send_sem=send_sem.at[source],
            recv_sem=recv_sem.at[source],
            device_id=(source,) + here,
            device_id_type=MESH,
        ).wait_recv()
    for copy in sends:
        copy.wait_send()
    own.wait()
    y_ref[...] = buf[...]


def gather_seq(x, slabs, collective_id):
    shape = (slabs,) + x.shape
    return pl.pallas_call(
        gather_kernel,
        out_shape=jax.ShapeDtypeStruct(shape, x.dtype),
        in_specs=[pl.BlockSpec(memory_space=pltpu.VMEM)],
        out_specs=pl.BlockSpec(memory_space=pltpu.VMEM),
        scratch_shapes=[
            pltpu.VMEM(shape, x.dtype),
            pltpu.SemaphoreType.DMA((slabs,)),
            pltpu.SemaphoreType.DMA((slabs,)),
            pltpu.SemaphoreType.DMA(()),
        ],
        compiler_params=pltpu.CompilerParams(collective_id=collective_id, has_side_effects=True),
    )(x)


def swap_kernel(x_ref, y_ref, send_sem, recv_sem):
    here = (lax.axis_index("seq"), lax.axis_index("z"))
    other = lax.axis_size("core") - 1 - lax.axis_index("core")
    barrier = pltpu.get_barrier_semaphore()
    pl.semaphore_signal(barrier, inc=1, device_id=here + (other,), device_id_type=MESH)
    pl.semaphore_wait(barrier, 1)
    copy = pltpu.make_async_remote_copy(
        src_ref=x_ref,
        dst_ref=y_ref,
        send_sem=send_sem,
        recv_sem=recv_sem,
        device_id=here + (other,),
        device_id_type=MESH,
    )
    copy.start()
    copy.wait()


def swap_cores(x, collective_id):
    return pl.pallas_call(
        swap_kernel,
        out_shape=jax.ShapeDtypeStruct(x.shape, x.dtype),
        in_specs=[pl.BlockSpec(memory_space=pl.ANY)],
        out_specs=pl.BlockSpec(memory_space=pl.ANY),
        scratch_shapes=[pltpu.SemaphoreType.DMA(()), pltpu.SemaphoreType.DMA(())],
        compiler_params=pltpu.CompilerParams(collective_id=collective_id, has_side_effects=True),
    )(x)


def opening_kernel(x_ref, w_ref, y_ref, w_all, buf, send_sem, recv_sem, own_sem, w_send, w_recv, w_own):
    n = x_ref.shape[0]
    cores = lax.axis_size("core")
    ring = n // cores
    me = chan_index()
    slab = lax.axis_index("seq")
    z = lax.axis_index("z")
    core = lax.axis_index("core")
    barrier = pltpu.get_barrier_semaphore()
    for step in range(1, n):
        peer = lax.rem(me + step, n)
        pl.semaphore_signal(barrier, inc=1, device_id=chan_device(slab, peer), device_id_type=MESH)
    pl.semaphore_wait(barrier, n - 1)
    own = pltpu.make_async_copy(x_ref.at[me], buf.at[me], own_sem)
    own.start()
    sends = []
    for step in range(1, n):
        peer = lax.rem(me + step, n)
        copy = pltpu.make_async_remote_copy(
            src_ref=x_ref.at[peer],
            dst_ref=buf.at[me],
            send_sem=send_sem.at[peer],
            recv_sem=recv_sem.at[me],
            device_id=chan_device(slab, peer),
            device_id_type=MESH,
        )
        copy.start()
        sends.append(copy)
    w_local = pltpu.make_async_copy(w_ref, w_all.at[me], w_own)
    w_local.start()
    right = (slab, lax.rem(z + 1, ring), core)
    left = (slab, lax.rem(z + ring - 1, ring), core)
    partner = (slab, z, cores - 1 - core)

    pieces = W_PIECES
    depth = w_ref.shape[0] // pieces

    def slot(origin):
        return lax.rem(origin + ring, ring) * cores + core

    def held(h, j):
        return w_all.at[h, pl.ds(j * depth, depth)]

    def send(source, h, j, kind, target):
        copy = pltpu.make_async_remote_copy(
            src_ref=source,
            dst_ref=held(h, j),
            send_sem=w_send.at[h, kind, j],
            recv_sem=w_recv.at[h, j],
            device_id=target,
            device_id_type=MESH,
        )
        copy.start()
        sends.append(copy)

    def arrive(h, j, source):
        pltpu.make_async_remote_copy(
            src_ref=w_ref.at[pl.ds(j * depth, depth)],
            dst_ref=held(h, j),
            send_sem=w_send.at[h, 0, j],
            recv_sem=w_recv.at[h, j],
            device_id=source,
            device_id_type=MESH,
        ).wait_recv()

    half = ring // 2
    full = half - 1 if ring % 2 == 0 else half

    def goes_right(step):
        return range(pieces) if step <= full else range(pieces // 2) if step == half else range(0)

    def goes_left(step):
        return range(pieces) if step <= full else range(pieces // 2, pieces) if step == half else range(0)

    for j in range(pieces):
        mine = w_ref.at[pl.ds(j * depth, depth)]
        if j in goes_right(1):
            send(mine, me, j, 0, right)
        if j in goes_left(1):
            send(mine, me, j, 1, left)
        send(mine, me, j, 2, partner)
    for step in range(1, half + 1):
        for j in range(pieces):
            if j in goes_right(step):
                h = slot(z - step)
                arrive(h, j, left)
                if j in goes_right(step + 1):
                    send(held(h, j), h, j, 0, right)
                send(held(h, j), h, j, 2, partner)
            if j in goes_left(step):
                h = slot(z + step)
                arrive(h, j, right)
                if j in goes_left(step + 1):
                    send(held(h, j), h, j, 1, left)
                send(held(h, j), h, j, 2, partner)
    for origin in range(ring):
        for j in range(pieces):
            arrive(origin * cores + (cores - 1 - core), j, partner)
    for step in range(1, n):
        source = lax.rem(me + n - step, n)
        pltpu.make_async_remote_copy(
            src_ref=x_ref.at[source],
            dst_ref=buf.at[source],
            send_sem=send_sem.at[source],
            recv_sem=recv_sem.at[source],
            device_id=chan_device(slab, source),
            device_id_type=MESH,
        ).wait_recv()
    for copy in sends:
        copy.wait_send()
    own.wait()
    w_local.wait()
    y_ref[...] = buf[...]


def opening(x, w, collective_id):
    n = x.shape[0]
    return pl.pallas_call(
        opening_kernel,
        out_shape=(
            jax.ShapeDtypeStruct(x.shape, x.dtype),
            jax.ShapeDtypeStruct((n,) + w.shape, w.dtype),
        ),
        in_specs=[pl.BlockSpec(memory_space=pltpu.VMEM), pl.BlockSpec(memory_space=pl.ANY)],
        out_specs=(pl.BlockSpec(memory_space=pltpu.VMEM), pl.BlockSpec(memory_space=pl.ANY)),
        scratch_shapes=[
            pltpu.VMEM(x.shape, x.dtype),
            pltpu.SemaphoreType.DMA((n,)),
            pltpu.SemaphoreType.DMA((n,)),
            pltpu.SemaphoreType.DMA(()),
            pltpu.SemaphoreType.DMA((n, 3, W_PIECES)),
            pltpu.SemaphoreType.DMA((n, W_PIECES)),
            pltpu.SemaphoreType.DMA(()),
        ],
        compiler_params=pltpu.CompilerParams(collective_id=collective_id, has_side_effects=True),
    )(x, w)


def split_rows(x, groups, collective_id):
    rows, cols = x.shape
    got = exchange(x.reshape(groups, rows // groups, cols), collective_id)
    return got.transpose(1, 0, 2).reshape(rows // groups, groups * cols)


def split_cols(x, groups, collective_id):
    rows, _, cols = x.shape
    got = exchange(x.transpose(1, 0, 2), collective_id)
    return got.reshape(groups * rows, cols)


def attend(query_rows, key_rows, value_rows, gain_mine, my_slab):
    highest = lax.Precision.HIGHEST
    tok_rows, per_group, _ = value_rows.shape
    blocks = tok_rows // BLOCK
    query_blocks = query_rows.reshape(blocks, BLOCK, per_group, FEAT)
    key_blocks = key_rows.reshape(blocks, BLOCK, per_group, FEAT)
    value_blocks = value_rows.reshape(blocks, BLOCK, per_group, HEAD_DIM)
    value_f32 = value_blocks.astype(jnp.float32)
    key_linear, key_square = feature_parts(key_blocks.astype(jnp.float32))
    own_zero = jnp.sum(value_f32, axis=1)[:, :, None, :]
    own_one = jnp.einsum("bthf,bthe->bhfe", key_linear, value_f32, precision=highest)
    own_two = jnp.einsum("bthf,bthe->bhfe", key_square, value_f32, precision=highest)
    own = jnp.concatenate([own_zero, own_one, own_two], axis=2)
    slab_total = jnp.sum(own, axis=0)
    state_rows = slab_total.shape[0] * slab_total.shape[1]
    pieces = gather_seq(
        slab_total.astype(jnp.bfloat16).reshape(state_rows, HEAD_DIM), lax.axis_size("seq"), 5
    ).astype(jnp.float32).reshape((-1,) + slab_total.shape)
    count = pieces.shape[0]
    earlier_mask = jnp.arange(count, dtype=jnp.int32) < my_slab
    prefix = jnp.sum(jnp.where(earlier_mask[:, None, None, None], pieces, 0.0), axis=0)
    earlier = jnp.concatenate([jnp.zeros_like(own[:1]), jnp.cumsum(own, axis=0)[:-1]], axis=0) + prefix[None]
    query_linear, query_square = feature_parts(query_blocks.astype(jnp.float32))
    inter = earlier[:, :, 0][:, None] + jnp.einsum(
        "bthf,bhfe->bthe", query_linear, earlier[:, :, 1 : 1 + FEAT], precision=highest
    )
    inter = inter + jnp.einsum(
        "bthf,bhfe->bthe", query_square, earlier[:, :, 1 + FEAT :], precision=highest
    )
    scores = jnp.einsum(
        "bthf,bshf->bhts", query_blocks, key_blocks, preferred_element_type=jnp.float32
    ) * FEAT ** (-0.5)
    kernel = 1.0 + scores + 0.5 * scores * scores
    causal = jnp.arange(BLOCK)[:, None] >= jnp.arange(BLOCK)[None, :]
    weights = jnp.where(causal, kernel, 0.0).astype(jnp.bfloat16)
    intra = jnp.einsum("bhts,bshe->bthe", weights, value_blocks, preferred_element_type=jnp.float32)
    numerator = (intra + inter).reshape(tok_rows, per_group, HEAD_DIM)
    mean_square = jnp.mean(numerator * numerator, axis=-1, keepdims=True)
    hidden = (numerator * lax.rsqrt(mean_square + 1e-05) * gain_mine).astype(jnp.bfloat16)
    return hidden.reshape(tok_rows, per_group * HEAD_DIM)


def per_device(tokens, w_query, w_key, w_value, w_out, gain):
    groups = lax.axis_size(CHAN)
    per_group = HEADS // groups
    my_group = chan_index()
    my_slab = lax.axis_index("seq")
    tok_rows_total, tok_cols = tokens.shape
    got, value_all = opening(tokens.reshape(groups, tok_rows_total // groups, tok_cols), w_value, 1)
    rows = got.transpose(1, 0, 2).reshape(tok_rows_total // groups, groups * tok_cols)
    chunk = rows.shape[0]
    pf = per_group * FEAT
    d_model = w_query.shape[0]
    w_qk = jnp.concatenate(
        [w_query.reshape(d_model, groups, pf), w_key.reshape(d_model, groups, pf)], axis=2
    )
    qk_t = jnp.einsum("tf,fgd->gdt", rows, w_qk, preferred_element_type=jnp.float32).astype(jnp.bfloat16)
    value = jnp.einsum("tf,gfe->gte", rows, value_all, preferred_element_type=jnp.float32).astype(jnp.bfloat16)
    qk_got, value_got = exchange_many((qk_t, value), 2)
    tok_rows = groups * chunk
    qk_rows = qk_got.transpose(0, 2, 1).reshape(tok_rows, 2 * pf)
    query_rows = qk_rows[:, :pf].reshape(tok_rows, per_group, FEAT)
    key_rows = qk_rows[:, pf:].reshape(tok_rows, per_group, FEAT)
    value_rows = value_got.reshape(tok_rows, per_group, HEAD_DIM)
    value_cols = per_group * HEAD_DIM
    gain_mine = lax.dynamic_slice_in_dim(gain, my_group * value_cols, value_cols, 0).reshape(
        per_group, HEAD_DIM
    )
    hidden = attend(query_rows, key_rows, value_rows, gain_mine, my_slab)
    hidden_got = exchange(hidden.reshape(groups, chunk, per_group * HEAD_DIM), 3)
    out_cols = w_out.shape[1] // groups
    mixed_rows = jnp.einsum(
        "gte,gef->tf",
        hidden_got,
        w_out.reshape(groups, per_group * HEAD_DIM, w_out.shape[1]),
        preferred_element_type=jnp.float32,
    ).astype(jnp.bfloat16)
    mixed_blocks = mixed_rows.reshape(chunk, groups, out_cols).transpose(1, 0, 2)
    return exchange(mixed_blocks, 4).reshape(tok_rows, out_cols)


def solution(mesh):
    seq, chan = mesh.devices.shape
    cores = 2 if chan % 2 == 0 else 1
    split = jax.sharding.Mesh(mesh.devices.reshape(seq, chan // cores, cores), ("seq", "z", "core"))
    return jax.shard_map(
        per_device,
        mesh=split,
        in_specs=(P("seq", CHAN), P(), P(), P(None, CHAN), P(), P()),
        out_specs=P("seq", CHAN),
        check_vma=False,
    )
```

```python
import functools

import jax
import jax.numpy as jnp
from jax import lax
from jax.experimental import pallas as pl
from jax.experimental.pallas import tpu as pltpu
from jax.sharding import PartitionSpec as P

MESH = pl.DeviceIdType.MESH
CHAN = ("z", "core")
W_PIECES = 4


def chan_index():
    return lax.axis_index("z") * lax.axis_size("core") + lax.axis_index("core")


def chan_device(slab, peer):
    cores = lax.axis_size("core")
    return (slab, peer // cores, peer % cores)

HEADS = 16
FEAT = 16
HEAD_DIM = 128
BLOCK = 896


def feature_parts(rows):
    linear = rows * FEAT ** (-0.25)
    square = (rows[..., :, None] * rows[..., None, :]).reshape(rows.shape[:-1] + (FEAT * FEAT,)) * (
        2.0 * FEAT
    ) ** (-0.5)
    return (linear, square)


def exchange_kernel(count, *refs):
    xs, ys, bufs = refs[:count], refs[count : 2 * count], refs[2 * count : 3 * count]
    send_sem, recv_sem, own_sem = refs[3 * count :]
    n = xs[0].shape[0]
    me = chan_index()
    slab = lax.axis_index("seq")
    barrier = pltpu.get_barrier_semaphore()
    for step in range(1, n):
        peer = lax.rem(me + step, n)
        pl.semaphore_signal(barrier, inc=1, device_id=chan_device(slab, peer), device_id_type=MESH)
    pl.semaphore_wait(barrier, n - 1)
    owns = []
    sends = []
    for a in range(count):
        own = pltpu.make_async_copy(xs[a].at[me], bufs[a].at[me], own_sem.at[a])
        own.start()
        owns.append(own)
    for step in range(1, n):
        peer = lax.rem(me + step, n)
        for a in range(count):
            copy = pltpu.make_async_remote_copy(
                src_ref=xs[a].at[peer],
                dst_ref=bufs[a].at[me],
                send_sem=send_sem.at[a, peer],
                recv_sem=recv_sem.at[a, me],
                device_id=chan_device(slab, peer),
                device_id_type=MESH,
            )
            copy.start()
            sends.append(copy)
    for step in range(1, n):
        source = lax.rem(me + n - step, n)
        for a in range(count):
            pltpu.make_async_remote_copy(
                src_ref=xs[a].at[source],
                dst_ref=bufs[a].at[source],
                send_sem=send_sem.at[a, source],
                recv_sem=recv_sem.at[a, source],
                device_id=chan_device(slab, source),
                device_id_type=MESH,
            ).wait_recv()
    for copy in sends:
        copy.wait_send()
    for a in range(count):
        owns[a].wait()
        ys[a][...] = bufs[a][...]


def exchange_many(xs, collective_id):
    count = len(xs)
    n = xs[0].shape[0]
    return pl.pallas_call(
        functools.partial(exchange_kernel, count),
        out_shape=tuple(jax.ShapeDtypeStruct(x.shape, x.dtype) for x in xs),
        in_specs=[pl.BlockSpec(memory_space=pltpu.VMEM)] * count,
        out_specs=tuple(pl.BlockSpec(memory_space=pltpu.VMEM) for _ in xs),
        scratch_shapes=[pltpu.VMEM(x.shape, x.dtype) for x in xs]
        + [
            pltpu.SemaphoreType.DMA((count, n)),
            pltpu.SemaphoreType.DMA((count, n)),
            pltpu.SemaphoreType.DMA((count,)),
        ],
        compiler_params=pltpu.CompilerParams(collective_id=collective_id, has_side_effects=True),
    )(*xs)


def exchange(x, collective_id):
    return exchange_many((x,), collective_id)[0]


def gather_kernel(x_ref, y_ref, buf, send_sem, recv_sem):
    n = buf.shape[0]
    me = lax.axis_index("seq")
    here = (lax.axis_index("z"), lax.axis_index("core"))
    buf[...] = jnp.zeros_like(buf)
    barrier = pltpu.get_barrier_semaphore()
    for step in range(1, n):
        peer = lax.rem(me + step, n)
        pl.semaphore_signal(barrier, inc=1, device_id=(peer,) + here, device_id_type=MESH)
    pl.semaphore_wait(barrier, n - 1)

    def copy_to(peer):
        return pltpu.make_async_remote_copy(
            src_ref=x_ref,
            dst_ref=buf.at[me],
            send_sem=send_sem.at[peer],
            recv_sem=recv_sem.at[me],
            device_id=(peer,) + here,
            device_id_type=MESH,
        )

    def copy_from(source):
        return pltpu.make_async_remote_copy(
            src_ref=x_ref,
            dst_ref=buf.at[source],
            send_sem=send_sem.at[source],
            recv_sem=recv_sem.at[source],
            device_id=(source,) + here,
            device_id_type=MESH,
        )

    for step in range(1, n):
        @pl.when(me + step < n)
        def _():
            copy_to(me + step).start()

    for step in range(1, n):
        @pl.when(me - step >= 0)
        def _():
            copy_from(me - step).wait_recv()

    for step in range(1, n):
        @pl.when(me + step < n)
        def _():
            copy_to(me + step).wait_send()

    y_ref[...] = buf[...]


def gather_seq(x, slabs, collective_id):
    shape = (slabs,) + x.shape
    return pl.pallas_call(
        gather_kernel,
        out_shape=jax.ShapeDtypeStruct(shape, x.dtype),
        in_specs=[pl.BlockSpec(memory_space=pltpu.VMEM)],
        out_specs=pl.BlockSpec(memory_space=pltpu.VMEM),
        scratch_shapes=[
            pltpu.VMEM(shape, x.dtype),
            pltpu.SemaphoreType.DMA((slabs,)),
            pltpu.SemaphoreType.DMA((slabs,)),
        ],
        compiler_params=pltpu.CompilerParams(collective_id=collective_id, has_side_effects=True),
    )(x)


def swap_kernel(x_ref, y_ref, send_sem, recv_sem):
    here = (lax.axis_index("seq"), lax.axis_index("z"))
    other = lax.axis_size("core") - 1 - lax.axis_index("core")
    barrier = pltpu.get_barrier_semaphore()
    pl.semaphore_signal(barrier, inc=1, device_id=here + (other,), device_id_type=MESH)
    pl.semaphore_wait(barrier, 1)
    copy = pltpu.make_async_remote_copy(
        src_ref=x_ref,
        dst_ref=y_ref,
        send_sem=send_sem,
        recv_sem=recv_sem,
        device_id=here + (other,),
        device_id_type=MESH,
    )
    copy.start()
    copy.wait()


def swap_cores(x, collective_id):
    return pl.pallas_call(
        swap_kernel,
        out_shape=jax.ShapeDtypeStruct(x.shape, x.dtype),
        in_specs=[pl.BlockSpec(memory_space=pl.ANY)],
        out_specs=pl.BlockSpec(memory_space=pl.ANY),
        scratch_shapes=[pltpu.SemaphoreType.DMA(()), pltpu.SemaphoreType.DMA(())],
        compiler_params=pltpu.CompilerParams(collective_id=collective_id, has_side_effects=True),
    )(x)


def opening_kernel(x_ref, w_ref, y_ref, w_all, buf, send_sem, recv_sem, own_sem, w_send, w_recv, w_own):
    n = x_ref.shape[0]
    cores = lax.axis_size("core")
    ring = n // cores
    me = chan_index()
    slab = lax.axis_index("seq")
    z = lax.axis_index("z")
    core = lax.axis_index("core")
    barrier = pltpu.get_barrier_semaphore()
    for step in range(1, n):
        peer = lax.rem(me + step, n)
        pl.semaphore_signal(barrier, inc=1, device_id=chan_device(slab, peer), device_id_type=MESH)
    pl.semaphore_wait(barrier, n - 1)
    own = pltpu.make_async_copy(x_ref.at[me], buf.at[me], own_sem)
    own.start()
    sends = []
    for step in range(1, n):
        peer = lax.rem(me + step, n)
        copy = pltpu.make_async_remote_copy(
            src_ref=x_ref.at[peer],
            dst_ref=buf.at[me],
            send_sem=send_sem.at[peer],
            recv_sem=recv_sem.at[me],
            device_id=chan_device(slab, peer),
            device_id_type=MESH,
        )
        copy.start()
        sends.append(copy)
    w_local = pltpu.make_async_copy(w_ref, w_all.at[me], w_own)
    w_local.start()
    right = (slab, lax.rem(z + 1, ring), core)
    left = (slab, lax.rem(z + ring - 1, ring), core)
    partner = (slab, z, cores - 1 - core)

    pieces = W_PIECES
    depth = w_ref.shape[0] // pieces

    def slot(origin):
        return lax.rem(origin + ring, ring) * cores + core

    def held(h, j):
        return w_all.at[h, pl.ds(j * depth, depth)]

    def send(source, h, j, kind, target):
        copy = pltpu.make_async_remote_copy(
            src_ref=source,
            dst_ref=held(h, j),
            send_sem=w_send.at[h, kind, j],
            recv_sem=w_recv.at[h, j],
            device_id=target,
            device_id_type=MESH,
        )
        copy.start()
        sends.append(copy)

    def arrive(h, j, source):
        pltpu.make_async_remote_copy(
            src_ref=w_ref.at[pl.ds(j * depth, depth)],
            dst_ref=held(h, j),
            send_sem=w_send.at[h, 0, j],
            recv_sem=w_recv.at[h, j],
            device_id=source,
            device_id_type=MESH,
        ).wait_recv()

    half = ring // 2
    full = half - 1 if ring % 2 == 0 else half

    def goes_right(step):
        return range(pieces) if step <= full else range(pieces // 2) if step == half else range(0)

    def goes_left(step):
        return range(pieces) if step <= full else range(pieces // 2, pieces) if step == half else range(0)

    for j in range(pieces):
        mine = w_ref.at[pl.ds(j * depth, depth)]
        if j in goes_right(1):
            send(mine, me, j, 0, right)
        if j in goes_left(1):
            send(mine, me, j, 1, left)
        send(mine, me, j, 2, partner)
    for step in range(1, half + 1):
        for j in range(pieces):
            if j in goes_right(step):
                h = slot(z - step)
                arrive(h, j, left)
                if j in goes_right(step + 1):
                    send(held(h, j), h, j, 0, right)
                send(held(h, j), h, j, 2, partner)
            if j in goes_left(step):
                h = slot(z + step)
                arrive(h, j, right)
                if j in goes_left(step + 1):
                    send(held(h, j), h, j, 1, left)
                send(held(h, j), h, j, 2, partner)
    for origin in range(ring):
        for j in range(pieces):
            arrive(origin * cores + (cores - 1 - core), j, partner)
    for step in range(1, n):
        source = lax.rem(me + n - step, n)
        pltpu.make_async_remote_copy(
            src_ref=x_ref.at[source],
            dst_ref=buf.at[source],
            send_sem=send_sem.at[source],
            recv_sem=recv_sem.at[source],
            device_id=chan_device(slab, source),
            device_id_type=MESH,
        ).wait_recv()
    for copy in sends:
        copy.wait_send()
    own.wait()
    w_local.wait()
    y_ref[...] = buf[...]


def opening(x, w, collective_id):
    n = x.shape[0]
    return pl.pallas_call(
        opening_kernel,
        out_shape=(
            jax.ShapeDtypeStruct(x.shape, x.dtype),
            jax.ShapeDtypeStruct((n,) + w.shape, w.dtype),
        ),
        in_specs=[pl.BlockSpec(memory_space=pltpu.VMEM), pl.BlockSpec(memory_space=pl.ANY)],
        out_specs=(pl.BlockSpec(memory_space=pltpu.VMEM), pl.BlockSpec(memory_space=pl.ANY)),
        scratch_shapes=[
            pltpu.VMEM(x.shape, x.dtype),
            pltpu.SemaphoreType.DMA((n,)),
            pltpu.SemaphoreType.DMA((n,)),
            pltpu.SemaphoreType.DMA(()),
            pltpu.SemaphoreType.DMA((n, 3, W_PIECES)),
            pltpu.SemaphoreType.DMA((n, W_PIECES)),
            pltpu.SemaphoreType.DMA(()),
        ],
        compiler_params=pltpu.CompilerParams(collective_id=collective_id, has_side_effects=True),
    )(x, w)


def split_rows(x, groups, collective_id):
    rows, cols = x.shape
    got = exchange(x.reshape(groups, rows // groups, cols), collective_id)
    return got.transpose(1, 0, 2).reshape(rows // groups, groups * cols)


def split_cols(x, groups, collective_id):
    rows, _, cols = x.shape
    got = exchange(x.transpose(1, 0, 2), collective_id)
    return got.reshape(groups * rows, cols)


def attend(query_rows, key_rows, value_rows, gain_mine, my_slab):
    highest = lax.Precision.HIGHEST
    tok_rows, per_group, _ = value_rows.shape
    blocks = tok_rows // BLOCK
    query_blocks = query_rows.reshape(blocks, BLOCK, per_group, FEAT)
    key_blocks = key_rows.reshape(blocks, BLOCK, per_group, FEAT)
    value_blocks = value_rows.reshape(blocks, BLOCK, per_group, HEAD_DIM)
    value_f32 = value_blocks.astype(jnp.float32)
    key_linear, key_square = feature_parts(key_blocks.astype(jnp.float32))
    own_zero = jnp.sum(value_f32, axis=1)[:, :, None, :]
    own_one = jnp.einsum("bthf,bthe->bhfe", key_linear, value_f32, precision=highest)
    own_two = jnp.einsum("bthf,bthe->bhfe", key_square, value_f32, precision=highest)
    own = jnp.concatenate([own_zero, own_one, own_two], axis=2)
    slab_total = jnp.sum(own, axis=0)
    state_rows = slab_total.shape[0] * slab_total.shape[1]
    pieces = gather_seq(
        slab_total.astype(jnp.bfloat16).reshape(state_rows, HEAD_DIM), lax.axis_size("seq"), 5
    ).astype(jnp.float32).reshape((-1,) + slab_total.shape)
    count = pieces.shape[0]
    earlier_mask = jnp.arange(count, dtype=jnp.int32) < my_slab
    prefix = jnp.sum(jnp.where(earlier_mask[:, None, None, None], pieces, 0.0), axis=0)
    earlier = jnp.concatenate([jnp.zeros_like(own[:1]), jnp.cumsum(own, axis=0)[:-1]], axis=0) + prefix[None]
    query_linear, query_square = feature_parts(query_blocks.astype(jnp.float32))
    inter = earlier[:, :, 0][:, None] + jnp.einsum(
        "bthf,bhfe->bthe", query_linear, earlier[:, :, 1 : 1 + FEAT], precision=highest
    )
    inter = inter + jnp.einsum(
        "bthf,bhfe->bthe", query_square, earlier[:, :, 1 + FEAT :], precision=highest
    )
    scores = jnp.einsum(
        "bthf,bshf->bhts", query_blocks, key_blocks, preferred_element_type=jnp.float32
    ) * FEAT ** (-0.5)
    kernel = 1.0 + scores + 0.5 * scores * scores
    causal = jnp.arange(BLOCK)[:, None] >= jnp.arange(BLOCK)[None, :]
    weights = jnp.where(causal, kernel, 0.0).astype(jnp.bfloat16)
    intra = jnp.einsum("bhts,bshe->bthe", weights, value_blocks, preferred_element_type=jnp.float32)
    numerator = (intra + inter).reshape(tok_rows, per_group, HEAD_DIM)
    mean_square = jnp.mean(numerator * numerator, axis=-1, keepdims=True)
    hidden = (numerator * lax.rsqrt(mean_square + 1e-05) * gain_mine).astype(jnp.bfloat16)
    return hidden.reshape(tok_rows, per_group * HEAD_DIM)


def per_device(tokens, w_query, w_key, w_value, w_out, gain):
    groups = lax.axis_size(CHAN)
    per_group = HEADS // groups
    my_group = chan_index()
    my_slab = lax.axis_index("seq")
    tok_rows_total, tok_cols = tokens.shape
    got, value_all = opening(tokens.reshape(groups, tok_rows_total // groups, tok_cols), w_value, 1)
    rows = got.transpose(1, 0, 2).reshape(tok_rows_total // groups, groups * tok_cols)
    chunk = rows.shape[0]
    pf = per_group * FEAT
    d_model = w_query.shape[0]
    w_qk = jnp.concatenate(
        [w_query.reshape(d_model, groups, pf), w_key.reshape(d_model, groups, pf)], axis=2
    )
    qk_t = jnp.einsum("tf,fgd->gdt", rows, w_qk, preferred_element_type=jnp.float32).astype(jnp.bfloat16)
    value = jnp.einsum("tf,gfe->gte", rows, value_all, preferred_element_type=jnp.float32).astype(jnp.bfloat16)
    qk_got, value_got = exchange_many((qk_t, value), 2)
    tok_rows = groups * chunk
    qk_rows = qk_got.transpose(0, 2, 1).reshape(tok_rows, 2 * pf)
    query_rows = qk_rows[:, :pf].reshape(tok_rows, per_group, FEAT)
    key_rows = qk_rows[:, pf:].reshape(tok_rows, per_group, FEAT)
    value_rows = value_got.reshape(tok_rows, per_group, HEAD_DIM)
    value_cols = per_group * HEAD_DIM
    gain_mine = lax.dynamic_slice_in_dim(gain, my_group * value_cols, value_cols, 0).reshape(
        per_group, HEAD_DIM
    )
    hidden = attend(query_rows, key_rows, value_rows, gain_mine, my_slab)
    hidden_got = exchange(hidden.reshape(groups, chunk, per_group * HEAD_DIM), 3)
    out_cols = w_out.shape[1] // groups
    mixed_rows = jnp.einsum(
        "gte,gef->tf",
        hidden_got,
        w_out.reshape(groups, per_group * HEAD_DIM, w_out.shape[1]),
        preferred_element_type=jnp.float32,
    ).astype(jnp.bfloat16)
    mixed_blocks = mixed_rows.reshape(chunk, groups, out_cols).transpose(1, 0, 2)
    return exchange(mixed_blocks, 4).reshape(tok_rows, out_cols)


def solution(mesh):
    seq, chan = mesh.devices.shape
    cores = 2 if chan % 2 == 0 else 1
    split = jax.sharding.Mesh(mesh.devices.reshape(seq, chan // cores, cores), ("seq", "z", "core"))
    return jax.shard_map(
        per_device,
        mesh=split,
        in_specs=(P("seq", CHAN), P(), P(), P(None, CHAN), P(), P()),
        out_specs=P("seq", CHAN),
        check_vma=False,
    )
```

```python
import functools

import jax
import jax.numpy as jnp
from jax import lax
from jax.experimental import pallas as pl
from jax.experimental.pallas import tpu as pltpu
from jax.sharding import PartitionSpec as P

MESH = pl.DeviceIdType.MESH
CHAN = ("z", "core")
W_PIECES = 4


def chan_index():
    return lax.axis_index("z") * lax.axis_size("core") + lax.axis_index("core")


def chan_device(slab, peer):
    cores = lax.axis_size("core")
    return (slab, peer // cores, peer % cores)

HEADS = 16
FEAT = 16
HEAD_DIM = 128
BLOCK = 896


def feature_parts(rows):
    linear = rows * FEAT ** (-0.25)
    square = (rows[..., :, None] * rows[..., None, :]).reshape(rows.shape[:-1] + (FEAT * FEAT,)) * (
        2.0 * FEAT
    ) ** (-0.5)
    return (linear, square)


def exchange_kernel(count, *refs):
    xs, ys, bufs = refs[:count], refs[count : 2 * count], refs[2 * count : 3 * count]
    send_sem, recv_sem, own_sem = refs[3 * count :]
    n = xs[0].shape[0]
    me = chan_index()
    slab = lax.axis_index("seq")
    barrier = pltpu.get_barrier_semaphore()
    for step in range(1, n):
        peer = lax.rem(me + step, n)
        pl.semaphore_signal(barrier, inc=1, device_id=chan_device(slab, peer), device_id_type=MESH)
    pl.semaphore_wait(barrier, n - 1)
    owns = []
    sends = []
    for a in range(count):
        own = pltpu.make_async_copy(xs[a].at[me], bufs[a].at[me], own_sem.at[a])
        own.start()
        owns.append(own)
    for step in range(1, n):
        peer = lax.rem(me + step, n)
        for a in range(count):
            copy = pltpu.make_async_remote_copy(
                src_ref=xs[a].at[peer],
                dst_ref=bufs[a].at[me],
                send_sem=send_sem.at[a, peer],
                recv_sem=recv_sem.at[a, me],
                device_id=chan_device(slab, peer),
                device_id_type=MESH,
            )
            copy.start()
            sends.append(copy)
    for step in range(1, n):
        source = lax.rem(me + n - step, n)
        for a in range(count):
            pltpu.make_async_remote_copy(
                src_ref=xs[a].at[source],
                dst_ref=bufs[a].at[source],
                send_sem=send_sem.at[a, source],
                recv_sem=recv_sem.at[a, source],
                device_id=chan_device(slab, source),
                device_id_type=MESH,
            ).wait_recv()
    for copy in sends:
        copy.wait_send()
    for a in range(count):
        owns[a].wait()
        ys[a][...] = bufs[a][...]


def exchange_many(xs, collective_id):
    count = len(xs)
    n = xs[0].shape[0]
    return pl.pallas_call(
        functools.partial(exchange_kernel, count),
        out_shape=tuple(jax.ShapeDtypeStruct(x.shape, x.dtype) for x in xs),
        in_specs=[pl.BlockSpec(memory_space=pltpu.VMEM)] * count,
        out_specs=tuple(pl.BlockSpec(memory_space=pltpu.VMEM) for _ in xs),
        scratch_shapes=[pltpu.VMEM(x.shape, x.dtype) for x in xs]
        + [
            pltpu.SemaphoreType.DMA((count, n)),
            pltpu.SemaphoreType.DMA((count, n)),
            pltpu.SemaphoreType.DMA((count,)),
        ],
        compiler_params=pltpu.CompilerParams(collective_id=collective_id, has_side_effects=True),
    )(*xs)


def exchange(x, collective_id):
    return exchange_many((x,), collective_id)[0]


def gather_kernel(x_ref, y_ref, buf, send_sem, recv_sem):
    n = buf.shape[0]
    me = lax.axis_index("seq")
    here = (lax.axis_index("z"), lax.axis_index("core"))
    buf[...] = jnp.zeros_like(buf)
    barrier = pltpu.get_barrier_semaphore()
    for step in range(1, n):
        peer = lax.rem(me + step, n)
        pl.semaphore_signal(barrier, inc=1, device_id=(peer,) + here, device_id_type=MESH)
    pl.semaphore_wait(barrier, n - 1)

    def copy_to(peer):
        return pltpu.make_async_remote_copy(
            src_ref=x_ref,
            dst_ref=buf.at[me],
            send_sem=send_sem.at[peer],
            recv_sem=recv_sem.at[me],
            device_id=(peer,) + here,
            device_id_type=MESH,
        )

    def copy_from(source):
        return pltpu.make_async_remote_copy(
            src_ref=x_ref,
            dst_ref=buf.at[source],
            send_sem=send_sem.at[source],
            recv_sem=recv_sem.at[source],
            device_id=(source,) + here,
            device_id_type=MESH,
        )

    for step in range(1, n):
        @pl.when(me + step < n)
        def _():
            copy_to(me + step).start()

    for step in range(1, n):
        @pl.when(me - step >= 0)
        def _():
            copy_from(me - step).wait_recv()

    for step in range(1, n):
        @pl.when(me + step < n)
        def _():
            copy_to(me + step).wait_send()

    y_ref[...] = buf[...]


def gather_seq(x, slabs, collective_id):
    shape = (slabs,) + x.shape
    return pl.pallas_call(
        gather_kernel,
        out_shape=jax.ShapeDtypeStruct(shape, x.dtype),
        in_specs=[pl.BlockSpec(memory_space=pltpu.VMEM)],
        out_specs=pl.BlockSpec(memory_space=pltpu.VMEM),
        scratch_shapes=[
            pltpu.VMEM(shape, x.dtype),
            pltpu.SemaphoreType.DMA((slabs,)),
            pltpu.SemaphoreType.DMA((slabs,)),
        ],
        compiler_params=pltpu.CompilerParams(collective_id=collective_id, has_side_effects=True),
    )(x)


def scan_kernel(width, x_ref, y_ref, row_buf, col_buf, total, row_send, row_recv, col_send, col_recv):
    n = lax.axis_size("seq")
    height = n // width
    me = lax.axis_index("seq")
    row, col = me // width, me % width
    here = (lax.axis_index("z"), lax.axis_index("core"))
    row_buf[...] = jnp.zeros_like(row_buf)
    col_buf[...] = jnp.zeros_like(col_buf)
    barrier = pltpu.get_barrier_semaphore()
    for step in range(1, width):
        peer = row * width + lax.rem(col + step, width)
        pl.semaphore_signal(barrier, inc=1, device_id=(peer,) + here, device_id_type=MESH)
    for step in range(1, height):
        peer = lax.rem(row + step, height) * width + col
        pl.semaphore_signal(barrier, inc=1, device_id=(peer,) + here, device_id_type=MESH)
    pl.semaphore_wait(barrier, width + height - 2)

    def row_copy(c, slot):
        return pltpu.make_async_remote_copy(
            src_ref=x_ref,
            dst_ref=row_buf.at[slot],
            send_sem=row_send.at[c],
            recv_sem=row_recv.at[slot],
            device_id=(row * width + c,) + here,
            device_id_type=MESH,
        )

    sends = []
    for step in range(1, width):
        c = lax.rem(col + step, width)
        copy = row_copy(c, col)
        copy.start()
        sends.append(copy)
    for step in range(1, width):
        c = lax.rem(col + width - step, width)
        row_copy(c, c).wait_recv()
    mine = x_ref[...].astype(jnp.float32)
    row_total = mine
    row_prefix = jnp.zeros_like(mine)
    for c in range(width):
        part = jnp.where(c == col, 0.0, row_buf[c].astype(jnp.float32))
        row_total = row_total + part
        row_prefix = row_prefix + jnp.where(c < col, part, 0.0)
    total[...] = row_total

    def col_copy(r, slot):
        return pltpu.make_async_remote_copy(
            src_ref=total,
            dst_ref=col_buf.at[slot],
            send_sem=col_send.at[r],
            recv_sem=col_recv.at[slot],
            device_id=(r * width + col,) + here,
            device_id_type=MESH,
        )

    for step in range(1, height):
        @pl.when(row + step < height)
        def _():
            col_copy(row + step, row).start()

    for step in range(1, height):
        @pl.when(row - step >= 0)
        def _():
            col_copy(row - step, row - step).wait_recv()

    for step in range(1, height):
        @pl.when(row + step < height)
        def _():
            col_copy(row + step, row).wait_send()

    for copy in sends:
        copy.wait_send()
    prefix = row_prefix
    for r in range(height):
        prefix = prefix + col_buf[r]
    y_ref[...] = prefix


def scan_seq(x, collective_id):
    n = lax.axis_size("seq")
    width = 1
    while (width + 1) * (width + 1) <= n:
        width += 1
    while n % width:
        width -= 1
    height = n // width
    return pl.pallas_call(
        functools.partial(scan_kernel, width),
        out_shape=jax.ShapeDtypeStruct(x.shape, jnp.float32),
        in_specs=[pl.BlockSpec(memory_space=pltpu.VMEM)],
        out_specs=pl.BlockSpec(memory_space=pltpu.VMEM),
        scratch_shapes=[
            pltpu.VMEM((width,) + x.shape, x.dtype),
            pltpu.VMEM((height,) + x.shape, jnp.float32),
            pltpu.VMEM(x.shape, jnp.float32),
            pltpu.SemaphoreType.DMA((width,)),
            pltpu.SemaphoreType.DMA((width,)),
            pltpu.SemaphoreType.DMA((height,)),
            pltpu.SemaphoreType.DMA((height,)),
        ],
        compiler_params=pltpu.CompilerParams(collective_id=collective_id, has_side_effects=True),
    )(x)


def swap_kernel(x_ref, y_ref, send_sem, recv_sem):
    here = (lax.axis_index("seq"), lax.axis_index("z"))
    other = lax.axis_size("core") - 1 - lax.axis_index("core")
    barrier = pltpu.get_barrier_semaphore()
    pl.semaphore_signal(barrier, inc=1, device_id=here + (other,), device_id_type=MESH)
    pl.semaphore_wait(barrier, 1)
    copy = pltpu.make_async_remote_copy(
        src_ref=x_ref,
        dst_ref=y_ref,
        send_sem=send_sem,
        recv_sem=recv_sem,
        device_id=here + (other,),
        device_id_type=MESH,
    )
    copy.start()
    copy.wait()


def swap_cores(x, collective_id):
    return pl.pallas_call(
        swap_kernel,
        out_shape=jax.ShapeDtypeStruct(x.shape, x.dtype),
        in_specs=[pl.BlockSpec(memory_space=pl.ANY)],
        out_specs=pl.BlockSpec(memory_space=pl.ANY),
        scratch_shapes=[pltpu.SemaphoreType.DMA(()), pltpu.SemaphoreType.DMA(())],
        compiler_params=pltpu.CompilerParams(collective_id=collective_id, has_side_effects=True),
    )(x)


def opening_kernel(x_ref, w_ref, y_ref, w_all, buf, send_sem, recv_sem, own_sem, w_send, w_recv, w_own):
    n = x_ref.shape[0]
    cores = lax.axis_size("core")
    ring = n // cores
    me = chan_index()
    slab = lax.axis_index("seq")
    z = lax.axis_index("z")
    core = lax.axis_index("core")
    barrier = pltpu.get_barrier_semaphore()
    for step in range(1, n):
        peer = lax.rem(me + step, n)
        pl.semaphore_signal(barrier, inc=1, device_id=chan_device(slab, peer), device_id_type=MESH)
    pl.semaphore_wait(barrier, n - 1)
    own = pltpu.make_async_copy(x_ref.at[me], buf.at[me], own_sem)
    own.start()
    sends = []
    for step in range(1, n):
        peer = lax.rem(me + step, n)
        copy = pltpu.make_async_remote_copy(
            src_ref=x_ref.at[peer],
            dst_ref=buf.at[me],
            send_sem=send_sem.at[peer],
            recv_sem=recv_sem.at[me],
            device_id=chan_device(slab, peer),
            device_id_type=MESH,
        )
        copy.start()
        sends.append(copy)
    w_local = pltpu.make_async_copy(w_ref, w_all.at[me], w_own)
    w_local.start()
    right = (slab, lax.rem(z + 1, ring), core)
    left = (slab, lax.rem(z + ring - 1, ring), core)
    partner = (slab, z, cores - 1 - core)

    pieces = W_PIECES
    depth = w_ref.shape[0] // pieces

    def slot(origin):
        return lax.rem(origin + ring, ring) * cores + core

    def held(h, j):
        return w_all.at[h, pl.ds(j * depth, depth)]

    def send(source, h, j, kind, target):
        copy = pltpu.make_async_remote_copy(
            src_ref=source,
            dst_ref=held(h, j),
            send_sem=w_send.at[h, kind, j],
            recv_sem=w_recv.at[h, j],
            device_id=target,
            device_id_type=MESH,
        )
        copy.start()
        sends.append(copy)

    def arrive(h, j, source):
        pltpu.make_async_remote_copy(
            src_ref=w_ref.at[pl.ds(j * depth, depth)],
            dst_ref=held(h, j),
            send_sem=w_send.at[h, 0, j],
            recv_sem=w_recv.at[h, j],
            device_id=source,
            device_id_type=MESH,
        ).wait_recv()

    half = ring // 2
    full = half - 1 if ring % 2 == 0 else half

    def goes_right(step):
        return range(pieces) if step <= full else range(pieces // 2) if step == half else range(0)

    def goes_left(step):
        return range(pieces) if step <= full else range(pieces // 2, pieces) if step == half else range(0)

    for j in range(pieces):
        mine = w_ref.at[pl.ds(j * depth, depth)]
        if j in goes_right(1):
            send(mine, me, j, 0, right)
        if j in goes_left(1):
            send(mine, me, j, 1, left)
        send(mine, me, j, 2, partner)
    for step in range(1, half + 1):
        for j in range(pieces):
            if j in goes_right(step):
                h = slot(z - step)
                arrive(h, j, left)
                if j in goes_right(step + 1):
                    send(held(h, j), h, j, 0, right)
                send(held(h, j), h, j, 2, partner)
            if j in goes_left(step):
                h = slot(z + step)
                arrive(h, j, right)
                if j in goes_left(step + 1):
                    send(held(h, j), h, j, 1, left)
                send(held(h, j), h, j, 2, partner)
    for origin in range(ring):
        for j in range(pieces):
            arrive(origin * cores + (cores - 1 - core), j, partner)
    for step in range(1, n):
        source = lax.rem(me + n - step, n)
        pltpu.make_async_remote_copy(
            src_ref=x_ref.at[source],
            dst_ref=buf.at[source],
            send_sem=send_sem.at[source],
            recv_sem=recv_sem.at[source],
            device_id=chan_device(slab, source),
            device_id_type=MESH,
        ).wait_recv()
    for copy in sends:
        copy.wait_send()
    own.wait()
    w_local.wait()
    y_ref[...] = buf[...]


def opening(x, w, collective_id):
    n = x.shape[0]
    return pl.pallas_call(
        opening_kernel,
        out_shape=(
            jax.ShapeDtypeStruct(x.shape, x.dtype),
            jax.ShapeDtypeStruct((n,) + w.shape, w.dtype),
        ),
        in_specs=[pl.BlockSpec(memory_space=pltpu.VMEM), pl.BlockSpec(memory_space=pl.ANY)],
        out_specs=(pl.BlockSpec(memory_space=pltpu.VMEM), pl.BlockSpec(memory_space=pl.ANY)),
        scratch_shapes=[
            pltpu.VMEM(x.shape, x.dtype),
            pltpu.SemaphoreType.DMA((n,)),
            pltpu.SemaphoreType.DMA((n,)),
            pltpu.SemaphoreType.DMA(()),
            pltpu.SemaphoreType.DMA((n, 3, W_PIECES)),
            pltpu.SemaphoreType.DMA((n, W_PIECES)),
            pltpu.SemaphoreType.DMA(()),
        ],
        compiler_params=pltpu.CompilerParams(collective_id=collective_id, has_side_effects=True),
    )(x, w)


def split_rows(x, groups, collective_id):
    rows, cols = x.shape
    got = exchange(x.reshape(groups, rows // groups, cols), collective_id)
    return got.transpose(1, 0, 2).reshape(rows // groups, groups * cols)


def split_cols(x, groups, collective_id):
    rows, _, cols = x.shape
    got = exchange(x.transpose(1, 0, 2), collective_id)
    return got.reshape(groups * rows, cols)


def attend(query_rows, key_rows, value_rows, gain_mine, my_slab):
    highest = lax.Precision.HIGHEST
    tok_rows, per_group, _ = value_rows.shape
    blocks = tok_rows // BLOCK
    query_blocks = query_rows.reshape(blocks, BLOCK, per_group, FEAT)
    key_blocks = key_rows.reshape(blocks, BLOCK, per_group, FEAT)
    value_blocks = value_rows.reshape(blocks, BLOCK, per_group, HEAD_DIM)
    value_f32 = value_blocks.astype(jnp.float32)
    key_linear, key_square = feature_parts(key_blocks.astype(jnp.float32))
    own_zero = jnp.sum(value_f32, axis=1)[:, :, None, :]
    own_one = jnp.einsum("bthf,bthe->bhfe", key_linear, value_f32, precision=highest)
    own_two = jnp.einsum("bthf,bthe->bhfe", key_square, value_f32, precision=highest)
    own = jnp.concatenate([own_zero, own_one, own_two], axis=2)
    slab_total = jnp.sum(own, axis=0)
    state_rows = slab_total.shape[0] * slab_total.shape[1]
    prefix = scan_seq(slab_total.astype(jnp.bfloat16).reshape(state_rows, HEAD_DIM), 7).reshape(slab_total.shape)
    earlier = jnp.concatenate([jnp.zeros_like(own[:1]), jnp.cumsum(own, axis=0)[:-1]], axis=0) + prefix[None]
    query_linear, query_square = feature_parts(query_blocks.astype(jnp.float32))
    inter = earlier[:, :, 0][:, None] + jnp.einsum(
        "bthf,bhfe->bthe", query_linear, earlier[:, :, 1 : 1 + FEAT], precision=highest
    )
    inter = inter + jnp.einsum(
        "bthf,bhfe->bthe", query_square, earlier[:, :, 1 + FEAT :], precision=highest
    )
    scores = jnp.einsum(
        "bthf,bshf->bhts", query_blocks, key_blocks, preferred_element_type=jnp.float32
    ) * FEAT ** (-0.5)
    kernel = 1.0 + scores + 0.5 * scores * scores
    causal = jnp.arange(BLOCK)[:, None] >= jnp.arange(BLOCK)[None, :]
    weights = jnp.where(causal, kernel, 0.0).astype(jnp.bfloat16)
    intra = jnp.einsum("bhts,bshe->bthe", weights, value_blocks, preferred_element_type=jnp.float32)
    numerator = (intra + inter).reshape(tok_rows, per_group, HEAD_DIM)
    mean_square = jnp.mean(numerator * numerator, axis=-1, keepdims=True)
    hidden = (numerator * lax.rsqrt(mean_square + 1e-05) * gain_mine).astype(jnp.bfloat16)
    return hidden.reshape(tok_rows, per_group * HEAD_DIM)


def per_device(tokens, w_query, w_key, w_value, w_out, gain):
    groups = lax.axis_size(CHAN)
    per_group = HEADS // groups
    my_group = chan_index()
    my_slab = lax.axis_index("seq")
    tok_rows_total, tok_cols = tokens.shape
    got, value_all = opening(tokens.reshape(groups, tok_rows_total // groups, tok_cols), w_value, 1)
    rows = got.transpose(1, 0, 2).reshape(tok_rows_total // groups, groups * tok_cols)
    chunk = rows.shape[0]
    pf = per_group * FEAT
    d_model = w_query.shape[0]
    w_qk = jnp.concatenate(
        [w_query.reshape(d_model, groups, pf), w_key.reshape(d_model, groups, pf)], axis=2
    )
    qk_t = jnp.einsum("tf,fgd->gdt", rows, w_qk, preferred_element_type=jnp.float32).astype(jnp.bfloat16)
    value = jnp.einsum("tf,gfe->gte", rows, value_all, preferred_element_type=jnp.float32).astype(jnp.bfloat16)
    qk_got, value_got = exchange_many((qk_t, value), 2)
    tok_rows = groups * chunk
    qk_rows = qk_got.transpose(0, 2, 1).reshape(tok_rows, 2 * pf)
    query_rows = qk_rows[:, :pf].reshape(tok_rows, per_group, FEAT)
    key_rows = qk_rows[:, pf:].reshape(tok_rows, per_group, FEAT)
    value_rows = value_got.reshape(tok_rows, per_group, HEAD_DIM)
    value_cols = per_group * HEAD_DIM
    gain_mine = lax.dynamic_slice_in_dim(gain, my_group * value_cols, value_cols, 0).reshape(
        per_group, HEAD_DIM
    )
    hidden = attend(query_rows, key_rows, value_rows, gain_mine, my_slab)
    hidden_got = exchange(hidden.reshape(groups, chunk, per_group * HEAD_DIM), 3)
    out_cols = w_out.shape[1] // groups
    mixed_rows = jnp.einsum(
        "gte,gef->tf",
        hidden_got,
        w_out.reshape(groups, per_group * HEAD_DIM, w_out.shape[1]),
        preferred_element_type=jnp.float32,
    ).astype(jnp.bfloat16)
    mixed_blocks = mixed_rows.reshape(chunk, groups, out_cols).transpose(1, 0, 2)
    return exchange(mixed_blocks, 4).reshape(tok_rows, out_cols)


def solution(mesh):
    seq, chan = mesh.devices.shape
    cores = 2 if chan % 2 == 0 else 1
    split = jax.sharding.Mesh(mesh.devices.reshape(seq, chan // cores, cores), ("seq", "z", "core"))
    return jax.shard_map(
        per_device,
        mesh=split,
        in_specs=(P("seq", CHAN), P(), P(), P(None, CHAN), P(), P()),
        out_specs=P("seq", CHAN),
        check_vma=False,
    )
```

```python
import functools

import jax
import jax.numpy as jnp
from jax import lax
from jax.experimental import pallas as pl
from jax.experimental.pallas import tpu as pltpu
from jax.sharding import PartitionSpec as P

MESH = pl.DeviceIdType.MESH
CHAN = ("z", "core")
W_PIECES = 4


def chan_index():
    return lax.axis_index("z") * lax.axis_size("core") + lax.axis_index("core")


def chan_device(slab, peer):
    cores = lax.axis_size("core")
    return (slab, peer // cores, peer % cores)

HEADS = 16
FEAT = 16
HEAD_DIM = 128
BLOCK = 896


def feature_parts(rows):
    linear = rows * FEAT ** (-0.25)
    square = (rows[..., :, None] * rows[..., None, :]).reshape(rows.shape[:-1] + (FEAT * FEAT,)) * (
        2.0 * FEAT
    ) ** (-0.5)
    return (linear, square)


def exchange_kernel(count, *refs):
    xs, ys, bufs = refs[:count], refs[count : 2 * count], refs[2 * count : 3 * count]
    send_sem, recv_sem, own_sem = refs[3 * count :]
    n = xs[0].shape[0]
    me = chan_index()
    slab = lax.axis_index("seq")
    barrier = pltpu.get_barrier_semaphore()
    for step in range(1, n):
        peer = lax.rem(me + step, n)
        pl.semaphore_signal(barrier, inc=1, device_id=chan_device(slab, peer), device_id_type=MESH)
    pl.semaphore_wait(barrier, n - 1)
    owns = []
    sends = []
    for a in range(count):
        own = pltpu.make_async_copy(xs[a].at[me], bufs[a].at[me], own_sem.at[a])
        own.start()
        owns.append(own)
    for step in range(1, n):
        peer = lax.rem(me + step, n)
        for a in range(count):
            copy = pltpu.make_async_remote_copy(
                src_ref=xs[a].at[peer],
                dst_ref=bufs[a].at[me],
                send_sem=send_sem.at[a, peer],
                recv_sem=recv_sem.at[a, me],
                device_id=chan_device(slab, peer),
                device_id_type=MESH,
            )
            copy.start()
            sends.append(copy)
    for step in range(1, n):
        source = lax.rem(me + n - step, n)
        for a in range(count):
            pltpu.make_async_remote_copy(
                src_ref=xs[a].at[source],
                dst_ref=bufs[a].at[source],
                send_sem=send_sem.at[a, source],
                recv_sem=recv_sem.at[a, source],
                device_id=chan_device(slab, source),
                device_id_type=MESH,
            ).wait_recv()
    for copy in sends:
        copy.wait_send()
    for a in range(count):
        owns[a].wait()
        ys[a][...] = bufs[a][...]


def exchange_many(xs, collective_id):
    count = len(xs)
    n = xs[0].shape[0]
    return pl.pallas_call(
        functools.partial(exchange_kernel, count),
        out_shape=tuple(jax.ShapeDtypeStruct(x.shape, x.dtype) for x in xs),
        in_specs=[pl.BlockSpec(memory_space=pltpu.VMEM)] * count,
        out_specs=tuple(pl.BlockSpec(memory_space=pltpu.VMEM) for _ in xs),
        scratch_shapes=[pltpu.VMEM(x.shape, x.dtype) for x in xs]
        + [
            pltpu.SemaphoreType.DMA((count, n)),
            pltpu.SemaphoreType.DMA((count, n)),
            pltpu.SemaphoreType.DMA((count,)),
        ],
        compiler_params=pltpu.CompilerParams(collective_id=collective_id, has_side_effects=True),
    )(*xs)


def exchange(x, collective_id):
    return exchange_many((x,), collective_id)[0]


def gather_kernel(x_ref, y_ref, buf, send_sem, recv_sem):
    n = buf.shape[0]
    me = lax.axis_index("seq")
    here = (lax.axis_index("z"), lax.axis_index("core"))
    buf[...] = jnp.zeros_like(buf)
    barrier = pltpu.get_barrier_semaphore()
    for step in range(1, n):
        peer = lax.rem(me + step, n)
        pl.semaphore_signal(barrier, inc=1, device_id=(peer,) + here, device_id_type=MESH)
    pl.semaphore_wait(barrier, n - 1)

    def copy_to(peer):
        return pltpu.make_async_remote_copy(
            src_ref=x_ref,
            dst_ref=buf.at[me],
            send_sem=send_sem.at[peer],
            recv_sem=recv_sem.at[me],
            device_id=(peer,) + here,
            device_id_type=MESH,
        )

    def copy_from(source):
        return pltpu.make_async_remote_copy(
            src_ref=x_ref,
            dst_ref=buf.at[source],
            send_sem=send_sem.at[source],
            recv_sem=recv_sem.at[source],
            device_id=(source,) + here,
            device_id_type=MESH,
        )

    for step in range(1, n):
        @pl.when(me + step < n)
        def _():
            copy_to(me + step).start()

    for step in range(1, n):
        @pl.when(me - step >= 0)
        def _():
            copy_from(me - step).wait_recv()

    for step in range(1, n):
        @pl.when(me + step < n)
        def _():
            copy_to(me + step).wait_send()

    y_ref[...] = buf[...]


def gather_seq(x, slabs, collective_id):
    shape = (slabs,) + x.shape
    return pl.pallas_call(
        gather_kernel,
        out_shape=jax.ShapeDtypeStruct(shape, x.dtype),
        in_specs=[pl.BlockSpec(memory_space=pltpu.VMEM)],
        out_specs=pl.BlockSpec(memory_space=pltpu.VMEM),
        scratch_shapes=[
            pltpu.VMEM(shape, x.dtype),
            pltpu.SemaphoreType.DMA((slabs,)),
            pltpu.SemaphoreType.DMA((slabs,)),
        ],
        compiler_params=pltpu.CompilerParams(collective_id=collective_id, has_side_effects=True),
    )(x)


def scan_kernel(width, x_ref, y_ref, row_buf, col_buf, total, row_send, row_recv, col_send, col_recv):
    n = lax.axis_size("seq")
    height = n // width
    me = lax.axis_index("seq")
    row, col = me // width, me % width
    here = (lax.axis_index("z"), lax.axis_index("core"))
    row_buf[...] = jnp.zeros_like(row_buf)
    col_buf[...] = jnp.zeros_like(col_buf)
    barrier = pltpu.get_barrier_semaphore()
    for step in range(1, width):
        peer = row * width + lax.rem(col + step, width)
        pl.semaphore_signal(barrier, inc=1, device_id=(peer,) + here, device_id_type=MESH)
    for step in range(1, height):
        peer = lax.rem(row + step, height) * width + col
        pl.semaphore_signal(barrier, inc=1, device_id=(peer,) + here, device_id_type=MESH)
    pl.semaphore_wait(barrier, width + height - 2)

    def row_copy(c, slot):
        return pltpu.make_async_remote_copy(
            src_ref=x_ref,
            dst_ref=row_buf.at[slot],
            send_sem=row_send.at[c],
            recv_sem=row_recv.at[slot],
            device_id=(row * width + c,) + here,
            device_id_type=MESH,
        )

    sends = []
    for step in range(1, width):
        c = lax.rem(col + step, width)
        copy = row_copy(c, col)
        copy.start()
        sends.append(copy)
    for step in range(1, width):
        c = lax.rem(col + width - step, width)
        row_copy(c, c).wait_recv()
    mine = x_ref[...].astype(jnp.float32)
    row_total = mine
    row_prefix = jnp.zeros_like(mine)
    for c in range(width):
        part = jnp.where(c == col, 0.0, row_buf[c].astype(jnp.float32))
        row_total = row_total + part
        row_prefix = row_prefix + jnp.where(c < col, part, 0.0)
    total[...] = row_total

    def col_copy(r, slot):
        return pltpu.make_async_remote_copy(
            src_ref=total,
            dst_ref=col_buf.at[slot],
            send_sem=col_send.at[r],
            recv_sem=col_recv.at[slot],
            device_id=(r * width + col,) + here,
            device_id_type=MESH,
        )

    for step in range(1, height):
        @pl.when(row + step < height)
        def _():
            col_copy(row + step, row).start()

    for step in range(1, height):
        @pl.when(row - step >= 0)
        def _():
            col_copy(row - step, row - step).wait_recv()

    for step in range(1, height):
        @pl.when(row + step < height)
        def _():
            col_copy(row + step, row).wait_send()

    for copy in sends:
        copy.wait_send()
    prefix = row_prefix
    for r in range(height):
        prefix = prefix + col_buf[r]
    y_ref[...] = prefix


def scan_seq(x, collective_id):
    n = lax.axis_size("seq")
    width = 1
    while (width + 1) * (width + 1) <= n:
        width += 1
    while n % width:
        width -= 1
    height = n // width
    return pl.pallas_call(
        functools.partial(scan_kernel, width),
        out_shape=jax.ShapeDtypeStruct(x.shape, jnp.float32),
        in_specs=[pl.BlockSpec(memory_space=pltpu.VMEM)],
        out_specs=pl.BlockSpec(memory_space=pltpu.VMEM),
        scratch_shapes=[
            pltpu.VMEM((width,) + x.shape, x.dtype),
            pltpu.VMEM((height,) + x.shape, jnp.float32),
            pltpu.VMEM(x.shape, jnp.float32),
            pltpu.SemaphoreType.DMA((width,)),
            pltpu.SemaphoreType.DMA((width,)),
            pltpu.SemaphoreType.DMA((height,)),
            pltpu.SemaphoreType.DMA((height,)),
        ],
        compiler_params=pltpu.CompilerParams(collective_id=collective_id, has_side_effects=True),
    )(x)


def swap_kernel(x_ref, y_ref, send_sem, recv_sem):
    here = (lax.axis_index("seq"), lax.axis_index("z"))
    other = lax.axis_size("core") - 1 - lax.axis_index("core")
    barrier = pltpu.get_barrier_semaphore()
    pl.semaphore_signal(barrier, inc=1, device_id=here + (other,), device_id_type=MESH)
    pl.semaphore_wait(barrier, 1)
    copy = pltpu.make_async_remote_copy(
        src_ref=x_ref,
        dst_ref=y_ref,
        send_sem=send_sem,
        recv_sem=recv_sem,
        device_id=here + (other,),
        device_id_type=MESH,
    )
    copy.start()
    copy.wait()


def swap_cores(x, collective_id):
    return pl.pallas_call(
        swap_kernel,
        out_shape=jax.ShapeDtypeStruct(x.shape, x.dtype),
        in_specs=[pl.BlockSpec(memory_space=pl.ANY)],
        out_specs=pl.BlockSpec(memory_space=pl.ANY),
        scratch_shapes=[pltpu.SemaphoreType.DMA(()), pltpu.SemaphoreType.DMA(())],
        compiler_params=pltpu.CompilerParams(collective_id=collective_id, has_side_effects=True),
    )(x)


def opening_kernel(x_ref, w_ref, y_ref, w_all, buf, send_sem, recv_sem, own_sem, w_send, w_recv, w_own):
    n = x_ref.shape[0]
    cores = lax.axis_size("core")
    ring = n // cores
    me = chan_index()
    slab = lax.axis_index("seq")
    z = lax.axis_index("z")
    core = lax.axis_index("core")
    barrier = pltpu.get_barrier_semaphore()
    for step in range(1, n):
        peer = lax.rem(me + step, n)
        pl.semaphore_signal(barrier, inc=1, device_id=chan_device(slab, peer), device_id_type=MESH)
    pl.semaphore_wait(barrier, n - 1)
    own = pltpu.make_async_copy(x_ref.at[me], buf.at[me], own_sem)
    own.start()
    sends = []
    for step in range(1, n):
        peer = lax.rem(me + step, n)
        copy = pltpu.make_async_remote_copy(
            src_ref=x_ref.at[peer],
            dst_ref=buf.at[me],
            send_sem=send_sem.at[peer],
            recv_sem=recv_sem.at[me],
            device_id=chan_device(slab, peer),
            device_id_type=MESH,
        )
        copy.start()
        sends.append(copy)
    w_local = pltpu.make_async_copy(w_ref, w_all.at[me], w_own)
    w_local.start()
    right = (slab, lax.rem(z + 1, ring), core)
    left = (slab, lax.rem(z + ring - 1, ring), core)
    partner = (slab, z, cores - 1 - core)

    pieces = W_PIECES
    depth = w_ref.shape[0] // pieces

    def slot(origin):
        return lax.rem(origin + ring, ring) * cores + core

    def held(h, j):
        return w_all.at[h, pl.ds(j * depth, depth)]

    def send(source, h, j, kind, target):
        copy = pltpu.make_async_remote_copy(
            src_ref=source,
            dst_ref=held(h, j),
            send_sem=w_send.at[h, kind, j],
            recv_sem=w_recv.at[h, j],
            device_id=target,
            device_id_type=MESH,
        )
        copy.start()
        sends.append(copy)

    def arrive(h, j, source):
        pltpu.make_async_remote_copy(
            src_ref=w_ref.at[pl.ds(j * depth, depth)],
            dst_ref=held(h, j),
            send_sem=w_send.at[h, 0, j],
            recv_sem=w_recv.at[h, j],
            device_id=source,
            device_id_type=MESH,
        ).wait_recv()

    half = ring // 2
    full = half - 1 if ring % 2 == 0 else half

    def goes_right(step):
        return range(pieces) if step <= full else range(pieces // 2) if step == half else range(0)

    def goes_left(step):
        return range(pieces) if step <= full else range(pieces // 2, pieces) if step == half else range(0)

    for j in range(pieces):
        mine = w_ref.at[pl.ds(j * depth, depth)]
        if j in goes_right(1):
            send(mine, me, j, 0, right)
        if j in goes_left(1):
            send(mine, me, j, 1, left)
        send(mine, me, j, 2, partner)
    for step in range(1, half + 1):
        for j in range(pieces):
            if j in goes_right(step):
                h = slot(z - step)
                arrive(h, j, left)
                if j in goes_right(step + 1):
                    send(held(h, j), h, j, 0, right)
                send(held(h, j), h, j, 2, partner)
            if j in goes_left(step):
                h = slot(z + step)
                arrive(h, j, right)
                if j in goes_left(step + 1):
                    send(held(h, j), h, j, 1, left)
                send(held(h, j), h, j, 2, partner)
    for origin in range(ring):
        for j in range(pieces):
            arrive(origin * cores + (cores - 1 - core), j, partner)
    for step in range(1, n):
        source = lax.rem(me + n - step, n)
        pltpu.make_async_remote_copy(
            src_ref=x_ref.at[source],
            dst_ref=buf.at[source],
            send_sem=send_sem.at[source],
            recv_sem=recv_sem.at[source],
            device_id=chan_device(slab, source),
            device_id_type=MESH,
        ).wait_recv()
    for copy in sends:
        copy.wait_send()
    own.wait()
    w_local.wait()
    y_ref[...] = buf[...]


def opening(x, w, collective_id):
    n = x.shape[0]
    return pl.pallas_call(
        opening_kernel,
        out_shape=(
            jax.ShapeDtypeStruct(x.shape, x.dtype),
            jax.ShapeDtypeStruct((n,) + w.shape, w.dtype),
        ),
        in_specs=[pl.BlockSpec(memory_space=pltpu.VMEM), pl.BlockSpec(memory_space=pl.ANY)],
        out_specs=(pl.BlockSpec(memory_space=pltpu.VMEM), pl.BlockSpec(memory_space=pl.ANY)),
        scratch_shapes=[
            pltpu.VMEM(x.shape, x.dtype),
            pltpu.SemaphoreType.DMA((n,)),
            pltpu.SemaphoreType.DMA((n,)),
            pltpu.SemaphoreType.DMA(()),
            pltpu.SemaphoreType.DMA((n, 3, W_PIECES)),
            pltpu.SemaphoreType.DMA((n, W_PIECES)),
            pltpu.SemaphoreType.DMA(()),
        ],
        compiler_params=pltpu.CompilerParams(collective_id=collective_id, has_side_effects=True),
    )(x, w)


def split_rows(x, groups, collective_id):
    rows, cols = x.shape
    got = exchange(x.reshape(groups, rows // groups, cols), collective_id)
    return got.transpose(1, 0, 2).reshape(rows // groups, groups * cols)


def split_cols(x, groups, collective_id):
    rows, _, cols = x.shape
    got = exchange(x.transpose(1, 0, 2), collective_id)
    return got.reshape(groups * rows, cols)


def intra_kernel(q_ref, k_ref, v_ref, o_ref):
    scores = lax.dot_general(
        q_ref[0], k_ref[0], (((1,), (1,)), ((), ())), preferred_element_type=jnp.float32
    ) * FEAT ** (-0.5)
    kernel = 1.0 + scores + 0.5 * scores * scores
    rows = lax.broadcasted_iota(jnp.int32, kernel.shape, 0)
    cols = lax.broadcasted_iota(jnp.int32, kernel.shape, 1)
    weights = jnp.where(rows >= cols, kernel, 0.0).astype(jnp.bfloat16)
    o_ref[0] = jnp.dot(weights, v_ref[0], preferred_element_type=jnp.float32)


def intra_attention(query_rows, key_rows, value_rows):
    tok_rows, per_group, _ = value_rows.shape
    blocks = tok_rows // BLOCK
    q = query_rows.transpose(1, 0, 2)
    k = key_rows.transpose(1, 0, 2)
    v = value_rows.transpose(1, 0, 2)
    out = pl.pallas_call(
        intra_kernel,
        out_shape=jax.ShapeDtypeStruct((per_group, tok_rows, HEAD_DIM), jnp.float32),
        grid=(per_group, blocks),
        in_specs=[
            pl.BlockSpec((1, BLOCK, FEAT), lambda h, b: (h, b, 0)),
            pl.BlockSpec((1, BLOCK, FEAT), lambda h, b: (h, b, 0)),
            pl.BlockSpec((1, BLOCK, HEAD_DIM), lambda h, b: (h, b, 0)),
        ],
        out_specs=pl.BlockSpec((1, BLOCK, HEAD_DIM), lambda h, b: (h, b, 0)),
    )(q, k, v)
    return out.transpose(1, 0, 2)


def attend(query_rows, key_rows, value_rows, gain_mine, my_slab):
    highest = lax.Precision.HIGHEST
    tok_rows, per_group, _ = value_rows.shape
    blocks = tok_rows // BLOCK
    query_blocks = query_rows.reshape(blocks, BLOCK, per_group, FEAT)
    key_blocks = key_rows.reshape(blocks, BLOCK, per_group, FEAT)
    value_blocks = value_rows.reshape(blocks, BLOCK, per_group, HEAD_DIM)
    value_f32 = value_blocks.astype(jnp.float32)
    key_linear, key_square = feature_parts(key_blocks.astype(jnp.float32))
    own_zero = jnp.sum(value_f32, axis=1)[:, :, None, :]
    own_one = jnp.einsum("bthf,bthe->bhfe", key_linear, value_f32, precision=highest)
    own_two = jnp.einsum("bthf,bthe->bhfe", key_square, value_f32, precision=highest)
    own = jnp.concatenate([own_zero, own_one, own_two], axis=2)
    slab_total = jnp.sum(own, axis=0)
    state_rows = slab_total.shape[0] * slab_total.shape[1]
    prefix = scan_seq(slab_total.astype(jnp.bfloat16).reshape(state_rows, HEAD_DIM), 7).reshape(slab_total.shape)
    earlier = jnp.concatenate([jnp.zeros_like(own[:1]), jnp.cumsum(own, axis=0)[:-1]], axis=0) + prefix[None]
    query_linear, query_square = feature_parts(query_blocks.astype(jnp.float32))
    inter = earlier[:, :, 0][:, None] + jnp.einsum(
        "bthf,bhfe->bthe", query_linear, earlier[:, :, 1 : 1 + FEAT], precision=highest
    )
    inter = inter + jnp.einsum(
        "bthf,bhfe->bthe", query_square, earlier[:, :, 1 + FEAT :], precision=highest
    )
    intra = intra_attention(query_rows, key_rows, value_rows).reshape(blocks, BLOCK, per_group, HEAD_DIM)
    numerator = (intra + inter).reshape(tok_rows, per_group, HEAD_DIM)
    mean_square = jnp.mean(numerator * numerator, axis=-1, keepdims=True)
    hidden = (numerator * lax.rsqrt(mean_square + 1e-05) * gain_mine).astype(jnp.bfloat16)
    return hidden.reshape(tok_rows, per_group * HEAD_DIM)


def per_device(tokens, w_query, w_key, w_value, w_out, gain):
    groups = lax.axis_size(CHAN)
    per_group = HEADS // groups
    my_group = chan_index()
    my_slab = lax.axis_index("seq")
    tok_rows_total, tok_cols = tokens.shape
    got, value_all = opening(tokens.reshape(groups, tok_rows_total // groups, tok_cols), w_value, 1)
    rows = got.transpose(1, 0, 2).reshape(tok_rows_total // groups, groups * tok_cols)
    chunk = rows.shape[0]
    pf = per_group * FEAT
    d_model = w_query.shape[0]
    w_qk = jnp.concatenate(
        [w_query.reshape(d_model, groups, pf), w_key.reshape(d_model, groups, pf)], axis=2
    )
    qk_t = jnp.einsum("tf,fgd->gdt", rows, w_qk, preferred_element_type=jnp.float32).astype(jnp.bfloat16)
    value = jnp.einsum("tf,gfe->gte", rows, value_all, preferred_element_type=jnp.float32).astype(jnp.bfloat16)
    qk_got, value_got = exchange_many((qk_t, value), 2)
    tok_rows = groups * chunk
    qk_rows = qk_got.transpose(0, 2, 1).reshape(tok_rows, 2 * pf)
    query_rows = qk_rows[:, :pf].reshape(tok_rows, per_group, FEAT)
    key_rows = qk_rows[:, pf:].reshape(tok_rows, per_group, FEAT)
    value_rows = value_got.reshape(tok_rows, per_group, HEAD_DIM)
    value_cols = per_group * HEAD_DIM
    gain_mine = lax.dynamic_slice_in_dim(gain, my_group * value_cols, value_cols, 0).reshape(
        per_group, HEAD_DIM
    )
    hidden = attend(query_rows, key_rows, value_rows, gain_mine, my_slab)
    hidden_got = exchange(hidden.reshape(groups, chunk, per_group * HEAD_DIM), 3)
    out_cols = w_out.shape[1] // groups
    mixed_rows = jnp.einsum(
        "gte,gef->tf",
        hidden_got,
        w_out.reshape(groups, per_group * HEAD_DIM, w_out.shape[1]),
        preferred_element_type=jnp.float32,
    ).astype(jnp.bfloat16)
    mixed_blocks = mixed_rows.reshape(chunk, groups, out_cols).transpose(1, 0, 2)
    return exchange(mixed_blocks, 4).reshape(tok_rows, out_cols)


def solution(mesh):
    seq, chan = mesh.devices.shape
    cores = 2 if chan % 2 == 0 else 1
    split = jax.sharding.Mesh(mesh.devices.reshape(seq, chan // cores, cores), ("seq", "z", "core"))
    return jax.shard_map(
        per_device,
        mesh=split,
        in_specs=(P("seq", CHAN), P(), P(), P(None, CHAN), P(), P()),
        out_specs=P("seq", CHAN),
        check_vma=False,
    )
```

```python
import functools

import jax
import jax.numpy as jnp
from jax import lax
from jax.experimental import pallas as pl
from jax.experimental.pallas import tpu as pltpu
from jax.sharding import PartitionSpec as P

MESH = pl.DeviceIdType.MESH
CHAN = ("z", "core")
W_PIECES = 4


def chan_index():
    return lax.axis_index("z") * lax.axis_size("core") + lax.axis_index("core")


def chan_device(slab, peer):
    cores = lax.axis_size("core")
    return (slab, peer // cores, peer % cores)

HEADS = 16
FEAT = 16
HEAD_DIM = 128
BLOCK = 896


def feature_parts(rows):
    linear = rows * FEAT ** (-0.25)
    square = (rows[..., :, None] * rows[..., None, :]).reshape(rows.shape[:-1] + (FEAT * FEAT,)) * (
        2.0 * FEAT
    ) ** (-0.5)
    return (linear, square)


def exchange_kernel(count, *refs):
    xs, ys, bufs = refs[:count], refs[count : 2 * count], refs[2 * count : 3 * count]
    send_sem, recv_sem, own_sem = refs[3 * count :]
    n = xs[0].shape[0]
    me = chan_index()
    slab = lax.axis_index("seq")
    barrier = pltpu.get_barrier_semaphore()
    for step in range(1, n):
        peer = lax.rem(me + step, n)
        pl.semaphore_signal(barrier, inc=1, device_id=chan_device(slab, peer), device_id_type=MESH)
    pl.semaphore_wait(barrier, n - 1)
    owns = []
    sends = []
    for a in range(count):
        own = pltpu.make_async_copy(xs[a].at[me], bufs[a].at[me], own_sem.at[a])
        own.start()
        owns.append(own)
    for step in range(1, n):
        peer = lax.rem(me + step, n)
        for a in range(count):
            copy = pltpu.make_async_remote_copy(
                src_ref=xs[a].at[peer],
                dst_ref=bufs[a].at[me],
                send_sem=send_sem.at[a, peer],
                recv_sem=recv_sem.at[a, me],
                device_id=chan_device(slab, peer),
                device_id_type=MESH,
            )
            copy.start()
            sends.append(copy)
    for step in range(1, n):
        source = lax.rem(me + n - step, n)
        for a in range(count):
            pltpu.make_async_remote_copy(
                src_ref=xs[a].at[source],
                dst_ref=bufs[a].at[source],
                send_sem=send_sem.at[a, source],
                recv_sem=recv_sem.at[a, source],
                device_id=chan_device(slab, source),
                device_id_type=MESH,
            ).wait_recv()
    for copy in sends:
        copy.wait_send()
    for a in range(count):
        owns[a].wait()
        ys[a][...] = bufs[a][...]


def exchange_many(xs, collective_id):
    count = len(xs)
    n = xs[0].shape[0]
    return pl.pallas_call(
        functools.partial(exchange_kernel, count),
        out_shape=tuple(jax.ShapeDtypeStruct(x.shape, x.dtype) for x in xs),
        in_specs=[pl.BlockSpec(memory_space=pltpu.VMEM)] * count,
        out_specs=tuple(pl.BlockSpec(memory_space=pltpu.VMEM) for _ in xs),
        scratch_shapes=[pltpu.VMEM(x.shape, x.dtype) for x in xs]
        + [
            pltpu.SemaphoreType.DMA((count, n)),
            pltpu.SemaphoreType.DMA((count, n)),
            pltpu.SemaphoreType.DMA((count,)),
        ],
        compiler_params=pltpu.CompilerParams(collective_id=collective_id, has_side_effects=True),
    )(*xs)


def exchange(x, collective_id):
    return exchange_many((x,), collective_id)[0]


def gather_kernel(x_ref, y_ref, buf, send_sem, recv_sem):
    n = buf.shape[0]
    me = lax.axis_index("seq")
    here = (lax.axis_index("z"), lax.axis_index("core"))
    buf[...] = jnp.zeros_like(buf)
    barrier = pltpu.get_barrier_semaphore()
    for step in range(1, n):
        peer = lax.rem(me + step, n)
        pl.semaphore_signal(barrier, inc=1, device_id=(peer,) + here, device_id_type=MESH)
    pl.semaphore_wait(barrier, n - 1)

    def copy_to(peer):
        return pltpu.make_async_remote_copy(
            src_ref=x_ref,
            dst_ref=buf.at[me],
            send_sem=send_sem.at[peer],
            recv_sem=recv_sem.at[me],
            device_id=(peer,) + here,
            device_id_type=MESH,
        )

    def copy_from(source):
        return pltpu.make_async_remote_copy(
            src_ref=x_ref,
            dst_ref=buf.at[source],
            send_sem=send_sem.at[source],
            recv_sem=recv_sem.at[source],
            device_id=(source,) + here,
            device_id_type=MESH,
        )

    for step in range(1, n):
        @pl.when(me + step < n)
        def _():
            copy_to(me + step).start()

    for step in range(1, n):
        @pl.when(me - step >= 0)
        def _():
            copy_from(me - step).wait_recv()

    for step in range(1, n):
        @pl.when(me + step < n)
        def _():
            copy_to(me + step).wait_send()

    y_ref[...] = buf[...]


def gather_seq(x, slabs, collective_id):
    shape = (slabs,) + x.shape
    return pl.pallas_call(
        gather_kernel,
        out_shape=jax.ShapeDtypeStruct(shape, x.dtype),
        in_specs=[pl.BlockSpec(memory_space=pltpu.VMEM)],
        out_specs=pl.BlockSpec(memory_space=pltpu.VMEM),
        scratch_shapes=[
            pltpu.VMEM(shape, x.dtype),
            pltpu.SemaphoreType.DMA((slabs,)),
            pltpu.SemaphoreType.DMA((slabs,)),
        ],
        compiler_params=pltpu.CompilerParams(collective_id=collective_id, has_side_effects=True),
    )(x)


def scan_kernel(width, x_ref, y_ref, row_buf, col_buf, total, row_send, row_recv, col_send, col_recv):
    n = lax.axis_size("seq")
    height = n // width
    me = lax.axis_index("seq")
    row, col = me // width, me % width
    here = (lax.axis_index("z"), lax.axis_index("core"))
    row_buf[...] = jnp.zeros_like(row_buf)
    col_buf[...] = jnp.zeros_like(col_buf)
    barrier = pltpu.get_barrier_semaphore()
    for step in range(1, width):
        peer = row * width + lax.rem(col + step, width)
        pl.semaphore_signal(barrier, inc=1, device_id=(peer,) + here, device_id_type=MESH)
    for step in range(1, height):
        peer = lax.rem(row + step, height) * width + col
        pl.semaphore_signal(barrier, inc=1, device_id=(peer,) + here, device_id_type=MESH)
    pl.semaphore_wait(barrier, width + height - 2)

    def row_copy(c, slot):
        return pltpu.make_async_remote_copy(
            src_ref=x_ref,
            dst_ref=row_buf.at[slot],
            send_sem=row_send.at[c],
            recv_sem=row_recv.at[slot],
            device_id=(row * width + c,) + here,
            device_id_type=MESH,
        )

    sends = []
    for step in range(1, width):
        c = lax.rem(col + step, width)
        copy = row_copy(c, col)
        copy.start()
        sends.append(copy)
    for step in range(1, width):
        c = lax.rem(col + width - step, width)
        row_copy(c, c).wait_recv()
    mine = x_ref[...].astype(jnp.float32)
    row_total = mine
    row_prefix = jnp.zeros_like(mine)
    for c in range(width):
        part = jnp.where(c == col, 0.0, row_buf[c].astype(jnp.float32))
        row_total = row_total + part
        row_prefix = row_prefix + jnp.where(c < col, part, 0.0)
    total[...] = row_total

    def col_copy(r, slot):
        return pltpu.make_async_remote_copy(
            src_ref=total,
            dst_ref=col_buf.at[slot],
            send_sem=col_send.at[r],
            recv_sem=col_recv.at[slot],
            device_id=(r * width + col,) + here,
            device_id_type=MESH,
        )

    for step in range(1, height):
        @pl.when(row + step < height)
        def _():
            col_copy(row + step, row).start()

    for step in range(1, height):
        @pl.when(row - step >= 0)
        def _():
            col_copy(row - step, row - step).wait_recv()

    for step in range(1, height):
        @pl.when(row + step < height)
        def _():
            col_copy(row + step, row).wait_send()

    for copy in sends:
        copy.wait_send()
    prefix = row_prefix
    for r in range(height):
        prefix = prefix + col_buf[r]
    y_ref[...] = prefix


def scan_seq(x, collective_id):
    n = lax.axis_size("seq")
    width = 1
    while (width + 1) * (width + 1) <= n:
        width += 1
    while n % width:
        width -= 1
    height = n // width
    return pl.pallas_call(
        functools.partial(scan_kernel, width),
        out_shape=jax.ShapeDtypeStruct(x.shape, jnp.float32),
        in_specs=[pl.BlockSpec(memory_space=pltpu.VMEM)],
        out_specs=pl.BlockSpec(memory_space=pltpu.VMEM),
        scratch_shapes=[
            pltpu.VMEM((width,) + x.shape, x.dtype),
            pltpu.VMEM((height,) + x.shape, jnp.float32),
            pltpu.VMEM(x.shape, jnp.float32),
            pltpu.SemaphoreType.DMA((width,)),
            pltpu.SemaphoreType.DMA((width,)),
            pltpu.SemaphoreType.DMA((height,)),
            pltpu.SemaphoreType.DMA((height,)),
        ],
        compiler_params=pltpu.CompilerParams(collective_id=collective_id, has_side_effects=True),
    )(x)


def swap_kernel(x_ref, y_ref, send_sem, recv_sem):
    here = (lax.axis_index("seq"), lax.axis_index("z"))
    other = lax.axis_size("core") - 1 - lax.axis_index("core")
    barrier = pltpu.get_barrier_semaphore()
    pl.semaphore_signal(barrier, inc=1, device_id=here + (other,), device_id_type=MESH)
    pl.semaphore_wait(barrier, 1)
    copy = pltpu.make_async_remote_copy(
        src_ref=x_ref,
        dst_ref=y_ref,
        send_sem=send_sem,
        recv_sem=recv_sem,
        device_id=here + (other,),
        device_id_type=MESH,
    )
    copy.start()
    copy.wait()


def swap_cores(x, collective_id):
    return pl.pallas_call(
        swap_kernel,
        out_shape=jax.ShapeDtypeStruct(x.shape, x.dtype),
        in_specs=[pl.BlockSpec(memory_space=pl.ANY)],
        out_specs=pl.BlockSpec(memory_space=pl.ANY),
        scratch_shapes=[pltpu.SemaphoreType.DMA(()), pltpu.SemaphoreType.DMA(())],
        compiler_params=pltpu.CompilerParams(collective_id=collective_id, has_side_effects=True),
    )(x)


def opening_kernel(x_ref, w_ref, y_ref, w_all, buf, send_sem, recv_sem, own_sem, w_send, w_recv, w_own):
    n = x_ref.shape[0]
    cores = lax.axis_size("core")
    ring = n // cores
    me = chan_index()
    slab = lax.axis_index("seq")
    z = lax.axis_index("z")
    core = lax.axis_index("core")
    barrier = pltpu.get_barrier_semaphore()
    for step in range(1, n):
        peer = lax.rem(me + step, n)
        pl.semaphore_signal(barrier, inc=1, device_id=chan_device(slab, peer), device_id_type=MESH)
    pl.semaphore_wait(barrier, n - 1)
    own = pltpu.make_async_copy(x_ref.at[me], buf.at[me], own_sem)
    own.start()
    sends = []
    for step in range(1, n):
        peer = lax.rem(me + step, n)
        copy = pltpu.make_async_remote_copy(
            src_ref=x_ref.at[peer],
            dst_ref=buf.at[me],
            send_sem=send_sem.at[peer],
            recv_sem=recv_sem.at[me],
            device_id=chan_device(slab, peer),
            device_id_type=MESH,
        )
        copy.start()
        sends.append(copy)
    w_local = pltpu.make_async_copy(w_ref, w_all.at[me], w_own)
    w_local.start()
    right = (slab, lax.rem(z + 1, ring), core)
    left = (slab, lax.rem(z + ring - 1, ring), core)
    partner = (slab, z, cores - 1 - core)

    pieces = W_PIECES
    depth = w_ref.shape[0] // pieces

    def slot(origin):
        return lax.rem(origin + ring, ring) * cores + core

    def held(h, j):
        return w_all.at[h, pl.ds(j * depth, depth)]

    def send(source, h, j, kind, target):
        copy = pltpu.make_async_remote_copy(
            src_ref=source,
            dst_ref=held(h, j),
            send_sem=w_send.at[h, kind, j],
            recv_sem=w_recv.at[h, j],
            device_id=target,
            device_id_type=MESH,
        )
        copy.start()
        sends.append(copy)

    def arrive(h, j, source):
        pltpu.make_async_remote_copy(
            src_ref=w_ref.at[pl.ds(j * depth, depth)],
            dst_ref=held(h, j),
            send_sem=w_send.at[h, 0, j],
            recv_sem=w_recv.at[h, j],
            device_id=source,
            device_id_type=MESH,
        ).wait_recv()

    half = ring // 2
    full = half - 1 if ring % 2 == 0 else half

    def goes_right(step):
        return range(pieces) if step <= full else range(pieces // 2) if step == half else range(0)

    def goes_left(step):
        return range(pieces) if step <= full else range(pieces // 2, pieces) if step == half else range(0)

    for j in range(pieces):
        mine = w_ref.at[pl.ds(j * depth, depth)]
        if j in goes_right(1):
            send(mine, me, j, 0, right)
        if j in goes_left(1):
            send(mine, me, j, 1, left)
        send(mine, me, j, 2, partner)
    for step in range(1, half + 1):
        for j in range(pieces):
            if j in goes_right(step):
                h = slot(z - step)
                arrive(h, j, left)
                if j in goes_right(step + 1):
                    send(held(h, j), h, j, 0, right)
                send(held(h, j), h, j, 2, partner)
            if j in goes_left(step):
                h = slot(z + step)
                arrive(h, j, right)
                if j in goes_left(step + 1):
                    send(held(h, j), h, j, 1, left)
                send(held(h, j), h, j, 2, partner)
    for origin in range(ring):
        for j in range(pieces):
            arrive(origin * cores + (cores - 1 - core), j, partner)
    for step in range(1, n):
        source = lax.rem(me + n - step, n)
        pltpu.make_async_remote_copy(
            src_ref=x_ref.at[source],
            dst_ref=buf.at[source],
            send_sem=send_sem.at[source],
            recv_sem=recv_sem.at[source],
            device_id=chan_device(slab, source),
            device_id_type=MESH,
        ).wait_recv()
    for copy in sends:
        copy.wait_send()
    own.wait()
    w_local.wait()
    y_ref[...] = buf[...]


def opening(x, w, collective_id):
    n = x.shape[0]
    return pl.pallas_call(
        opening_kernel,
        out_shape=(
            jax.ShapeDtypeStruct(x.shape, x.dtype),
            jax.ShapeDtypeStruct((n,) + w.shape, w.dtype),
        ),
        in_specs=[pl.BlockSpec(memory_space=pltpu.VMEM), pl.BlockSpec(memory_space=pl.ANY)],
        out_specs=(pl.BlockSpec(memory_space=pltpu.VMEM), pl.BlockSpec(memory_space=pl.ANY)),
        scratch_shapes=[
            pltpu.VMEM(x.shape, x.dtype),
            pltpu.SemaphoreType.DMA((n,)),
            pltpu.SemaphoreType.DMA((n,)),
            pltpu.SemaphoreType.DMA(()),
            pltpu.SemaphoreType.DMA((n, 3, W_PIECES)),
            pltpu.SemaphoreType.DMA((n, W_PIECES)),
            pltpu.SemaphoreType.DMA(()),
        ],
        compiler_params=pltpu.CompilerParams(collective_id=collective_id, has_side_effects=True),
    )(x, w)


def split_rows(x, groups, collective_id):
    rows, cols = x.shape
    got = exchange(x.reshape(groups, rows // groups, cols), collective_id)
    return got.transpose(1, 0, 2).reshape(rows // groups, groups * cols)


def split_cols(x, groups, collective_id):
    rows, _, cols = x.shape
    got = exchange(x.transpose(1, 0, 2), collective_id)
    return got.reshape(groups * rows, cols)


def closing_kernel(x_ref, w_ref, y_ref, got, rows, out, back, send_sem, recv_sem, own_sem):
    n = x_ref.shape[0]
    cols = out.shape[2]
    me = chan_index()
    slab = lax.axis_index("seq")
    barrier = pltpu.get_barrier_semaphore()
    for step in range(1, n):
        peer = lax.rem(me + step, n)
        pl.semaphore_signal(barrier, inc=1, device_id=chan_device(slab, peer), device_id_type=MESH)
    pl.semaphore_wait(barrier, n - 1)

    def remote(phase, src, dst, peer, sender):
        return pltpu.make_async_remote_copy(
            src_ref=src,
            dst_ref=dst,
            send_sem=send_sem.at[phase, peer],
            recv_sem=recv_sem.at[phase, sender],
            device_id=chan_device(slab, peer),
            device_id_type=MESH,
        )

    sends = []
    for phase, (source, landing) in enumerate(((x_ref, got), (out, back))):
        own = pltpu.make_async_copy(source.at[me], landing.at[me], own_sem.at[phase])
        if phase == 1:
            hidden_rows = rows[...]
            for step in range(n):
                c = lax.rem(me + step, n)
                block = w_ref[:, pl.ds(pl.multiple_of(c * cols, cols), cols)]
                out[c] = jnp.dot(hidden_rows, block, preferred_element_type=jnp.float32).astype(out.dtype)
                if step == 0:
                    own.start()
                else:
                    copy = remote(phase, out.at[c], back.at[me], c, me)
                    copy.start()
                    sends.append(copy)
        else:
            own.start()
            for step in range(1, n):
                peer = lax.rem(me + step, n)
                copy = remote(phase, x_ref.at[peer], got.at[me], peer, me)
                copy.start()
                sends.append(copy)
        for step in range(1, n):
            source_dev = lax.rem(me + n - step, n)
            remote(phase, source.at[source_dev], landing.at[source_dev], source_dev, source_dev).wait_recv()
        own.wait()
        if phase == 0:
            width = got.shape[2]
            for g in range(n):
                rows[:, g * width : (g + 1) * width] = got[g]
    for copy in sends:
        copy.wait_send()
    y_ref[...] = back[...]


def closing(hidden_blocks, w_out, collective_id):
    n, chunk, width = hidden_blocks.shape
    cols = w_out.shape[1] // n
    block = (n, chunk, cols)
    return pl.pallas_call(
        closing_kernel,
        out_shape=jax.ShapeDtypeStruct(block, hidden_blocks.dtype),
        in_specs=[pl.BlockSpec(memory_space=pltpu.VMEM)] * 2,
        out_specs=pl.BlockSpec(memory_space=pltpu.VMEM),
        scratch_shapes=[
            pltpu.VMEM(hidden_blocks.shape, hidden_blocks.dtype),
            pltpu.VMEM((chunk, n * width), hidden_blocks.dtype),
            pltpu.VMEM(block, hidden_blocks.dtype),
            pltpu.VMEM(block, hidden_blocks.dtype),
            pltpu.SemaphoreType.DMA((2, n)),
            pltpu.SemaphoreType.DMA((2, n)),
            pltpu.SemaphoreType.DMA((2,)),
        ],
        compiler_params=pltpu.CompilerParams(
            collective_id=collective_id, has_side_effects=True, vmem_limit_bytes=48 * 1024 * 1024
        ),
    )(hidden_blocks, w_out)


def attend(query_rows, key_rows, value_rows, gain_mine, my_slab):
    highest = lax.Precision.HIGHEST
    tok_rows, per_group, _ = value_rows.shape
    blocks = tok_rows // BLOCK
    query_blocks = query_rows.reshape(blocks, BLOCK, per_group, FEAT)
    key_blocks = key_rows.reshape(blocks, BLOCK, per_group, FEAT)
    value_blocks = value_rows.reshape(blocks, BLOCK, per_group, HEAD_DIM)
    value_f32 = value_blocks.astype(jnp.float32)
    key_linear, key_square = feature_parts(key_blocks.astype(jnp.float32))
    own_zero = jnp.sum(value_f32, axis=1)[:, :, None, :]
    own_one = jnp.einsum("bthf,bthe->bhfe", key_linear, value_f32, precision=highest)
    own_two = jnp.einsum("bthf,bthe->bhfe", key_square, value_f32, precision=highest)
    own = jnp.concatenate([own_zero, own_one, own_two], axis=2)
    slab_total = jnp.sum(own, axis=0)
    state_rows = slab_total.shape[0] * slab_total.shape[1]
    prefix = scan_seq(slab_total.astype(jnp.bfloat16).reshape(state_rows, HEAD_DIM), 7).reshape(slab_total.shape)
    earlier = jnp.concatenate([jnp.zeros_like(own[:1]), jnp.cumsum(own, axis=0)[:-1]], axis=0) + prefix[None]
    query_linear, query_square = feature_parts(query_blocks.astype(jnp.float32))
    inter = earlier[:, :, 0][:, None] + jnp.einsum(
        "bthf,bhfe->bthe", query_linear, earlier[:, :, 1 : 1 + FEAT], precision=highest
    )
    inter = inter + jnp.einsum(
        "bthf,bhfe->bthe", query_square, earlier[:, :, 1 + FEAT :], precision=highest
    )
    scores = jnp.einsum(
        "bthf,bshf->bhts", query_blocks, key_blocks, preferred_element_type=jnp.float32
    ) * FEAT ** (-0.5)
    kernel = 1.0 + scores + 0.5 * scores * scores
    causal = jnp.arange(BLOCK)[:, None] >= jnp.arange(BLOCK)[None, :]
    weights = jnp.where(causal, kernel, 0.0).astype(jnp.bfloat16)
    intra = jnp.einsum("bhts,bshe->bthe", weights, value_blocks, preferred_element_type=jnp.float32)
    numerator = (intra + inter).reshape(tok_rows, per_group, HEAD_DIM)
    mean_square = jnp.mean(numerator * numerator, axis=-1, keepdims=True)
    hidden = (numerator * lax.rsqrt(mean_square + 1e-05) * gain_mine).astype(jnp.bfloat16)
    return hidden.reshape(tok_rows, per_group * HEAD_DIM)


def per_device(tokens, w_query, w_key, w_value, w_out, gain):
    groups = lax.axis_size(CHAN)
    per_group = HEADS // groups
    my_group = chan_index()
    my_slab = lax.axis_index("seq")
    tok_rows_total, tok_cols = tokens.shape
    got, value_all = opening(tokens.reshape(groups, tok_rows_total // groups, tok_cols), w_value, 1)
    rows = got.transpose(1, 0, 2).reshape(tok_rows_total // groups, groups * tok_cols)
    chunk = rows.shape[0]
    pf = per_group * FEAT
    d_model = w_query.shape[0]
    w_qk = jnp.concatenate(
        [w_query.reshape(d_model, groups, pf), w_key.reshape(d_model, groups, pf)], axis=2
    )
    qk_t = jnp.einsum("tf,fgd->gdt", rows, w_qk, preferred_element_type=jnp.float32).astype(jnp.bfloat16)
    value = jnp.einsum("tf,gfe->gte", rows, value_all, preferred_element_type=jnp.float32).astype(jnp.bfloat16)
    qk_got, value_got = exchange_many((qk_t, value), 2)
    tok_rows = groups * chunk
    qk_rows = qk_got.transpose(0, 2, 1).reshape(tok_rows, 2 * pf)
    query_rows = qk_rows[:, :pf].reshape(tok_rows, per_group, FEAT)
    key_rows = qk_rows[:, pf:].reshape(tok_rows, per_group, FEAT)
    value_rows = value_got.reshape(tok_rows, per_group, HEAD_DIM)
    value_cols = per_group * HEAD_DIM
    gain_mine = lax.dynamic_slice_in_dim(gain, my_group * value_cols, value_cols, 0).reshape(
        per_group, HEAD_DIM
    )
    hidden = attend(query_rows, key_rows, value_rows, gain_mine, my_slab)
    out_cols = w_out.shape[1] // groups
    mixed_blocks = closing(hidden.reshape(groups, chunk, per_group * HEAD_DIM), w_out, 3)
    return mixed_blocks.reshape(tok_rows, out_cols)

def solution(mesh):
    seq, chan = mesh.devices.shape
    cores = 2 if chan % 2 == 0 else 1
    split = jax.sharding.Mesh(mesh.devices.reshape(seq, chan // cores, cores), ("seq", "z", "core"))
    return jax.shard_map(
        per_device,
        mesh=split,
        in_specs=(P("seq", CHAN), P(), P(), P(None, CHAN), P(), P()),
        out_specs=P("seq", CHAN),
        check_vma=False,
    )
```

```python
import functools

import jax
import jax.numpy as jnp
from jax import lax
from jax.experimental import pallas as pl
from jax.experimental.pallas import tpu as pltpu
from jax.sharding import PartitionSpec as P

MESH = pl.DeviceIdType.MESH
CHAN = ("z", "core")
W_PIECES = 4


def chan_index():
    return lax.axis_index("z") * lax.axis_size("core") + lax.axis_index("core")


def chan_device(slab, peer):
    cores = lax.axis_size("core")
    return (slab, peer // cores, peer % cores)

HEADS = 16
FEAT = 16
HEAD_DIM = 128
BLOCK = 896


def feature_parts(rows):
    linear = rows * FEAT ** (-0.25)
    square = (rows[..., :, None] * rows[..., None, :]).reshape(rows.shape[:-1] + (FEAT * FEAT,)) * (
        2.0 * FEAT
    ) ** (-0.5)
    return (linear, square)


def exchange_kernel(count, *refs):
    xs, ys, bufs = refs[:count], refs[count : 2 * count], refs[2 * count : 3 * count]
    send_sem, recv_sem, own_sem = refs[3 * count :]
    n = xs[0].shape[0]
    me = chan_index()
    slab = lax.axis_index("seq")
    barrier = pltpu.get_barrier_semaphore()
    for step in range(1, n):
        peer = lax.rem(me + step, n)
        pl.semaphore_signal(barrier, inc=1, device_id=chan_device(slab, peer), device_id_type=MESH)
    pl.semaphore_wait(barrier, n - 1)
    owns = []
    sends = []
    for a in range(count):
        own = pltpu.make_async_copy(xs[a].at[me], bufs[a].at[me], own_sem.at[a])
        own.start()
        owns.append(own)
    for step in range(1, n):
        peer = lax.rem(me + step, n)
        for a in range(count):
            copy = pltpu.make_async_remote_copy(
                src_ref=xs[a].at[peer],
                dst_ref=bufs[a].at[me],
                send_sem=send_sem.at[a, peer],
                recv_sem=recv_sem.at[a, me],
                device_id=chan_device(slab, peer),
                device_id_type=MESH,
            )
            copy.start()
            sends.append(copy)
    for step in range(1, n):
        source = lax.rem(me + n - step, n)
        for a in range(count):
            pltpu.make_async_remote_copy(
                src_ref=xs[a].at[source],
                dst_ref=bufs[a].at[source],
                send_sem=send_sem.at[a, source],
                recv_sem=recv_sem.at[a, source],
                device_id=chan_device(slab, source),
                device_id_type=MESH,
            ).wait_recv()
    for copy in sends:
        copy.wait_send()
    for a in range(count):
        owns[a].wait()
        ys[a][...] = bufs[a][...]


def exchange_many(xs, collective_id):
    count = len(xs)
    n = xs[0].shape[0]
    return pl.pallas_call(
        functools.partial(exchange_kernel, count),
        out_shape=tuple(jax.ShapeDtypeStruct(x.shape, x.dtype) for x in xs),
        in_specs=[pl.BlockSpec(memory_space=pltpu.VMEM)] * count,
        out_specs=tuple(pl.BlockSpec(memory_space=pltpu.VMEM) for _ in xs),
        scratch_shapes=[pltpu.VMEM(x.shape, x.dtype) for x in xs]
        + [
            pltpu.SemaphoreType.DMA((count, n)),
            pltpu.SemaphoreType.DMA((count, n)),
            pltpu.SemaphoreType.DMA((count,)),
        ],
        compiler_params=pltpu.CompilerParams(collective_id=collective_id, has_side_effects=True),
    )(*xs)


def exchange(x, collective_id):
    return exchange_many((x,), collective_id)[0]


def gather_kernel(x_ref, y_ref, buf, send_sem, recv_sem):
    n = buf.shape[0]
    me = lax.axis_index("seq")
    here = (lax.axis_index("z"), lax.axis_index("core"))
    buf[...] = jnp.zeros_like(buf)
    barrier = pltpu.get_barrier_semaphore()
    for step in range(1, n):
        peer = lax.rem(me + step, n)
        pl.semaphore_signal(barrier, inc=1, device_id=(peer,) + here, device_id_type=MESH)
    pl.semaphore_wait(barrier, n - 1)

    def copy_to(peer):
        return pltpu.make_async_remote_copy(
            src_ref=x_ref,
            dst_ref=buf.at[me],
            send_sem=send_sem.at[peer],
            recv_sem=recv_sem.at[me],
            device_id=(peer,) + here,
            device_id_type=MESH,
        )

    def copy_from(source):
        return pltpu.make_async_remote_copy(
            src_ref=x_ref,
            dst_ref=buf.at[source],
            send_sem=send_sem.at[source],
            recv_sem=recv_sem.at[source],
            device_id=(source,) + here,
            device_id_type=MESH,
        )

    for step in range(1, n):
        @pl.when(me + step < n)
        def _():
            copy_to(me + step).start()

    for step in range(1, n):
        @pl.when(me - step >= 0)
        def _():
            copy_from(me - step).wait_recv()

    for step in range(1, n):
        @pl.when(me + step < n)
        def _():
            copy_to(me + step).wait_send()

    y_ref[...] = buf[...]


def gather_seq(x, slabs, collective_id):
    shape = (slabs,) + x.shape
    return pl.pallas_call(
        gather_kernel,
        out_shape=jax.ShapeDtypeStruct(shape, x.dtype),
        in_specs=[pl.BlockSpec(memory_space=pltpu.VMEM)],
        out_specs=pl.BlockSpec(memory_space=pltpu.VMEM),
        scratch_shapes=[
            pltpu.VMEM(shape, x.dtype),
            pltpu.SemaphoreType.DMA((slabs,)),
            pltpu.SemaphoreType.DMA((slabs,)),
        ],
        compiler_params=pltpu.CompilerParams(collective_id=collective_id, has_side_effects=True),
    )(x)


def scan_kernel(width, x_ref, y_ref, row_buf, col_buf, total, row_send, row_recv, col_send, col_recv):
    n = lax.axis_size("seq")
    height = n // width
    me = lax.axis_index("seq")
    row, col = me // width, me % width
    here = (lax.axis_index("z"), lax.axis_index("core"))
    row_buf[...] = jnp.zeros_like(row_buf)
    col_buf[...] = jnp.zeros_like(col_buf)
    barrier = pltpu.get_barrier_semaphore()
    for step in range(1, width):
        peer = row * width + lax.rem(col + step, width)
        pl.semaphore_signal(barrier, inc=1, device_id=(peer,) + here, device_id_type=MESH)
    for step in range(1, height):
        peer = lax.rem(row + step, height) * width + col
        pl.semaphore_signal(barrier, inc=1, device_id=(peer,) + here, device_id_type=MESH)
    pl.semaphore_wait(barrier, width + height - 2)

    def row_copy(c, slot):
        return pltpu.make_async_remote_copy(
            src_ref=x_ref,
            dst_ref=row_buf.at[slot],
            send_sem=row_send.at[c],
            recv_sem=row_recv.at[slot],
            device_id=(row * width + c,) + here,
            device_id_type=MESH,
        )

    sends = []
    for step in range(1, width):
        c = lax.rem(col + step, width)
        copy = row_copy(c, col)
        copy.start()
        sends.append(copy)
    for step in range(1, width):
        c = lax.rem(col + width - step, width)
        row_copy(c, c).wait_recv()
    mine = x_ref[...].astype(jnp.float32)
    row_total = mine
    row_prefix = jnp.zeros_like(mine)
    for c in range(width):
        part = jnp.where(c == col, 0.0, row_buf[c].astype(jnp.float32))
        row_total = row_total + part
        row_prefix = row_prefix + jnp.where(c < col, part, 0.0)
    total[...] = row_total

    def col_copy(r, slot):
        return pltpu.make_async_remote_copy(
            src_ref=total,
            dst_ref=col_buf.at[slot],
            send_sem=col_send.at[r],
            recv_sem=col_recv.at[slot],
            device_id=(r * width + col,) + here,
            device_id_type=MESH,
        )

    for step in range(1, height):
        @pl.when(row + step < height)
        def _():
            col_copy(row + step, row).start()

    for step in range(1, height):
        @pl.when(row - step >= 0)
        def _():
            col_copy(row - step, row - step).wait_recv()

    for step in range(1, height):
        @pl.when(row + step < height)
        def _():
            col_copy(row + step, row).wait_send()

    for copy in sends:
        copy.wait_send()
    prefix = row_prefix
    for r in range(height):
        prefix = prefix + col_buf[r]
    y_ref[...] = prefix


def scan_seq(x, collective_id):
    n = lax.axis_size("seq")
    width = 1
    while (width + 1) * (width + 1) <= n:
        width += 1
    while n % width:
        width -= 1
    height = n // width
    return pl.pallas_call(
        functools.partial(scan_kernel, width),
        out_shape=jax.ShapeDtypeStruct(x.shape, jnp.float32),
        in_specs=[pl.BlockSpec(memory_space=pltpu.VMEM)],
        out_specs=pl.BlockSpec(memory_space=pltpu.VMEM),
        scratch_shapes=[
            pltpu.VMEM((width,) + x.shape, x.dtype),
            pltpu.VMEM((height,) + x.shape, jnp.float32),
            pltpu.VMEM(x.shape, jnp.float32),
            pltpu.SemaphoreType.DMA((width,)),
            pltpu.SemaphoreType.DMA((width,)),
            pltpu.SemaphoreType.DMA((height,)),
            pltpu.SemaphoreType.DMA((height,)),
        ],
        compiler_params=pltpu.CompilerParams(collective_id=collective_id, has_side_effects=True),
    )(x)


def swap_kernel(x_ref, y_ref, send_sem, recv_sem):
    here = (lax.axis_index("seq"), lax.axis_index("z"))
    other = lax.axis_size("core") - 1 - lax.axis_index("core")
    barrier = pltpu.get_barrier_semaphore()
    pl.semaphore_signal(barrier, inc=1, device_id=here + (other,), device_id_type=MESH)
    pl.semaphore_wait(barrier, 1)
    copy = pltpu.make_async_remote_copy(
        src_ref=x_ref,
        dst_ref=y_ref,
        send_sem=send_sem,
        recv_sem=recv_sem,
        device_id=here + (other,),
        device_id_type=MESH,
    )
    copy.start()
    copy.wait()


def swap_cores(x, collective_id):
    return pl.pallas_call(
        swap_kernel,
        out_shape=jax.ShapeDtypeStruct(x.shape, x.dtype),
        in_specs=[pl.BlockSpec(memory_space=pl.ANY)],
        out_specs=pl.BlockSpec(memory_space=pl.ANY),
        scratch_shapes=[pltpu.SemaphoreType.DMA(()), pltpu.SemaphoreType.DMA(())],
        compiler_params=pltpu.CompilerParams(collective_id=collective_id, has_side_effects=True),
    )(x)


def opening_kernel(x_ref, w_ref, y_ref, w_all, buf, send_sem, recv_sem, own_sem, w_send, w_recv, w_own):
    n = x_ref.shape[0]
    cores = lax.axis_size("core")
    ring = n // cores
    me = chan_index()
    slab = lax.axis_index("seq")
    z = lax.axis_index("z")
    core = lax.axis_index("core")
    barrier = pltpu.get_barrier_semaphore()
    for step in range(1, n):
        peer = lax.rem(me + step, n)
        pl.semaphore_signal(barrier, inc=1, device_id=chan_device(slab, peer), device_id_type=MESH)
    pl.semaphore_wait(barrier, n - 1)
    own = pltpu.make_async_copy(x_ref.at[me], buf.at[me], own_sem)
    own.start()
    sends = []
    for step in range(1, n):
        peer = lax.rem(me + step, n)
        copy = pltpu.make_async_remote_copy(
            src_ref=x_ref.at[peer],
            dst_ref=buf.at[me],
            send_sem=send_sem.at[peer],
            recv_sem=recv_sem.at[me],
            device_id=chan_device(slab, peer),
            device_id_type=MESH,
        )
        copy.start()
        sends.append(copy)
    w_local = pltpu.make_async_copy(w_ref, w_all.at[me], w_own)
    w_local.start()
    right = (slab, lax.rem(z + 1, ring), core)
    left = (slab, lax.rem(z + ring - 1, ring), core)
    partner = (slab, z, cores - 1 - core)

    pieces = W_PIECES
    depth = w_ref.shape[0] // pieces

    def slot(origin):
        return lax.rem(origin + ring, ring) * cores + core

    def held(h, j):
        return w_all.at[h, pl.ds(j * depth, depth)]

    def send(source, h, j, kind, target):
        copy = pltpu.make_async_remote_copy(
            src_ref=source,
            dst_ref=held(h, j),
            send_sem=w_send.at[h, kind, j],
            recv_sem=w_recv.at[h, j],
            device_id=target,
            device_id_type=MESH,
        )
        copy.start()
        sends.append(copy)

    def arrive(h, j, source):
        pltpu.make_async_remote_copy(
            src_ref=w_ref.at[pl.ds(j * depth, depth)],
            dst_ref=held(h, j),
            send_sem=w_send.at[h, 0, j],
            recv_sem=w_recv.at[h, j],
            device_id=source,
            device_id_type=MESH,
        ).wait_recv()

    half = ring // 2
    full = half - 1 if ring % 2 == 0 else half

    def goes_right(step):
        return range(pieces) if step <= full else range(pieces // 2) if step == half else range(0)

    def goes_left(step):
        return range(pieces) if step <= full else range(pieces // 2, pieces) if step == half else range(0)

    for j in range(pieces):
        mine = w_ref.at[pl.ds(j * depth, depth)]
        if j in goes_right(1):
            send(mine, me, j, 0, right)
        if j in goes_left(1):
            send(mine, me, j, 1, left)
        send(mine, me, j, 2, partner)
    for step in range(1, half + 1):
        for j in range(pieces):
            if j in goes_right(step):
                h = slot(z - step)
                arrive(h, j, left)
                if j in goes_right(step + 1):
                    send(held(h, j), h, j, 0, right)
                send(held(h, j), h, j, 2, partner)
            if j in goes_left(step):
                h = slot(z + step)
                arrive(h, j, right)
                if j in goes_left(step + 1):
                    send(held(h, j), h, j, 1, left)
                send(held(h, j), h, j, 2, partner)
    for origin in range(ring):
        for j in range(pieces):
            arrive(origin * cores + (cores - 1 - core), j, partner)
    for step in range(1, n):
        source = lax.rem(me + n - step, n)
        pltpu.make_async_remote_copy(
            src_ref=x_ref.at[source],
            dst_ref=buf.at[source],
            send_sem=send_sem.at[source],
            recv_sem=recv_sem.at[source],
            device_id=chan_device(slab, source),
            device_id_type=MESH,
        ).wait_recv()
    for copy in sends:
        copy.wait_send()
    own.wait()
    w_local.wait()
    y_ref[...] = buf[...]


def opening(x, w, collective_id):
    n = x.shape[0]
    return pl.pallas_call(
        opening_kernel,
        out_shape=(
            jax.ShapeDtypeStruct(x.shape, x.dtype),
            jax.ShapeDtypeStruct((n,) + w.shape, w.dtype),
        ),
        in_specs=[pl.BlockSpec(memory_space=pltpu.VMEM), pl.BlockSpec(memory_space=pl.ANY)],
        out_specs=(pl.BlockSpec(memory_space=pltpu.VMEM), pl.BlockSpec(memory_space=pl.ANY)),
        scratch_shapes=[
            pltpu.VMEM(x.shape, x.dtype),
            pltpu.SemaphoreType.DMA((n,)),
            pltpu.SemaphoreType.DMA((n,)),
            pltpu.SemaphoreType.DMA(()),
            pltpu.SemaphoreType.DMA((n, 3, W_PIECES)),
            pltpu.SemaphoreType.DMA((n, W_PIECES)),
            pltpu.SemaphoreType.DMA(()),
        ],
        compiler_params=pltpu.CompilerParams(collective_id=collective_id, has_side_effects=True),
    )(x, w)


def split_rows(x, groups, collective_id):
    rows, cols = x.shape
    got = exchange(x.reshape(groups, rows // groups, cols), collective_id)
    return got.transpose(1, 0, 2).reshape(rows // groups, groups * cols)


def split_cols(x, groups, collective_id):
    rows, _, cols = x.shape
    got = exchange(x.transpose(1, 0, 2), collective_id)
    return got.reshape(groups * rows, cols)


def closing_kernel(x_ref, w_ref, y_ref, got, rows, out, back, send_sem, recv_sem, own_sem):
    n = x_ref.shape[0]
    cols = out.shape[2]
    me = chan_index()
    slab = lax.axis_index("seq")
    barrier = pltpu.get_barrier_semaphore()
    for step in range(1, n):
        peer = lax.rem(me + step, n)
        pl.semaphore_signal(barrier, inc=1, device_id=chan_device(slab, peer), device_id_type=MESH)
    pl.semaphore_wait(barrier, n - 1)

    def remote(phase, src, dst, peer, sender):
        return pltpu.make_async_remote_copy(
            src_ref=src,
            dst_ref=dst,
            send_sem=send_sem.at[phase, peer],
            recv_sem=recv_sem.at[phase, sender],
            device_id=chan_device(slab, peer),
            device_id_type=MESH,
        )

    sends = []
    for phase, (source, landing) in enumerate(((x_ref, got), (out, back))):
        own = pltpu.make_async_copy(source.at[me], landing.at[me], own_sem.at[phase])
        if phase == 1:
            hidden_rows = rows[...]
            for step in range(n):
                c = lax.rem(me + step, n)
                block = w_ref[:, pl.ds(pl.multiple_of(c * cols, cols), cols)]
                out[c] = jnp.dot(hidden_rows, block, preferred_element_type=jnp.float32).astype(out.dtype)
                if step == 0:
                    own.start()
                else:
                    copy = remote(phase, out.at[c], back.at[me], c, me)
                    copy.start()
                    sends.append(copy)
        else:
            own.start()
            for step in range(1, n):
                peer = lax.rem(me + step, n)
                copy = remote(phase, x_ref.at[peer], got.at[me], peer, me)
                copy.start()
                sends.append(copy)
        for step in range(1, n):
            source_dev = lax.rem(me + n - step, n)
            remote(phase, source.at[source_dev], landing.at[source_dev], source_dev, source_dev).wait_recv()
        own.wait()
        if phase == 0:
            width = got.shape[2]
            for g in range(n):
                rows[:, g * width : (g + 1) * width] = got[g]
    for copy in sends:
        copy.wait_send()
    y_ref[...] = back[...]


def closing(hidden_blocks, w_out, collective_id):
    n, chunk, width = hidden_blocks.shape
    cols = w_out.shape[1] // n
    block = (n, chunk, cols)
    return pl.pallas_call(
        closing_kernel,
        out_shape=jax.ShapeDtypeStruct(block, hidden_blocks.dtype),
        in_specs=[pl.BlockSpec(memory_space=pltpu.VMEM)] * 2,
        out_specs=pl.BlockSpec(memory_space=pltpu.VMEM),
        scratch_shapes=[
            pltpu.VMEM(hidden_blocks.shape, hidden_blocks.dtype),
            pltpu.VMEM((chunk, n * width), hidden_blocks.dtype),
            pltpu.VMEM(block, hidden_blocks.dtype),
            pltpu.VMEM(block, hidden_blocks.dtype),
            pltpu.SemaphoreType.DMA((2, n)),
            pltpu.SemaphoreType.DMA((2, n)),
            pltpu.SemaphoreType.DMA((2,)),
        ],
        compiler_params=pltpu.CompilerParams(
            collective_id=collective_id, has_side_effects=True, vmem_limit_bytes=48 * 1024 * 1024
        ),
    )(hidden_blocks, w_out)


def middle_kernel(rows_ref, w_ref, wqk_ref, qk_out, v_out, qk_send, v_send, qk_got, v_got, send_sem, recv_sem, own_sem):
    n = w_ref.shape[0]
    me = chan_index()
    slab = lax.axis_index("seq")
    barrier = pltpu.get_barrier_semaphore()
    for step in range(1, n):
        peer = lax.rem(me + step, n)
        pl.semaphore_signal(barrier, inc=1, device_id=chan_device(slab, peer), device_id_type=MESH)
    pl.semaphore_wait(barrier, n - 1)
    pairs = ((qk_send, qk_got), (v_send, v_got))

    def remote(kind, peer, sender, slot):
        source, landing = pairs[kind]
        return pltpu.make_async_remote_copy(
            src_ref=source.at[slot],
            dst_ref=landing.at[sender],
            send_sem=send_sem.at[kind, peer],
            recv_sem=recv_sem.at[kind, sender],
            device_id=chan_device(slab, peer),
            device_id_type=MESH,
        )

    rows = rows_ref[...]
    owns = []
    sends = []
    for step in range(n):
        g = lax.rem(me + step, n)
        v_send[g] = jnp.dot(rows, w_ref[g], preferred_element_type=jnp.float32).astype(v_send.dtype)
        qk_send[g] = lax.dot_general(
            wqk_ref[g], rows, (((1,), (1,)), ((), ())), preferred_element_type=jnp.float32
        ).astype(qk_send.dtype)
        for kind in range(2):
            source, landing = pairs[kind]
            if step == 0:
                own = pltpu.make_async_copy(source.at[me], landing.at[me], own_sem.at[kind])
                own.start()
                owns.append(own)
            else:
                copy = remote(kind, g, me, g)
                copy.start()
                sends.append(copy)
    for step in range(1, n):
        source_dev = lax.rem(me + n - step, n)
        for kind in range(2):
            remote(kind, source_dev, source_dev, source_dev).wait_recv()
    for own in owns:
        own.wait()
    for copy in sends:
        copy.wait_send()
    qk_out[...] = qk_got[...]
    v_out[...] = v_got[...]


def middle(rows, w_all, wqk_t, collective_id):
    n = w_all.shape[0]
    chunk = rows.shape[0]
    qk_shape = (n, wqk_t.shape[1], chunk)
    v_shape = (n, chunk, w_all.shape[2])
    return pl.pallas_call(
        middle_kernel,
        out_shape=(
            jax.ShapeDtypeStruct(qk_shape, rows.dtype),
            jax.ShapeDtypeStruct(v_shape, rows.dtype),
        ),
        in_specs=[pl.BlockSpec(memory_space=pltpu.VMEM)] * 3,
        out_specs=(pl.BlockSpec(memory_space=pltpu.VMEM), pl.BlockSpec(memory_space=pltpu.VMEM)),
        scratch_shapes=[
            pltpu.VMEM(qk_shape, rows.dtype),
            pltpu.VMEM(v_shape, rows.dtype),
            pltpu.VMEM(qk_shape, rows.dtype),
            pltpu.VMEM(v_shape, rows.dtype),
            pltpu.SemaphoreType.DMA((2, n)),
            pltpu.SemaphoreType.DMA((2, n)),
            pltpu.SemaphoreType.DMA((2,)),
        ],
        compiler_params=pltpu.CompilerParams(
            collective_id=collective_id, has_side_effects=True, vmem_limit_bytes=48 * 1024 * 1024
        ),
    )(rows, w_all, wqk_t)


def attend(query_rows, key_rows, value_rows, gain_mine, my_slab):
    highest = lax.Precision.HIGHEST
    tok_rows, per_group, _ = value_rows.shape
    blocks = tok_rows // BLOCK
    query_blocks = query_rows.reshape(blocks, BLOCK, per_group, FEAT)
    key_blocks = key_rows.reshape(blocks, BLOCK, per_group, FEAT)
    value_blocks = value_rows.reshape(blocks, BLOCK, per_group, HEAD_DIM)
    value_f32 = value_blocks.astype(jnp.float32)
    key_linear, key_square = feature_parts(key_blocks.astype(jnp.float32))
    own_zero = jnp.sum(value_f32, axis=1)[:, :, None, :]
    own_one = jnp.einsum("bthf,bthe->bhfe", key_linear, value_f32, precision=highest)
    own_two = jnp.einsum("bthf,bthe->bhfe", key_square, value_f32, precision=highest)
    own = jnp.concatenate([own_zero, own_one, own_two], axis=2)
    slab_total = jnp.sum(own, axis=0)
    state_rows = slab_total.shape[0] * slab_total.shape[1]
    prefix = scan_seq(slab_total.astype(jnp.bfloat16).reshape(state_rows, HEAD_DIM), 7).reshape(slab_total.shape)
    earlier = jnp.concatenate([jnp.zeros_like(own[:1]), jnp.cumsum(own, axis=0)[:-1]], axis=0) + prefix[None]
    query_linear, query_square = feature_parts(query_blocks.astype(jnp.float32))
    inter = earlier[:, :, 0][:, None] + jnp.einsum(
        "bthf,bhfe->bthe", query_linear, earlier[:, :, 1 : 1 + FEAT], precision=highest
    )
    inter = inter + jnp.einsum(
        "bthf,bhfe->bthe", query_square, earlier[:, :, 1 + FEAT :], precision=highest
    )
    scores = jnp.einsum(
        "bthf,bshf->bhts", query_blocks, key_blocks, preferred_element_type=jnp.float32
    ) * FEAT ** (-0.5)
    kernel = 1.0 + scores + 0.5 * scores * scores
    causal = jnp.arange(BLOCK)[:, None] >= jnp.arange(BLOCK)[None, :]
    weights = jnp.where(causal, kernel, 0.0).astype(jnp.bfloat16)
    intra = jnp.einsum("bhts,bshe->bthe", weights, value_blocks, preferred_element_type=jnp.float32)
    numerator = (intra + inter).reshape(tok_rows, per_group, HEAD_DIM)
    mean_square = jnp.mean(numerator * numerator, axis=-1, keepdims=True)
    hidden = (numerator * lax.rsqrt(mean_square + 1e-05) * gain_mine).astype(jnp.bfloat16)
    return hidden.reshape(tok_rows, per_group * HEAD_DIM)


def per_device(tokens, w_query, w_key, w_value, w_out, gain):
    groups = lax.axis_size(CHAN)
    per_group = HEADS // groups
    my_group = chan_index()
    my_slab = lax.axis_index("seq")
    tok_rows_total, tok_cols = tokens.shape
    got, value_all = opening(tokens.reshape(groups, tok_rows_total // groups, tok_cols), w_value, 1)
    rows = got.transpose(1, 0, 2).reshape(tok_rows_total // groups, groups * tok_cols)
    chunk = rows.shape[0]
    pf = per_group * FEAT
    d_model = w_query.shape[0]
    w_qk = jnp.concatenate(
        [w_query.reshape(d_model, groups, pf), w_key.reshape(d_model, groups, pf)], axis=2
    )
    qk_got, value_got = middle(rows, value_all, w_qk.transpose(1, 2, 0), 2)
    tok_rows = groups * chunk
    qk_rows = qk_got.transpose(0, 2, 1).reshape(tok_rows, 2 * pf)
    query_rows = qk_rows[:, :pf].reshape(tok_rows, per_group, FEAT)
    key_rows = qk_rows[:, pf:].reshape(tok_rows, per_group, FEAT)
    value_rows = value_got.reshape(tok_rows, per_group, HEAD_DIM)
    value_cols = per_group * HEAD_DIM
    gain_mine = lax.dynamic_slice_in_dim(gain, my_group * value_cols, value_cols, 0).reshape(
        per_group, HEAD_DIM
    )
    hidden = attend(query_rows, key_rows, value_rows, gain_mine, my_slab)
    out_cols = w_out.shape[1] // groups
    mixed_blocks = closing(hidden.reshape(groups, chunk, per_group * HEAD_DIM), w_out, 3)
    return mixed_blocks.reshape(tok_rows, out_cols)

def solution(mesh):
    seq, chan = mesh.devices.shape
    cores = 2 if chan % 2 == 0 else 1
    split = jax.sharding.Mesh(mesh.devices.reshape(seq, chan // cores, cores), ("seq", "z", "core"))
    return jax.shard_map(
        per_device,
        mesh=split,
        in_specs=(P("seq", CHAN), P(), P(), P(None, CHAN), P(), P()),
        out_specs=P("seq", CHAN),
        check_vma=False,
    )
```

```python
import functools

import jax
import jax.numpy as jnp
from jax import lax
from jax.experimental import pallas as pl
from jax.experimental.pallas import tpu as pltpu
from jax.sharding import PartitionSpec as P

MESH = pl.DeviceIdType.MESH
CHAN = ("z", "core")
W_PIECES = 4


def chan_index():
    return lax.axis_index("z") * lax.axis_size("core") + lax.axis_index("core")


def chan_device(slab, peer):
    cores = lax.axis_size("core")
    return (slab, peer // cores, peer % cores)

HEADS = 16
FEAT = 16
HEAD_DIM = 128
BLOCK = 896


def feature_parts(rows):
    linear = rows * FEAT ** (-0.25)
    square = (rows[..., :, None] * rows[..., None, :]).reshape(rows.shape[:-1] + (FEAT * FEAT,)) * (
        2.0 * FEAT
    ) ** (-0.5)
    return (linear, square)


def exchange_kernel(count, *refs):
    xs, ys, bufs = refs[:count], refs[count : 2 * count], refs[2 * count : 3 * count]
    send_sem, recv_sem, own_sem = refs[3 * count :]
    n = xs[0].shape[0]
    me = chan_index()
    slab = lax.axis_index("seq")
    barrier = pltpu.get_barrier_semaphore()
    for step in range(1, n):
        peer = lax.rem(me + step, n)
        pl.semaphore_signal(barrier, inc=1, device_id=chan_device(slab, peer), device_id_type=MESH)
    pl.semaphore_wait(barrier, n - 1)
    owns = []
    sends = []
    for a in range(count):
        own = pltpu.make_async_copy(xs[a].at[me], bufs[a].at[me], own_sem.at[a])
        own.start()
        owns.append(own)
    for step in range(1, n):
        peer = lax.rem(me + step, n)
        for a in range(count):
            copy = pltpu.make_async_remote_copy(
                src_ref=xs[a].at[peer],
                dst_ref=bufs[a].at[me],
                send_sem=send_sem.at[a, peer],
                recv_sem=recv_sem.at[a, me],
                device_id=chan_device(slab, peer),
                device_id_type=MESH,
            )
            copy.start()
            sends.append(copy)
    for step in range(1, n):
        source = lax.rem(me + n - step, n)
        for a in range(count):
            pltpu.make_async_remote_copy(
                src_ref=xs[a].at[source],
                dst_ref=bufs[a].at[source],
                send_sem=send_sem.at[a, source],
                recv_sem=recv_sem.at[a, source],
                device_id=chan_device(slab, source),
                device_id_type=MESH,
            ).wait_recv()
    for copy in sends:
        copy.wait_send()
    for a in range(count):
        owns[a].wait()
        ys[a][...] = bufs[a][...]


def exchange_many(xs, collective_id):
    count = len(xs)
    n = xs[0].shape[0]
    return pl.pallas_call(
        functools.partial(exchange_kernel, count),
        out_shape=tuple(jax.ShapeDtypeStruct(x.shape, x.dtype) for x in xs),
        in_specs=[pl.BlockSpec(memory_space=pltpu.VMEM)] * count,
        out_specs=tuple(pl.BlockSpec(memory_space=pltpu.VMEM) for _ in xs),
        scratch_shapes=[pltpu.VMEM(x.shape, x.dtype) for x in xs]
        + [
            pltpu.SemaphoreType.DMA((count, n)),
            pltpu.SemaphoreType.DMA((count, n)),
            pltpu.SemaphoreType.DMA((count,)),
        ],
        compiler_params=pltpu.CompilerParams(collective_id=collective_id, has_side_effects=True),
    )(*xs)


def exchange(x, collective_id):
    return exchange_many((x,), collective_id)[0]


def gather_kernel(x_ref, y_ref, buf, send_sem, recv_sem):
    n = buf.shape[0]
    me = lax.axis_index("seq")
    here = (lax.axis_index("z"), lax.axis_index("core"))
    buf[...] = jnp.zeros_like(buf)
    barrier = pltpu.get_barrier_semaphore()
    for step in range(1, n):
        peer = lax.rem(me + step, n)
        pl.semaphore_signal(barrier, inc=1, device_id=(peer,) + here, device_id_type=MESH)
    pl.semaphore_wait(barrier, n - 1)

    def copy_to(peer):
        return pltpu.make_async_remote_copy(
            src_ref=x_ref,
            dst_ref=buf.at[me],
            send_sem=send_sem.at[peer],
            recv_sem=recv_sem.at[me],
            device_id=(peer,) + here,
            device_id_type=MESH,
        )

    def copy_from(source):
        return pltpu.make_async_remote_copy(
            src_ref=x_ref,
            dst_ref=buf.at[source],
            send_sem=send_sem.at[source],
            recv_sem=recv_sem.at[source],
            device_id=(source,) + here,
            device_id_type=MESH,
        )

    for step in range(1, n):
        @pl.when(me + step < n)
        def _():
            copy_to(me + step).start()

    for step in range(1, n):
        @pl.when(me - step >= 0)
        def _():
            copy_from(me - step).wait_recv()

    for step in range(1, n):
        @pl.when(me + step < n)
        def _():
            copy_to(me + step).wait_send()

    y_ref[...] = buf[...]


def gather_seq(x, slabs, collective_id):
    shape = (slabs,) + x.shape
    return pl.pallas_call(
        gather_kernel,
        out_shape=jax.ShapeDtypeStruct(shape, x.dtype),
        in_specs=[pl.BlockSpec(memory_space=pltpu.VMEM)],
        out_specs=pl.BlockSpec(memory_space=pltpu.VMEM),
        scratch_shapes=[
            pltpu.VMEM(shape, x.dtype),
            pltpu.SemaphoreType.DMA((slabs,)),
            pltpu.SemaphoreType.DMA((slabs,)),
        ],
        compiler_params=pltpu.CompilerParams(collective_id=collective_id, has_side_effects=True),
    )(x)


def scan_kernel(width, x_ref, y_ref, row_buf, col_buf, total, row_send, row_recv, col_send, col_recv):
    n = lax.axis_size("seq")
    height = n // width
    me = lax.axis_index("seq")
    row, col = me // width, me % width
    here = (lax.axis_index("z"), lax.axis_index("core"))
    row_buf[...] = jnp.zeros_like(row_buf)
    col_buf[...] = jnp.zeros_like(col_buf)
    barrier = pltpu.get_barrier_semaphore()
    for step in range(1, width):
        peer = row * width + lax.rem(col + step, width)
        pl.semaphore_signal(barrier, inc=1, device_id=(peer,) + here, device_id_type=MESH)
    for step in range(1, height):
        peer = lax.rem(row + step, height) * width + col
        pl.semaphore_signal(barrier, inc=1, device_id=(peer,) + here, device_id_type=MESH)
    pl.semaphore_wait(barrier, width + height - 2)

    def row_copy(c, slot):
        return pltpu.make_async_remote_copy(
            src_ref=x_ref,
            dst_ref=row_buf.at[slot],
            send_sem=row_send.at[c],
            recv_sem=row_recv.at[slot],
            device_id=(row * width + c,) + here,
            device_id_type=MESH,
        )

    sends = []
    for step in range(1, width):
        c = lax.rem(col + step, width)
        copy = row_copy(c, col)
        copy.start()
        sends.append(copy)
    for step in range(1, width):
        c = lax.rem(col + width - step, width)
        row_copy(c, c).wait_recv()
    mine = x_ref[...].astype(jnp.float32)
    row_total = mine
    row_prefix = jnp.zeros_like(mine)
    for c in range(width):
        part = jnp.where(c == col, 0.0, row_buf[c].astype(jnp.float32))
        row_total = row_total + part
        row_prefix = row_prefix + jnp.where(c < col, part, 0.0)
    total[...] = row_total

    def col_copy(r, slot):
        return pltpu.make_async_remote_copy(
            src_ref=total,
            dst_ref=col_buf.at[slot],
            send_sem=col_send.at[r],
            recv_sem=col_recv.at[slot],
            device_id=(r * width + col,) + here,
            device_id_type=MESH,
        )

    for step in range(1, height):
        @pl.when(row + step < height)
        def _():
            col_copy(row + step, row).start()

    for step in range(1, height):
        @pl.when(row - step >= 0)
        def _():
            col_copy(row - step, row - step).wait_recv()

    for step in range(1, height):
        @pl.when(row + step < height)
        def _():
            col_copy(row + step, row).wait_send()

    for copy in sends:
        copy.wait_send()
    prefix = row_prefix
    for r in range(height):
        prefix = prefix + col_buf[r]
    y_ref[...] = prefix


def scan_seq(x, collective_id):
    n = lax.axis_size("seq")
    width = 1
    while (width + 1) * (width + 1) <= n:
        width += 1
    while n % width:
        width -= 1
    height = n // width
    return pl.pallas_call(
        functools.partial(scan_kernel, width),
        out_shape=jax.ShapeDtypeStruct(x.shape, jnp.float32),
        in_specs=[pl.BlockSpec(memory_space=pltpu.VMEM)],
        out_specs=pl.BlockSpec(memory_space=pltpu.VMEM),
        scratch_shapes=[
            pltpu.VMEM((width,) + x.shape, x.dtype),
            pltpu.VMEM((height,) + x.shape, jnp.float32),
            pltpu.VMEM(x.shape, jnp.float32),
            pltpu.SemaphoreType.DMA((width,)),
            pltpu.SemaphoreType.DMA((width,)),
            pltpu.SemaphoreType.DMA((height,)),
            pltpu.SemaphoreType.DMA((height,)),
        ],
        compiler_params=pltpu.CompilerParams(collective_id=collective_id, has_side_effects=True),
    )(x)


def swap_kernel(x_ref, y_ref, send_sem, recv_sem):
    here = (lax.axis_index("seq"), lax.axis_index("z"))
    other = lax.axis_size("core") - 1 - lax.axis_index("core")
    barrier = pltpu.get_barrier_semaphore()
    pl.semaphore_signal(barrier, inc=1, device_id=here + (other,), device_id_type=MESH)
    pl.semaphore_wait(barrier, 1)
    copy = pltpu.make_async_remote_copy(
        src_ref=x_ref,
        dst_ref=y_ref,
        send_sem=send_sem,
        recv_sem=recv_sem,
        device_id=here + (other,),
        device_id_type=MESH,
    )
    copy.start()
    copy.wait()


def swap_cores(x, collective_id):
    return pl.pallas_call(
        swap_kernel,
        out_shape=jax.ShapeDtypeStruct(x.shape, x.dtype),
        in_specs=[pl.BlockSpec(memory_space=pl.ANY)],
        out_specs=pl.BlockSpec(memory_space=pl.ANY),
        scratch_shapes=[pltpu.SemaphoreType.DMA(()), pltpu.SemaphoreType.DMA(())],
        compiler_params=pltpu.CompilerParams(collective_id=collective_id, has_side_effects=True),
    )(x)


def opening_kernel(x_ref, w_ref, y_ref, w_all, buf, send_sem, recv_sem, own_sem, w_send, w_recv, w_own):
    n = x_ref.shape[0]
    cores = lax.axis_size("core")
    ring = n // cores
    me = chan_index()
    slab = lax.axis_index("seq")
    z = lax.axis_index("z")
    core = lax.axis_index("core")
    barrier = pltpu.get_barrier_semaphore()
    for step in range(1, n):
        peer = lax.rem(me + step, n)
        pl.semaphore_signal(barrier, inc=1, device_id=chan_device(slab, peer), device_id_type=MESH)
    pl.semaphore_wait(barrier, n - 1)
    own = pltpu.make_async_copy(x_ref.at[me], buf.at[me], own_sem)
    own.start()
    sends = []
    for step in range(1, n):
        peer = lax.rem(me + step, n)
        copy = pltpu.make_async_remote_copy(
            src_ref=x_ref.at[peer],
            dst_ref=buf.at[me],
            send_sem=send_sem.at[peer],
            recv_sem=recv_sem.at[me],
            device_id=chan_device(slab, peer),
            device_id_type=MESH,
        )
        copy.start()
        sends.append(copy)
    w_local = pltpu.make_async_copy(w_ref, w_all.at[me], w_own)
    w_local.start()
    right = (slab, lax.rem(z + 1, ring), core)
    left = (slab, lax.rem(z + ring - 1, ring), core)
    partner = (slab, z, cores - 1 - core)

    pieces = W_PIECES
    depth = w_ref.shape[0] // pieces

    def slot(origin):
        return lax.rem(origin + ring, ring) * cores + core

    def held(h, j):
        return w_all.at[h, pl.ds(j * depth, depth)]

    def send(source, h, j, kind, target):
        copy = pltpu.make_async_remote_copy(
            src_ref=source,
            dst_ref=held(h, j),
            send_sem=w_send.at[h, kind, j],
            recv_sem=w_recv.at[h, j],
            device_id=target,
            device_id_type=MESH,
        )
        copy.start()
        sends.append(copy)

    def arrive(h, j, source):
        pltpu.make_async_remote_copy(
            src_ref=w_ref.at[pl.ds(j * depth, depth)],
            dst_ref=held(h, j),
            send_sem=w_send.at[h, 0, j],
            recv_sem=w_recv.at[h, j],
            device_id=source,
            device_id_type=MESH,
        ).wait_recv()

    half = ring // 2
    full = half - 1 if ring % 2 == 0 else half

    def goes_right(step):
        return range(pieces) if step <= full else range(pieces // 2) if step == half else range(0)

    def goes_left(step):
        return range(pieces) if step <= full else range(pieces // 2, pieces) if step == half else range(0)

    for j in range(pieces):
        mine = w_ref.at[pl.ds(j * depth, depth)]
        if j in goes_right(1):
            send(mine, me, j, 0, right)
        if j in goes_left(1):
            send(mine, me, j, 1, left)
        send(mine, me, j, 2, partner)
    for step in range(1, half + 1):
        for j in range(pieces):
            if j in goes_right(step):
                h = slot(z - step)
                arrive(h, j, left)
                if j in goes_right(step + 1):
                    send(held(h, j), h, j, 0, right)
                send(held(h, j), h, j, 2, partner)
            if j in goes_left(step):
                h = slot(z + step)
                arrive(h, j, right)
                if j in goes_left(step + 1):
                    send(held(h, j), h, j, 1, left)
                send(held(h, j), h, j, 2, partner)
    for origin in range(ring):
        for j in range(pieces):
            arrive(origin * cores + (cores - 1 - core), j, partner)
    for step in range(1, n):
        source = lax.rem(me + n - step, n)
        pltpu.make_async_remote_copy(
            src_ref=x_ref.at[source],
            dst_ref=buf.at[source],
            send_sem=send_sem.at[source],
            recv_sem=recv_sem.at[source],
            device_id=chan_device(slab, source),
            device_id_type=MESH,
        ).wait_recv()
    for copy in sends:
        copy.wait_send()
    own.wait()
    w_local.wait()
    y_ref[...] = buf[...]


def opening(x, w, collective_id):
    n = x.shape[0]
    return pl.pallas_call(
        opening_kernel,
        out_shape=(
            jax.ShapeDtypeStruct(x.shape, x.dtype),
            jax.ShapeDtypeStruct((n,) + w.shape, w.dtype),
        ),
        in_specs=[pl.BlockSpec(memory_space=pltpu.VMEM), pl.BlockSpec(memory_space=pl.ANY)],
        out_specs=(pl.BlockSpec(memory_space=pltpu.VMEM), pl.BlockSpec(memory_space=pl.ANY)),
        scratch_shapes=[
            pltpu.VMEM(x.shape, x.dtype),
            pltpu.SemaphoreType.DMA((n,)),
            pltpu.SemaphoreType.DMA((n,)),
            pltpu.SemaphoreType.DMA(()),
            pltpu.SemaphoreType.DMA((n, 3, W_PIECES)),
            pltpu.SemaphoreType.DMA((n, W_PIECES)),
            pltpu.SemaphoreType.DMA(()),
        ],
        compiler_params=pltpu.CompilerParams(collective_id=collective_id, has_side_effects=True),
    )(x, w)


def split_rows(x, groups, collective_id):
    rows, cols = x.shape
    got = exchange(x.reshape(groups, rows // groups, cols), collective_id)
    return got.transpose(1, 0, 2).reshape(rows // groups, groups * cols)


def split_cols(x, groups, collective_id):
    rows, _, cols = x.shape
    got = exchange(x.transpose(1, 0, 2), collective_id)
    return got.reshape(groups * rows, cols)


def closing_kernel(x_ref, w_ref, y_ref, got, rows, out, back, send_sem, recv_sem, own_sem):
    n = x_ref.shape[0]
    cols = out.shape[2]
    me = chan_index()
    slab = lax.axis_index("seq")
    barrier = pltpu.get_barrier_semaphore()
    for step in range(1, n):
        peer = lax.rem(me + step, n)
        pl.semaphore_signal(barrier, inc=1, device_id=chan_device(slab, peer), device_id_type=MESH)
    pl.semaphore_wait(barrier, n - 1)

    def remote(phase, src, dst, peer, sender):
        return pltpu.make_async_remote_copy(
            src_ref=src,
            dst_ref=dst,
            send_sem=send_sem.at[phase, peer],
            recv_sem=recv_sem.at[phase, sender],
            device_id=chan_device(slab, peer),
            device_id_type=MESH,
        )

    sends = []
    for phase, (source, landing) in enumerate(((x_ref, got), (out, back))):
        own = pltpu.make_async_copy(source.at[me], landing.at[me], own_sem.at[phase])
        if phase == 1:
            hidden_rows = rows[...]
            for step in range(n):
                c = lax.rem(me + step, n)
                block = w_ref[:, pl.ds(pl.multiple_of(c * cols, cols), cols)]
                out[c] = jnp.dot(hidden_rows, block, preferred_element_type=jnp.float32).astype(out.dtype)
                if step == 0:
                    own.start()
                else:
                    copy = remote(phase, out.at[c], back.at[me], c, me)
                    copy.start()
                    sends.append(copy)
        else:
            own.start()
            for step in range(1, n):
                peer = lax.rem(me + step, n)
                copy = remote(phase, x_ref.at[peer], got.at[me], peer, me)
                copy.start()
                sends.append(copy)
        for step in range(1, n):
            source_dev = lax.rem(me + n - step, n)
            remote(phase, source.at[source_dev], landing.at[source_dev], source_dev, source_dev).wait_recv()
        own.wait()
        if phase == 0:
            width = got.shape[2]
            for g in range(n):
                rows[:, g * width : (g + 1) * width] = got[g]
    for copy in sends:
        copy.wait_send()
    y_ref[...] = back[...]


def closing(hidden_blocks, w_out, collective_id):
    n, chunk, width = hidden_blocks.shape
    cols = w_out.shape[1] // n
    block = (n, chunk, cols)
    return pl.pallas_call(
        closing_kernel,
        out_shape=jax.ShapeDtypeStruct(block, hidden_blocks.dtype),
        in_specs=[pl.BlockSpec(memory_space=pltpu.VMEM)] * 2,
        out_specs=pl.BlockSpec(memory_space=pltpu.VMEM),
        scratch_shapes=[
            pltpu.VMEM(hidden_blocks.shape, hidden_blocks.dtype),
            pltpu.VMEM((chunk, n * width), hidden_blocks.dtype),
            pltpu.VMEM(block, hidden_blocks.dtype),
            pltpu.VMEM(block, hidden_blocks.dtype),
            pltpu.SemaphoreType.DMA((2, n)),
            pltpu.SemaphoreType.DMA((2, n)),
            pltpu.SemaphoreType.DMA((2,)),
        ],
        compiler_params=pltpu.CompilerParams(
            collective_id=collective_id, has_side_effects=True, vmem_limit_bytes=48 * 1024 * 1024
        ),
    )(hidden_blocks, w_out)


def middle_kernel(rows_ref, w_ref, wq_ref, wk_ref, qk_out, v_out, qk_send, v_send, qk_got, v_got, q_all, k_all, send_sem, recv_sem, own_sem):
    n = w_ref.shape[0]
    me = chan_index()
    slab = lax.axis_index("seq")
    barrier = pltpu.get_barrier_semaphore()
    for step in range(1, n):
        peer = lax.rem(me + step, n)
        pl.semaphore_signal(barrier, inc=1, device_id=chan_device(slab, peer), device_id_type=MESH)
    pl.semaphore_wait(barrier, n - 1)
    pairs = ((qk_send, qk_got), (v_send, v_got))

    def remote(kind, peer, sender, slot):
        source, landing = pairs[kind]
        return pltpu.make_async_remote_copy(
            src_ref=source.at[slot],
            dst_ref=landing.at[sender],
            send_sem=send_sem.at[kind, peer],
            recv_sem=recv_sem.at[kind, sender],
            device_id=chan_device(slab, peer),
            device_id_type=MESH,
        )

    rows = rows_ref[...]
    pf = qk_send.shape[1] // 2
    q_all[...] = jnp.dot(rows, wq_ref[...], preferred_element_type=jnp.float32).T
    k_all[...] = jnp.dot(rows, wk_ref[...], preferred_element_type=jnp.float32).T
    owns = []
    sends = []
    for step in range(n):
        g = lax.rem(me + step, n)
        v_send[g] = jnp.dot(rows, w_ref[g], preferred_element_type=jnp.float32).astype(v_send.dtype)
        head = pl.ds(pl.multiple_of(g * pf, pf), pf)
        qk_send[g, :pf, :] = q_all[head, :].astype(qk_send.dtype)
        qk_send[g, pf:, :] = k_all[head, :].astype(qk_send.dtype)
        for kind in range(2):
            source, landing = pairs[kind]
            if step == 0:
                own = pltpu.make_async_copy(source.at[me], landing.at[me], own_sem.at[kind])
                own.start()
                owns.append(own)
            else:
                copy = remote(kind, g, me, g)
                copy.start()
                sends.append(copy)
    for step in range(1, n):
        source_dev = lax.rem(me + n - step, n)
        for kind in range(2):
            remote(kind, source_dev, source_dev, source_dev).wait_recv()
    for own in owns:
        own.wait()
    for copy in sends:
        copy.wait_send()
    qk_out[...] = qk_got[...]
    v_out[...] = v_got[...]


def middle(rows, w_all, w_query, w_key, collective_id):
    n = w_all.shape[0]
    chunk = rows.shape[0]
    qk_shape = (n, 2 * w_query.shape[1] // n, chunk)
    v_shape = (n, chunk, w_all.shape[2])
    return pl.pallas_call(
        middle_kernel,
        out_shape=(
            jax.ShapeDtypeStruct(qk_shape, rows.dtype),
            jax.ShapeDtypeStruct(v_shape, rows.dtype),
        ),
        in_specs=[pl.BlockSpec(memory_space=pltpu.VMEM)] * 4,
        out_specs=(pl.BlockSpec(memory_space=pltpu.VMEM), pl.BlockSpec(memory_space=pltpu.VMEM)),
        scratch_shapes=[
            pltpu.VMEM(qk_shape, rows.dtype),
            pltpu.VMEM(v_shape, rows.dtype),
            pltpu.VMEM(qk_shape, rows.dtype),
            pltpu.VMEM(v_shape, rows.dtype),
            pltpu.VMEM((w_query.shape[1], chunk), jnp.float32),
            pltpu.VMEM((w_key.shape[1], chunk), jnp.float32),
            pltpu.SemaphoreType.DMA((2, n)),
            pltpu.SemaphoreType.DMA((2, n)),
            pltpu.SemaphoreType.DMA((2,)),
        ],
        compiler_params=pltpu.CompilerParams(
            collective_id=collective_id, has_side_effects=True, vmem_limit_bytes=48 * 1024 * 1024
        ),
    )(rows, w_all, w_query, w_key)


def attend(query_rows, key_rows, value_rows, gain_mine, my_slab):
    highest = lax.Precision.HIGHEST
    tok_rows, per_group, _ = value_rows.shape
    blocks = tok_rows // BLOCK
    query_blocks = query_rows.reshape(blocks, BLOCK, per_group, FEAT)
    key_blocks = key_rows.reshape(blocks, BLOCK, per_group, FEAT)
    value_blocks = value_rows.reshape(blocks, BLOCK, per_group, HEAD_DIM)
    value_f32 = value_blocks.astype(jnp.float32)
    key_linear, key_square = feature_parts(key_blocks.astype(jnp.float32))
    own_zero = jnp.sum(value_f32, axis=1)[:, :, None, :]
    own_one = jnp.einsum("bthf,bthe->bhfe", key_linear, value_f32, precision=highest)
    own_two = jnp.einsum("bthf,bthe->bhfe", key_square, value_f32, precision=highest)
    own = jnp.concatenate([own_zero, own_one, own_two], axis=2)
    slab_total = jnp.sum(own, axis=0)
    state_rows = slab_total.shape[0] * slab_total.shape[1]
    prefix = scan_seq(slab_total.astype(jnp.bfloat16).reshape(state_rows, HEAD_DIM), 7).reshape(slab_total.shape)
    earlier = jnp.concatenate([jnp.zeros_like(own[:1]), jnp.cumsum(own, axis=0)[:-1]], axis=0) + prefix[None]
    query_linear, query_square = feature_parts(query_blocks.astype(jnp.float32))
    inter = earlier[:, :, 0][:, None] + jnp.einsum(
        "bthf,bhfe->bthe", query_linear, earlier[:, :, 1 : 1 + FEAT], precision=highest
    )
    inter = inter + jnp.einsum(
        "bthf,bhfe->bthe", query_square, earlier[:, :, 1 + FEAT :], precision=highest
    )
    scores = jnp.einsum(
        "bthf,bshf->bhts", query_blocks, key_blocks, preferred_element_type=jnp.float32
    ) * FEAT ** (-0.5)
    kernel = 1.0 + scores + 0.5 * scores * scores
    causal = jnp.arange(BLOCK)[:, None] >= jnp.arange(BLOCK)[None, :]
    weights = jnp.where(causal, kernel, 0.0).astype(jnp.bfloat16)
    intra = jnp.einsum("bhts,bshe->bthe", weights, value_blocks, preferred_element_type=jnp.float32)
    numerator = (intra + inter).reshape(tok_rows, per_group, HEAD_DIM)
    mean_square = jnp.mean(numerator * numerator, axis=-1, keepdims=True)
    hidden = (numerator * lax.rsqrt(mean_square + 1e-05) * gain_mine).astype(jnp.bfloat16)
    return hidden.reshape(tok_rows, per_group * HEAD_DIM)


def per_device(tokens, w_query, w_key, w_value, w_out, gain):
    groups = lax.axis_size(CHAN)
    per_group = HEADS // groups
    my_group = chan_index()
    my_slab = lax.axis_index("seq")
    tok_rows_total, tok_cols = tokens.shape
    got, value_all = opening(tokens.reshape(groups, tok_rows_total // groups, tok_cols), w_value, 1)
    rows = got.transpose(1, 0, 2).reshape(tok_rows_total // groups, groups * tok_cols)
    chunk = rows.shape[0]
    pf = per_group * FEAT
    d_model = w_query.shape[0]
    qk_got, value_got = middle(rows, value_all, w_query, w_key, 2)
    tok_rows = groups * chunk
    qk_rows = qk_got.transpose(0, 2, 1).reshape(tok_rows, 2 * pf)
    query_rows = qk_rows[:, :pf].reshape(tok_rows, per_group, FEAT)
    key_rows = qk_rows[:, pf:].reshape(tok_rows, per_group, FEAT)
    value_rows = value_got.reshape(tok_rows, per_group, HEAD_DIM)
    value_cols = per_group * HEAD_DIM
    gain_mine = lax.dynamic_slice_in_dim(gain, my_group * value_cols, value_cols, 0).reshape(
        per_group, HEAD_DIM
    )
    hidden = attend(query_rows, key_rows, value_rows, gain_mine, my_slab)
    out_cols = w_out.shape[1] // groups
    mixed_blocks = closing(hidden.reshape(groups, chunk, per_group * HEAD_DIM), w_out, 3)
    return mixed_blocks.reshape(tok_rows, out_cols)

def solution(mesh):
    seq, chan = mesh.devices.shape
    cores = 2 if chan % 2 == 0 else 1
    split = jax.sharding.Mesh(mesh.devices.reshape(seq, chan // cores, cores), ("seq", "z", "core"))
    return jax.shard_map(
        per_device,
        mesh=split,
        in_specs=(P("seq", CHAN), P(), P(), P(None, CHAN), P(), P()),
        out_specs=P("seq", CHAN),
        check_vma=False,
    )
```

```python
import functools

import jax
import jax.numpy as jnp
from jax import lax
from jax.experimental import pallas as pl
from jax.experimental.pallas import tpu as pltpu
from jax.sharding import PartitionSpec as P

MESH = pl.DeviceIdType.MESH
CHAN = ("z", "core")
W_PIECES = 8


def chan_index():
    return lax.axis_index("z") * lax.axis_size("core") + lax.axis_index("core")


def chan_device(slab, peer):
    cores = lax.axis_size("core")
    return (slab, peer // cores, peer % cores)

HEADS = 16
FEAT = 16
HEAD_DIM = 128
BLOCK = 896


def feature_parts(rows):
    linear = rows * FEAT ** (-0.25)
    square = (rows[..., :, None] * rows[..., None, :]).reshape(rows.shape[:-1] + (FEAT * FEAT,)) * (
        2.0 * FEAT
    ) ** (-0.5)
    return (linear, square)


def exchange_kernel(count, *refs):
    xs, ys, bufs = refs[:count], refs[count : 2 * count], refs[2 * count : 3 * count]
    send_sem, recv_sem, own_sem = refs[3 * count :]
    n = xs[0].shape[0]
    me = chan_index()
    slab = lax.axis_index("seq")
    barrier = pltpu.get_barrier_semaphore()
    for step in range(1, n):
        peer = lax.rem(me + step, n)
        pl.semaphore_signal(barrier, inc=1, device_id=chan_device(slab, peer), device_id_type=MESH)
    pl.semaphore_wait(barrier, n - 1)
    owns = []
    sends = []
    for a in range(count):
        own = pltpu.make_async_copy(xs[a].at[me], bufs[a].at[me], own_sem.at[a])
        own.start()
        owns.append(own)
    for step in range(1, n):
        peer = lax.rem(me + step, n)
        for a in range(count):
            copy = pltpu.make_async_remote_copy(
                src_ref=xs[a].at[peer],
                dst_ref=bufs[a].at[me],
                send_sem=send_sem.at[a, peer],
                recv_sem=recv_sem.at[a, me],
                device_id=chan_device(slab, peer),
                device_id_type=MESH,
            )
            copy.start()
            sends.append(copy)
    for step in range(1, n):
        source = lax.rem(me + n - step, n)
        for a in range(count):
            pltpu.make_async_remote_copy(
                src_ref=xs[a].at[source],
                dst_ref=bufs[a].at[source],
                send_sem=send_sem.at[a, source],
                recv_sem=recv_sem.at[a, source],
                device_id=chan_device(slab, source),
                device_id_type=MESH,
            ).wait_recv()
    for copy in sends:
        copy.wait_send()
    for a in range(count):
        owns[a].wait()
        ys[a][...] = bufs[a][...]


def exchange_many(xs, collective_id):
    count = len(xs)
    n = xs[0].shape[0]
    return pl.pallas_call(
        functools.partial(exchange_kernel, count),
        out_shape=tuple(jax.ShapeDtypeStruct(x.shape, x.dtype) for x in xs),
        in_specs=[pl.BlockSpec(memory_space=pltpu.VMEM)] * count,
        out_specs=tuple(pl.BlockSpec(memory_space=pltpu.VMEM) for _ in xs),
        scratch_shapes=[pltpu.VMEM(x.shape, x.dtype) for x in xs]
        + [
            pltpu.SemaphoreType.DMA((count, n)),
            pltpu.SemaphoreType.DMA((count, n)),
            pltpu.SemaphoreType.DMA((count,)),
        ],
        compiler_params=pltpu.CompilerParams(collective_id=collective_id, has_side_effects=True),
    )(*xs)


def exchange(x, collective_id):
    return exchange_many((x,), collective_id)[0]


def gather_kernel(x_ref, y_ref, buf, send_sem, recv_sem):
    n = buf.shape[0]
    me = lax.axis_index("seq")
    here = (lax.axis_index("z"), lax.axis_index("core"))
    buf[...] = jnp.zeros_like(buf)
    barrier = pltpu.get_barrier_semaphore()
    for step in range(1, n):
        peer = lax.rem(me + step, n)
        pl.semaphore_signal(barrier, inc=1, device_id=(peer,) + here, device_id_type=MESH)
    pl.semaphore_wait(barrier, n - 1)

    def copy_to(peer):
        return pltpu.make_async_remote_copy(
            src_ref=x_ref,
            dst_ref=buf.at[me],
            send_sem=send_sem.at[peer],
            recv_sem=recv_sem.at[me],
            device_id=(peer,) + here,
            device_id_type=MESH,
        )

    def copy_from(source):
        return pltpu.make_async_remote_copy(
            src_ref=x_ref,
            dst_ref=buf.at[source],
            send_sem=send_sem.at[source],
            recv_sem=recv_sem.at[source],
            device_id=(source,) + here,
            device_id_type=MESH,
        )

    for step in range(1, n):
        @pl.when(me + step < n)
        def _():
            copy_to(me + step).start()

    for step in range(1, n):
        @pl.when(me - step >= 0)
        def _():
            copy_from(me - step).wait_recv()

    for step in range(1, n):
        @pl.when(me + step < n)
        def _():
            copy_to(me + step).wait_send()

    y_ref[...] = buf[...]


def gather_seq(x, slabs, collective_id):
    shape = (slabs,) + x.shape
    return pl.pallas_call(
        gather_kernel,
        out_shape=jax.ShapeDtypeStruct(shape, x.dtype),
        in_specs=[pl.BlockSpec(memory_space=pltpu.VMEM)],
        out_specs=pl.BlockSpec(memory_space=pltpu.VMEM),
        scratch_shapes=[
            pltpu.VMEM(shape, x.dtype),
            pltpu.SemaphoreType.DMA((slabs,)),
            pltpu.SemaphoreType.DMA((slabs,)),
        ],
        compiler_params=pltpu.CompilerParams(collective_id=collective_id, has_side_effects=True),
    )(x)


def scan_kernel(width, x_ref, y_ref, row_buf, col_buf, total, row_send, row_recv, col_send, col_recv):
    n = lax.axis_size("seq")
    height = n // width
    me = lax.axis_index("seq")
    row, col = me // width, me % width
    here = (lax.axis_index("z"), lax.axis_index("core"))
    row_buf[...] = jnp.zeros_like(row_buf)
    col_buf[...] = jnp.zeros_like(col_buf)
    barrier = pltpu.get_barrier_semaphore()
    for step in range(1, width):
        peer = row * width + lax.rem(col + step, width)
        pl.semaphore_signal(barrier, inc=1, device_id=(peer,) + here, device_id_type=MESH)
    for step in range(1, height):
        peer = lax.rem(row + step, height) * width + col
        pl.semaphore_signal(barrier, inc=1, device_id=(peer,) + here, device_id_type=MESH)
    pl.semaphore_wait(barrier, width + height - 2)

    def row_copy(c, slot):
        return pltpu.make_async_remote_copy(
            src_ref=x_ref,
            dst_ref=row_buf.at[slot],
            send_sem=row_send.at[c],
            recv_sem=row_recv.at[slot],
            device_id=(row * width + c,) + here,
            device_id_type=MESH,
        )

    sends = []
    for step in range(1, width):
        c = lax.rem(col + step, width)
        copy = row_copy(c, col)
        copy.start()
        sends.append(copy)
    for step in range(1, width):
        c = lax.rem(col + width - step, width)
        row_copy(c, c).wait_recv()
    mine = x_ref[...].astype(jnp.float32)
    row_total = mine
    row_prefix = jnp.zeros_like(mine)
    for c in range(width):
        part = jnp.where(c == col, 0.0, row_buf[c].astype(jnp.float32))
        row_total = row_total + part
        row_prefix = row_prefix + jnp.where(c < col, part, 0.0)
    total[...] = row_total

    def col_copy(r, slot):
        return pltpu.make_async_remote_copy(
            src_ref=total,
            dst_ref=col_buf.at[slot],
            send_sem=col_send.at[r],
            recv_sem=col_recv.at[slot],
            device_id=(r * width + col,) + here,
            device_id_type=MESH,
        )

    for step in range(1, height):
        @pl.when(row + step < height)
        def _():
            col_copy(row + step, row).start()

    for step in range(1, height):
        @pl.when(row - step >= 0)
        def _():
            col_copy(row - step, row - step).wait_recv()

    for step in range(1, height):
        @pl.when(row + step < height)
        def _():
            col_copy(row + step, row).wait_send()

    for copy in sends:
        copy.wait_send()
    prefix = row_prefix
    for r in range(height):
        prefix = prefix + col_buf[r]
    y_ref[...] = prefix


def scan_seq(x, collective_id):
    n = lax.axis_size("seq")
    width = 1
    while (width + 1) * (width + 1) <= n:
        width += 1
    while n % width:
        width -= 1
    height = n // width
    return pl.pallas_call(
        functools.partial(scan_kernel, width),
        out_shape=jax.ShapeDtypeStruct(x.shape, jnp.float32),
        in_specs=[pl.BlockSpec(memory_space=pltpu.VMEM)],
        out_specs=pl.BlockSpec(memory_space=pltpu.VMEM),
        scratch_shapes=[
            pltpu.VMEM((width,) + x.shape, x.dtype),
            pltpu.VMEM((height,) + x.shape, jnp.float32),
            pltpu.VMEM(x.shape, jnp.float32),
            pltpu.SemaphoreType.DMA((width,)),
            pltpu.SemaphoreType.DMA((width,)),
            pltpu.SemaphoreType.DMA((height,)),
            pltpu.SemaphoreType.DMA((height,)),
        ],
        compiler_params=pltpu.CompilerParams(collective_id=collective_id, has_side_effects=True),
    )(x)


def swap_kernel(x_ref, y_ref, send_sem, recv_sem):
    here = (lax.axis_index("seq"), lax.axis_index("z"))
    other = lax.axis_size("core") - 1 - lax.axis_index("core")
    barrier = pltpu.get_barrier_semaphore()
    pl.semaphore_signal(barrier, inc=1, device_id=here + (other,), device_id_type=MESH)
    pl.semaphore_wait(barrier, 1)
    copy = pltpu.make_async_remote_copy(
        src_ref=x_ref,
        dst_ref=y_ref,
        send_sem=send_sem,
        recv_sem=recv_sem,
        device_id=here + (other,),
        device_id_type=MESH,
    )
    copy.start()
    copy.wait()


def swap_cores(x, collective_id):
    return pl.pallas_call(
        swap_kernel,
        out_shape=jax.ShapeDtypeStruct(x.shape, x.dtype),
        in_specs=[pl.BlockSpec(memory_space=pl.ANY)],
        out_specs=pl.BlockSpec(memory_space=pl.ANY),
        scratch_shapes=[pltpu.SemaphoreType.DMA(()), pltpu.SemaphoreType.DMA(())],
        compiler_params=pltpu.CompilerParams(collective_id=collective_id, has_side_effects=True),
    )(x)


def opening_kernel(x_ref, w_ref, y_ref, w_all, buf, send_sem, recv_sem, own_sem, w_send, w_recv, w_own):
    n = x_ref.shape[0]
    cores = lax.axis_size("core")
    ring = n // cores
    me = chan_index()
    slab = lax.axis_index("seq")
    z = lax.axis_index("z")
    core = lax.axis_index("core")
    barrier = pltpu.get_barrier_semaphore()
    for step in range(1, n):
        peer = lax.rem(me + step, n)
        pl.semaphore_signal(barrier, inc=1, device_id=chan_device(slab, peer), device_id_type=MESH)
    pl.semaphore_wait(barrier, n - 1)
    own = pltpu.make_async_copy(x_ref.at[me], buf.at[me], own_sem)
    own.start()
    sends = []
    for step in range(1, n):
        peer = lax.rem(me + step, n)
        copy = pltpu.make_async_remote_copy(
            src_ref=x_ref.at[peer],
            dst_ref=buf.at[me],
            send_sem=send_sem.at[peer],
            recv_sem=recv_sem.at[me],
            device_id=chan_device(slab, peer),
            device_id_type=MESH,
        )
        copy.start()
        sends.append(copy)
    w_local = pltpu.make_async_copy(w_ref, w_all.at[me], w_own)
    w_local.start()
    right = (slab, lax.rem(z + 1, ring), core)
    left = (slab, lax.rem(z + ring - 1, ring), core)
    partner = (slab, z, cores - 1 - core)

    pieces = W_PIECES
    depth = w_ref.shape[0] // pieces

    def slot(origin):
        return lax.rem(origin + ring, ring) * cores + core

    def held(h, j):
        return w_all.at[h, pl.ds(j * depth, depth)]

    def send(source, h, j, kind, target):
        copy = pltpu.make_async_remote_copy(
            src_ref=source,
            dst_ref=held(h, j),
            send_sem=w_send.at[h, kind, j],
            recv_sem=w_recv.at[h, j],
            device_id=target,
            device_id_type=MESH,
        )
        copy.start()
        sends.append(copy)

    def arrive(h, j, source):
        pltpu.make_async_remote_copy(
            src_ref=w_ref.at[pl.ds(j * depth, depth)],
            dst_ref=held(h, j),
            send_sem=w_send.at[h, 0, j],
            recv_sem=w_recv.at[h, j],
            device_id=source,
            device_id_type=MESH,
        ).wait_recv()

    half = ring // 2
    full = half - 1 if ring % 2 == 0 else half

    def goes_right(step):
        return range(pieces) if step <= full else range(pieces // 2) if step == half else range(0)

    def goes_left(step):
        return range(pieces) if step <= full else range(pieces // 2, pieces) if step == half else range(0)

    for j in range(pieces):
        mine = w_ref.at[pl.ds(j * depth, depth)]
        if j in goes_right(1):
            send(mine, me, j, 0, right)
        if j in goes_left(1):
            send(mine, me, j, 1, left)
        send(mine, me, j, 2, partner)
    for step in range(1, half + 1):
        for j in range(pieces):
            if j in goes_right(step):
                h = slot(z - step)
                arrive(h, j, left)
                if j in goes_right(step + 1):
                    send(held(h, j), h, j, 0, right)
                send(held(h, j), h, j, 2, partner)
            if j in goes_left(step):
                h = slot(z + step)
                arrive(h, j, right)
                if j in goes_left(step + 1):
                    send(held(h, j), h, j, 1, left)
                send(held(h, j), h, j, 2, partner)
    for origin in range(ring):
        for j in range(pieces):
            arrive(origin * cores + (cores - 1 - core), j, partner)
    for step in range(1, n):
        source = lax.rem(me + n - step, n)
        pltpu.make_async_remote_copy(
            src_ref=x_ref.at[source],
            dst_ref=buf.at[source],
            send_sem=send_sem.at[source],
            recv_sem=recv_sem.at[source],
            device_id=chan_device(slab, source),
            device_id_type=MESH,
        ).wait_recv()
    for copy in sends:
        copy.wait_send()
    own.wait()
    w_local.wait()
    width = buf.shape[2]
    for g in range(n):
        y_ref[:, g * width : (g + 1) * width] = buf[g]


def opening(x, w, collective_id):
    n = x.shape[0]
    return pl.pallas_call(
        opening_kernel,
        out_shape=(
            jax.ShapeDtypeStruct((x.shape[1], n * x.shape[2]), x.dtype),
            jax.ShapeDtypeStruct((n,) + w.shape, w.dtype),
        ),
        in_specs=[pl.BlockSpec(memory_space=pltpu.VMEM), pl.BlockSpec(memory_space=pl.ANY)],
        out_specs=(pl.BlockSpec(memory_space=pltpu.VMEM), pl.BlockSpec(memory_space=pl.ANY)),
        scratch_shapes=[
            pltpu.VMEM(x.shape, x.dtype),
            pltpu.SemaphoreType.DMA((n,)),
            pltpu.SemaphoreType.DMA((n,)),
            pltpu.SemaphoreType.DMA(()),
            pltpu.SemaphoreType.DMA((n, 3, W_PIECES)),
            pltpu.SemaphoreType.DMA((n, W_PIECES)),
            pltpu.SemaphoreType.DMA(()),
        ],
        compiler_params=pltpu.CompilerParams(collective_id=collective_id, has_side_effects=True),
    )(x, w)


def split_rows(x, groups, collective_id):
    rows, cols = x.shape
    got = exchange(x.reshape(groups, rows // groups, cols), collective_id)
    return got.transpose(1, 0, 2).reshape(rows // groups, groups * cols)


def split_cols(x, groups, collective_id):
    rows, _, cols = x.shape
    got = exchange(x.transpose(1, 0, 2), collective_id)
    return got.reshape(groups * rows, cols)


def closing_kernel(x_ref, w_ref, y_ref, got, rows, out, back, send_sem, recv_sem, own_sem):
    n = x_ref.shape[0]
    cols = out.shape[2]
    me = chan_index()
    slab = lax.axis_index("seq")
    barrier = pltpu.get_barrier_semaphore()
    for step in range(1, n):
        peer = lax.rem(me + step, n)
        pl.semaphore_signal(barrier, inc=1, device_id=chan_device(slab, peer), device_id_type=MESH)
    pl.semaphore_wait(barrier, n - 1)

    def remote(phase, src, dst, peer, sender):
        return pltpu.make_async_remote_copy(
            src_ref=src,
            dst_ref=dst,
            send_sem=send_sem.at[phase, peer],
            recv_sem=recv_sem.at[phase, sender],
            device_id=chan_device(slab, peer),
            device_id_type=MESH,
        )

    sends = []
    for phase, (source, landing) in enumerate(((x_ref, got), (out, back))):
        own = pltpu.make_async_copy(source.at[me], landing.at[me], own_sem.at[phase])
        if phase == 1:
            hidden_rows = rows[...]
            for step in range(n):
                c = lax.rem(me + step, n)
                block = w_ref[:, pl.ds(pl.multiple_of(c * cols, cols), cols)]
                out[c] = jnp.dot(hidden_rows, block, preferred_element_type=jnp.float32).astype(out.dtype)
                if step == 0:
                    own.start()
                else:
                    copy = remote(phase, out.at[c], back.at[me], c, me)
                    copy.start()
                    sends.append(copy)
        else:
            own.start()
            for step in range(1, n):
                peer = lax.rem(me + step, n)
                copy = remote(phase, x_ref.at[peer], got.at[me], peer, me)
                copy.start()
                sends.append(copy)
        for step in range(1, n):
            source_dev = lax.rem(me + n - step, n)
            remote(phase, source.at[source_dev], landing.at[source_dev], source_dev, source_dev).wait_recv()
        own.wait()
        if phase == 0:
            width = got.shape[2]
            for g in range(n):
                rows[:, g * width : (g + 1) * width] = got[g]
    for copy in sends:
        copy.wait_send()
    y_ref[...] = back[...]


def closing(hidden_blocks, w_out, collective_id):
    n, chunk, width = hidden_blocks.shape
    cols = w_out.shape[1] // n
    block = (n, chunk, cols)
    return pl.pallas_call(
        closing_kernel,
        out_shape=jax.ShapeDtypeStruct(block, hidden_blocks.dtype),
        in_specs=[pl.BlockSpec(memory_space=pltpu.VMEM)] * 2,
        out_specs=pl.BlockSpec(memory_space=pltpu.VMEM),
        scratch_shapes=[
            pltpu.VMEM(hidden_blocks.shape, hidden_blocks.dtype),
            pltpu.VMEM((chunk, n * width), hidden_blocks.dtype),
            pltpu.VMEM(block, hidden_blocks.dtype),
            pltpu.VMEM(block, hidden_blocks.dtype),
            pltpu.SemaphoreType.DMA((2, n)),
            pltpu.SemaphoreType.DMA((2, n)),
            pltpu.SemaphoreType.DMA((2,)),
        ],
        compiler_params=pltpu.CompilerParams(
            collective_id=collective_id, has_side_effects=True, vmem_limit_bytes=48 * 1024 * 1024
        ),
    )(hidden_blocks, w_out)


def middle_kernel(rows_ref, w_ref, wq_ref, wk_ref, qk_out, v_out, qk_send, v_send, qk_got, v_got, q_all, k_all, send_sem, recv_sem, own_sem):
    n = w_ref.shape[0]
    me = chan_index()
    slab = lax.axis_index("seq")
    barrier = pltpu.get_barrier_semaphore()
    for step in range(1, n):
        peer = lax.rem(me + step, n)
        pl.semaphore_signal(barrier, inc=1, device_id=chan_device(slab, peer), device_id_type=MESH)
    pl.semaphore_wait(barrier, n - 1)
    pairs = ((qk_send, qk_got), (v_send, v_got))

    def remote(kind, peer, sender, slot):
        source, landing = pairs[kind]
        return pltpu.make_async_remote_copy(
            src_ref=source.at[slot],
            dst_ref=landing.at[sender],
            send_sem=send_sem.at[kind, peer],
            recv_sem=recv_sem.at[kind, sender],
            device_id=chan_device(slab, peer),
            device_id_type=MESH,
        )

    rows = rows_ref[...]
    pf = qk_send.shape[1] // 2
    q_all[...] = jnp.dot(rows, wq_ref[...], preferred_element_type=jnp.float32).T
    k_all[...] = jnp.dot(rows, wk_ref[...], preferred_element_type=jnp.float32).T
    owns = []
    sends = []
    for step in range(n):
        g = lax.rem(me + step, n)
        v_send[g] = jnp.dot(rows, w_ref[g], preferred_element_type=jnp.float32).astype(v_send.dtype)
        head = pl.ds(pl.multiple_of(g * pf, pf), pf)
        qk_send[g, :pf, :] = q_all[head, :].astype(qk_send.dtype)
        qk_send[g, pf:, :] = k_all[head, :].astype(qk_send.dtype)
        for kind in range(2):
            source, landing = pairs[kind]
            if step == 0:
                own = pltpu.make_async_copy(source.at[me], landing.at[me], own_sem.at[kind])
                own.start()
                owns.append(own)
            else:
                copy = remote(kind, g, me, g)
                copy.start()
                sends.append(copy)
    for step in range(1, n):
        source_dev = lax.rem(me + n - step, n)
        for kind in range(2):
            remote(kind, source_dev, source_dev, source_dev).wait_recv()
    for own in owns:
        own.wait()
    for copy in sends:
        copy.wait_send()
    qk_out[...] = qk_got[...]
    v_out[...] = v_got[...]


def middle(rows, w_all, w_query, w_key, collective_id):
    n = w_all.shape[0]
    chunk = rows.shape[0]
    qk_shape = (n, 2 * w_query.shape[1] // n, chunk)
    v_shape = (n, chunk, w_all.shape[2])
    return pl.pallas_call(
        middle_kernel,
        out_shape=(
            jax.ShapeDtypeStruct(qk_shape, rows.dtype),
            jax.ShapeDtypeStruct(v_shape, rows.dtype),
        ),
        in_specs=[pl.BlockSpec(memory_space=pltpu.VMEM)] * 4,
        out_specs=(pl.BlockSpec(memory_space=pltpu.VMEM), pl.BlockSpec(memory_space=pltpu.VMEM)),
        scratch_shapes=[
            pltpu.VMEM(qk_shape, rows.dtype),
            pltpu.VMEM(v_shape, rows.dtype),
            pltpu.VMEM(qk_shape, rows.dtype),
            pltpu.VMEM(v_shape, rows.dtype),
            pltpu.VMEM((w_query.shape[1], chunk), jnp.float32),
            pltpu.VMEM((w_key.shape[1], chunk), jnp.float32),
            pltpu.SemaphoreType.DMA((2, n)),
            pltpu.SemaphoreType.DMA((2, n)),
            pltpu.SemaphoreType.DMA((2,)),
        ],
        compiler_params=pltpu.CompilerParams(
            collective_id=collective_id, has_side_effects=True, vmem_limit_bytes=48 * 1024 * 1024
        ),
    )(rows, w_all, w_query, w_key)


def attend(query_rows, key_rows, value_rows, gain_mine, my_slab):
    highest = lax.Precision.HIGHEST
    tok_rows, per_group, _ = value_rows.shape
    blocks = tok_rows // BLOCK
    query_blocks = query_rows.reshape(blocks, BLOCK, per_group, FEAT)
    key_blocks = key_rows.reshape(blocks, BLOCK, per_group, FEAT)
    value_blocks = value_rows.reshape(blocks, BLOCK, per_group, HEAD_DIM)
    value_f32 = value_blocks.astype(jnp.float32)
    key_linear, key_square = feature_parts(key_blocks.astype(jnp.float32))
    own_zero = jnp.sum(value_f32, axis=1)[:, :, None, :]
    own_one = jnp.einsum("bthf,bthe->bhfe", key_linear, value_f32, precision=highest)
    own_two = jnp.einsum("bthf,bthe->bhfe", key_square, value_f32, precision=highest)
    own = jnp.concatenate([own_zero, own_one, own_two], axis=2)
    slab_total = jnp.sum(own, axis=0)
    state_rows = slab_total.shape[0] * slab_total.shape[1]
    prefix = scan_seq(slab_total.astype(jnp.bfloat16).reshape(state_rows, HEAD_DIM), 7).reshape(slab_total.shape)
    earlier = jnp.concatenate([jnp.zeros_like(own[:1]), jnp.cumsum(own, axis=0)[:-1]], axis=0) + prefix[None]
    query_linear, query_square = feature_parts(query_blocks.astype(jnp.float32))
    inter = earlier[:, :, 0][:, None] + jnp.einsum(
        "bthf,bhfe->bthe", query_linear, earlier[:, :, 1 : 1 + FEAT], precision=highest
    )
    inter = inter + jnp.einsum(
        "bthf,bhfe->bthe", query_square, earlier[:, :, 1 + FEAT :], precision=highest
    )
    scores = jnp.einsum(
        "bthf,bshf->bhts", query_blocks, key_blocks, preferred_element_type=jnp.float32
    ) * FEAT ** (-0.5)
    kernel = 1.0 + scores + 0.5 * scores * scores
    causal = jnp.arange(BLOCK)[:, None] >= jnp.arange(BLOCK)[None, :]
    weights = jnp.where(causal, kernel, 0.0).astype(jnp.bfloat16)
    intra = jnp.einsum("bhts,bshe->bthe", weights, value_blocks, preferred_element_type=jnp.float32)
    numerator = (intra + inter).reshape(tok_rows, per_group, HEAD_DIM)
    mean_square = jnp.mean(numerator * numerator, axis=-1, keepdims=True)
    hidden = (numerator * lax.rsqrt(mean_square + 1e-05) * gain_mine).astype(jnp.bfloat16)
    return hidden.reshape(tok_rows, per_group * HEAD_DIM)


def per_device(tokens, w_query, w_key, w_value, w_out, gain):
    groups = lax.axis_size(CHAN)
    per_group = HEADS // groups
    my_group = chan_index()
    my_slab = lax.axis_index("seq")
    tok_rows_total, tok_cols = tokens.shape
    rows, value_all = opening(tokens.reshape(groups, tok_rows_total // groups, tok_cols), w_value, 1)
    chunk = rows.shape[0]
    pf = per_group * FEAT
    d_model = w_query.shape[0]
    qk_got, value_got = middle(rows, value_all, w_query, w_key, 2)
    tok_rows = groups * chunk
    qk_rows = qk_got.transpose(0, 2, 1).reshape(tok_rows, 2 * pf)
    query_rows = qk_rows[:, :pf].reshape(tok_rows, per_group, FEAT)
    key_rows = qk_rows[:, pf:].reshape(tok_rows, per_group, FEAT)
    value_rows = value_got.reshape(tok_rows, per_group, HEAD_DIM)
    value_cols = per_group * HEAD_DIM
    gain_mine = lax.dynamic_slice_in_dim(gain, my_group * value_cols, value_cols, 0).reshape(
        per_group, HEAD_DIM
    )
    hidden = attend(query_rows, key_rows, value_rows, gain_mine, my_slab)
    out_cols = w_out.shape[1] // groups
    mixed_blocks = closing(hidden.reshape(groups, chunk, per_group * HEAD_DIM), w_out, 3)
    return mixed_blocks.reshape(tok_rows, out_cols)

def solution(mesh):
    seq, chan = mesh.devices.shape
    cores = 2 if chan % 2 == 0 else 1
    split = jax.sharding.Mesh(mesh.devices.reshape(seq, chan // cores, cores), ("seq", "z", "core"))
    return jax.shard_map(
        per_device,
        mesh=split,
        in_specs=(P("seq", CHAN), P(), P(), P(None, CHAN), P(), P()),
        out_specs=P("seq", CHAN),
        check_vma=False,
    )
```

```python
import functools

import jax
import jax.numpy as jnp
from jax import lax
from jax.experimental import pallas as pl
from jax.experimental.pallas import tpu as pltpu
from jax.sharding import PartitionSpec as P

MESH = pl.DeviceIdType.MESH
CHAN = ("z", "core")
W_PIECES = 4


def chan_index():
    return lax.axis_index("z") * lax.axis_size("core") + lax.axis_index("core")


def chan_device(slab, peer):
    cores = lax.axis_size("core")
    return (slab, peer // cores, peer % cores)

HEADS = 16
FEAT = 16
HEAD_DIM = 128
BLOCK = 896


def feature_parts(rows):
    linear = rows * FEAT ** (-0.25)
    square = (rows[..., :, None] * rows[..., None, :]).reshape(rows.shape[:-1] + (FEAT * FEAT,)) * (
        2.0 * FEAT
    ) ** (-0.5)
    return (linear, square)


def exchange_kernel(count, *refs):
    xs, ys, bufs = refs[:count], refs[count : 2 * count], refs[2 * count : 3 * count]
    send_sem, recv_sem, own_sem = refs[3 * count :]
    n = xs[0].shape[0]
    me = chan_index()
    slab = lax.axis_index("seq")
    barrier = pltpu.get_barrier_semaphore()
    for step in range(1, n):
        peer = lax.rem(me + step, n)
        pl.semaphore_signal(barrier, inc=1, device_id=chan_device(slab, peer), device_id_type=MESH)
    pl.semaphore_wait(barrier, n - 1)
    owns = []
    sends = []
    for a in range(count):
        own = pltpu.make_async_copy(xs[a].at[me], bufs[a].at[me], own_sem.at[a])
        own.start()
        owns.append(own)
    for step in range(1, n):
        peer = lax.rem(me + step, n)
        for a in range(count):
            copy = pltpu.make_async_remote_copy(
                src_ref=xs[a].at[peer],
                dst_ref=bufs[a].at[me],
                send_sem=send_sem.at[a, peer],
                recv_sem=recv_sem.at[a, me],
                device_id=chan_device(slab, peer),
                device_id_type=MESH,
            )
            copy.start()
            sends.append(copy)
    for step in range(1, n):
        source = lax.rem(me + n - step, n)
        for a in range(count):
            pltpu.make_async_remote_copy(
                src_ref=xs[a].at[source],
                dst_ref=bufs[a].at[source],
                send_sem=send_sem.at[a, source],
                recv_sem=recv_sem.at[a, source],
                device_id=chan_device(slab, source),
                device_id_type=MESH,
            ).wait_recv()
    for copy in sends:
        copy.wait_send()
    for a in range(count):
        owns[a].wait()
        ys[a][...] = bufs[a][...]


def exchange_many(xs, collective_id):
    count = len(xs)
    n = xs[0].shape[0]
    return pl.pallas_call(
        functools.partial(exchange_kernel, count),
        out_shape=tuple(jax.ShapeDtypeStruct(x.shape, x.dtype) for x in xs),
        in_specs=[pl.BlockSpec(memory_space=pltpu.VMEM)] * count,
        out_specs=tuple(pl.BlockSpec(memory_space=pltpu.VMEM) for _ in xs),
        scratch_shapes=[pltpu.VMEM(x.shape, x.dtype) for x in xs]
        + [
            pltpu.SemaphoreType.DMA((count, n)),
            pltpu.SemaphoreType.DMA((count, n)),
            pltpu.SemaphoreType.DMA((count,)),
        ],
        compiler_params=pltpu.CompilerParams(collective_id=collective_id, has_side_effects=True),
    )(*xs)


def exchange(x, collective_id):
    return exchange_many((x,), collective_id)[0]


def gather_kernel(x_ref, y_ref, buf, send_sem, recv_sem):
    n = buf.shape[0]
    me = lax.axis_index("seq")
    here = (lax.axis_index("z"), lax.axis_index("core"))
    buf[...] = jnp.zeros_like(buf)
    barrier = pltpu.get_barrier_semaphore()
    for step in range(1, n):
        peer = lax.rem(me + step, n)
        pl.semaphore_signal(barrier, inc=1, device_id=(peer,) + here, device_id_type=MESH)
    pl.semaphore_wait(barrier, n - 1)

    def copy_to(peer):
        return pltpu.make_async_remote_copy(
            src_ref=x_ref,
            dst_ref=buf.at[me],
            send_sem=send_sem.at[peer],
            recv_sem=recv_sem.at[me],
            device_id=(peer,) + here,
            device_id_type=MESH,
        )

    def copy_from(source):
        return pltpu.make_async_remote_copy(
            src_ref=x_ref,
            dst_ref=buf.at[source],
            send_sem=send_sem.at[source],
            recv_sem=recv_sem.at[source],
            device_id=(source,) + here,
            device_id_type=MESH,
        )

    for step in range(1, n):
        @pl.when(me + step < n)
        def _():
            copy_to(me + step).start()

    for step in range(1, n):
        @pl.when(me - step >= 0)
        def _():
            copy_from(me - step).wait_recv()

    for step in range(1, n):
        @pl.when(me + step < n)
        def _():
            copy_to(me + step).wait_send()

    y_ref[...] = buf[...]


def gather_seq(x, slabs, collective_id):
    shape = (slabs,) + x.shape
    return pl.pallas_call(
        gather_kernel,
        out_shape=jax.ShapeDtypeStruct(shape, x.dtype),
        in_specs=[pl.BlockSpec(memory_space=pltpu.VMEM)],
        out_specs=pl.BlockSpec(memory_space=pltpu.VMEM),
        scratch_shapes=[
            pltpu.VMEM(shape, x.dtype),
            pltpu.SemaphoreType.DMA((slabs,)),
            pltpu.SemaphoreType.DMA((slabs,)),
        ],
        compiler_params=pltpu.CompilerParams(collective_id=collective_id, has_side_effects=True),
    )(x)


def scan_kernel(width, x_ref, y_ref, row_buf, col_buf, total, row_send, row_recv, col_send, col_recv):
    n = lax.axis_size("seq")
    height = n // width
    me = lax.axis_index("seq")
    row, col = me // width, me % width
    here = (lax.axis_index("z"), lax.axis_index("core"))
    row_buf[...] = jnp.zeros_like(row_buf)
    col_buf[...] = jnp.zeros_like(col_buf)
    barrier = pltpu.get_barrier_semaphore()
    for step in range(1, width):
        peer = row * width + lax.rem(col + step, width)
        pl.semaphore_signal(barrier, inc=1, device_id=(peer,) + here, device_id_type=MESH)
    for step in range(1, height):
        peer = lax.rem(row + step, height) * width + col
        pl.semaphore_signal(barrier, inc=1, device_id=(peer,) + here, device_id_type=MESH)
    pl.semaphore_wait(barrier, width + height - 2)

    def row_copy(c, slot):
        return pltpu.make_async_remote_copy(
            src_ref=x_ref,
            dst_ref=row_buf.at[slot],
            send_sem=row_send.at[c],
            recv_sem=row_recv.at[slot],
            device_id=(row * width + c,) + here,
            device_id_type=MESH,
        )

    sends = []
    for step in range(1, width):
        c = lax.rem(col + step, width)
        copy = row_copy(c, col)
        copy.start()
        sends.append(copy)
    for step in range(1, width):
        c = lax.rem(col + width - step, width)
        row_copy(c, c).wait_recv()
    mine = x_ref[...].astype(jnp.float32)
    row_total = mine
    row_prefix = jnp.zeros_like(mine)
    for c in range(width):
        part = jnp.where(c == col, 0.0, row_buf[c].astype(jnp.float32))
        row_total = row_total + part
        row_prefix = row_prefix + jnp.where(c < col, part, 0.0)
    total[...] = row_total

    def col_copy(r, slot):
        return pltpu.make_async_remote_copy(
            src_ref=total,
            dst_ref=col_buf.at[slot],
            send_sem=col_send.at[r],
            recv_sem=col_recv.at[slot],
            device_id=(r * width + col,) + here,
            device_id_type=MESH,
        )

    for step in range(1, height):
        @pl.when(row + step < height)
        def _():
            col_copy(row + step, row).start()

    for step in range(1, height):
        @pl.when(row - step >= 0)
        def _():
            col_copy(row - step, row - step).wait_recv()

    for step in range(1, height):
        @pl.when(row + step < height)
        def _():
            col_copy(row + step, row).wait_send()

    for copy in sends:
        copy.wait_send()
    prefix = row_prefix
    for r in range(height):
        prefix = prefix + col_buf[r]
    y_ref[...] = prefix


def scan_seq(x, collective_id):
    n = lax.axis_size("seq")
    width = 1
    while (width + 1) * (width + 1) <= n:
        width += 1
    while n % width:
        width -= 1
    height = n // width
    return pl.pallas_call(
        functools.partial(scan_kernel, width),
        out_shape=jax.ShapeDtypeStruct(x.shape, jnp.float32),
        in_specs=[pl.BlockSpec(memory_space=pltpu.VMEM)],
        out_specs=pl.BlockSpec(memory_space=pltpu.VMEM),
        scratch_shapes=[
            pltpu.VMEM((width,) + x.shape, x.dtype),
            pltpu.VMEM((height,) + x.shape, jnp.float32),
            pltpu.VMEM(x.shape, jnp.float32),
            pltpu.SemaphoreType.DMA((width,)),
            pltpu.SemaphoreType.DMA((width,)),
            pltpu.SemaphoreType.DMA((height,)),
            pltpu.SemaphoreType.DMA((height,)),
        ],
        compiler_params=pltpu.CompilerParams(collective_id=collective_id, has_side_effects=True),
    )(x)


def swap_kernel(x_ref, y_ref, send_sem, recv_sem):
    here = (lax.axis_index("seq"), lax.axis_index("z"))
    other = lax.axis_size("core") - 1 - lax.axis_index("core")
    barrier = pltpu.get_barrier_semaphore()
    pl.semaphore_signal(barrier, inc=1, device_id=here + (other,), device_id_type=MESH)
    pl.semaphore_wait(barrier, 1)
    copy = pltpu.make_async_remote_copy(
        src_ref=x_ref,
        dst_ref=y_ref,
        send_sem=send_sem,
        recv_sem=recv_sem,
        device_id=here + (other,),
        device_id_type=MESH,
    )
    copy.start()
    copy.wait()


def swap_cores(x, collective_id):
    return pl.pallas_call(
        swap_kernel,
        out_shape=jax.ShapeDtypeStruct(x.shape, x.dtype),
        in_specs=[pl.BlockSpec(memory_space=pl.ANY)],
        out_specs=pl.BlockSpec(memory_space=pl.ANY),
        scratch_shapes=[pltpu.SemaphoreType.DMA(()), pltpu.SemaphoreType.DMA(())],
        compiler_params=pltpu.CompilerParams(collective_id=collective_id, has_side_effects=True),
    )(x)


def opening_kernel(x_ref, w_ref, y_ref, w_all, buf, send_sem, recv_sem, own_sem, w_send, w_recv, w_own):
    n = x_ref.shape[0]
    cores = lax.axis_size("core")
    ring = n // cores
    me = chan_index()
    slab = lax.axis_index("seq")
    z = lax.axis_index("z")
    core = lax.axis_index("core")
    barrier = pltpu.get_barrier_semaphore()
    for step in range(1, n):
        peer = lax.rem(me + step, n)
        pl.semaphore_signal(barrier, inc=1, device_id=chan_device(slab, peer), device_id_type=MESH)
    pl.semaphore_wait(barrier, n - 1)
    own = pltpu.make_async_copy(x_ref.at[me], buf.at[me], own_sem)
    own.start()
    sends = []
    for step in range(1, n):
        peer = lax.rem(me + step, n)
        copy = pltpu.make_async_remote_copy(
            src_ref=x_ref.at[peer],
            dst_ref=buf.at[me],
            send_sem=send_sem.at[peer],
            recv_sem=recv_sem.at[me],
            device_id=chan_device(slab, peer),
            device_id_type=MESH,
        )
        copy.start()
        sends.append(copy)
    w_local = pltpu.make_async_copy(w_ref, w_all.at[me], w_own)
    w_local.start()
    right = (slab, lax.rem(z + 1, ring), core)
    left = (slab, lax.rem(z + ring - 1, ring), core)
    partner = (slab, z, cores - 1 - core)

    pieces = W_PIECES
    depth = w_ref.shape[0] // pieces

    def slot(origin):
        return lax.rem(origin + ring, ring) * cores + core

    def held(h, j):
        return w_all.at[h, pl.ds(j * depth, depth)]

    def send(source, h, j, kind, target):
        copy = pltpu.make_async_remote_copy(
            src_ref=source,
            dst_ref=held(h, j),
            send_sem=w_send.at[h, kind, j],
            recv_sem=w_recv.at[h, j],
            device_id=target,
            device_id_type=MESH,
        )
        copy.start()
        sends.append(copy)

    def arrive(h, j, source):
        pltpu.make_async_remote_copy(
            src_ref=w_ref.at[pl.ds(j * depth, depth)],
            dst_ref=held(h, j),
            send_sem=w_send.at[h, 0, j],
            recv_sem=w_recv.at[h, j],
            device_id=source,
            device_id_type=MESH,
        ).wait_recv()

    half = ring // 2
    full = half - 1 if ring % 2 == 0 else half

    def goes_right(step):
        return range(pieces) if step <= full else range(pieces // 2) if step == half else range(0)

    def goes_left(step):
        return range(pieces) if step <= full else range(pieces // 2, pieces) if step == half else range(0)

    for j in range(pieces):
        mine = w_ref.at[pl.ds(j * depth, depth)]
        if j in goes_right(1):
            send(mine, me, j, 0, right)
        if j in goes_left(1):
            send(mine, me, j, 1, left)
        send(mine, me, j, 2, partner)
    for step in range(1, half + 1):
        for j in range(pieces):
            if j in goes_right(step):
                h = slot(z - step)
                arrive(h, j, left)
                if j in goes_right(step + 1):
                    send(held(h, j), h, j, 0, right)
                send(held(h, j), h, j, 2, partner)
            if j in goes_left(step):
                h = slot(z + step)
                arrive(h, j, right)
                if j in goes_left(step + 1):
                    send(held(h, j), h, j, 1, left)
                send(held(h, j), h, j, 2, partner)
    for origin in range(ring):
        for j in range(pieces):
            arrive(origin * cores + (cores - 1 - core), j, partner)
    for step in range(1, n):
        source = lax.rem(me + n - step, n)
        pltpu.make_async_remote_copy(
            src_ref=x_ref.at[source],
            dst_ref=buf.at[source],
            send_sem=send_sem.at[source],
            recv_sem=recv_sem.at[source],
            device_id=chan_device(slab, source),
            device_id_type=MESH,
        ).wait_recv()
    for copy in sends:
        copy.wait_send()
    own.wait()
    w_local.wait()
    width = buf.shape[2]
    for g in range(n):
        y_ref[:, g * width : (g + 1) * width] = buf[g]


def opening(x, w, collective_id):
    n = x.shape[0]
    return pl.pallas_call(
        opening_kernel,
        out_shape=(
            jax.ShapeDtypeStruct((x.shape[1], n * x.shape[2]), x.dtype),
            jax.ShapeDtypeStruct((n,) + w.shape, w.dtype),
        ),
        in_specs=[pl.BlockSpec(memory_space=pltpu.VMEM), pl.BlockSpec(memory_space=pl.ANY)],
        out_specs=(pl.BlockSpec(memory_space=pltpu.VMEM), pl.BlockSpec(memory_space=pl.ANY)),
        scratch_shapes=[
            pltpu.VMEM(x.shape, x.dtype),
            pltpu.SemaphoreType.DMA((n,)),
            pltpu.SemaphoreType.DMA((n,)),
            pltpu.SemaphoreType.DMA(()),
            pltpu.SemaphoreType.DMA((n, 3, W_PIECES)),
            pltpu.SemaphoreType.DMA((n, W_PIECES)),
            pltpu.SemaphoreType.DMA(()),
        ],
        compiler_params=pltpu.CompilerParams(collective_id=collective_id, has_side_effects=True),
    )(x, w)


def split_rows(x, groups, collective_id):
    rows, cols = x.shape
    got = exchange(x.reshape(groups, rows // groups, cols), collective_id)
    return got.transpose(1, 0, 2).reshape(rows // groups, groups * cols)


def split_cols(x, groups, collective_id):
    rows, _, cols = x.shape
    got = exchange(x.transpose(1, 0, 2), collective_id)
    return got.reshape(groups * rows, cols)


def closing_kernel(x_ref, w_ref, y_ref, got, rows, out, back, send_sem, recv_sem, own_sem):
    n = x_ref.shape[0]
    cols = out.shape[2]
    me = chan_index()
    slab = lax.axis_index("seq")
    barrier = pltpu.get_barrier_semaphore()
    for step in range(1, n):
        peer = lax.rem(me + step, n)
        pl.semaphore_signal(barrier, inc=1, device_id=chan_device(slab, peer), device_id_type=MESH)
    pl.semaphore_wait(barrier, n - 1)

    def remote(phase, src, dst, peer, sender):
        return pltpu.make_async_remote_copy(
            src_ref=src,
            dst_ref=dst,
            send_sem=send_sem.at[phase, peer],
            recv_sem=recv_sem.at[phase, sender],
            device_id=chan_device(slab, peer),
            device_id_type=MESH,
        )

    sends = []
    for phase, (source, landing) in enumerate(((x_ref, got), (out, back))):
        own = pltpu.make_async_copy(source.at[me], landing.at[me], own_sem.at[phase])
        if phase == 1:
            hidden_rows = rows[...]
            for step in range(n):
                c = lax.rem(me + step, n)
                block = w_ref[:, pl.ds(pl.multiple_of(c * cols, cols), cols)]
                out[c] = jnp.dot(hidden_rows, block, preferred_element_type=jnp.float32).astype(out.dtype)
                if step == 0:
                    own.start()
                else:
                    copy = remote(phase, out.at[c], back.at[me], c, me)
                    copy.start()
                    sends.append(copy)
        else:
            own.start()
            for step in range(1, n):
                peer = lax.rem(me + step, n)
                copy = remote(phase, x_ref.at[peer], got.at[me], peer, me)
                copy.start()
                sends.append(copy)
        for step in range(1, n):
            source_dev = lax.rem(me + n - step, n)
            remote(phase, source.at[source_dev], landing.at[source_dev], source_dev, source_dev).wait_recv()
        own.wait()
        if phase == 0:
            width = got.shape[2]
            for g in range(n):
                rows[:, g * width : (g + 1) * width] = got[g]
    for copy in sends:
        copy.wait_send()
    y_ref[...] = back[...]


def closing(hidden_blocks, w_out, collective_id):
    n, chunk, width = hidden_blocks.shape
    cols = w_out.shape[1] // n
    block = (n, chunk, cols)
    return pl.pallas_call(
        closing_kernel,
        out_shape=jax.ShapeDtypeStruct(block, hidden_blocks.dtype),
        in_specs=[pl.BlockSpec(memory_space=pltpu.VMEM)] * 2,
        out_specs=pl.BlockSpec(memory_space=pltpu.VMEM),
        scratch_shapes=[
            pltpu.VMEM(hidden_blocks.shape, hidden_blocks.dtype),
            pltpu.VMEM((chunk, n * width), hidden_blocks.dtype),
            pltpu.VMEM(block, hidden_blocks.dtype),
            pltpu.VMEM(block, hidden_blocks.dtype),
            pltpu.SemaphoreType.DMA((2, n)),
            pltpu.SemaphoreType.DMA((2, n)),
            pltpu.SemaphoreType.DMA((2,)),
        ],
        compiler_params=pltpu.CompilerParams(
            collective_id=collective_id, has_side_effects=True, vmem_limit_bytes=48 * 1024 * 1024
        ),
    )(hidden_blocks, w_out)


def middle_kernel(rows_ref, w_ref, wq_ref, wk_ref, qk_out, v_out, qk_send, v_send, qk_got, v_got, q_all, k_all, send_sem, recv_sem, own_sem):
    n = w_ref.shape[0]
    me = chan_index()
    slab = lax.axis_index("seq")
    barrier = pltpu.get_barrier_semaphore()
    for step in range(1, n):
        peer = lax.rem(me + step, n)
        pl.semaphore_signal(barrier, inc=1, device_id=chan_device(slab, peer), device_id_type=MESH)
    pl.semaphore_wait(barrier, n - 1)
    pairs = ((qk_send, qk_got), (v_send, v_got))

    def remote(kind, peer, sender, slot):
        source, landing = pairs[kind]
        return pltpu.make_async_remote_copy(
            src_ref=source.at[slot],
            dst_ref=landing.at[sender],
            send_sem=send_sem.at[kind, peer],
            recv_sem=recv_sem.at[kind, sender],
            device_id=chan_device(slab, peer),
            device_id_type=MESH,
        )

    rows = rows_ref[...]
    pf = qk_send.shape[1] // 2
    q_all[...] = jnp.dot(rows, wq_ref[...], preferred_element_type=jnp.float32).T
    k_all[...] = jnp.dot(rows, wk_ref[...], preferred_element_type=jnp.float32).T
    owns = []
    sends = []
    for step in range(n):
        g = lax.rem(me + step, n)
        v_send[g] = jnp.dot(rows, w_ref[g], preferred_element_type=jnp.float32).astype(v_send.dtype)
        head = pl.ds(pl.multiple_of(g * pf, pf), pf)
        qk_send[g, :pf, :] = q_all[head, :].astype(qk_send.dtype)
        qk_send[g, pf:, :] = k_all[head, :].astype(qk_send.dtype)
        for kind in range(2):
            source, landing = pairs[kind]
            if step == 0:
                own = pltpu.make_async_copy(source.at[me], landing.at[me], own_sem.at[kind])
                own.start()
                owns.append(own)
            else:
                copy = remote(kind, g, me, g)
                copy.start()
                sends.append(copy)
    for step in range(1, n):
        source_dev = lax.rem(me + n - step, n)
        for kind in range(2):
            remote(kind, source_dev, source_dev, source_dev).wait_recv()
    for own in owns:
        own.wait()
    for copy in sends:
        copy.wait_send()
    qk_out[...] = qk_got[...]
    v_out[...] = v_got[...]


def middle(rows, w_all, w_query, w_key, collective_id):
    n = w_all.shape[0]
    chunk = rows.shape[0]
    qk_shape = (n, 2 * w_query.shape[1] // n, chunk)
    v_shape = (n, chunk, w_all.shape[2])
    return pl.pallas_call(
        middle_kernel,
        out_shape=(
            jax.ShapeDtypeStruct(qk_shape, rows.dtype),
            jax.ShapeDtypeStruct(v_shape, rows.dtype),
        ),
        in_specs=[pl.BlockSpec(memory_space=pltpu.VMEM)] * 4,
        out_specs=(pl.BlockSpec(memory_space=pltpu.VMEM), pl.BlockSpec(memory_space=pltpu.VMEM)),
        scratch_shapes=[
            pltpu.VMEM(qk_shape, rows.dtype),
            pltpu.VMEM(v_shape, rows.dtype),
            pltpu.VMEM(qk_shape, rows.dtype),
            pltpu.VMEM(v_shape, rows.dtype),
            pltpu.VMEM((w_query.shape[1], chunk), jnp.float32),
            pltpu.VMEM((w_key.shape[1], chunk), jnp.float32),
            pltpu.SemaphoreType.DMA((2, n)),
            pltpu.SemaphoreType.DMA((2, n)),
            pltpu.SemaphoreType.DMA((2,)),
        ],
        compiler_params=pltpu.CompilerParams(
            collective_id=collective_id, has_side_effects=True, vmem_limit_bytes=48 * 1024 * 1024
        ),
    )(rows, w_all, w_query, w_key)


def attend(query_rows, key_rows, value_rows, gain_mine, my_slab):
    highest = lax.Precision.HIGHEST
    tok_rows, per_group, _ = value_rows.shape
    blocks = tok_rows // BLOCK
    query_blocks = query_rows.reshape(blocks, BLOCK, per_group, FEAT)
    key_blocks = key_rows.reshape(blocks, BLOCK, per_group, FEAT)
    value_blocks = value_rows.reshape(blocks, BLOCK, per_group, HEAD_DIM)
    value_f32 = value_blocks.astype(jnp.float32)
    key_linear, key_square = feature_parts(key_blocks.astype(jnp.float32))
    own_zero = jnp.sum(value_f32, axis=1)[:, :, None, :]
    own_one = jnp.einsum("bthf,bthe->bhfe", key_linear, value_f32, precision=highest)
    own_two = jnp.einsum("bthf,bthe->bhfe", key_square, value_f32, precision=highest)
    own = jnp.concatenate([own_zero, own_one, own_two], axis=2)
    slab_total = jnp.sum(own, axis=0)
    state_rows = slab_total.shape[0] * slab_total.shape[1]
    prefix = scan_seq(slab_total.astype(jnp.bfloat16).reshape(state_rows, HEAD_DIM), 7).reshape(slab_total.shape)
    earlier = jnp.concatenate([jnp.zeros_like(own[:1]), jnp.cumsum(own, axis=0)[:-1]], axis=0) + prefix[None]
    query_linear, query_square = feature_parts(query_blocks.astype(jnp.float32))
    inter = earlier[:, :, 0][:, None] + jnp.einsum(
        "bthf,bhfe->bthe", query_linear, earlier[:, :, 1 : 1 + FEAT], precision=highest
    )
    inter = inter + jnp.einsum(
        "bthf,bhfe->bthe", query_square, earlier[:, :, 1 + FEAT :], precision=highest
    )
    scores = jnp.einsum(
        "bthf,bshf->bhts", query_blocks, key_blocks, preferred_element_type=jnp.float32
    ) * FEAT ** (-0.5)
    kernel = 1.0 + scores + 0.5 * scores * scores
    causal = jnp.arange(BLOCK)[:, None] >= jnp.arange(BLOCK)[None, :]
    weights = jnp.where(causal, kernel, 0.0).astype(jnp.bfloat16)
    intra = jnp.einsum("bhts,bshe->bthe", weights, value_blocks, preferred_element_type=jnp.float32)
    numerator = (intra + inter).reshape(tok_rows, per_group, HEAD_DIM)
    mean_square = jnp.mean(numerator * numerator, axis=-1, keepdims=True)
    hidden = (numerator * lax.rsqrt(mean_square + 1e-05) * gain_mine).astype(jnp.bfloat16)
    return hidden.reshape(tok_rows, per_group * HEAD_DIM)


def per_device(tokens, w_query, w_key, w_value, w_out, gain):
    groups = lax.axis_size(CHAN)
    per_group = HEADS // groups
    my_group = chan_index()
    my_slab = lax.axis_index("seq")
    tok_rows_total, tok_cols = tokens.shape
    rows, value_all = opening(tokens.reshape(groups, tok_rows_total // groups, tok_cols), w_value, 1)
    chunk = rows.shape[0]
    pf = per_group * FEAT
    d_model = w_query.shape[0]
    qk_got, value_got = middle(rows, value_all, w_query, w_key, 2)
    tok_rows = groups * chunk
    qk_rows = qk_got.transpose(0, 2, 1).reshape(tok_rows, 2 * pf)
    query_rows = qk_rows[:, :pf].reshape(tok_rows, per_group, FEAT)
    key_rows = qk_rows[:, pf:].reshape(tok_rows, per_group, FEAT)
    value_rows = value_got.reshape(tok_rows, per_group, HEAD_DIM)
    value_cols = per_group * HEAD_DIM
    gain_mine = lax.dynamic_slice_in_dim(gain, my_group * value_cols, value_cols, 0).reshape(
        per_group, HEAD_DIM
    )
    hidden = attend(query_rows, key_rows, value_rows, gain_mine, my_slab)
    out_cols = w_out.shape[1] // groups
    mixed_blocks = closing(hidden.reshape(groups, chunk, per_group * HEAD_DIM), w_out, 3)
    return mixed_blocks.reshape(tok_rows, out_cols)

def solution(mesh):
    seq, chan = mesh.devices.shape
    cores = 2 if chan % 2 == 0 else 1
    split = jax.sharding.Mesh(mesh.devices.reshape(seq, chan // cores, cores), ("seq", "z", "core"))
    return jax.shard_map(
        per_device,
        mesh=split,
        in_specs=(P("seq", CHAN), P(), P(), P(None, CHAN), P(), P()),
        out_specs=P("seq", CHAN),
        check_vma=False,
    )
```

```python
import functools

import jax
import jax.numpy as jnp
from jax import lax
from jax.experimental import pallas as pl
from jax.experimental.pallas import tpu as pltpu
from jax.sharding import PartitionSpec as P

MESH = pl.DeviceIdType.MESH
CHAN = ("z", "core")
W_PIECES = 2


def chan_index():
    return lax.axis_index("z") * lax.axis_size("core") + lax.axis_index("core")


def chan_device(slab, peer):
    cores = lax.axis_size("core")
    return (slab, peer // cores, peer % cores)

HEADS = 16
FEAT = 16
HEAD_DIM = 128
BLOCK = 896


def feature_parts(rows):
    linear = rows * FEAT ** (-0.25)
    square = (rows[..., :, None] * rows[..., None, :]).reshape(rows.shape[:-1] + (FEAT * FEAT,)) * (
        2.0 * FEAT
    ) ** (-0.5)
    return (linear, square)


def exchange_kernel(count, *refs):
    xs, ys, bufs = refs[:count], refs[count : 2 * count], refs[2 * count : 3 * count]
    send_sem, recv_sem, own_sem = refs[3 * count :]
    n = xs[0].shape[0]
    me = chan_index()
    slab = lax.axis_index("seq")
    barrier = pltpu.get_barrier_semaphore()
    for step in range(1, n):
        peer = lax.rem(me + step, n)
        pl.semaphore_signal(barrier, inc=1, device_id=chan_device(slab, peer), device_id_type=MESH)
    pl.semaphore_wait(barrier, n - 1)
    owns = []
    sends = []
    for a in range(count):
        own = pltpu.make_async_copy(xs[a].at[me], bufs[a].at[me], own_sem.at[a])
        own.start()
        owns.append(own)
    for step in range(1, n):
        peer = lax.rem(me + step, n)
        for a in range(count):
            copy = pltpu.make_async_remote_copy(
                src_ref=xs[a].at[peer],
                dst_ref=bufs[a].at[me],
                send_sem=send_sem.at[a, peer],
                recv_sem=recv_sem.at[a, me],
                device_id=chan_device(slab, peer),
                device_id_type=MESH,
            )
            copy.start()
            sends.append(copy)
    for step in range(1, n):
        source = lax.rem(me + n - step, n)
        for a in range(count):
            pltpu.make_async_remote_copy(
                src_ref=xs[a].at[source],
                dst_ref=bufs[a].at[source],
                send_sem=send_sem.at[a, source],
                recv_sem=recv_sem.at[a, source],
                device_id=chan_device(slab, source),
                device_id_type=MESH,
            ).wait_recv()
    for copy in sends:
        copy.wait_send()
    for a in range(count):
        owns[a].wait()
        ys[a][...] = bufs[a][...]


def exchange_many(xs, collective_id):
    count = len(xs)
    n = xs[0].shape[0]
    return pl.pallas_call(
        functools.partial(exchange_kernel, count),
        out_shape=tuple(jax.ShapeDtypeStruct(x.shape, x.dtype) for x in xs),
        in_specs=[pl.BlockSpec(memory_space=pltpu.VMEM)] * count,
        out_specs=tuple(pl.BlockSpec(memory_space=pltpu.VMEM) for _ in xs),
        scratch_shapes=[pltpu.VMEM(x.shape, x.dtype) for x in xs]
        + [
            pltpu.SemaphoreType.DMA((count, n)),
            pltpu.SemaphoreType.DMA((count, n)),
            pltpu.SemaphoreType.DMA((count,)),
        ],
        compiler_params=pltpu.CompilerParams(collective_id=collective_id, has_side_effects=True),
    )(*xs)


def exchange(x, collective_id):
    return exchange_many((x,), collective_id)[0]


def gather_kernel(x_ref, y_ref, buf, send_sem, recv_sem):
    n = buf.shape[0]
    me = lax.axis_index("seq")
    here = (lax.axis_index("z"), lax.axis_index("core"))
    buf[...] = jnp.zeros_like(buf)
    barrier = pltpu.get_barrier_semaphore()
    for step in range(1, n):
        peer = lax.rem(me + step, n)
        pl.semaphore_signal(barrier, inc=1, device_id=(peer,) + here, device_id_type=MESH)
    pl.semaphore_wait(barrier, n - 1)

    def copy_to(peer):
        return pltpu.make_async_remote_copy(
            src_ref=x_ref,
            dst_ref=buf.at[me],
            send_sem=send_sem.at[peer],
            recv_sem=recv_sem.at[me],
            device_id=(peer,) + here,
            device_id_type=MESH,
        )

    def copy_from(source):
        return pltpu.make_async_remote_copy(
            src_ref=x_ref,
            dst_ref=buf.at[source],
            send_sem=send_sem.at[source],
            recv_sem=recv_sem.at[source],
            device_id=(source,) + here,
            device_id_type=MESH,
        )

    for step in range(1, n):
        @pl.when(me + step < n)
        def _():
            copy_to(me + step).start()

    for step in range(1, n):
        @pl.when(me - step >= 0)
        def _():
            copy_from(me - step).wait_recv()

    for step in range(1, n):
        @pl.when(me + step < n)
        def _():
            copy_to(me + step).wait_send()

    y_ref[...] = buf[...]


def gather_seq(x, slabs, collective_id):
    shape = (slabs,) + x.shape
    return pl.pallas_call(
        gather_kernel,
        out_shape=jax.ShapeDtypeStruct(shape, x.dtype),
        in_specs=[pl.BlockSpec(memory_space=pltpu.VMEM)],
        out_specs=pl.BlockSpec(memory_space=pltpu.VMEM),
        scratch_shapes=[
            pltpu.VMEM(shape, x.dtype),
            pltpu.SemaphoreType.DMA((slabs,)),
            pltpu.SemaphoreType.DMA((slabs,)),
        ],
        compiler_params=pltpu.CompilerParams(collective_id=collective_id, has_side_effects=True),
    )(x)


def scan_kernel(width, x_ref, y_ref, row_buf, col_buf, total, row_send, row_recv, col_send, col_recv):
    n = lax.axis_size("seq")
    height = n // width
    me = lax.axis_index("seq")
    row, col = me // width, me % width
    here = (lax.axis_index("z"), lax.axis_index("core"))
    row_buf[...] = jnp.zeros_like(row_buf)
    col_buf[...] = jnp.zeros_like(col_buf)
    barrier = pltpu.get_barrier_semaphore()
    for step in range(1, width):
        peer = row * width + lax.rem(col + step, width)
        pl.semaphore_signal(barrier, inc=1, device_id=(peer,) + here, device_id_type=MESH)
    for step in range(1, height):
        peer = lax.rem(row + step, height) * width + col
        pl.semaphore_signal(barrier, inc=1, device_id=(peer,) + here, device_id_type=MESH)
    pl.semaphore_wait(barrier, width + height - 2)

    def row_copy(c, slot):
        return pltpu.make_async_remote_copy(
            src_ref=x_ref,
            dst_ref=row_buf.at[slot],
            send_sem=row_send.at[c],
            recv_sem=row_recv.at[slot],
            device_id=(row * width + c,) + here,
            device_id_type=MESH,
        )

    sends = []
    for step in range(1, width):
        c = lax.rem(col + step, width)
        copy = row_copy(c, col)
        copy.start()
        sends.append(copy)
    for step in range(1, width):
        c = lax.rem(col + width - step, width)
        row_copy(c, c).wait_recv()
    mine = x_ref[...].astype(jnp.float32)
    row_total = mine
    row_prefix = jnp.zeros_like(mine)
    for c in range(width):
        part = jnp.where(c == col, 0.0, row_buf[c].astype(jnp.float32))
        row_total = row_total + part
        row_prefix = row_prefix + jnp.where(c < col, part, 0.0)
    total[...] = row_total

    def col_copy(r, slot):
        return pltpu.make_async_remote_copy(
            src_ref=total,
            dst_ref=col_buf.at[slot],
            send_sem=col_send.at[r],
            recv_sem=col_recv.at[slot],
            device_id=(r * width + col,) + here,
            device_id_type=MESH,
        )

    for step in range(1, height):
        @pl.when(row + step < height)
        def _():
            col_copy(row + step, row).start()

    for step in range(1, height):
        @pl.when(row - step >= 0)
        def _():
            col_copy(row - step, row - step).wait_recv()

    for step in range(1, height):
        @pl.when(row + step < height)
        def _():
            col_copy(row + step, row).wait_send()

    for copy in sends:
        copy.wait_send()
    prefix = row_prefix
    for r in range(height):
        prefix = prefix + col_buf[r]
    y_ref[...] = prefix


def scan_seq(x, collective_id):
    n = lax.axis_size("seq")
    width = 1
    while (width + 1) * (width + 1) <= n:
        width += 1
    while n % width:
        width -= 1
    height = n // width
    return pl.pallas_call(
        functools.partial(scan_kernel, width),
        out_shape=jax.ShapeDtypeStruct(x.shape, jnp.float32),
        in_specs=[pl.BlockSpec(memory_space=pltpu.VMEM)],
        out_specs=pl.BlockSpec(memory_space=pltpu.VMEM),
        scratch_shapes=[
            pltpu.VMEM((width,) + x.shape, x.dtype),
            pltpu.VMEM((height,) + x.shape, jnp.float32),
            pltpu.VMEM(x.shape, jnp.float32),
            pltpu.SemaphoreType.DMA((width,)),
            pltpu.SemaphoreType.DMA((width,)),
            pltpu.SemaphoreType.DMA((height,)),
            pltpu.SemaphoreType.DMA((height,)),
        ],
        compiler_params=pltpu.CompilerParams(collective_id=collective_id, has_side_effects=True),
    )(x)


def swap_kernel(x_ref, y_ref, send_sem, recv_sem):
    here = (lax.axis_index("seq"), lax.axis_index("z"))
    other = lax.axis_size("core") - 1 - lax.axis_index("core")
    barrier = pltpu.get_barrier_semaphore()
    pl.semaphore_signal(barrier, inc=1, device_id=here + (other,), device_id_type=MESH)
    pl.semaphore_wait(barrier, 1)
    copy = pltpu.make_async_remote_copy(
        src_ref=x_ref,
        dst_ref=y_ref,
        send_sem=send_sem,
        recv_sem=recv_sem,
        device_id=here + (other,),
        device_id_type=MESH,
    )
    copy.start()
    copy.wait()


def swap_cores(x, collective_id):
    return pl.pallas_call(
        swap_kernel,
        out_shape=jax.ShapeDtypeStruct(x.shape, x.dtype),
        in_specs=[pl.BlockSpec(memory_space=pl.ANY)],
        out_specs=pl.BlockSpec(memory_space=pl.ANY),
        scratch_shapes=[pltpu.SemaphoreType.DMA(()), pltpu.SemaphoreType.DMA(())],
        compiler_params=pltpu.CompilerParams(collective_id=collective_id, has_side_effects=True),
    )(x)


def opening_kernel(x_ref, w_ref, y_ref, w_all, buf, send_sem, recv_sem, own_sem, w_send, w_recv, w_own):
    n = x_ref.shape[0]
    cores = lax.axis_size("core")
    ring = n // cores
    me = chan_index()
    slab = lax.axis_index("seq")
    z = lax.axis_index("z")
    core = lax.axis_index("core")
    barrier = pltpu.get_barrier_semaphore()
    for step in range(1, n):
        peer = lax.rem(me + step, n)
        pl.semaphore_signal(barrier, inc=1, device_id=chan_device(slab, peer), device_id_type=MESH)
    pl.semaphore_wait(barrier, n - 1)
    own = pltpu.make_async_copy(x_ref.at[me], buf.at[me], own_sem)
    own.start()
    sends = []
    for step in range(1, n):
        peer = lax.rem(me + step, n)
        copy = pltpu.make_async_remote_copy(
            src_ref=x_ref.at[peer],
            dst_ref=buf.at[me],
            send_sem=send_sem.at[peer],
            recv_sem=recv_sem.at[me],
            device_id=chan_device(slab, peer),
            device_id_type=MESH,
        )
        copy.start()
        sends.append(copy)
    w_local = pltpu.make_async_copy(w_ref, w_all.at[me], w_own)
    w_local.start()
    right = (slab, lax.rem(z + 1, ring), core)
    left = (slab, lax.rem(z + ring - 1, ring), core)
    partner = (slab, z, cores - 1 - core)

    pieces = W_PIECES
    depth = w_ref.shape[0] // pieces

    def slot(origin):
        return lax.rem(origin + ring, ring) * cores + core

    def held(h, j):
        return w_all.at[h, pl.ds(j * depth, depth)]

    def send(source, h, j, kind, target):
        copy = pltpu.make_async_remote_copy(
            src_ref=source,
            dst_ref=held(h, j),
            send_sem=w_send.at[h, kind, j],
            recv_sem=w_recv.at[h, j],
            device_id=target,
            device_id_type=MESH,
        )
        copy.start()
        sends.append(copy)

    def arrive(h, j, source):
        pltpu.make_async_remote_copy(
            src_ref=w_ref.at[pl.ds(j * depth, depth)],
            dst_ref=held(h, j),
            send_sem=w_send.at[h, 0, j],
            recv_sem=w_recv.at[h, j],
            device_id=source,
            device_id_type=MESH,
        ).wait_recv()

    half = ring // 2
    full = half - 1 if ring % 2 == 0 else half

    def goes_right(step):
        return range(pieces) if step <= full else range(pieces // 2) if step == half else range(0)

    def goes_left(step):
        return range(pieces) if step <= full else range(pieces // 2, pieces) if step == half else range(0)

    for j in range(pieces):
        mine = w_ref.at[pl.ds(j * depth, depth)]
        if j in goes_right(1):
            send(mine, me, j, 0, right)
        if j in goes_left(1):
            send(mine, me, j, 1, left)
        send(mine, me, j, 2, partner)
    for step in range(1, half + 1):
        for j in range(pieces):
            if j in goes_right(step):
                h = slot(z - step)
                arrive(h, j, left)
                if j in goes_right(step + 1):
                    send(held(h, j), h, j, 0, right)
                send(held(h, j), h, j, 2, partner)
            if j in goes_left(step):
                h = slot(z + step)
                arrive(h, j, right)
                if j in goes_left(step + 1):
                    send(held(h, j), h, j, 1, left)
                send(held(h, j), h, j, 2, partner)
    for origin in range(ring):
        for j in range(pieces):
            arrive(origin * cores + (cores - 1 - core), j, partner)
    for step in range(1, n):
        source = lax.rem(me + n - step, n)
        pltpu.make_async_remote_copy(
            src_ref=x_ref.at[source],
            dst_ref=buf.at[source],
            send_sem=send_sem.at[source],
            recv_sem=recv_sem.at[source],
            device_id=chan_device(slab, source),
            device_id_type=MESH,
        ).wait_recv()
    for copy in sends:
        copy.wait_send()
    own.wait()
    w_local.wait()
    y_ref[...] = buf[...]


def opening(x, w, collective_id):
    n = x.shape[0]
    return pl.pallas_call(
        opening_kernel,
        out_shape=(
            jax.ShapeDtypeStruct(x.shape, x.dtype),
            jax.ShapeDtypeStruct((n,) + w.shape, w.dtype),
        ),
        in_specs=[pl.BlockSpec(memory_space=pltpu.VMEM), pl.BlockSpec(memory_space=pl.ANY)],
        out_specs=(pl.BlockSpec(memory_space=pltpu.VMEM), pl.BlockSpec(memory_space=pl.ANY)),
        scratch_shapes=[
            pltpu.VMEM(x.shape, x.dtype),
            pltpu.SemaphoreType.DMA((n,)),
            pltpu.SemaphoreType.DMA((n,)),
            pltpu.SemaphoreType.DMA(()),
            pltpu.SemaphoreType.DMA((n, 3, W_PIECES)),
            pltpu.SemaphoreType.DMA((n, W_PIECES)),
            pltpu.SemaphoreType.DMA(()),
        ],
        compiler_params=pltpu.CompilerParams(collective_id=collective_id, has_side_effects=True),
    )(x, w)


def split_rows(x, groups, collective_id):
    rows, cols = x.shape
    got = exchange(x.reshape(groups, rows // groups, cols), collective_id)
    return got.transpose(1, 0, 2).reshape(rows // groups, groups * cols)


def split_cols(x, groups, collective_id):
    rows, _, cols = x.shape
    got = exchange(x.transpose(1, 0, 2), collective_id)
    return got.reshape(groups * rows, cols)


def closing_kernel(x_ref, w_ref, y_ref, got, rows, out, back, send_sem, recv_sem, own_sem):
    n = x_ref.shape[0]
    cols = out.shape[2]
    me = chan_index()
    slab = lax.axis_index("seq")
    barrier = pltpu.get_barrier_semaphore()
    for step in range(1, n):
        peer = lax.rem(me + step, n)
        pl.semaphore_signal(barrier, inc=1, device_id=chan_device(slab, peer), device_id_type=MESH)
    pl.semaphore_wait(barrier, n - 1)

    def remote(phase, src, dst, peer, sender):
        return pltpu.make_async_remote_copy(
            src_ref=src,
            dst_ref=dst,
            send_sem=send_sem.at[phase, peer],
            recv_sem=recv_sem.at[phase, sender],
            device_id=chan_device(slab, peer),
            device_id_type=MESH,
        )

    sends = []
    for phase, (source, landing) in enumerate(((x_ref, got), (out, back))):
        own = pltpu.make_async_copy(source.at[me], landing.at[me], own_sem.at[phase])
        if phase == 1:
            hidden_rows = rows[...]
            for step in range(n):
                c = lax.rem(me + step, n)
                block = w_ref[:, pl.ds(pl.multiple_of(c * cols, cols), cols)]
                out[c] = jnp.dot(hidden_rows, block, preferred_element_type=jnp.float32).astype(out.dtype)
                if step == 0:
                    own.start()
                else:
                    copy = remote(phase, out.at[c], back.at[me], c, me)
                    copy.start()
                    sends.append(copy)
        else:
            own.start()
            for step in range(1, n):
                peer = lax.rem(me + step, n)
                copy = remote(phase, x_ref.at[peer], got.at[me], peer, me)
                copy.start()
                sends.append(copy)
        for step in range(1, n):
            source_dev = lax.rem(me + n - step, n)
            remote(phase, source.at[source_dev], landing.at[source_dev], source_dev, source_dev).wait_recv()
        own.wait()
        if phase == 0:
            width = got.shape[2]
            for g in range(n):
                rows[:, g * width : (g + 1) * width] = got[g]
    for copy in sends:
        copy.wait_send()
    y_ref[...] = back[...]


def closing(hidden_blocks, w_out, collective_id):
    n, chunk, width = hidden_blocks.shape
    cols = w_out.shape[1] // n
    block = (n, chunk, cols)
    return pl.pallas_call(
        closing_kernel,
        out_shape=jax.ShapeDtypeStruct(block, hidden_blocks.dtype),
        in_specs=[pl.BlockSpec(memory_space=pltpu.VMEM)] * 2,
        out_specs=pl.BlockSpec(memory_space=pltpu.VMEM),
        scratch_shapes=[
            pltpu.VMEM(hidden_blocks.shape, hidden_blocks.dtype),
            pltpu.VMEM((chunk, n * width), hidden_blocks.dtype),
            pltpu.VMEM(block, hidden_blocks.dtype),
            pltpu.VMEM(block, hidden_blocks.dtype),
            pltpu.SemaphoreType.DMA((2, n)),
            pltpu.SemaphoreType.DMA((2, n)),
            pltpu.SemaphoreType.DMA((2,)),
        ],
        compiler_params=pltpu.CompilerParams(
            collective_id=collective_id, has_side_effects=True, vmem_limit_bytes=48 * 1024 * 1024
        ),
    )(hidden_blocks, w_out)


def middle_kernel(rows_ref, w_ref, wq_ref, wk_ref, qk_out, v_out, qk_send, v_send, qk_got, v_got, q_all, k_all, send_sem, recv_sem, own_sem):
    n = w_ref.shape[0]
    me = chan_index()
    slab = lax.axis_index("seq")
    barrier = pltpu.get_barrier_semaphore()
    for step in range(1, n):
        peer = lax.rem(me + step, n)
        pl.semaphore_signal(barrier, inc=1, device_id=chan_device(slab, peer), device_id_type=MESH)
    pl.semaphore_wait(barrier, n - 1)
    pairs = ((qk_send, qk_got), (v_send, v_got))

    def remote(kind, peer, sender, slot):
        source, landing = pairs[kind]
        return pltpu.make_async_remote_copy(
            src_ref=source.at[slot],
            dst_ref=landing.at[sender],
            send_sem=send_sem.at[kind, peer],
            recv_sem=recv_sem.at[kind, sender],
            device_id=chan_device(slab, peer),
            device_id_type=MESH,
        )

    rows = rows_ref[...]
    pf = qk_send.shape[1] // 2
    q_all[...] = jnp.dot(rows, wq_ref[...], preferred_element_type=jnp.float32).T
    k_all[...] = jnp.dot(rows, wk_ref[...], preferred_element_type=jnp.float32).T
    owns = []
    sends = []
    for step in range(n):
        g = lax.rem(me + step, n)
        v_send[g] = jnp.dot(rows, w_ref[g], preferred_element_type=jnp.float32).astype(v_send.dtype)
        head = pl.ds(pl.multiple_of(g * pf, pf), pf)
        qk_send[g, :pf, :] = q_all[head, :].astype(qk_send.dtype)
        qk_send[g, pf:, :] = k_all[head, :].astype(qk_send.dtype)
        for kind in range(2):
            source, landing = pairs[kind]
            if step == 0:
                own = pltpu.make_async_copy(source.at[me], landing.at[me], own_sem.at[kind])
                own.start()
                owns.append(own)
            else:
                copy = remote(kind, g, me, g)
                copy.start()
                sends.append(copy)
    for step in range(1, n):
        source_dev = lax.rem(me + n - step, n)
        for kind in range(2):
            remote(kind, source_dev, source_dev, source_dev).wait_recv()
    for own in owns:
        own.wait()
    for copy in sends:
        copy.wait_send()
    qk_out[...] = qk_got[...]
    v_out[...] = v_got[...]


def middle(rows, w_all, w_query, w_key, collective_id):
    n = w_all.shape[0]
    chunk = rows.shape[0]
    qk_shape = (n, 2 * w_query.shape[1] // n, chunk)
    v_shape = (n, chunk, w_all.shape[2])
    return pl.pallas_call(
        middle_kernel,
        out_shape=(
            jax.ShapeDtypeStruct(qk_shape, rows.dtype),
            jax.ShapeDtypeStruct(v_shape, rows.dtype),
        ),
        in_specs=[pl.BlockSpec(memory_space=pltpu.VMEM)] * 4,
        out_specs=(pl.BlockSpec(memory_space=pltpu.VMEM), pl.BlockSpec(memory_space=pltpu.VMEM)),
        scratch_shapes=[
            pltpu.VMEM(qk_shape, rows.dtype),
            pltpu.VMEM(v_shape, rows.dtype),
            pltpu.VMEM(qk_shape, rows.dtype),
            pltpu.VMEM(v_shape, rows.dtype),
            pltpu.VMEM((w_query.shape[1], chunk), jnp.float32),
            pltpu.VMEM((w_key.shape[1], chunk), jnp.float32),
            pltpu.SemaphoreType.DMA((2, n)),
            pltpu.SemaphoreType.DMA((2, n)),
            pltpu.SemaphoreType.DMA((2,)),
        ],
        compiler_params=pltpu.CompilerParams(
            collective_id=collective_id, has_side_effects=True, vmem_limit_bytes=48 * 1024 * 1024
        ),
    )(rows, w_all, w_query, w_key)


def attend(query_rows, key_rows, value_rows, gain_mine, my_slab):
    highest = lax.Precision.HIGHEST
    tok_rows, per_group, _ = value_rows.shape
    blocks = tok_rows // BLOCK
    query_blocks = query_rows.reshape(blocks, BLOCK, per_group, FEAT)
    key_blocks = key_rows.reshape(blocks, BLOCK, per_group, FEAT)
    value_blocks = value_rows.reshape(blocks, BLOCK, per_group, HEAD_DIM)
    value_f32 = value_blocks.astype(jnp.float32)
    key_linear, key_square = feature_parts(key_blocks.astype(jnp.float32))
    own_zero = jnp.sum(value_f32, axis=1)[:, :, None, :]
    own_one = jnp.einsum("bthf,bthe->bhfe", key_linear, value_f32, precision=highest)
    own_two = jnp.einsum("bthf,bthe->bhfe", key_square, value_f32, precision=highest)
    own = jnp.concatenate([own_zero, own_one, own_two], axis=2)
    slab_total = jnp.sum(own, axis=0)
    state_rows = slab_total.shape[0] * slab_total.shape[1]
    prefix = scan_seq(slab_total.astype(jnp.bfloat16).reshape(state_rows, HEAD_DIM), 7).reshape(slab_total.shape)
    earlier = jnp.concatenate([jnp.zeros_like(own[:1]), jnp.cumsum(own, axis=0)[:-1]], axis=0) + prefix[None]
    query_linear, query_square = feature_parts(query_blocks.astype(jnp.float32))
    inter = earlier[:, :, 0][:, None] + jnp.einsum(
        "bthf,bhfe->bthe", query_linear, earlier[:, :, 1 : 1 + FEAT], precision=highest
    )
    inter = inter + jnp.einsum(
        "bthf,bhfe->bthe", query_square, earlier[:, :, 1 + FEAT :], precision=highest
    )
    scores = jnp.einsum(
        "bthf,bshf->bhts", query_blocks, key_blocks, preferred_element_type=jnp.float32
    ) * FEAT ** (-0.5)
    kernel = 1.0 + scores + 0.5 * scores * scores
    causal = jnp.arange(BLOCK)[:, None] >= jnp.arange(BLOCK)[None, :]
    weights = jnp.where(causal, kernel, 0.0).astype(jnp.bfloat16)
    intra = jnp.einsum("bhts,bshe->bthe", weights, value_blocks, preferred_element_type=jnp.float32)
    numerator = (intra + inter).reshape(tok_rows, per_group, HEAD_DIM)
    mean_square = jnp.mean(numerator * numerator, axis=-1, keepdims=True)
    hidden = (numerator * lax.rsqrt(mean_square + 1e-05) * gain_mine).astype(jnp.bfloat16)
    return hidden.reshape(tok_rows, per_group * HEAD_DIM)


def per_device(tokens, w_query, w_key, w_value, w_out, gain):
    groups = lax.axis_size(CHAN)
    per_group = HEADS // groups
    my_group = chan_index()
    my_slab = lax.axis_index("seq")
    tok_rows_total, tok_cols = tokens.shape
    got, value_all = opening(tokens.reshape(groups, tok_rows_total // groups, tok_cols), w_value, 1)
    rows = got.transpose(1, 0, 2).reshape(tok_rows_total // groups, groups * tok_cols)
    chunk = rows.shape[0]
    pf = per_group * FEAT
    d_model = w_query.shape[0]
    qk_got, value_got = middle(rows, value_all, w_query, w_key, 2)
    tok_rows = groups * chunk
    qk_rows = qk_got.transpose(0, 2, 1).reshape(tok_rows, 2 * pf)
    query_rows = qk_rows[:, :pf].reshape(tok_rows, per_group, FEAT)
    key_rows = qk_rows[:, pf:].reshape(tok_rows, per_group, FEAT)
    value_rows = value_got.reshape(tok_rows, per_group, HEAD_DIM)
    value_cols = per_group * HEAD_DIM
    gain_mine = lax.dynamic_slice_in_dim(gain, my_group * value_cols, value_cols, 0).reshape(
        per_group, HEAD_DIM
    )
    hidden = attend(query_rows, key_rows, value_rows, gain_mine, my_slab)
    out_cols = w_out.shape[1] // groups
    mixed_blocks = closing(hidden.reshape(groups, chunk, per_group * HEAD_DIM), w_out, 3)
    return mixed_blocks.reshape(tok_rows, out_cols)

def solution(mesh):
    seq, chan = mesh.devices.shape
    cores = 2 if chan % 2 == 0 else 1
    split = jax.sharding.Mesh(mesh.devices.reshape(seq, chan // cores, cores), ("seq", "z", "core"))
    return jax.shard_map(
        per_device,
        mesh=split,
        in_specs=(P("seq", CHAN), P(), P(), P(None, CHAN), P(), P()),
        out_specs=P("seq", CHAN),
        check_vma=False,
    )
```

```python
import functools

import jax
import jax.numpy as jnp
from jax import lax
from jax.experimental import pallas as pl
from jax.experimental.pallas import tpu as pltpu
from jax.sharding import PartitionSpec as P

MESH = pl.DeviceIdType.MESH
CHAN = ("z", "core")
W_PIECES = 4


def chan_index():
    return lax.axis_index("z") * lax.axis_size("core") + lax.axis_index("core")


def chan_device(slab, peer):
    cores = lax.axis_size("core")
    return (slab, peer // cores, peer % cores)

HEADS = 16
FEAT = 16
HEAD_DIM = 128
BLOCK = 896


def feature_parts(rows):
    linear = rows * FEAT ** (-0.25)
    square = (rows[..., :, None] * rows[..., None, :]).reshape(rows.shape[:-1] + (FEAT * FEAT,)) * (
        2.0 * FEAT
    ) ** (-0.5)
    return (linear, square)


def exchange_kernel(count, *refs):
    xs, ys, bufs = refs[:count], refs[count : 2 * count], refs[2 * count : 3 * count]
    send_sem, recv_sem, own_sem = refs[3 * count :]
    n = xs[0].shape[0]
    me = chan_index()
    slab = lax.axis_index("seq")
    barrier = pltpu.get_barrier_semaphore()
    for step in range(1, n):
        peer = lax.rem(me + step, n)
        pl.semaphore_signal(barrier, inc=1, device_id=chan_device(slab, peer), device_id_type=MESH)
    pl.semaphore_wait(barrier, n - 1)
    owns = []
    sends = []
    for a in range(count):
        own = pltpu.make_async_copy(xs[a].at[me], bufs[a].at[me], own_sem.at[a])
        own.start()
        owns.append(own)
    for step in range(1, n):
        peer = lax.rem(me + step, n)
        for a in range(count):
            copy = pltpu.make_async_remote_copy(
                src_ref=xs[a].at[peer],
                dst_ref=bufs[a].at[me],
                send_sem=send_sem.at[a, peer],
                recv_sem=recv_sem.at[a, me],
                device_id=chan_device(slab, peer),
                device_id_type=MESH,
            )
            copy.start()
            sends.append(copy)
    for step in range(1, n):
        source = lax.rem(me + n - step, n)
        for a in range(count):
            pltpu.make_async_remote_copy(
                src_ref=xs[a].at[source],
                dst_ref=bufs[a].at[source],
                send_sem=send_sem.at[a, source],
                recv_sem=recv_sem.at[a, source],
                device_id=chan_device(slab, source),
                device_id_type=MESH,
            ).wait_recv()
    for copy in sends:
        copy.wait_send()
    for a in range(count):
        owns[a].wait()
        ys[a][...] = bufs[a][...]


def exchange_many(xs, collective_id):
    count = len(xs)
    n = xs[0].shape[0]
    return pl.pallas_call(
        functools.partial(exchange_kernel, count),
        out_shape=tuple(jax.ShapeDtypeStruct(x.shape, x.dtype) for x in xs),
        in_specs=[pl.BlockSpec(memory_space=pltpu.VMEM)] * count,
        out_specs=tuple(pl.BlockSpec(memory_space=pltpu.VMEM) for _ in xs),
        scratch_shapes=[pltpu.VMEM(x.shape, x.dtype) for x in xs]
        + [
            pltpu.SemaphoreType.DMA((count, n)),
            pltpu.SemaphoreType.DMA((count, n)),
            pltpu.SemaphoreType.DMA((count,)),
        ],
        compiler_params=pltpu.CompilerParams(collective_id=collective_id, has_side_effects=True),
    )(*xs)


def exchange(x, collective_id):
    return exchange_many((x,), collective_id)[0]


def gather_kernel(x_ref, y_ref, buf, send_sem, recv_sem):
    n = buf.shape[0]
    me = lax.axis_index("seq")
    here = (lax.axis_index("z"), lax.axis_index("core"))
    buf[...] = jnp.zeros_like(buf)
    barrier = pltpu.get_barrier_semaphore()
    for step in range(1, n):
        peer = lax.rem(me + step, n)
        pl.semaphore_signal(barrier, inc=1, device_id=(peer,) + here, device_id_type=MESH)
    pl.semaphore_wait(barrier, n - 1)

    def copy_to(peer):
        return pltpu.make_async_remote_copy(
            src_ref=x_ref,
            dst_ref=buf.at[me],
            send_sem=send_sem.at[peer],
            recv_sem=recv_sem.at[me],
            device_id=(peer,) + here,
            device_id_type=MESH,
        )

    def copy_from(source):
        return pltpu.make_async_remote_copy(
            src_ref=x_ref,
            dst_ref=buf.at[source],
            send_sem=send_sem.at[source],
            recv_sem=recv_sem.at[source],
            device_id=(source,) + here,
            device_id_type=MESH,
        )

    for step in range(1, n):
        @pl.when(me + step < n)
        def _():
            copy_to(me + step).start()

    for step in range(1, n):
        @pl.when(me - step >= 0)
        def _():
            copy_from(me - step).wait_recv()

    for step in range(1, n):
        @pl.when(me + step < n)
        def _():
            copy_to(me + step).wait_send()

    y_ref[...] = buf[...]


def gather_seq(x, slabs, collective_id):
    shape = (slabs,) + x.shape
    return pl.pallas_call(
        gather_kernel,
        out_shape=jax.ShapeDtypeStruct(shape, x.dtype),
        in_specs=[pl.BlockSpec(memory_space=pltpu.VMEM)],
        out_specs=pl.BlockSpec(memory_space=pltpu.VMEM),
        scratch_shapes=[
            pltpu.VMEM(shape, x.dtype),
            pltpu.SemaphoreType.DMA((slabs,)),
            pltpu.SemaphoreType.DMA((slabs,)),
        ],
        compiler_params=pltpu.CompilerParams(collective_id=collective_id, has_side_effects=True),
    )(x)


def scan_kernel(width, x_ref, y_ref, row_buf, col_buf, total, row_send, row_recv, col_send, col_recv):
    n = lax.axis_size("seq")
    height = n // width
    me = lax.axis_index("seq")
    row, col = me // width, me % width
    here = (lax.axis_index("z"), lax.axis_index("core"))
    row_buf[...] = jnp.zeros_like(row_buf)
    col_buf[...] = jnp.zeros_like(col_buf)
    barrier = pltpu.get_barrier_semaphore()
    for step in range(1, width):
        peer = row * width + lax.rem(col + step, width)
        pl.semaphore_signal(barrier, inc=1, device_id=(peer,) + here, device_id_type=MESH)
    for step in range(1, height):
        peer = lax.rem(row + step, height) * width + col
        pl.semaphore_signal(barrier, inc=1, device_id=(peer,) + here, device_id_type=MESH)
    pl.semaphore_wait(barrier, width + height - 2)

    def row_copy(c, slot):
        return pltpu.make_async_remote_copy(
            src_ref=x_ref,
            dst_ref=row_buf.at[slot],
            send_sem=row_send.at[c],
            recv_sem=row_recv.at[slot],
            device_id=(row * width + c,) + here,
            device_id_type=MESH,
        )

    sends = []
    for step in range(1, width):
        c = lax.rem(col + step, width)
        copy = row_copy(c, col)
        copy.start()
        sends.append(copy)
    for step in range(1, width):
        c = lax.rem(col + width - step, width)
        row_copy(c, c).wait_recv()
    mine = x_ref[...].astype(jnp.float32)
    row_total = mine
    row_prefix = jnp.zeros_like(mine)
    for c in range(width):
        part = jnp.where(c == col, 0.0, row_buf[c].astype(jnp.float32))
        row_total = row_total + part
        row_prefix = row_prefix + jnp.where(c < col, part, 0.0)
    total[...] = row_total

    def col_copy(r, slot):
        return pltpu.make_async_remote_copy(
            src_ref=total,
            dst_ref=col_buf.at[slot],
            send_sem=col_send.at[r],
            recv_sem=col_recv.at[slot],
            device_id=(r * width + col,) + here,
            device_id_type=MESH,
        )

    for step in range(1, height):
        @pl.when(row + step < height)
        def _():
            col_copy(row + step, row).start()

    for step in range(1, height):
        @pl.when(row - step >= 0)
        def _():
            col_copy(row - step, row - step).wait_recv()

    for step in range(1, height):
        @pl.when(row + step < height)
        def _():
            col_copy(row + step, row).wait_send()

    for copy in sends:
        copy.wait_send()
    prefix = row_prefix
    for r in range(height):
        prefix = prefix + col_buf[r]
    y_ref[...] = prefix


def scan_seq(x, collective_id):
    n = lax.axis_size("seq")
    width = 1
    while (width + 1) * (width + 1) <= n:
        width += 1
    while n % width:
        width -= 1
    height = n // width
    return pl.pallas_call(
        functools.partial(scan_kernel, width),
        out_shape=jax.ShapeDtypeStruct(x.shape, jnp.float32),
        in_specs=[pl.BlockSpec(memory_space=pltpu.VMEM)],
        out_specs=pl.BlockSpec(memory_space=pltpu.VMEM),
        scratch_shapes=[
            pltpu.VMEM((width,) + x.shape, x.dtype),
            pltpu.VMEM((height,) + x.shape, jnp.float32),
            pltpu.VMEM(x.shape, jnp.float32),
            pltpu.SemaphoreType.DMA((width,)),
            pltpu.SemaphoreType.DMA((width,)),
            pltpu.SemaphoreType.DMA((height,)),
            pltpu.SemaphoreType.DMA((height,)),
        ],
        compiler_params=pltpu.CompilerParams(collective_id=collective_id, has_side_effects=True),
    )(x)


def swap_kernel(x_ref, y_ref, send_sem, recv_sem):
    here = (lax.axis_index("seq"), lax.axis_index("z"))
    other = lax.axis_size("core") - 1 - lax.axis_index("core")
    barrier = pltpu.get_barrier_semaphore()
    pl.semaphore_signal(barrier, inc=1, device_id=here + (other,), device_id_type=MESH)
    pl.semaphore_wait(barrier, 1)
    copy = pltpu.make_async_remote_copy(
        src_ref=x_ref,
        dst_ref=y_ref,
        send_sem=send_sem,
        recv_sem=recv_sem,
        device_id=here + (other,),
        device_id_type=MESH,
    )
    copy.start()
    copy.wait()


def swap_cores(x, collective_id):
    return pl.pallas_call(
        swap_kernel,
        out_shape=jax.ShapeDtypeStruct(x.shape, x.dtype),
        in_specs=[pl.BlockSpec(memory_space=pl.ANY)],
        out_specs=pl.BlockSpec(memory_space=pl.ANY),
        scratch_shapes=[pltpu.SemaphoreType.DMA(()), pltpu.SemaphoreType.DMA(())],
        compiler_params=pltpu.CompilerParams(collective_id=collective_id, has_side_effects=True),
    )(x)


def opening_kernel(x_ref, w_ref, y_ref, w_all, buf, send_sem, recv_sem, own_sem, w_send, w_recv, w_own):
    n = x_ref.shape[0]
    cores = lax.axis_size("core")
    ring = n // cores
    me = chan_index()
    slab = lax.axis_index("seq")
    z = lax.axis_index("z")
    core = lax.axis_index("core")
    barrier = pltpu.get_barrier_semaphore()
    for step in range(1, n):
        peer = lax.rem(me + step, n)
        pl.semaphore_signal(barrier, inc=1, device_id=chan_device(slab, peer), device_id_type=MESH)
    pl.semaphore_wait(barrier, n - 1)
    own = pltpu.make_async_copy(x_ref.at[me], buf.at[me], own_sem)
    own.start()
    sends = []
    for step in range(1, n):
        peer = lax.rem(me + step, n)
        copy = pltpu.make_async_remote_copy(
            src_ref=x_ref.at[peer],
            dst_ref=buf.at[me],
            send_sem=send_sem.at[peer],
            recv_sem=recv_sem.at[me],
            device_id=chan_device(slab, peer),
            device_id_type=MESH,
        )
        copy.start()
        sends.append(copy)
    w_local = pltpu.make_async_copy(w_ref, w_all.at[me], w_own)
    w_local.start()
    right = (slab, lax.rem(z + 1, ring), core)
    left = (slab, lax.rem(z + ring - 1, ring), core)
    partner = (slab, z, cores - 1 - core)

    pieces = W_PIECES
    depth = w_ref.shape[0] // pieces

    def slot(origin):
        return lax.rem(origin + ring, ring) * cores + core

    def held(h, j):
        return w_all.at[h, pl.ds(j * depth, depth)]

    def send(source, h, j, kind, target):
        copy = pltpu.make_async_remote_copy(
            src_ref=source,
            dst_ref=held(h, j),
            send_sem=w_send.at[h, kind, j],
            recv_sem=w_recv.at[h, j],
            device_id=target,
            device_id_type=MESH,
        )
        copy.start()
        sends.append(copy)

    def arrive(h, j, source):
        pltpu.make_async_remote_copy(
            src_ref=w_ref.at[pl.ds(j * depth, depth)],
            dst_ref=held(h, j),
            send_sem=w_send.at[h, 0, j],
            recv_sem=w_recv.at[h, j],
            device_id=source,
            device_id_type=MESH,
        ).wait_recv()

    half = ring // 2
    full = half - 1 if ring % 2 == 0 else half

    def goes_right(step):
        return range(pieces) if step <= full else range(pieces // 2) if step == half else range(0)

    def goes_left(step):
        return range(pieces) if step <= full else range(pieces // 2, pieces) if step == half else range(0)

    for j in range(pieces):
        mine = w_ref.at[pl.ds(j * depth, depth)]
        if j in goes_right(1):
            send(mine, me, j, 0, right)
        if j in goes_left(1):
            send(mine, me, j, 1, left)
        send(mine, me, j, 2, partner)
    for step in range(1, half + 1):
        for j in range(pieces):
            if j in goes_right(step):
                h = slot(z - step)
                arrive(h, j, left)
                if j in goes_right(step + 1):
                    send(held(h, j), h, j, 0, right)
                send(held(h, j), h, j, 2, partner)
            if j in goes_left(step):
                h = slot(z + step)
                arrive(h, j, right)
                if j in goes_left(step + 1):
                    send(held(h, j), h, j, 1, left)
                send(held(h, j), h, j, 2, partner)
    for origin in range(ring):
        for j in range(pieces):
            arrive(origin * cores + (cores - 1 - core), j, partner)
    for step in range(1, n):
        source = lax.rem(me + n - step, n)
        pltpu.make_async_remote_copy(
            src_ref=x_ref.at[source],
            dst_ref=buf.at[source],
            send_sem=send_sem.at[source],
            recv_sem=recv_sem.at[source],
            device_id=chan_device(slab, source),
            device_id_type=MESH,
        ).wait_recv()
    for copy in sends:
        copy.wait_send()
    own.wait()
    w_local.wait()
    y_ref[...] = buf[...]


def opening(x, w, collective_id):
    n = x.shape[0]
    return pl.pallas_call(
        opening_kernel,
        out_shape=(
            jax.ShapeDtypeStruct(x.shape, x.dtype),
            jax.ShapeDtypeStruct((n,) + w.shape, w.dtype),
        ),
        in_specs=[pl.BlockSpec(memory_space=pltpu.VMEM), pl.BlockSpec(memory_space=pl.ANY)],
        out_specs=(pl.BlockSpec(memory_space=pltpu.VMEM), pl.BlockSpec(memory_space=pl.ANY)),
        scratch_shapes=[
            pltpu.VMEM(x.shape, x.dtype),
            pltpu.SemaphoreType.DMA((n,)),
            pltpu.SemaphoreType.DMA((n,)),
            pltpu.SemaphoreType.DMA(()),
            pltpu.SemaphoreType.DMA((n, 3, W_PIECES)),
            pltpu.SemaphoreType.DMA((n, W_PIECES)),
            pltpu.SemaphoreType.DMA(()),
        ],
        compiler_params=pltpu.CompilerParams(collective_id=collective_id, has_side_effects=True),
    )(x, w)


def split_rows(x, groups, collective_id):
    rows, cols = x.shape
    got = exchange(x.reshape(groups, rows // groups, cols), collective_id)
    return got.transpose(1, 0, 2).reshape(rows // groups, groups * cols)


def split_cols(x, groups, collective_id):
    rows, _, cols = x.shape
    got = exchange(x.transpose(1, 0, 2), collective_id)
    return got.reshape(groups * rows, cols)


def closing_kernel(x_ref, w_ref, y_ref, got, rows, out, back, send_sem, recv_sem, own_sem):
    n = x_ref.shape[0]
    cols = out.shape[2]
    me = chan_index()
    slab = lax.axis_index("seq")
    barrier = pltpu.get_barrier_semaphore()
    for step in range(1, n):
        peer = lax.rem(me + step, n)
        pl.semaphore_signal(barrier, inc=1, device_id=chan_device(slab, peer), device_id_type=MESH)
    pl.semaphore_wait(barrier, n - 1)

    def remote(phase, src, dst, peer, sender):
        return pltpu.make_async_remote_copy(
            src_ref=src,
            dst_ref=dst,
            send_sem=send_sem.at[phase, peer],
            recv_sem=recv_sem.at[phase, sender],
            device_id=chan_device(slab, peer),
            device_id_type=MESH,
        )

    sends = []
    for phase, (source, landing) in enumerate(((x_ref, got), (out, back))):
        own = pltpu.make_async_copy(source.at[me], landing.at[me], own_sem.at[phase])
        if phase == 1:
            hidden_rows = rows[...]
            for step in range(n):
                c = lax.rem(me + step, n)
                block = w_ref[:, pl.ds(pl.multiple_of(c * cols, cols), cols)]
                out[c] = jnp.dot(hidden_rows, block, preferred_element_type=jnp.float32).astype(out.dtype)
                if step == 0:
                    own.start()
                else:
                    copy = remote(phase, out.at[c], back.at[me], c, me)
                    copy.start()
                    sends.append(copy)
        else:
            own.start()
            for step in range(1, n):
                peer = lax.rem(me + step, n)
                copy = remote(phase, x_ref.at[peer], got.at[me], peer, me)
                copy.start()
                sends.append(copy)
        for step in range(1, n):
            source_dev = lax.rem(me + n - step, n)
            remote(phase, source.at[source_dev], landing.at[source_dev], source_dev, source_dev).wait_recv()
        own.wait()
        if phase == 0:
            width = got.shape[2]
            for g in range(n):
                rows[:, g * width : (g + 1) * width] = got[g]
    for copy in sends:
        copy.wait_send()
    y_ref[...] = back[...]


def closing(hidden_blocks, w_out, collective_id):
    n, chunk, width = hidden_blocks.shape
    cols = w_out.shape[1] // n
    block = (n, chunk, cols)
    return pl.pallas_call(
        closing_kernel,
        out_shape=jax.ShapeDtypeStruct(block, hidden_blocks.dtype),
        in_specs=[pl.BlockSpec(memory_space=pltpu.VMEM)] * 2,
        out_specs=pl.BlockSpec(memory_space=pltpu.VMEM),
        scratch_shapes=[
            pltpu.VMEM(hidden_blocks.shape, hidden_blocks.dtype),
            pltpu.VMEM((chunk, n * width), hidden_blocks.dtype),
            pltpu.VMEM(block, hidden_blocks.dtype),
            pltpu.VMEM(block, hidden_blocks.dtype),
            pltpu.SemaphoreType.DMA((2, n)),
            pltpu.SemaphoreType.DMA((2, n)),
            pltpu.SemaphoreType.DMA((2,)),
        ],
        compiler_params=pltpu.CompilerParams(
            collective_id=collective_id, has_side_effects=True, vmem_limit_bytes=48 * 1024 * 1024
        ),
    )(hidden_blocks, w_out)


def middle_kernel(rows_ref, w_ref, wq_ref, wk_ref, qk_out, v_out, qk_send, v_send, qk_got, v_got, q_all, k_all, send_sem, recv_sem, own_sem):
    n = w_ref.shape[0]
    me = chan_index()
    slab = lax.axis_index("seq")
    barrier = pltpu.get_barrier_semaphore()
    for step in range(1, n):
        peer = lax.rem(me + step, n)
        pl.semaphore_signal(barrier, inc=1, device_id=chan_device(slab, peer), device_id_type=MESH)
    pl.semaphore_wait(barrier, n - 1)
    pairs = ((qk_send, qk_got), (v_send, v_got))

    def remote(kind, peer, sender, slot):
        source, landing = pairs[kind]
        return pltpu.make_async_remote_copy(
            src_ref=source.at[slot],
            dst_ref=landing.at[sender],
            send_sem=send_sem.at[kind, peer],
            recv_sem=recv_sem.at[kind, sender],
            device_id=chan_device(slab, peer),
            device_id_type=MESH,
        )

    rows = rows_ref[...]
    pf = qk_send.shape[1] // 2
    q_all[...] = jnp.dot(rows, wq_ref[...], preferred_element_type=jnp.float32).T
    k_all[...] = jnp.dot(rows, wk_ref[...], preferred_element_type=jnp.float32).T
    owns = []
    sends = []
    for step in range(n):
        g = lax.rem(me + step, n)
        v_send[g] = jnp.dot(rows, w_ref[g], preferred_element_type=jnp.float32).astype(v_send.dtype)
        head = pl.ds(pl.multiple_of(g * pf, pf), pf)
        qk_send[g, :pf, :] = q_all[head, :].astype(qk_send.dtype)
        qk_send[g, pf:, :] = k_all[head, :].astype(qk_send.dtype)
        for kind in range(2):
            source, landing = pairs[kind]
            if step == 0:
                own = pltpu.make_async_copy(source.at[me], landing.at[me], own_sem.at[kind])
                own.start()
                owns.append(own)
            else:
                copy = remote(kind, g, me, g)
                copy.start()
                sends.append(copy)
    for step in range(1, n):
        source_dev = lax.rem(me + n - step, n)
        for kind in range(2):
            remote(kind, source_dev, source_dev, source_dev).wait_recv()
    for own in owns:
        own.wait()
    for copy in sends:
        copy.wait_send()
    qk_out[...] = qk_got[...]
    v_out[...] = v_got[...]


def middle(rows, w_all, w_query, w_key, collective_id):
    n = w_all.shape[0]
    chunk = rows.shape[0]
    qk_shape = (n, 2 * w_query.shape[1] // n, chunk)
    v_shape = (n, chunk, w_all.shape[2])
    return pl.pallas_call(
        middle_kernel,
        out_shape=(
            jax.ShapeDtypeStruct(qk_shape, rows.dtype),
            jax.ShapeDtypeStruct(v_shape, rows.dtype),
        ),
        in_specs=[pl.BlockSpec(memory_space=pltpu.VMEM)] * 4,
        out_specs=(pl.BlockSpec(memory_space=pltpu.VMEM), pl.BlockSpec(memory_space=pltpu.VMEM)),
        scratch_shapes=[
            pltpu.VMEM(qk_shape, rows.dtype),
            pltpu.VMEM(v_shape, rows.dtype),
            pltpu.VMEM(qk_shape, rows.dtype),
            pltpu.VMEM(v_shape, rows.dtype),
            pltpu.VMEM((w_query.shape[1], chunk), jnp.float32),
            pltpu.VMEM((w_key.shape[1], chunk), jnp.float32),
            pltpu.SemaphoreType.DMA((2, n)),
            pltpu.SemaphoreType.DMA((2, n)),
            pltpu.SemaphoreType.DMA((2,)),
        ],
        compiler_params=pltpu.CompilerParams(
            collective_id=collective_id, has_side_effects=True, vmem_limit_bytes=48 * 1024 * 1024
        ),
    )(rows, w_all, w_query, w_key)


def attend(query_rows, key_rows, value_rows, gain_mine, my_slab):
    highest = lax.Precision.HIGH
    tok_rows, per_group, _ = value_rows.shape
    blocks = tok_rows // BLOCK
    query_blocks = query_rows.reshape(blocks, BLOCK, per_group, FEAT)
    key_blocks = key_rows.reshape(blocks, BLOCK, per_group, FEAT)
    value_blocks = value_rows.reshape(blocks, BLOCK, per_group, HEAD_DIM)
    value_f32 = value_blocks.astype(jnp.float32)
    key_linear, key_square = feature_parts(key_blocks.astype(jnp.float32))
    own_zero = jnp.sum(value_f32, axis=1)[:, :, None, :]
    own_one = jnp.einsum("bthf,bthe->bhfe", key_linear, value_f32, precision=highest)
    own_two = jnp.einsum("bthf,bthe->bhfe", key_square, value_f32, precision=highest)
    own = jnp.concatenate([own_zero, own_one, own_two], axis=2)
    slab_total = jnp.sum(own, axis=0)
    state_rows = slab_total.shape[0] * slab_total.shape[1]
    prefix = scan_seq(slab_total.astype(jnp.bfloat16).reshape(state_rows, HEAD_DIM), 7).reshape(slab_total.shape)
    earlier = jnp.concatenate([jnp.zeros_like(own[:1]), jnp.cumsum(own, axis=0)[:-1]], axis=0) + prefix[None]
    query_linear, query_square = feature_parts(query_blocks.astype(jnp.float32))
    inter = earlier[:, :, 0][:, None] + jnp.einsum(
        "bthf,bhfe->bthe", query_linear, earlier[:, :, 1 : 1 + FEAT], precision=highest
    )
    inter = inter + jnp.einsum(
        "bthf,bhfe->bthe", query_square, earlier[:, :, 1 + FEAT :], precision=highest
    )
    scores = jnp.einsum(
        "bthf,bshf->bhts", query_blocks, key_blocks, preferred_element_type=jnp.float32
    ) * FEAT ** (-0.5)
    kernel = 1.0 + scores + 0.5 * scores * scores
    causal = jnp.arange(BLOCK)[:, None] >= jnp.arange(BLOCK)[None, :]
    weights = jnp.where(causal, kernel, 0.0).astype(jnp.bfloat16)
    intra = jnp.einsum("bhts,bshe->bthe", weights, value_blocks, preferred_element_type=jnp.float32)
    numerator = (intra + inter).reshape(tok_rows, per_group, HEAD_DIM)
    mean_square = jnp.mean(numerator * numerator, axis=-1, keepdims=True)
    hidden = (numerator * lax.rsqrt(mean_square + 1e-05) * gain_mine).astype(jnp.bfloat16)
    return hidden.reshape(tok_rows, per_group * HEAD_DIM)


def per_device(tokens, w_query, w_key, w_value, w_out, gain):
    groups = lax.axis_size(CHAN)
    per_group = HEADS // groups
    my_group = chan_index()
    my_slab = lax.axis_index("seq")
    tok_rows_total, tok_cols = tokens.shape
    got, value_all = opening(tokens.reshape(groups, tok_rows_total // groups, tok_cols), w_value, 1)
    rows = got.transpose(1, 0, 2).reshape(tok_rows_total // groups, groups * tok_cols)
    chunk = rows.shape[0]
    pf = per_group * FEAT
    d_model = w_query.shape[0]
    qk_got, value_got = middle(rows, value_all, w_query, w_key, 2)
    tok_rows = groups * chunk
    qk_rows = qk_got.transpose(0, 2, 1).reshape(tok_rows, 2 * pf)
    query_rows = qk_rows[:, :pf].reshape(tok_rows, per_group, FEAT)
    key_rows = qk_rows[:, pf:].reshape(tok_rows, per_group, FEAT)
    value_rows = value_got.reshape(tok_rows, per_group, HEAD_DIM)
    value_cols = per_group * HEAD_DIM
    gain_mine = lax.dynamic_slice_in_dim(gain, my_group * value_cols, value_cols, 0).reshape(
        per_group, HEAD_DIM
    )
    hidden = attend(query_rows, key_rows, value_rows, gain_mine, my_slab)
    out_cols = w_out.shape[1] // groups
    mixed_blocks = closing(hidden.reshape(groups, chunk, per_group * HEAD_DIM), w_out, 3)
    return mixed_blocks.reshape(tok_rows, out_cols)

def solution(mesh):
    seq, chan = mesh.devices.shape
    cores = 2 if chan % 2 == 0 else 1
    split = jax.sharding.Mesh(mesh.devices.reshape(seq, chan // cores, cores), ("seq", "z", "core"))
    return jax.shard_map(
        per_device,
        mesh=split,
        in_specs=(P("seq", CHAN), P(), P(), P(None, CHAN), P(), P()),
        out_specs=P("seq", CHAN),
        check_vma=False,
    )
```

```python
import functools

import jax
import jax.numpy as jnp
from jax import lax
from jax.experimental import pallas as pl
from jax.experimental.pallas import tpu as pltpu
from jax.sharding import PartitionSpec as P

MESH = pl.DeviceIdType.MESH
CHAN = ("z", "core")
W_PIECES = 4


def chan_index():
    return lax.axis_index("z") * lax.axis_size("core") + lax.axis_index("core")


def chan_device(slab, peer):
    cores = lax.axis_size("core")
    return (slab, peer // cores, peer % cores)

HEADS = 16
FEAT = 16
HEAD_DIM = 128
BLOCK = 896


def feature_parts(rows):
    linear = rows * FEAT ** (-0.25)
    square = (rows[..., :, None] * rows[..., None, :]).reshape(rows.shape[:-1] + (FEAT * FEAT,)) * (
        2.0 * FEAT
    ) ** (-0.5)
    return (linear, square)


def exchange_kernel(count, *refs):
    xs, ys, bufs = refs[:count], refs[count : 2 * count], refs[2 * count : 3 * count]
    send_sem, recv_sem, own_sem = refs[3 * count :]
    n = xs[0].shape[0]
    me = chan_index()
    slab = lax.axis_index("seq")
    barrier = pltpu.get_barrier_semaphore()
    for step in range(1, n):
        peer = lax.rem(me + step, n)
        pl.semaphore_signal(barrier, inc=1, device_id=chan_device(slab, peer), device_id_type=MESH)
    pl.semaphore_wait(barrier, n - 1)
    owns = []
    sends = []
    for a in range(count):
        own = pltpu.make_async_copy(xs[a].at[me], bufs[a].at[me], own_sem.at[a])
        own.start()
        owns.append(own)
    for step in range(1, n):
        peer = lax.rem(me + step, n)
        for a in range(count):
            copy = pltpu.make_async_remote_copy(
                src_ref=xs[a].at[peer],
                dst_ref=bufs[a].at[me],
                send_sem=send_sem.at[a, peer],
                recv_sem=recv_sem.at[a, me],
                device_id=chan_device(slab, peer),
                device_id_type=MESH,
            )
            copy.start()
            sends.append(copy)
    for step in range(1, n):
        source = lax.rem(me + n - step, n)
        for a in range(count):
            pltpu.make_async_remote_copy(
                src_ref=xs[a].at[source],
                dst_ref=bufs[a].at[source],
                send_sem=send_sem.at[a, source],
                recv_sem=recv_sem.at[a, source],
                device_id=chan_device(slab, source),
                device_id_type=MESH,
            ).wait_recv()
    for copy in sends:
        copy.wait_send()
    for a in range(count):
        owns[a].wait()
        ys[a][...] = bufs[a][...]


def exchange_many(xs, collective_id):
    count = len(xs)
    n = xs[0].shape[0]
    return pl.pallas_call(
        functools.partial(exchange_kernel, count),
        out_shape=tuple(jax.ShapeDtypeStruct(x.shape, x.dtype) for x in xs),
        in_specs=[pl.BlockSpec(memory_space=pltpu.VMEM)] * count,
        out_specs=tuple(pl.BlockSpec(memory_space=pltpu.VMEM) for _ in xs),
        scratch_shapes=[pltpu.VMEM(x.shape, x.dtype) for x in xs]
        + [
            pltpu.SemaphoreType.DMA((count, n)),
            pltpu.SemaphoreType.DMA((count, n)),
            pltpu.SemaphoreType.DMA((count,)),
        ],
        compiler_params=pltpu.CompilerParams(collective_id=collective_id, has_side_effects=True),
    )(*xs)


def exchange(x, collective_id):
    return exchange_many((x,), collective_id)[0]


def gather_kernel(x_ref, y_ref, buf, send_sem, recv_sem):
    n = buf.shape[0]
    me = lax.axis_index("seq")
    here = (lax.axis_index("z"), lax.axis_index("core"))
    buf[...] = jnp.zeros_like(buf)
    barrier = pltpu.get_barrier_semaphore()
    for step in range(1, n):
        peer = lax.rem(me + step, n)
        pl.semaphore_signal(barrier, inc=1, device_id=(peer,) + here, device_id_type=MESH)
    pl.semaphore_wait(barrier, n - 1)

    def copy_to(peer):
        return pltpu.make_async_remote_copy(
            src_ref=x_ref,
            dst_ref=buf.at[me],
            send_sem=send_sem.at[peer],
            recv_sem=recv_sem.at[me],
            device_id=(peer,) + here,
            device_id_type=MESH,
        )

    def copy_from(source):
        return pltpu.make_async_remote_copy(
            src_ref=x_ref,
            dst_ref=buf.at[source],
            send_sem=send_sem.at[source],
            recv_sem=recv_sem.at[source],
            device_id=(source,) + here,
            device_id_type=MESH,
        )

    for step in range(1, n):
        @pl.when(me + step < n)
        def _():
            copy_to(me + step).start()

    for step in range(1, n):
        @pl.when(me - step >= 0)
        def _():
            copy_from(me - step).wait_recv()

    for step in range(1, n):
        @pl.when(me + step < n)
        def _():
            copy_to(me + step).wait_send()

    y_ref[...] = buf[...]


def gather_seq(x, slabs, collective_id):
    shape = (slabs,) + x.shape
    return pl.pallas_call(
        gather_kernel,
        out_shape=jax.ShapeDtypeStruct(shape, x.dtype),
        in_specs=[pl.BlockSpec(memory_space=pltpu.VMEM)],
        out_specs=pl.BlockSpec(memory_space=pltpu.VMEM),
        scratch_shapes=[
            pltpu.VMEM(shape, x.dtype),
            pltpu.SemaphoreType.DMA((slabs,)),
            pltpu.SemaphoreType.DMA((slabs,)),
        ],
        compiler_params=pltpu.CompilerParams(collective_id=collective_id, has_side_effects=True),
    )(x)


def scan_kernel(width, x_ref, y_ref, row_buf, col_buf, total, row_send, row_recv, col_send, col_recv):
    n = lax.axis_size("seq")
    height = n // width
    me = lax.axis_index("seq")
    row, col = me // width, me % width
    here = (lax.axis_index("z"), lax.axis_index("core"))
    row_buf[...] = jnp.zeros_like(row_buf)
    col_buf[...] = jnp.zeros_like(col_buf)
    barrier = pltpu.get_barrier_semaphore()
    for step in range(1, width):
        peer = row * width + lax.rem(col + step, width)
        pl.semaphore_signal(barrier, inc=1, device_id=(peer,) + here, device_id_type=MESH)
    for step in range(1, height):
        peer = lax.rem(row + step, height) * width + col
        pl.semaphore_signal(barrier, inc=1, device_id=(peer,) + here, device_id_type=MESH)
    pl.semaphore_wait(barrier, width + height - 2)

    def row_copy(c, slot):
        return pltpu.make_async_remote_copy(
            src_ref=x_ref,
            dst_ref=row_buf.at[slot],
            send_sem=row_send.at[c],
            recv_sem=row_recv.at[slot],
            device_id=(row * width + c,) + here,
            device_id_type=MESH,
        )

    sends = []
    for step in range(1, width):
        c = lax.rem(col + step, width)
        copy = row_copy(c, col)
        copy.start()
        sends.append(copy)
    for step in range(1, width):
        c = lax.rem(col + width - step, width)
        row_copy(c, c).wait_recv()
    mine = x_ref[...].astype(jnp.float32)
    row_total = mine
    row_prefix = jnp.zeros_like(mine)
    for c in range(width):
        part = jnp.where(c == col, 0.0, row_buf[c].astype(jnp.float32))
        row_total = row_total + part
        row_prefix = row_prefix + jnp.where(c < col, part, 0.0)
    total[...] = row_total

    def col_copy(r, slot):
        return pltpu.make_async_remote_copy(
            src_ref=total,
            dst_ref=col_buf.at[slot],
            send_sem=col_send.at[r],
            recv_sem=col_recv.at[slot],
            device_id=(r * width + col,) + here,
            device_id_type=MESH,
        )

    for step in range(1, height):
        @pl.when(row + step < height)
        def _():
            col_copy(row + step, row).start()

    for step in range(1, height):
        @pl.when(row - step >= 0)
        def _():
            col_copy(row - step, row - step).wait_recv()

    for step in range(1, height):
        @pl.when(row + step < height)
        def _():
            col_copy(row + step, row).wait_send()

    for copy in sends:
        copy.wait_send()
    prefix = row_prefix
    for r in range(height):
        prefix = prefix + col_buf[r]
    y_ref[...] = prefix


def scan_seq(x, collective_id):
    n = lax.axis_size("seq")
    width = 1
    while (width + 1) * (width + 1) <= n:
        width += 1
    while n % width:
        width -= 1
    height = n // width
    return pl.pallas_call(
        functools.partial(scan_kernel, width),
        out_shape=jax.ShapeDtypeStruct(x.shape, jnp.float32),
        in_specs=[pl.BlockSpec(memory_space=pltpu.VMEM)],
        out_specs=pl.BlockSpec(memory_space=pltpu.VMEM),
        scratch_shapes=[
            pltpu.VMEM((width,) + x.shape, x.dtype),
            pltpu.VMEM((height,) + x.shape, jnp.float32),
            pltpu.VMEM(x.shape, jnp.float32),
            pltpu.SemaphoreType.DMA((width,)),
            pltpu.SemaphoreType.DMA((width,)),
            pltpu.SemaphoreType.DMA((height,)),
            pltpu.SemaphoreType.DMA((height,)),
        ],
        compiler_params=pltpu.CompilerParams(collective_id=collective_id, has_side_effects=True),
    )(x)


def swap_kernel(x_ref, y_ref, send_sem, recv_sem):
    here = (lax.axis_index("seq"), lax.axis_index("z"))
    other = lax.axis_size("core") - 1 - lax.axis_index("core")
    barrier = pltpu.get_barrier_semaphore()
    pl.semaphore_signal(barrier, inc=1, device_id=here + (other,), device_id_type=MESH)
    pl.semaphore_wait(barrier, 1)
    copy = pltpu.make_async_remote_copy(
        src_ref=x_ref,
        dst_ref=y_ref,
        send_sem=send_sem,
        recv_sem=recv_sem,
        device_id=here + (other,),
        device_id_type=MESH,
    )
    copy.start()
    copy.wait()


def swap_cores(x, collective_id):
    return pl.pallas_call(
        swap_kernel,
        out_shape=jax.ShapeDtypeStruct(x.shape, x.dtype),
        in_specs=[pl.BlockSpec(memory_space=pl.ANY)],
        out_specs=pl.BlockSpec(memory_space=pl.ANY),
        scratch_shapes=[pltpu.SemaphoreType.DMA(()), pltpu.SemaphoreType.DMA(())],
        compiler_params=pltpu.CompilerParams(collective_id=collective_id, has_side_effects=True),
    )(x)


def opening_kernel(x_ref, w_ref, y_ref, w_all, buf, send_sem, recv_sem, own_sem, w_send, w_recv, w_own):
    n = x_ref.shape[0]
    cores = lax.axis_size("core")
    ring = n // cores
    me = chan_index()
    slab = lax.axis_index("seq")
    z = lax.axis_index("z")
    core = lax.axis_index("core")
    barrier = pltpu.get_barrier_semaphore()
    for step in range(1, n):
        peer = lax.rem(me + step, n)
        pl.semaphore_signal(barrier, inc=1, device_id=chan_device(slab, peer), device_id_type=MESH)
    pl.semaphore_wait(barrier, n - 1)
    own = pltpu.make_async_copy(x_ref.at[me], buf.at[me], own_sem)
    own.start()
    sends = []
    for step in range(1, n):
        peer = lax.rem(me + step, n)
        copy = pltpu.make_async_remote_copy(
            src_ref=x_ref.at[peer],
            dst_ref=buf.at[me],
            send_sem=send_sem.at[peer],
            recv_sem=recv_sem.at[me],
            device_id=chan_device(slab, peer),
            device_id_type=MESH,
        )
        copy.start()
        sends.append(copy)
    w_local = pltpu.make_async_copy(w_ref, w_all.at[me], w_own)
    w_local.start()
    right = (slab, lax.rem(z + 1, ring), core)
    left = (slab, lax.rem(z + ring - 1, ring), core)
    partner = (slab, z, cores - 1 - core)

    pieces = W_PIECES
    depth = w_ref.shape[0] // pieces

    def slot(origin):
        return lax.rem(origin + ring, ring) * cores + core

    def held(h, j):
        return w_all.at[h, pl.ds(j * depth, depth)]

    def send(source, h, j, kind, target):
        copy = pltpu.make_async_remote_copy(
            src_ref=source,
            dst_ref=held(h, j),
            send_sem=w_send.at[h, kind, j],
            recv_sem=w_recv.at[h, j],
            device_id=target,
            device_id_type=MESH,
        )
        copy.start()
        sends.append(copy)

    def arrive(h, j, source):
        pltpu.make_async_remote_copy(
            src_ref=w_ref.at[pl.ds(j * depth, depth)],
            dst_ref=held(h, j),
            send_sem=w_send.at[h, 0, j],
            recv_sem=w_recv.at[h, j],
            device_id=source,
            device_id_type=MESH,
        ).wait_recv()

    half = ring // 2
    full = half - 1 if ring % 2 == 0 else half

    def goes_right(step):
        return range(pieces) if step <= full else range(pieces // 2) if step == half else range(0)

    def goes_left(step):
        return range(pieces) if step <= full else range(pieces // 2, pieces) if step == half else range(0)

    for j in range(pieces):
        mine = w_ref.at[pl.ds(j * depth, depth)]
        if j in goes_right(1):
            send(mine, me, j, 0, right)
        if j in goes_left(1):
            send(mine, me, j, 1, left)
        send(mine, me, j, 2, partner)
    for step in range(1, half + 1):
        for j in range(pieces):
            if j in goes_right(step):
                h = slot(z - step)
                arrive(h, j, left)
                if j in goes_right(step + 1):
                    send(held(h, j), h, j, 0, right)
                send(held(h, j), h, j, 2, partner)
            if j in goes_left(step):
                h = slot(z + step)
                arrive(h, j, right)
                if j in goes_left(step + 1):
                    send(held(h, j), h, j, 1, left)
                send(held(h, j), h, j, 2, partner)
    for origin in range(ring):
        for j in range(pieces):
            arrive(origin * cores + (cores - 1 - core), j, partner)
    for step in range(1, n):
        source = lax.rem(me + n - step, n)
        pltpu.make_async_remote_copy(
            src_ref=x_ref.at[source],
            dst_ref=buf.at[source],
            send_sem=send_sem.at[source],
            recv_sem=recv_sem.at[source],
            device_id=chan_device(slab, source),
            device_id_type=MESH,
        ).wait_recv()
    for copy in sends:
        copy.wait_send()
    own.wait()
    w_local.wait()
    y_ref[...] = buf[...]


def opening(x, w, collective_id):
    n = x.shape[0]
    return pl.pallas_call(
        opening_kernel,
        out_shape=(
            jax.ShapeDtypeStruct(x.shape, x.dtype),
            jax.ShapeDtypeStruct((n,) + w.shape, w.dtype),
        ),
        in_specs=[pl.BlockSpec(memory_space=pltpu.VMEM), pl.BlockSpec(memory_space=pl.ANY)],
        out_specs=(pl.BlockSpec(memory_space=pltpu.VMEM), pl.BlockSpec(memory_space=pl.ANY)),
        scratch_shapes=[
            pltpu.VMEM(x.shape, x.dtype),
            pltpu.SemaphoreType.DMA((n,)),
            pltpu.SemaphoreType.DMA((n,)),
            pltpu.SemaphoreType.DMA(()),
            pltpu.SemaphoreType.DMA((n, 3, W_PIECES)),
            pltpu.SemaphoreType.DMA((n, W_PIECES)),
            pltpu.SemaphoreType.DMA(()),
        ],
        compiler_params=pltpu.CompilerParams(collective_id=collective_id, has_side_effects=True),
    )(x, w)


def split_rows(x, groups, collective_id):
    rows, cols = x.shape
    got = exchange(x.reshape(groups, rows // groups, cols), collective_id)
    return got.transpose(1, 0, 2).reshape(rows // groups, groups * cols)


def split_cols(x, groups, collective_id):
    rows, _, cols = x.shape
    got = exchange(x.transpose(1, 0, 2), collective_id)
    return got.reshape(groups * rows, cols)


def closing_kernel(x_ref, w_ref, y_ref, got, rows, out, back, send_sem, recv_sem, own_sem):
    n = x_ref.shape[0]
    cols = out.shape[2]
    me = chan_index()
    slab = lax.axis_index("seq")
    barrier = pltpu.get_barrier_semaphore()
    for step in range(1, n):
        peer = lax.rem(me + step, n)
        pl.semaphore_signal(barrier, inc=1, device_id=chan_device(slab, peer), device_id_type=MESH)
    pl.semaphore_wait(barrier, n - 1)

    def remote(phase, src, dst, peer, sender):
        return pltpu.make_async_remote_copy(
            src_ref=src,
            dst_ref=dst,
            send_sem=send_sem.at[phase, peer],
            recv_sem=recv_sem.at[phase, sender],
            device_id=chan_device(slab, peer),
            device_id_type=MESH,
        )

    sends = []
    for phase, (source, landing) in enumerate(((x_ref, got), (out, back))):
        own = pltpu.make_async_copy(source.at[me], landing.at[me], own_sem.at[phase])
        if phase == 1:
            hidden_rows = rows[...]
            for step in range(n):
                c = lax.rem(me + step, n)
                block = w_ref[:, pl.ds(pl.multiple_of(c * cols, cols), cols)]
                out[c] = jnp.dot(hidden_rows, block, preferred_element_type=jnp.float32).astype(out.dtype)
                if step == 0:
                    own.start()
                else:
                    copy = remote(phase, out.at[c], back.at[me], c, me)
                    copy.start()
                    sends.append(copy)
        else:
            own.start()
            for step in range(1, n):
                peer = lax.rem(me + step, n)
                copy = remote(phase, x_ref.at[peer], got.at[me], peer, me)
                copy.start()
                sends.append(copy)
        for step in range(1, n):
            source_dev = lax.rem(me + n - step, n)
            remote(phase, source.at[source_dev], landing.at[source_dev], source_dev, source_dev).wait_recv()
        own.wait()
        if phase == 0:
            width = got.shape[2]
            for g in range(n):
                rows[:, g * width : (g + 1) * width] = got[g]
    for copy in sends:
        copy.wait_send()
    y_ref[...] = back[...]


def closing(hidden_blocks, w_out, collective_id):
    n, chunk, width = hidden_blocks.shape
    cols = w_out.shape[1] // n
    block = (n, chunk, cols)
    return pl.pallas_call(
        closing_kernel,
        out_shape=jax.ShapeDtypeStruct(block, hidden_blocks.dtype),
        in_specs=[pl.BlockSpec(memory_space=pltpu.VMEM)] * 2,
        out_specs=pl.BlockSpec(memory_space=pltpu.VMEM),
        scratch_shapes=[
            pltpu.VMEM(hidden_blocks.shape, hidden_blocks.dtype),
            pltpu.VMEM((chunk, n * width), hidden_blocks.dtype),
            pltpu.VMEM(block, hidden_blocks.dtype),
            pltpu.VMEM(block, hidden_blocks.dtype),
            pltpu.SemaphoreType.DMA((2, n)),
            pltpu.SemaphoreType.DMA((2, n)),
            pltpu.SemaphoreType.DMA((2,)),
        ],
        compiler_params=pltpu.CompilerParams(
            collective_id=collective_id, has_side_effects=True, vmem_limit_bytes=48 * 1024 * 1024
        ),
    )(hidden_blocks, w_out)


def middle_kernel(rows_ref, w_ref, wq_ref, wk_ref, qk_out, v_out, qk_send, v_send, qk_got, v_got, q_all, k_all, send_sem, recv_sem, own_sem):
    n = w_ref.shape[0]
    me = chan_index()
    slab = lax.axis_index("seq")
    barrier = pltpu.get_barrier_semaphore()
    for step in range(1, n):
        peer = lax.rem(me + step, n)
        pl.semaphore_signal(barrier, inc=1, device_id=chan_device(slab, peer), device_id_type=MESH)
    pl.semaphore_wait(barrier, n - 1)
    pairs = ((qk_send, qk_got), (v_send, v_got))

    def remote(kind, peer, sender, slot):
        source, landing = pairs[kind]
        return pltpu.make_async_remote_copy(
            src_ref=source.at[slot],
            dst_ref=landing.at[sender],
            send_sem=send_sem.at[kind, peer],
            recv_sem=recv_sem.at[kind, sender],
            device_id=chan_device(slab, peer),
            device_id_type=MESH,
        )

    rows = rows_ref[...]
    pf = qk_send.shape[1] // 2
    q_all[...] = jnp.dot(rows, wq_ref[...], preferred_element_type=jnp.float32).T
    k_all[...] = jnp.dot(rows, wk_ref[...], preferred_element_type=jnp.float32).T
    owns = []
    sends = []
    for step in range(n):
        g = lax.rem(me + step, n)
        v_send[g] = jnp.dot(rows, w_ref[g], preferred_element_type=jnp.float32).astype(v_send.dtype)
        head = pl.ds(pl.multiple_of(g * pf, pf), pf)
        qk_send[g, :pf, :] = q_all[head, :].astype(qk_send.dtype)
        qk_send[g, pf:, :] = k_all[head, :].astype(qk_send.dtype)
        for kind in range(2):
            source, landing = pairs[kind]
            if step == 0:
                own = pltpu.make_async_copy(source.at[me], landing.at[me], own_sem.at[kind])
                own.start()
                owns.append(own)
            else:
                copy = remote(kind, g, me, g)
                copy.start()
                sends.append(copy)
    for step in range(1, n):
        source_dev = lax.rem(me + n - step, n)
        for kind in range(2):
            remote(kind, source_dev, source_dev, source_dev).wait_recv()
    for own in owns:
        own.wait()
    for copy in sends:
        copy.wait_send()
    qk_out[...] = qk_got[...]
    v_out[...] = v_got[...]


def middle(rows, w_all, w_query, w_key, collective_id):
    n = w_all.shape[0]
    chunk = rows.shape[0]
    qk_shape = (n, 2 * w_query.shape[1] // n, chunk)
    v_shape = (n, chunk, w_all.shape[2])
    return pl.pallas_call(
        middle_kernel,
        out_shape=(
            jax.ShapeDtypeStruct(qk_shape, rows.dtype),
            jax.ShapeDtypeStruct(v_shape, rows.dtype),
        ),
        in_specs=[pl.BlockSpec(memory_space=pltpu.VMEM)] * 4,
        out_specs=(pl.BlockSpec(memory_space=pltpu.VMEM), pl.BlockSpec(memory_space=pltpu.VMEM)),
        scratch_shapes=[
            pltpu.VMEM(qk_shape, rows.dtype),
            pltpu.VMEM(v_shape, rows.dtype),
            pltpu.VMEM(qk_shape, rows.dtype),
            pltpu.VMEM(v_shape, rows.dtype),
            pltpu.VMEM((w_query.shape[1], chunk), jnp.float32),
            pltpu.VMEM((w_key.shape[1], chunk), jnp.float32),
            pltpu.SemaphoreType.DMA((2, n)),
            pltpu.SemaphoreType.DMA((2, n)),
            pltpu.SemaphoreType.DMA((2,)),
        ],
        compiler_params=pltpu.CompilerParams(
            collective_id=collective_id, has_side_effects=True, vmem_limit_bytes=48 * 1024 * 1024
        ),
    )(rows, w_all, w_query, w_key)


def attend(query_rows, key_rows, value_rows, gain_mine, my_slab):
    highest = lax.Precision.DEFAULT
    tok_rows, per_group, _ = value_rows.shape
    blocks = tok_rows // BLOCK
    query_blocks = query_rows.reshape(blocks, BLOCK, per_group, FEAT)
    key_blocks = key_rows.reshape(blocks, BLOCK, per_group, FEAT)
    value_blocks = value_rows.reshape(blocks, BLOCK, per_group, HEAD_DIM)
    value_f32 = value_blocks.astype(jnp.float32)
    key_linear, key_square = feature_parts(key_blocks.astype(jnp.float32))
    own_zero = jnp.sum(value_f32, axis=1)[:, :, None, :]
    own_one = jnp.einsum("bthf,bthe->bhfe", key_linear, value_f32, precision=highest)
    own_two = jnp.einsum("bthf,bthe->bhfe", key_square, value_f32, precision=highest)
    own = jnp.concatenate([own_zero, own_one, own_two], axis=2)
    slab_total = jnp.sum(own, axis=0)
    state_rows = slab_total.shape[0] * slab_total.shape[1]
    prefix = scan_seq(slab_total.astype(jnp.bfloat16).reshape(state_rows, HEAD_DIM), 7).reshape(slab_total.shape)
    earlier = jnp.concatenate([jnp.zeros_like(own[:1]), jnp.cumsum(own, axis=0)[:-1]], axis=0) + prefix[None]
    query_linear, query_square = feature_parts(query_blocks.astype(jnp.float32))
    inter = earlier[:, :, 0][:, None] + jnp.einsum(
        "bthf,bhfe->bthe", query_linear, earlier[:, :, 1 : 1 + FEAT], precision=highest
    )
    inter = inter + jnp.einsum(
        "bthf,bhfe->bthe", query_square, earlier[:, :, 1 + FEAT :], precision=highest
    )
    scores = jnp.einsum(
        "bthf,bshf->bhts", query_blocks, key_blocks, preferred_element_type=jnp.float32
    ) * FEAT ** (-0.5)
    kernel = 1.0 + scores + 0.5 * scores * scores
    causal = jnp.arange(BLOCK)[:, None] >= jnp.arange(BLOCK)[None, :]
    weights = jnp.where(causal, kernel, 0.0).astype(jnp.bfloat16)
    intra = jnp.einsum("bhts,bshe->bthe", weights, value_blocks, preferred_element_type=jnp.float32)
    numerator = (intra + inter).reshape(tok_rows, per_group, HEAD_DIM)
    mean_square = jnp.mean(numerator * numerator, axis=-1, keepdims=True)
    hidden = (numerator * lax.rsqrt(mean_square + 1e-05) * gain_mine).astype(jnp.bfloat16)
    return hidden.reshape(tok_rows, per_group * HEAD_DIM)


def per_device(tokens, w_query, w_key, w_value, w_out, gain):
    groups = lax.axis_size(CHAN)
    per_group = HEADS // groups
    my_group = chan_index()
    my_slab = lax.axis_index("seq")
    tok_rows_total, tok_cols = tokens.shape
    got, value_all = opening(tokens.reshape(groups, tok_rows_total // groups, tok_cols), w_value, 1)
    rows = got.transpose(1, 0, 2).reshape(tok_rows_total // groups, groups * tok_cols)
    chunk = rows.shape[0]
    pf = per_group * FEAT
    d_model = w_query.shape[0]
    qk_got, value_got = middle(rows, value_all, w_query, w_key, 2)
    tok_rows = groups * chunk
    qk_rows = qk_got.transpose(0, 2, 1).reshape(tok_rows, 2 * pf)
    query_rows = qk_rows[:, :pf].reshape(tok_rows, per_group, FEAT)
    key_rows = qk_rows[:, pf:].reshape(tok_rows, per_group, FEAT)
    value_rows = value_got.reshape(tok_rows, per_group, HEAD_DIM)
    value_cols = per_group * HEAD_DIM
    gain_mine = lax.dynamic_slice_in_dim(gain, my_group * value_cols, value_cols, 0).reshape(
        per_group, HEAD_DIM
    )
    hidden = attend(query_rows, key_rows, value_rows, gain_mine, my_slab)
    out_cols = w_out.shape[1] // groups
    mixed_blocks = closing(hidden.reshape(groups, chunk, per_group * HEAD_DIM), w_out, 3)
    return mixed_blocks.reshape(tok_rows, out_cols)

def solution(mesh):
    seq, chan = mesh.devices.shape
    cores = 2 if chan % 2 == 0 else 1
    split = jax.sharding.Mesh(mesh.devices.reshape(seq, chan // cores, cores), ("seq", "z", "core"))
    return jax.shard_map(
        per_device,
        mesh=split,
        in_specs=(P("seq", CHAN), P(), P(), P(None, CHAN), P(), P()),
        out_specs=P("seq", CHAN),
        check_vma=False,
    )
```

```python
import functools

import jax
import jax.numpy as jnp
from jax import lax
from jax.experimental import pallas as pl
from jax.experimental.pallas import tpu as pltpu
from jax.sharding import PartitionSpec as P

MESH = pl.DeviceIdType.MESH
CHAN = ("z", "core")
W_PIECES = 4


def chan_index():
    return lax.axis_index("z") * lax.axis_size("core") + lax.axis_index("core")


def chan_device(slab, peer):
    cores = lax.axis_size("core")
    return (slab, peer // cores, peer % cores)

HEADS = 16
FEAT = 16
HEAD_DIM = 128
BLOCK = 896


def feature_parts(rows):
    linear = rows * FEAT ** (-0.25)
    square = (rows[..., :, None] * rows[..., None, :]).reshape(rows.shape[:-1] + (FEAT * FEAT,)) * (
        2.0 * FEAT
    ) ** (-0.5)
    return (linear, square)


def exchange_kernel(count, *refs):
    xs, ys, bufs = refs[:count], refs[count : 2 * count], refs[2 * count : 3 * count]
    send_sem, recv_sem, own_sem = refs[3 * count :]
    n = xs[0].shape[0]
    me = chan_index()
    slab = lax.axis_index("seq")
    barrier = pltpu.get_barrier_semaphore()
    for step in range(1, n):
        peer = lax.rem(me + step, n)
        pl.semaphore_signal(barrier, inc=1, device_id=chan_device(slab, peer), device_id_type=MESH)
    pl.semaphore_wait(barrier, n - 1)
    owns = []
    sends = []
    for a in range(count):
        own = pltpu.make_async_copy(xs[a].at[me], bufs[a].at[me], own_sem.at[a])
        own.start()
        owns.append(own)
    for step in range(1, n):
        peer = lax.rem(me + step, n)
        for a in range(count):
            copy = pltpu.make_async_remote_copy(
                src_ref=xs[a].at[peer],
                dst_ref=bufs[a].at[me],
                send_sem=send_sem.at[a, peer],
                recv_sem=recv_sem.at[a, me],
                device_id=chan_device(slab, peer),
                device_id_type=MESH,
            )
            copy.start()
            sends.append(copy)
    for step in range(1, n):
        source = lax.rem(me + n - step, n)
        for a in range(count):
            pltpu.make_async_remote_copy(
                src_ref=xs[a].at[source],
                dst_ref=bufs[a].at[source],
                send_sem=send_sem.at[a, source],
                recv_sem=recv_sem.at[a, source],
                device_id=chan_device(slab, source),
                device_id_type=MESH,
            ).wait_recv()
    for copy in sends:
        copy.wait_send()
    for a in range(count):
        owns[a].wait()
        ys[a][...] = bufs[a][...]


def exchange_many(xs, collective_id):
    count = len(xs)
    n = xs[0].shape[0]
    return pl.pallas_call(
        functools.partial(exchange_kernel, count),
        out_shape=tuple(jax.ShapeDtypeStruct(x.shape, x.dtype) for x in xs),
        in_specs=[pl.BlockSpec(memory_space=pltpu.VMEM)] * count,
        out_specs=tuple(pl.BlockSpec(memory_space=pltpu.VMEM) for _ in xs),
        scratch_shapes=[pltpu.VMEM(x.shape, x.dtype) for x in xs]
        + [
            pltpu.SemaphoreType.DMA((count, n)),
            pltpu.SemaphoreType.DMA((count, n)),
            pltpu.SemaphoreType.DMA((count,)),
        ],
        compiler_params=pltpu.CompilerParams(collective_id=collective_id, has_side_effects=True),
    )(*xs)


def exchange(x, collective_id):
    return exchange_many((x,), collective_id)[0]


def gather_kernel(x_ref, y_ref, buf, send_sem, recv_sem):
    n = buf.shape[0]
    me = lax.axis_index("seq")
    here = (lax.axis_index("z"), lax.axis_index("core"))
    buf[...] = jnp.zeros_like(buf)
    barrier = pltpu.get_barrier_semaphore()
    for step in range(1, n):
        peer = lax.rem(me + step, n)
        pl.semaphore_signal(barrier, inc=1, device_id=(peer,) + here, device_id_type=MESH)
    pl.semaphore_wait(barrier, n - 1)

    def copy_to(peer):
        return pltpu.make_async_remote_copy(
            src_ref=x_ref,
            dst_ref=buf.at[me],
            send_sem=send_sem.at[peer],
            recv_sem=recv_sem.at[me],
            device_id=(peer,) + here,
            device_id_type=MESH,
        )

    def copy_from(source):
        return pltpu.make_async_remote_copy(
            src_ref=x_ref,
            dst_ref=buf.at[source],
            send_sem=send_sem.at[source],
            recv_sem=recv_sem.at[source],
            device_id=(source,) + here,
            device_id_type=MESH,
        )

    for step in range(1, n):
        @pl.when(me + step < n)
        def _():
            copy_to(me + step).start()

    for step in range(1, n):
        @pl.when(me - step >= 0)
        def _():
            copy_from(me - step).wait_recv()

    for step in range(1, n):
        @pl.when(me + step < n)
        def _():
            copy_to(me + step).wait_send()

    y_ref[...] = buf[...]


def gather_seq(x, slabs, collective_id):
    shape = (slabs,) + x.shape
    return pl.pallas_call(
        gather_kernel,
        out_shape=jax.ShapeDtypeStruct(shape, x.dtype),
        in_specs=[pl.BlockSpec(memory_space=pltpu.VMEM)],
        out_specs=pl.BlockSpec(memory_space=pltpu.VMEM),
        scratch_shapes=[
            pltpu.VMEM(shape, x.dtype),
            pltpu.SemaphoreType.DMA((slabs,)),
            pltpu.SemaphoreType.DMA((slabs,)),
        ],
        compiler_params=pltpu.CompilerParams(collective_id=collective_id, has_side_effects=True),
    )(x)


def scan_kernel(width, x_ref, y_ref, row_buf, col_buf, total, row_send, row_recv, col_send, col_recv):
    n = lax.axis_size("seq")
    height = n // width
    me = lax.axis_index("seq")
    row, col = me // width, me % width
    here = (lax.axis_index("z"), lax.axis_index("core"))
    row_buf[...] = jnp.zeros_like(row_buf)
    col_buf[...] = jnp.zeros_like(col_buf)
    barrier = pltpu.get_barrier_semaphore()
    for step in range(1, width):
        peer = row * width + lax.rem(col + step, width)
        pl.semaphore_signal(barrier, inc=1, device_id=(peer,) + here, device_id_type=MESH)
    for step in range(1, height):
        peer = lax.rem(row + step, height) * width + col
        pl.semaphore_signal(barrier, inc=1, device_id=(peer,) + here, device_id_type=MESH)
    pl.semaphore_wait(barrier, width + height - 2)

    def row_copy(c, slot):
        return pltpu.make_async_remote_copy(
            src_ref=x_ref,
            dst_ref=row_buf.at[slot],
            send_sem=row_send.at[c],
            recv_sem=row_recv.at[slot],
            device_id=(row * width + c,) + here,
            device_id_type=MESH,
        )

    sends = []
    for step in range(1, width):
        c = lax.rem(col + step, width)
        copy = row_copy(c, col)
        copy.start()
        sends.append(copy)
    for step in range(1, width):
        c = lax.rem(col + width - step, width)
        row_copy(c, c).wait_recv()
    mine = x_ref[...].astype(jnp.float32)
    row_total = mine
    row_prefix = jnp.zeros_like(mine)
    for c in range(width):
        part = jnp.where(c == col, 0.0, row_buf[c].astype(jnp.float32))
        row_total = row_total + part
        row_prefix = row_prefix + jnp.where(c < col, part, 0.0)
    total[...] = row_total

    def col_copy(r, slot):
        return pltpu.make_async_remote_copy(
            src_ref=total,
            dst_ref=col_buf.at[slot],
            send_sem=col_send.at[r],
            recv_sem=col_recv.at[slot],
            device_id=(r * width + col,) + here,
            device_id_type=MESH,
        )

    for step in range(1, height):
        @pl.when(row + step < height)
        def _():
            col_copy(row + step, row).start()

    for step in range(1, height):
        @pl.when(row - step >= 0)
        def _():
            col_copy(row - step, row - step).wait_recv()

    for step in range(1, height):
        @pl.when(row + step < height)
        def _():
            col_copy(row + step, row).wait_send()

    for copy in sends:
        copy.wait_send()
    prefix = row_prefix
    for r in range(height):
        prefix = prefix + col_buf[r]
    y_ref[...] = prefix


def scan_seq(x, collective_id):
    n = lax.axis_size("seq")
    width = 1
    while (width + 1) * (width + 1) <= n:
        width += 1
    while n % width:
        width -= 1
    height = n // width
    return pl.pallas_call(
        functools.partial(scan_kernel, width),
        out_shape=jax.ShapeDtypeStruct(x.shape, jnp.float32),
        in_specs=[pl.BlockSpec(memory_space=pltpu.VMEM)],
        out_specs=pl.BlockSpec(memory_space=pltpu.VMEM),
        scratch_shapes=[
            pltpu.VMEM((width,) + x.shape, x.dtype),
            pltpu.VMEM((height,) + x.shape, jnp.float32),
            pltpu.VMEM(x.shape, jnp.float32),
            pltpu.SemaphoreType.DMA((width,)),
            pltpu.SemaphoreType.DMA((width,)),
            pltpu.SemaphoreType.DMA((height,)),
            pltpu.SemaphoreType.DMA((height,)),
        ],
        compiler_params=pltpu.CompilerParams(collective_id=collective_id, has_side_effects=True),
    )(x)


def swap_kernel(x_ref, y_ref, send_sem, recv_sem):
    here = (lax.axis_index("seq"), lax.axis_index("z"))
    other = lax.axis_size("core") - 1 - lax.axis_index("core")
    barrier = pltpu.get_barrier_semaphore()
    pl.semaphore_signal(barrier, inc=1, device_id=here + (other,), device_id_type=MESH)
    pl.semaphore_wait(barrier, 1)
    copy = pltpu.make_async_remote_copy(
        src_ref=x_ref,
        dst_ref=y_ref,
        send_sem=send_sem,
        recv_sem=recv_sem,
        device_id=here + (other,),
        device_id_type=MESH,
    )
    copy.start()
    copy.wait()


def swap_cores(x, collective_id):
    return pl.pallas_call(
        swap_kernel,
        out_shape=jax.ShapeDtypeStruct(x.shape, x.dtype),
        in_specs=[pl.BlockSpec(memory_space=pl.ANY)],
        out_specs=pl.BlockSpec(memory_space=pl.ANY),
        scratch_shapes=[pltpu.SemaphoreType.DMA(()), pltpu.SemaphoreType.DMA(())],
        compiler_params=pltpu.CompilerParams(collective_id=collective_id, has_side_effects=True),
    )(x)


def opening_kernel(x_ref, w_ref, y_ref, w_all, buf, send_sem, recv_sem, own_sem, w_send, w_recv, w_own):
    n = x_ref.shape[0]
    cores = lax.axis_size("core")
    ring = n // cores
    me = chan_index()
    slab = lax.axis_index("seq")
    z = lax.axis_index("z")
    core = lax.axis_index("core")
    barrier = pltpu.get_barrier_semaphore()
    for step in range(1, n):
        peer = lax.rem(me + step, n)
        pl.semaphore_signal(barrier, inc=1, device_id=chan_device(slab, peer), device_id_type=MESH)
    pl.semaphore_wait(barrier, n - 1)
    own = pltpu.make_async_copy(x_ref.at[me], buf.at[me], own_sem)
    own.start()
    sends = []
    for step in range(1, n):
        peer = lax.rem(me + step, n)
        copy = pltpu.make_async_remote_copy(
            src_ref=x_ref.at[peer],
            dst_ref=buf.at[me],
            send_sem=send_sem.at[peer],
            recv_sem=recv_sem.at[me],
            device_id=chan_device(slab, peer),
            device_id_type=MESH,
        )
        copy.start()
        sends.append(copy)
    w_local = pltpu.make_async_copy(w_ref, w_all.at[me], w_own)
    w_local.start()
    right = (slab, lax.rem(z + 1, ring), core)
    left = (slab, lax.rem(z + ring - 1, ring), core)
    partner = (slab, z, cores - 1 - core)

    pieces = W_PIECES
    depth = w_ref.shape[0] // pieces

    def slot(origin):
        return lax.rem(origin + ring, ring) * cores + core

    def held(h, j):
        return w_all.at[h, pl.ds(j * depth, depth)]

    def send(source, h, j, kind, target):
        copy = pltpu.make_async_remote_copy(
            src_ref=source,
            dst_ref=held(h, j),
            send_sem=w_send.at[h, kind, j],
            recv_sem=w_recv.at[h, j],
            device_id=target,
            device_id_type=MESH,
        )
        copy.start()
        sends.append(copy)

    def arrive(h, j, source):
        pltpu.make_async_remote_copy(
            src_ref=w_ref.at[pl.ds(j * depth, depth)],
            dst_ref=held(h, j),
            send_sem=w_send.at[h, 0, j],
            recv_sem=w_recv.at[h, j],
            device_id=source,
            device_id_type=MESH,
        ).wait_recv()

    half = ring // 2
    full = half - 1 if ring % 2 == 0 else half

    def goes_right(step):
        return range(pieces) if step <= full else range(pieces // 2) if step == half else range(0)

    def goes_left(step):
        return range(pieces) if step <= full else range(pieces // 2, pieces) if step == half else range(0)

    for j in range(pieces):
        mine = w_ref.at[pl.ds(j * depth, depth)]
        if j in goes_right(1):
            send(mine, me, j, 0, right)
        if j in goes_left(1):
            send(mine, me, j, 1, left)
        send(mine, me, j, 2, partner)
    for step in range(1, half + 1):
        for j in range(pieces):
            if j in goes_right(step):
                h = slot(z - step)
                arrive(h, j, left)
                if j in goes_right(step + 1):
                    send(held(h, j), h, j, 0, right)
                send(held(h, j), h, j, 2, partner)
            if j in goes_left(step):
                h = slot(z + step)
                arrive(h, j, right)
                if j in goes_left(step + 1):
                    send(held(h, j), h, j, 1, left)
                send(held(h, j), h, j, 2, partner)
    for origin in range(ring):
        for j in range(pieces):
            arrive(origin * cores + (cores - 1 - core), j, partner)
    for step in range(1, n):
        source = lax.rem(me + n - step, n)
        pltpu.make_async_remote_copy(
            src_ref=x_ref.at[source],
            dst_ref=buf.at[source],
            send_sem=send_sem.at[source],
            recv_sem=recv_sem.at[source],
            device_id=chan_device(slab, source),
            device_id_type=MESH,
        ).wait_recv()
    for copy in sends:
        copy.wait_send()
    own.wait()
    w_local.wait()
    y_ref[...] = buf[...]


def opening(x, w, collective_id):
    n = x.shape[0]
    return pl.pallas_call(
        opening_kernel,
        out_shape=(
            jax.ShapeDtypeStruct(x.shape, x.dtype),
            jax.ShapeDtypeStruct((n,) + w.shape, w.dtype),
        ),
        in_specs=[pl.BlockSpec(memory_space=pltpu.VMEM), pl.BlockSpec(memory_space=pl.ANY)],
        out_specs=(pl.BlockSpec(memory_space=pltpu.VMEM), pl.BlockSpec(memory_space=pl.ANY)),
        scratch_shapes=[
            pltpu.VMEM(x.shape, x.dtype),
            pltpu.SemaphoreType.DMA((n,)),
            pltpu.SemaphoreType.DMA((n,)),
            pltpu.SemaphoreType.DMA(()),
            pltpu.SemaphoreType.DMA((n, 3, W_PIECES)),
            pltpu.SemaphoreType.DMA((n, W_PIECES)),
            pltpu.SemaphoreType.DMA(()),
        ],
        compiler_params=pltpu.CompilerParams(collective_id=collective_id, has_side_effects=True),
    )(x, w)


def split_rows(x, groups, collective_id):
    rows, cols = x.shape
    got = exchange(x.reshape(groups, rows // groups, cols), collective_id)
    return got.transpose(1, 0, 2).reshape(rows // groups, groups * cols)


def split_cols(x, groups, collective_id):
    rows, _, cols = x.shape
    got = exchange(x.transpose(1, 0, 2), collective_id)
    return got.reshape(groups * rows, cols)


def closing_kernel(x_ref, w_ref, y_ref, got, rows, out, back, send_sem, recv_sem, own_sem):
    n = x_ref.shape[0]
    cols = out.shape[2]
    me = chan_index()
    slab = lax.axis_index("seq")
    barrier = pltpu.get_barrier_semaphore()
    for step in range(1, n):
        peer = lax.rem(me + step, n)
        pl.semaphore_signal(barrier, inc=1, device_id=chan_device(slab, peer), device_id_type=MESH)
    pl.semaphore_wait(barrier, n - 1)

    def remote(phase, src, dst, peer, sender):
        return pltpu.make_async_remote_copy(
            src_ref=src,
            dst_ref=dst,
            send_sem=send_sem.at[phase, peer],
            recv_sem=recv_sem.at[phase, sender],
            device_id=chan_device(slab, peer),
            device_id_type=MESH,
        )

    sends = []
    for phase, (source, landing) in enumerate(((x_ref, got), (out, back))):
        own = pltpu.make_async_copy(source.at[me], landing.at[me], own_sem.at[phase])
        if phase == 1:
            hidden_rows = rows[...]
            for step in range(n):
                c = lax.rem(me + step, n)
                block = w_ref[:, pl.ds(pl.multiple_of(c * cols, cols), cols)]
                out[c] = jnp.dot(hidden_rows, block, preferred_element_type=jnp.float32).astype(out.dtype)
                if step == 0:
                    own.start()
                else:
                    copy = remote(phase, out.at[c], back.at[me], c, me)
                    copy.start()
                    sends.append(copy)
        else:
            own.start()
            for step in range(1, n):
                peer = lax.rem(me + step, n)
                copy = remote(phase, x_ref.at[peer], got.at[me], peer, me)
                copy.start()
                sends.append(copy)
        for step in range(1, n):
            source_dev = lax.rem(me + n - step, n)
            remote(phase, source.at[source_dev], landing.at[source_dev], source_dev, source_dev).wait_recv()
        own.wait()
        if phase == 0:
            width = got.shape[2]
            for g in range(n):
                rows[:, g * width : (g + 1) * width] = got[g]
    for copy in sends:
        copy.wait_send()
    y_ref[...] = back[...]


def closing(hidden_blocks, w_out, collective_id):
    n, chunk, width = hidden_blocks.shape
    cols = w_out.shape[1] // n
    block = (n, chunk, cols)
    return pl.pallas_call(
        closing_kernel,
        out_shape=jax.ShapeDtypeStruct(block, hidden_blocks.dtype),
        in_specs=[pl.BlockSpec(memory_space=pltpu.VMEM)] * 2,
        out_specs=pl.BlockSpec(memory_space=pltpu.VMEM),
        scratch_shapes=[
            pltpu.VMEM(hidden_blocks.shape, hidden_blocks.dtype),
            pltpu.VMEM((chunk, n * width), hidden_blocks.dtype),
            pltpu.VMEM(block, hidden_blocks.dtype),
            pltpu.VMEM(block, hidden_blocks.dtype),
            pltpu.SemaphoreType.DMA((2, n)),
            pltpu.SemaphoreType.DMA((2, n)),
            pltpu.SemaphoreType.DMA((2,)),
        ],
        compiler_params=pltpu.CompilerParams(
            collective_id=collective_id, has_side_effects=True, vmem_limit_bytes=48 * 1024 * 1024
        ),
    )(hidden_blocks, w_out)


def middle_kernel(rows_ref, w_ref, wq_ref, wk_ref, qk_out, v_out, qk_send, v_send, qk_got, v_got, q_all, k_all, send_sem, recv_sem, own_sem):
    n = w_ref.shape[0]
    me = chan_index()
    slab = lax.axis_index("seq")
    barrier = pltpu.get_barrier_semaphore()
    for step in range(1, n):
        peer = lax.rem(me + step, n)
        pl.semaphore_signal(barrier, inc=1, device_id=chan_device(slab, peer), device_id_type=MESH)
    pl.semaphore_wait(barrier, n - 1)
    pairs = ((qk_send, qk_got), (v_send, v_got))

    def remote(kind, peer, sender, slot):
        source, landing = pairs[kind]
        return pltpu.make_async_remote_copy(
            src_ref=source.at[slot],
            dst_ref=landing.at[sender],
            send_sem=send_sem.at[kind, peer],
            recv_sem=recv_sem.at[kind, sender],
            device_id=chan_device(slab, peer),
            device_id_type=MESH,
        )

    rows = rows_ref[...]
    pf = qk_send.shape[1] // 2
    q_all[...] = jnp.dot(rows, wq_ref[...], preferred_element_type=jnp.float32).T
    k_all[...] = jnp.dot(rows, wk_ref[...], preferred_element_type=jnp.float32).T
    owns = []
    sends = []
    for step in range(n):
        g = lax.rem(me + step, n)
        v_send[g] = jnp.dot(rows, w_ref[g], preferred_element_type=jnp.float32).astype(v_send.dtype)
        head = pl.ds(pl.multiple_of(g * pf, pf), pf)
        qk_send[g, :pf, :] = q_all[head, :].astype(qk_send.dtype)
        qk_send[g, pf:, :] = k_all[head, :].astype(qk_send.dtype)
        for kind in range(2):
            source, landing = pairs[kind]
            if step == 0:
                own = pltpu.make_async_copy(source.at[me], landing.at[me], own_sem.at[kind])
                own.start()
                owns.append(own)
            else:
                copy = remote(kind, g, me, g)
                copy.start()
                sends.append(copy)
    for step in range(1, n):
        source_dev = lax.rem(me + n - step, n)
        for kind in range(2):
            remote(kind, source_dev, source_dev, source_dev).wait_recv()
    for own in owns:
        own.wait()
    for copy in sends:
        copy.wait_send()
    qk_out[...] = qk_got[...]
    v_out[...] = v_got[...]


def middle(rows, w_all, w_query, w_key, collective_id):
    n = w_all.shape[0]
    chunk = rows.shape[0]
    qk_shape = (n, 2 * w_query.shape[1] // n, chunk)
    v_shape = (n, chunk, w_all.shape[2])
    return pl.pallas_call(
        middle_kernel,
        out_shape=(
            jax.ShapeDtypeStruct(qk_shape, rows.dtype),
            jax.ShapeDtypeStruct(v_shape, rows.dtype),
        ),
        in_specs=[pl.BlockSpec(memory_space=pltpu.VMEM)] * 4,
        out_specs=(pl.BlockSpec(memory_space=pltpu.VMEM), pl.BlockSpec(memory_space=pltpu.VMEM)),
        scratch_shapes=[
            pltpu.VMEM(qk_shape, rows.dtype),
            pltpu.VMEM(v_shape, rows.dtype),
            pltpu.VMEM(qk_shape, rows.dtype),
            pltpu.VMEM(v_shape, rows.dtype),
            pltpu.VMEM((w_query.shape[1], chunk), jnp.float32),
            pltpu.VMEM((w_key.shape[1], chunk), jnp.float32),
            pltpu.SemaphoreType.DMA((2, n)),
            pltpu.SemaphoreType.DMA((2, n)),
            pltpu.SemaphoreType.DMA((2,)),
        ],
        compiler_params=pltpu.CompilerParams(
            collective_id=collective_id, has_side_effects=True, vmem_limit_bytes=48 * 1024 * 1024
        ),
    )(rows, w_all, w_query, w_key)


def attend(query_rows, key_rows, value_rows, gain_mine, my_slab):
    highest = lax.Precision.DEFAULT
    tok_rows, per_group, _ = value_rows.shape
    blocks = tok_rows // BLOCK
    query_blocks = query_rows.reshape(blocks, BLOCK, per_group, FEAT)
    key_blocks = key_rows.reshape(blocks, BLOCK, per_group, FEAT)
    value_blocks = value_rows.reshape(blocks, BLOCK, per_group, HEAD_DIM)
    value_f32 = value_blocks.astype(jnp.float32)
    key_linear, key_square = feature_parts(key_blocks.astype(jnp.float32))
    own_zero = jnp.sum(value_f32, axis=1)[:, :, None, :]
    own_one = jnp.einsum("bthf,bthe->bhfe", key_linear, value_f32, precision=highest)
    own_two = jnp.einsum("bthf,bthe->bhfe", key_square, value_f32, precision=highest)
    own = jnp.concatenate([own_two, own_one, own_zero], axis=2)
    slab_total = jnp.sum(own, axis=0)
    state_rows = slab_total.shape[0] * slab_total.shape[1]
    prefix = scan_seq(slab_total.astype(jnp.bfloat16).reshape(state_rows, HEAD_DIM), 7).reshape(slab_total.shape)
    earlier = jnp.concatenate([jnp.zeros_like(own[:1]), jnp.cumsum(own, axis=0)[:-1]], axis=0) + prefix[None]
    query_linear, query_square = feature_parts(query_blocks.astype(jnp.float32))
    square_rows = FEAT * FEAT
    inter = earlier[:, :, square_rows + FEAT][:, None] + jnp.einsum(
        "bthf,bhfe->bthe", query_linear, earlier[:, :, square_rows : square_rows + FEAT], precision=highest
    )
    inter = inter + jnp.einsum(
        "bthf,bhfe->bthe", query_square, earlier[:, :, :square_rows], precision=highest
    )
    scores = jnp.einsum(
        "bthf,bshf->bhts", query_blocks, key_blocks, preferred_element_type=jnp.float32
    ) * FEAT ** (-0.5)
    kernel = 1.0 + scores + 0.5 * scores * scores
    causal = jnp.arange(BLOCK)[:, None] >= jnp.arange(BLOCK)[None, :]
    weights = jnp.where(causal, kernel, 0.0).astype(jnp.bfloat16)
    intra = jnp.einsum("bhts,bshe->bthe", weights, value_blocks, preferred_element_type=jnp.float32)
    numerator = (intra + inter).reshape(tok_rows, per_group, HEAD_DIM)
    mean_square = jnp.mean(numerator * numerator, axis=-1, keepdims=True)
    hidden = (numerator * lax.rsqrt(mean_square + 1e-05) * gain_mine).astype(jnp.bfloat16)
    return hidden.reshape(tok_rows, per_group * HEAD_DIM)


def per_device(tokens, w_query, w_key, w_value, w_out, gain):
    groups = lax.axis_size(CHAN)
    per_group = HEADS // groups
    my_group = chan_index()
    my_slab = lax.axis_index("seq")
    tok_rows_total, tok_cols = tokens.shape
    got, value_all = opening(tokens.reshape(groups, tok_rows_total // groups, tok_cols), w_value, 1)
    rows = got.transpose(1, 0, 2).reshape(tok_rows_total // groups, groups * tok_cols)
    chunk = rows.shape[0]
    pf = per_group * FEAT
    d_model = w_query.shape[0]
    qk_got, value_got = middle(rows, value_all, w_query, w_key, 2)
    tok_rows = groups * chunk
    qk_rows = qk_got.transpose(0, 2, 1).reshape(tok_rows, 2 * pf)
    query_rows = qk_rows[:, :pf].reshape(tok_rows, per_group, FEAT)
    key_rows = qk_rows[:, pf:].reshape(tok_rows, per_group, FEAT)
    value_rows = value_got.reshape(tok_rows, per_group, HEAD_DIM)
    value_cols = per_group * HEAD_DIM
    gain_mine = lax.dynamic_slice_in_dim(gain, my_group * value_cols, value_cols, 0).reshape(
        per_group, HEAD_DIM
    )
    hidden = attend(query_rows, key_rows, value_rows, gain_mine, my_slab)
    out_cols = w_out.shape[1] // groups
    mixed_blocks = closing(hidden.reshape(groups, chunk, per_group * HEAD_DIM), w_out, 3)
    return mixed_blocks.reshape(tok_rows, out_cols)

def solution(mesh):
    seq, chan = mesh.devices.shape
    cores = 2 if chan % 2 == 0 else 1
    split = jax.sharding.Mesh(mesh.devices.reshape(seq, chan // cores, cores), ("seq", "z", "core"))
    return jax.shard_map(
        per_device,
        mesh=split,
        in_specs=(P("seq", CHAN), P(), P(), P(None, CHAN), P(), P()),
        out_specs=P("seq", CHAN),
        check_vma=False,
    )
```
